32 devices in a mesh: dp: 16 (over z, y, x), head: 2 (over core).
Axes of the slice: x: 2, y: 2, z: 4, core: 2. Of those that a mesh axis runs over, the one named last changes fastest.
Arguments:
- tokens: bfloat16 [49152, 384], P(('dp', 'head')), may hold values from -6 to 6
- cotangent: bfloat16 [49152, 384], P(('dp', 'head')), may hold values from -6 to 6
- token_counts: int32 [192], P('dp'), may hold values from 64 to 256, as said below
- head_mask: int32 [192, 6], P('dp', 'head'), may hold values 0 or 1
- norm_params: float32 [4, 384], replicated, may hold values from -2 to 2
- norm_state: float32 [4, 384], replicated, may hold values from 0.1 to 1
- weights: float32 [2, 3, 128, 48, 48], P('head', None, 'dp'), may hold values from -1 to 1
- stat_left: float32 [2, 3, 128, 48, 48], P('head', None, 'dp'), may hold values from 0 to 2, as said below
- stat_right: float32 [2, 3, 128, 48, 48], P('head', None, 'dp'), may hold values from 0 to 2, as said below
Outputs:
- block_out: float32 [49152, 384], P(('dp', 'head'))
- input_grad: float32 [49152, 384], P(('dp', 'head'))
- weight_grads: float32 [2, 3, 128, 48, 48], P('head', None, 'dp')
- left_new: float32 [2, 3, 128, 48, 48], P('head', None, 'dp')
- right_new: float32 [2, 3, 128, 48, 48], P('head', None, 'dp')
- new_weights: float32 [2, 3, 128, 48, 48], P('head', None, 'dp')
- norm_grads: float32 [4, 384], replicated
- state_new: float32 [4, 384], replicated
- norm_new: float32 [4, 384], replicated
The draws below stay inside these ranges and needn't reach their ends.
Inputs may be any that keep to these rules, and one draw needn't show every extreme that they name: `token_counts`: some image has all 256 tokens valid and some has a quarter of 256. `stat_left`: diagonal and positive. `stat_right`: diagonal and positive.
All inputs are finite; a program needn't handle non-finite values. No bound on the sum of `head_mask` on one device may be relied on, other than what follows from the above.
Results may differ from the reference program's by a relative error of at most 0.0092.
Values may be sent and summed in bfloat16 or wider, within the bound.
No kernel may reach another device: no remote copies, remote signals or barrier semaphores. Data moves between devices by JAX's collectives and lax.ppermute only.
A program may use at most 128 MiB of HBM per device.

```python
import math
import jax
import jax.numpy as jnp
from jax import lax

D = 384
HEADS = 6
HEAD_DIM = 64
MLP = 1536
S = 256
ITERS = 8
BLK = 48
IMAGES = 192
TOKENS = 49152


def draw_weights(key, part):
    key = jax.random.fold_in(key, 3)
    base = jnp.clip(jax.random.normal(key, (2, 3, 128, BLK, BLK), jnp.float32), -1.7320508, 1.7320508)
    block_index = lax.broadcasted_iota(jnp.int32, (1, 3, 128, 1, 1), 2)
    group_index = lax.broadcasted_iota(jnp.int32, (1, 3, 128, 1, 1), 1)
    scaling = jnp.where(group_index == 2, MLP ** (-0.5), D ** (-0.5))
    scaling = jnp.where((group_index == 0) & (block_index >= 96), 4.0 * D ** (-0.5), scaling)
    return base * scaling


def statistic(key):
    diagonal = jnp.exp(jax.random.uniform(key, (2, 3, 128, BLK), jnp.float32, math.log(0.02), math.log(2.0)))
    identity = jnp.eye(BLK, dtype=jnp.float32)
    return diagonal[..., None] * identity


def draw_stat_left(key, part):
    return statistic(jax.random.fold_in(key, 1))


def draw_stat_right(key, part):
    return statistic(jax.random.fold_in(key, 2))


def draw_norm_params(key, part):
    key = jax.random.fold_in(key, 4)
    key_gain, key_shift = jax.random.split(key)
    gains = 1.0 + 0.1 * jnp.clip(jax.random.normal(key_gain, (4, D), jnp.float32), -3.0, 3.0)
    shifts = 0.3 * jnp.clip(jax.random.normal(key_shift, (4, D), jnp.float32), -5.0, 5.0)
    row_index = lax.broadcasted_iota(jnp.int32, (4, D), 0)
    return jnp.where(row_index % 2 == 0, gains, shifts)


def draw_token_counts(key, part):
    key = jax.random.fold_in(key, 5)
    key_counts, key_longest, key_offset = jax.random.split(key, 3)
    counts = jax.random.randint(key_counts, (IMAGES,), S // 4, S + 1)
    longest = jax.random.randint(key_longest, (), 0, IMAGES)
    offset = jax.random.randint(key_offset, (), 1, IMAGES)
    shortest = (longest + offset) % IMAGES
    positions = lax.broadcasted_iota(jnp.int32, (IMAGES,), 0)
    counts = jnp.where(positions == longest, S, counts)
    return jnp.where(positions == shortest, S // 4, counts).astype(jnp.int32)


def touch_ends(values, key, least, high):
    dims = values.shape
    spot = [jax.random.randint(jax.random.fold_in(key, axis), (), 0, dims[axis]) for axis in range(len(dims))]
    values = values.at[tuple(spot)].set(least)
    longest = dims.index(max(dims))
    spot[longest] = (spot[longest] + 1) % dims[longest]
    return values.at[tuple(spot)].set(high)


def level_of(own_key, extent, cuts, smallest, largest):
    def one(dim, blocks):
        draws = jax.random.uniform(jax.random.fold_in(jax.random.fold_in(own_key, 6), dim), (blocks,), jnp.float32, smallest / len(cuts), largest / len(cuts))
        return jnp.repeat(jnp.exp(draws), extent[dim] // blocks).reshape((-1,) + (1,) * (len(extent) - dim - 1))

    level = one(*cuts[0])
    for cut in cuts[1:]:
        level = level * one(*cut)
    return level


def noise(own_key, extent, deviation, most, shards=(), held_as=jnp.bfloat16):
    array = jax.random.normal(own_key, extent, jnp.float32) * deviation
    if len(shards) > 0:
        array = level_of(own_key, extent, shards, -0.22, 0.18) * array
    return jnp.clip(array, min=-most, max=most).astype(held_as)


def setup_inputs(seed: int = 0) -> dict:
    key_list = jax.random.split(jax.random.key(seed), 10)
    tokens = noise(key_list[0], (TOKENS, D), 1.0, 6.0, ((0, 32),))
    cotangent = noise(key_list[1], (TOKENS, D), 1.0, 6.0, ((0, 32),))
    token_counts = draw_token_counts(jax.random.fold_in(key_list[9], 71), 0)
    head_mask = touch_ends((jax.random.randint(key_list[3], (IMAGES, HEADS), 0, 4) < 3).astype(jnp.int32), jax.random.fold_in(key_list[3], 1), 0, 1)
    norm_params = draw_norm_params(jax.random.fold_in(key_list[9], 71), 0)
    norm_state = jnp.clip(jnp.exp(jax.random.uniform(key_list[5], (4, D), jnp.float32, math.log(0.1), math.log(1.0))), 0.1, 1.0)
    weights = draw_weights(jax.random.fold_in(key_list[9], 71), 0)
    stat_left = draw_stat_left(jax.random.fold_in(key_list[9], 71), 0)
    stat_right = draw_stat_right(jax.random.fold_in(key_list[9], 71), 0)
    return {"tokens": tokens, "cotangent": cotangent, "token_counts": token_counts, "head_mask": head_mask, "norm_params": norm_params, "norm_state": norm_state, "weights": weights, "stat_left": stat_left, "stat_right": stat_right}


@jax.custom_vjp
def low(v):
    return lax.optimization_barrier(v.astype(jnp.bfloat16)).astype(jnp.float32)

@jax.custom_vjp
def low_back(v):
    return v

def low_keep(v):
    return (low(v), None)

def low_pass(kept, grad):
    return (grad,)

def back_keep(v):
    return (v, None)

def back_low(kept, grad):
    return (low(grad),)
low.defvjp(low_keep, low_pass)
low_back.defvjp(back_keep, back_low)

def matmul(left, right):
    return jnp.dot(left, right, precision=lax.Precision.HIGHEST, preferred_element_type=jnp.float32)

def batched(left, right):
    return jnp.einsum('...ij,...jk->...ik', left, right, precision=lax.Precision.HIGHEST)

def unpack(blocks, row_count, col_count):
    edge = blocks.shape[-1]
    shaped = blocks.reshape(row_count // edge, col_count // edge, edge, edge)
    return shaped.transpose(0, 2, 1, 3).reshape(row_count, col_count)

def layer_norm(values, gain, shift):
    centered = values - lax.optimization_barrier(jnp.mean(values, axis=-1, keepdims=True))
    variance = lax.optimization_barrier(jnp.mean(centered * centered, axis=-1, keepdims=True))
    return centered * lax.rsqrt(variance + 1e-06) * gain + shift

def attend(pieces):
    queries, keys_all, values_all, counts, heads_on = pieces
    scores = jnp.einsum('gqhd,gkhd->ghqk', queries, keys_all, precision=lax.Precision.HIGHEST)
    scores = low_back(0.125 * scores)
    position = jnp.arange(scores.shape[-1])
    key_valid = position[None, :] < counts[:, None]
    scores = jnp.where(key_valid[:, None, None, :], scores, -1e+30)
    row_max = lax.optimization_barrier(jnp.max(scores, axis=-1, keepdims=True))
    exp_scores = jnp.exp(scores - row_max)
    probabilities = low(exp_scores / lax.optimization_barrier(jnp.sum(exp_scores, axis=-1, keepdims=True)))
    head_out = jnp.einsum('ghqk,gkhd->gqhd', probabilities, values_all, precision=lax.Precision.HIGHEST)
    head_out = head_out * heads_on[:, None, :, None]
    return low(low_back(head_out))

def inverse_root(matrix):
    identity = jnp.eye(matrix.shape[-1], dtype=matrix.dtype)
    frobenius = jnp.sqrt(lax.optimization_barrier(jnp.sum(matrix * matrix, axis=(-2, -1), keepdims=True)))
    factor = 2.5 / frobenius
    result = jnp.sqrt(jnp.sqrt(factor)) * identity
    current = factor * matrix
    for iteration in range(ITERS):
        middle = (5.0 * identity - current) * 0.25
        result = batched(result, middle)
        square = batched(middle, middle)
        current = batched(batched(square, square), current)
    return result

def reference(tokens, cotangent, token_counts, head_mask, norm_params, norm_state, weights, stat_left, stat_right):
    inputs = tokens.astype(jnp.float32)
    heads_on = head_mask.astype(jnp.float32)
    group_count = IMAGES // 16

    def grouped(values):
        return values.reshape(group_count, 16, S, HEADS, HEAD_DIM)

    def forward(inputs, norm_params, weights):
        normed_one = low(layer_norm(inputs, norm_params[0], norm_params[1]))
        query_parts, key_parts, value_parts = ([], [], [])
        out_parts, up_parts, down_parts = ([], [], [])
        for half_index in range(2):
            qkv_weight = low(unpack(weights[half_index, 0, :96], D, 3 * D // 2))
            out_parts.append(low(unpack(weights[half_index, 0, 96:], D // 2, D)))
            up_parts.append(low(unpack(weights[half_index, 1], D, MLP // 2)))
            down_parts.append(low(unpack(weights[half_index, 2], MLP // 2, D)))
            projected = low(low_back(matmul(normed_one, qkv_weight)))
            split_heads = projected.reshape(TOKENS, 3, HEADS // 2, HEAD_DIM)
            query_parts.append(split_heads[:, 0])
            key_parts.append(split_heads[:, 1])
            value_parts.append(split_heads[:, 2])
        queries = jnp.concatenate(query_parts, axis=1)
        keys_all = jnp.concatenate(key_parts, axis=1)
        values_all = jnp.concatenate(value_parts, axis=1)
        attended = lax.map(jax.checkpoint(attend), (grouped(queries), grouped(keys_all), grouped(values_all), token_counts.reshape(group_count, 16), heads_on.reshape(group_count, 16, HEADS)))
        attended = attended.reshape(TOKENS, D)
        attention_out = low_back(matmul(attended, jnp.concatenate(out_parts, axis=0)))
        middle = inputs + attention_out
        normed_two = low(layer_norm(middle, norm_params[2], norm_params[3]))
        pre_act = low_back(jnp.concatenate([matmul(normed_two, up_part) for up_part in up_parts], axis=1))
        activated = low(jax.nn.gelu(pre_act, approximate=False))
        return middle + low_back(matmul(activated, jnp.concatenate(down_parts, axis=0)))
    block_out, pullback = jax.vjp(forward, inputs, norm_params, weights)
    input_grad, norm_raw, weight_raw = pullback(cotangent.astype(jnp.float32))
    scale = 1.0 / math.sqrt(TOKENS)
    grads = weight_raw * scale
    left_new = 0.5 * stat_left + 0.5 * batched(grads, jnp.swapaxes(grads, -1, -2))
    right_new = 0.5 * stat_right + 0.5 * batched(jnp.swapaxes(grads, -1, -2), grads)
    direction = batched(batched(inverse_root(left_new), grads), inverse_root(right_new))
    new_weights = weights - 0.25 * direction
    norm_grads = norm_raw * scale
    state_new = 0.5 * norm_state + 0.5 * norm_grads * norm_grads
    norm_new = norm_params - 0.2 * norm_grads / jnp.sqrt(state_new)
    return (block_out, input_grad, grads, left_new, right_new, new_weights, norm_grads, state_new, norm_new)
```

```python
import math

import jax
import jax.numpy as jnp
from jax import lax
from jax.experimental import pallas as pl
from jax.experimental.pallas import tpu as pltpu
from jax.sharding import PartitionSpec as P

D = 384
HEAD_DIM = 64
MLP = 1536
S = 256
ITERS = 8
PAIR = 2 * HEAD_DIM
PAIRS = D // PAIR
HALF = D // 2
SLABS = 16
ROOT_HALF = 0.7071067811865476
DENSITY_FACTOR = 0.3989422804014327
BF = jnp.bfloat16
F32 = jnp.float32
VMEM_LIMIT = 56 << 20


def nn(left, right):
    return jnp.dot(left, right, preferred_element_type=F32)


def nt(left, right):
    return lax.dot_general(left, right, (((1,), (1,)), ((), ())), preferred_element_type=F32)


def tn(left, right):
    return lax.dot_general(left, right, (((0,), (0,)), ((), ())), preferred_element_type=F32)


def normalize(values):
    centered = values - jnp.mean(values, axis=-1, keepdims=True)
    variance = jnp.mean(centered * centered, axis=-1, keepdims=True)
    inverse_std = lax.rsqrt(variance + 1e-06)
    return centered * inverse_std, inverse_std


def norm_backward(grad_out, normed, inverse_std, gain):
    grad_normed = grad_out * gain
    mean_first = jnp.mean(grad_normed, axis=-1, keepdims=True)
    mean_second = jnp.mean(grad_normed * normed, axis=-1, keepdims=True)
    grad_in = inverse_std * (grad_normed - mean_first - normed * mean_second)
    gain_grad = jnp.sum(grad_out * normed, axis=0, keepdims=True)
    shift_grad = jnp.sum(grad_out, axis=0, keepdims=True)
    return grad_in, jnp.concatenate([gain_grad, shift_grad], axis=0)


def lane_halves():
    lane = lax.broadcasted_iota(jnp.int32, (1, PAIR), 1)
    first = (lane < HEAD_DIM).astype(BF)
    return first, (1 - first).astype(BF)


def stacked(values, first, second):
    return jnp.concatenate([values * first, values * second], axis=0)


def attn_forward_kernel(
    counts_ref, x_ref, mask_ref, norm_ref, own_ref, other_ref,
    prob_ref, qkv_ref, out_ref, middle_ref, wqkv_ref, wo_ref,
):
    step = pl.program_id(0)

    @pl.when(step == 0)
    def _():
        slabs = (own_ref, other_ref)
        for row in range(D // 48):
            for part in range(3):
                pieces = []
                for ref in slabs:
                    slab, side = divmod(3 * row + part, 2)
                    pieces.append(ref[slab][:, side * HALF : (side + 1) * HALF])
                joined = jnp.concatenate(pieces, axis=1)
                if part == 0:
                    joined = joined * 0.125
                wqkv_ref[48 * row : 48 * row + 48, D * part : D * part + D] = joined
        for side, ref in enumerate(slabs):
            for row in range(HALF // 48):
                start = side * HALF + 48 * row
                wo_ref[start : start + 48, :] = ref[12 + row]

    x = x_ref[...].astype(F32)
    normed, _ = normalize(x)
    rows = (normed * norm_ref[0:1, :] + norm_ref[1:2, :]).astype(BF)
    qkv_ref[...] = nn(rows, wqkv_ref[...]).astype(BF)
    first, second = lane_halves()
    count = counts_ref[step]
    column = lax.broadcasted_iota(jnp.int32, (1, S), 1)
    valid = column < count
    for pair in range(PAIRS):
        lanes = slice(PAIR * pair, PAIR * (pair + 1))
        queries = qkv_ref[:, lanes]
        keys = qkv_ref[:, D + PAIR * pair : D + PAIR * (pair + 1)]
        values = qkv_ref[:, 2 * D + PAIR * pair : 2 * D + PAIR * (pair + 1)]
        scores = nt(stacked(queries, first, second), keys)
        scores = jnp.where(valid, scores, -1e30)
        top = jnp.max(scores, axis=-1, keepdims=True)
        exp_scores = jnp.exp(scores - top)
        total = jnp.sum(exp_scores, axis=-1, keepdims=True)
        prob = (exp_scores * (1.0 / total)).astype(BF)
        prob_ref[0, pair] = prob
        head_out = nn(prob[:S], values * first) + nn(prob[S:], values * second)
        out_ref[:, lanes] = (head_out * mask_ref[0, :, lanes]).astype(BF)
    middle_ref[...] = x + nn(out_ref[...], wo_ref[...])


def attn_forward(counts, tokens, mask_lanes, norm_params, own, other):
    rows = tokens.shape[0]
    images = rows // S
    return pl.pallas_call(
        attn_forward_kernel,
        grid=(images,),
        in_specs=[
            pl.BlockSpec(memory_space=pltpu.SMEM),
            pl.BlockSpec((S, D), lambda i: (i, 0)),
            pl.BlockSpec((1, 1, D), lambda i: (i, 0, 0)),
            pl.BlockSpec((4, D), lambda i: (0, 0)),
            pl.BlockSpec((SLABS, 48, D), lambda i: (0, 0, 0)),
            pl.BlockSpec((SLABS, 48, D), lambda i: (0, 0, 0)),
        ],
        out_specs=[
            pl.BlockSpec((1, PAIRS, 2 * S, S), lambda i: (i, 0, 0, 0)),
            pl.BlockSpec((S, 3 * D), lambda i: (i, 0)),
            pl.BlockSpec((S, D), lambda i: (i, 0)),
            pl.BlockSpec((S, D), lambda i: (i, 0)),
            pl.BlockSpec((D, 3 * D), lambda i: (0, 0)),
            pl.BlockSpec((D, D), lambda i: (0, 0)),
        ],
        out_shape=[
            jax.ShapeDtypeStruct((images, PAIRS, 2 * S, S), BF),
            jax.ShapeDtypeStruct((rows, 3 * D), BF),
            jax.ShapeDtypeStruct((rows, D), BF),
            jax.ShapeDtypeStruct((rows, D), F32),
            jax.ShapeDtypeStruct((D, 3 * D), BF),
            jax.ShapeDtypeStruct((D, D), BF),
        ],
        compiler_params=pltpu.CompilerParams(vmem_limit_bytes=VMEM_LIMIT),
        name="attn_forward",
    )(counts, tokens, mask_lanes, norm_params, own, other)


def mlp_kernel(
    middle_ref, cot_ref, norm_ref, up_own_ref, up_other_ref, down_own_ref, down_other_ref,
    out_ref, grad_ref, up_grad_ref, down_grad_ref, norm_grad_ref,
):
    step = pl.program_id(0)

    @pl.when(step == 0)
    def _():
        up_grad_ref[...] = jnp.zeros_like(up_grad_ref)
        down_grad_ref[...] = jnp.zeros_like(down_grad_ref)
        norm_grad_ref[...] = jnp.zeros_like(norm_grad_ref)

    middle = middle_ref[...]
    normed, inverse_std = normalize(middle)
    rows = (normed * norm_ref[2:3, :] + norm_ref[3:4, :]).astype(BF)
    cot = cot_ref[...]
    total = middle
    back = None
    for side, (up_ref, down_ref) in enumerate(
        ((up_own_ref, down_own_ref), (up_other_ref, down_other_ref))
    ):
        for part in range(2):
            up = jnp.concatenate([up_ref[2 * r + part] for r in range(8)], axis=0)
            down = jnp.concatenate([down_ref[8 * part + r] for r in range(8)], axis=0)
            pre = nn(rows, up)
            cumulative = 0.5 * (1.0 + lax.erf(pre * ROOT_HALF))
            density = jnp.exp(-0.5 * pre * pre) * DENSITY_FACTOR
            act = (pre * cumulative).astype(BF)
            total = total + nn(act, down)
            act_grad = nt(cot, down)
            pre_grad = (act_grad * (cumulative + pre * density)).astype(BF)
            down_part = tn(act, cot)
            up_part = tn(rows, pre_grad)
            for r in range(8):
                down_grad_ref[side, 8 * part + r] += down_part[48 * r : 48 * r + 48]
                up_grad_ref[side, 2 * r + part] += up_part[48 * r : 48 * r + 48]
            term = nt(pre_grad, up)
            back = term if back is None else back + term
    out_ref[...] = total
    grad_in, norm_part = norm_backward(back, normed, inverse_std, norm_ref[2:3, :])
    norm_grad_ref[...] += norm_part
    grad_ref[...] = cot.astype(F32) + grad_in


def mlp(middle, cotangent, norm_params, up_own, up_other, down_own, down_other):
    rows = middle.shape[0]
    slab = pl.BlockSpec((SLABS, 48, D), lambda i: (0, 0, 0))
    tile = pl.BlockSpec((S, D), lambda i: (i, 0))
    grad = pl.BlockSpec((2, SLABS, 48, D), lambda i: (0, 0, 0, 0))
    return pl.pallas_call(
        mlp_kernel,
        grid=(rows // S,),
        in_specs=[tile, tile, pl.BlockSpec((4, D), lambda i: (0, 0)), slab, slab, slab, slab],
        out_specs=[tile, tile, grad, grad, pl.BlockSpec((2, D), lambda i: (0, 0))],
        out_shape=[
            jax.ShapeDtypeStruct((rows, D), F32),
            jax.ShapeDtypeStruct((rows, D), F32),
            jax.ShapeDtypeStruct((2, SLABS, 48, D), F32),
            jax.ShapeDtypeStruct((2, SLABS, 48, D), F32),
            jax.ShapeDtypeStruct((2, D), F32),
        ],
        compiler_params=pltpu.CompilerParams(vmem_limit_bytes=VMEM_LIMIT),
        name="mlp",
    )(middle, cotangent, norm_params, up_own, up_other, down_own, down_other)


def attn_backward_kernel(
    x_ref, grad_ref, prob_ref, qkv_ref, out_ref, mask_ref, norm_ref, wqkv_ref, wo_ref,
    in_grad_ref, slab_grad_ref, norm_grad_ref, dqkv_ref, wqkv_grad_ref, wo_grad_ref,
):
    step = pl.program_id(0)

    @pl.when(step == 0)
    def _():
        wqkv_grad_ref[...] = jnp.zeros_like(wqkv_grad_ref)
        wo_grad_ref[...] = jnp.zeros_like(wo_grad_ref)
        norm_grad_ref[...] = jnp.zeros_like(norm_grad_ref)

    x = x_ref[...].astype(F32)
    normed, inverse_std = normalize(x)
    rows = (normed * norm_ref[0:1, :] + norm_ref[1:2, :]).astype(BF)
    grad = grad_ref[...]
    low_grad = grad.astype(BF)
    head_out = out_ref[...]
    wo_grad_ref[...] += tn(head_out, low_grad)
    out_grad = (nt(low_grad, wo_ref[...]).astype(BF) * mask_ref[0].astype(BF))
    first, second = lane_halves()
    for pair in range(PAIRS):
        lanes = slice(PAIR * pair, PAIR * (pair + 1))
        key_lanes = slice(D + PAIR * pair, D + PAIR * (pair + 1))
        value_lanes = slice(2 * D + PAIR * pair, 2 * D + PAIR * (pair + 1))
        queries = qkv_ref[:, lanes]
        keys = qkv_ref[:, key_lanes]
        values = qkv_ref[:, value_lanes]
        prob = prob_ref[0, pair]
        pair_grad = stacked(out_grad[:, lanes], first, second)
        dots = out_grad[:, lanes].astype(F32) * head_out[:, lanes].astype(F32)
        row_dot = jnp.concatenate(
            [
                jnp.sum(dots * first.astype(F32), axis=-1, keepdims=True),
                jnp.sum(dots * second.astype(F32), axis=-1, keepdims=True),
            ],
            axis=0,
        )
        prob_grad = nt(pair_grad, values)
        score_grad = (prob.astype(F32) * (prob_grad - row_dot)).astype(BF)
        dqkv_ref[:, lanes] = (
            nn(score_grad[:S], keys * first) + nn(score_grad[S:], keys * second)
        ).astype(BF)
        dqkv_ref[:, key_lanes] = tn(score_grad, stacked(queries, first, second)).astype(BF)
        dqkv_ref[:, value_lanes] = tn(prob, pair_grad).astype(BF)
    dqkv = dqkv_ref[...]
    wqkv_grad_ref[...] += tn(rows, dqkv)
    back = nt(dqkv, wqkv_ref[...])
    grad_in, norm_part = norm_backward(back, normed, inverse_std, norm_ref[0:1, :])
    norm_grad_ref[...] += norm_part
    in_grad_ref[...] = grad + grad_in

    @pl.when(step == pl.num_programs(0) - 1)
    def _():
        for side in range(2):
            for slab in range(12):
                pieces = []
                for unit in (2 * slab, 2 * slab + 1):
                    row, part = divmod(unit, 3)
                    start = D * part + HALF * side
                    piece = wqkv_grad_ref[48 * row : 48 * row + 48, D * part : D * part + D]
                    piece = piece[:, HALF * side : HALF * side + HALF]
                    pieces.append(piece * 0.125 if part == 0 else piece)
                slab_grad_ref[side, slab] = jnp.concatenate(pieces, axis=1)
            for row in range(HALF // 48):
                start = HALF * side + 48 * row
                slab_grad_ref[side, 12 + row] = wo_grad_ref[start : start + 48, :]


def attn_backward(tokens, grad, prob, qkv, out, mask_lanes, norm_params, wqkv, wo):
    rows = tokens.shape[0]
    images = rows // S
    tile = pl.BlockSpec((S, D), lambda i: (i, 0))
    return pl.pallas_call(
        attn_backward_kernel,
        grid=(images,),
        in_specs=[
            tile,
            tile,
            pl.BlockSpec((1, PAIRS, 2 * S, S), lambda i: (i, 0, 0, 0)),
            pl.BlockSpec((S, 3 * D), lambda i: (i, 0)),
            tile,
            pl.BlockSpec((1, 1, D), lambda i: (i, 0, 0)),
            pl.BlockSpec((4, D), lambda i: (0, 0)),
            pl.BlockSpec((D, 3 * D), lambda i: (0, 0)),
            pl.BlockSpec((D, D), lambda i: (0, 0)),
        ],
        out_specs=[
            tile,
            pl.BlockSpec((2, SLABS, 48, D), lambda i: (0, 0, 0, 0)),
            pl.BlockSpec((2, D), lambda i: (0, 0)),
        ],
        out_shape=[
            jax.ShapeDtypeStruct((rows, D), F32),
            jax.ShapeDtypeStruct((2, SLABS, 48, D), F32),
            jax.ShapeDtypeStruct((2, D), F32),
        ],
        scratch_shapes=[
            pltpu.VMEM((S, 3 * D), BF),
            pltpu.VMEM((D, 3 * D), F32),
            pltpu.VMEM((D, D), F32),
        ],
        compiler_params=pltpu.CompilerParams(vmem_limit_bytes=VMEM_LIMIT),
        name="attn_backward",
    )(tokens, grad, prob, qkv, out, mask_lanes, norm_params, wqkv, wo)


def split(values):
    high = values.astype(BF)
    return high, (values - high.astype(F32)).astype(BF)


def product(left, right):
    left_high, left_low = left
    right_high, right_low = right
    return nn(left_high, right_high) + (nn(left_high, right_low) + nn(left_low, right_high))


def shampoo_kernel(
    scale, grad_ref, weight_ref, left_ref, right_ref,
    out_grad_ref, left_new_ref, right_new_ref, new_weight_ref, root_ref, power_ref,
):
    count, edge = weight_ref.shape[1], weight_ref.shape[2]
    row = lax.broadcasted_iota(jnp.int32, (edge, edge), 0)
    column = lax.broadcasted_iota(jnp.int32, (edge, edge), 1)
    identity = (row == column).astype(F32)
    whole = grad_ref[0] * scale
    for block in range(count):
        grad = whole[:, edge * block : edge * block + edge]
        out_grad_ref[0, block] = grad
        high, low = split(grad)
        high_t, low_t = split(jnp.transpose(grad))
        for kind, (old_ref, new_ref, one, two) in enumerate(
            (
                (left_ref, left_new_ref, (high, low), (high_t, low_t)),
                (right_ref, right_new_ref, (high_t, low_t), (high, low)),
            )
        ):
            new = 0.5 * old_ref[0, block] + 0.5 * product(one, two)
            new_ref[0, block] = new
            squares = jnp.sum(jnp.sum(new * new, axis=1, keepdims=True), axis=0, keepdims=True)
            factor = 2.5 * lax.rsqrt(squares)
            root_ref[2 * block + kind] = jnp.sqrt(jnp.sqrt(factor)) * identity
            power_ref[2 * block + kind] = factor * new

    def iteration(_, carry):
        for index in range(2 * count):
            power = power_ref[index]
            middle = split((5.0 * identity - power) * 0.25)
            root_ref[index] = product(split(root_ref[index]), middle)
            square = split(product(middle, middle))
            fourth = split(product(square, square))
            power_ref[index] = product(fourth, split(power))
        return carry

    lax.fori_loop(0, ITERS, iteration, 0)
    for block in range(count):
        grad = split(out_grad_ref[0, block])
        step = product(split(root_ref[2 * block]), grad)
        step = product(split(step), split(root_ref[2 * block + 1]))
        new_weight_ref[0, block] = weight_ref[0, block] - 0.25 * step


def shampoo(grads, weights, stat_left, stat_right, scale):
    groups, count, edge, _ = weights.shape
    block = pl.BlockSpec((1, count, edge, edge), lambda i: (i, 0, 0, 0))
    shape = jax.ShapeDtypeStruct(weights.shape, F32)
    return pl.pallas_call(
        lambda *refs: shampoo_kernel(scale, *refs),
        grid=(groups,),
        in_specs=[pl.BlockSpec((1, edge, count * edge), lambda i: (i, 0, 0)), block, block, block],
        out_specs=[block] * 4,
        out_shape=[shape] * 4,
        scratch_shapes=[
            pltpu.VMEM((2 * count, edge, edge), F32),
            pltpu.VMEM((2 * count, edge, edge), F32),
        ],
        compiler_params=pltpu.CompilerParams(vmem_limit_bytes=VMEM_LIMIT),
        name="shampoo",
    )(grads, weights, stat_left, stat_right)


def swap_heads(values):
    return lax.ppermute(values, "head", [(0, 1), (1, 0)])


def gather_slabs(weights):
    groups, count, edge, _ = weights.shape
    local = weights.astype(BF)
    if count * lax.axis_size("dp") != SLABS * (D // edge):
        raise ValueError("block count")
    if count * edge == D:
        local = local.transpose(0, 2, 1, 3).reshape(groups, edge, D)
        return lax.all_gather(local, "dp", axis=1)
    blocks = lax.all_gather(local, "dp", axis=1, tiled=True)
    blocks = blocks.reshape(groups, SLABS, D // edge, edge, edge)
    return blocks.transpose(0, 1, 3, 2, 4).reshape(groups, SLABS, edge, D)


def scatter_slabs(slabs, count, edge):
    groups = slabs.shape[0]
    if count * edge == D:
        return lax.psum_scatter(slabs, "dp", scatter_dimension=1)
    blocks = slabs.reshape(groups, SLABS, edge, D // edge, edge).transpose(0, 1, 3, 2, 4)
    blocks = blocks.reshape(groups, SLABS * (D // edge), edge, edge)
    owned = lax.psum_scatter(blocks, "dp", scatter_dimension=1, tiled=True)
    return owned.transpose(0, 2, 1, 3).reshape(groups, edge, count * edge)


def per_device(
    tokens,
    cotangent,
    token_counts,
    head_mask,
    norm_params,
    norm_state,
    weights,
    stat_left,
    stat_right,
):
    weights, stat_left, stat_right = weights[0], stat_left[0], stat_right[0]
    _, count, edge, _ = weights.shape
    images = tokens.shape[0] // S
    half = lax.axis_index("head")
    counts = lax.dynamic_slice_in_dim(token_counts, half * images, images)
    own_mask = lax.dynamic_slice_in_dim(head_mask, half * images, images)
    sent_mask = lax.dynamic_slice_in_dim(head_mask, (1 - half) * images, images)
    mask = jnp.concatenate([own_mask, swap_heads(sent_mask)], axis=1)
    mask_lanes = jnp.repeat(mask.astype(F32), HEAD_DIM, axis=1)[:, None, :]

    own = gather_slabs(weights)
    other = swap_heads(own)
    prob, qkv, out, middle, wqkv, wo = attn_forward(
        counts, tokens, mask_lanes, norm_params, own[0], other[0]
    )
    block_out, middle_grad, up_grad, down_grad, norm_two = mlp(
        middle, cotangent, norm_params, own[1], other[1], own[2], other[2]
    )
    input_grad, early_grad, norm_one = attn_backward(
        tokens, middle_grad, prob, qkv, out, mask_lanes, norm_params, wqkv, wo
    )
    all_grads = jnp.stack([early_grad, up_grad, down_grad])
    received = swap_heads(all_grads[:, 1].astype(BF))
    summed = (all_grads[:, 0] + received.astype(F32)).astype(BF)
    owned = scatter_slabs(summed, count, edge).astype(F32)
    norm_total = lax.psum(jnp.concatenate([norm_one, norm_two], axis=0), ("dp", "head"))
    token_total = tokens.shape[0] * lax.axis_size("dp") * lax.axis_size("head")
    scale = 1.0 / math.sqrt(token_total)
    grads, left_new, right_new, new_weights = shampoo(owned, weights, stat_left, stat_right, scale)
    norm_grads = norm_total * scale
    state_new = 0.5 * norm_state + 0.5 * norm_grads * norm_grads
    norm_new = norm_params - 0.2 * norm_grads / jnp.sqrt(state_new)
    return (
        block_out,
        input_grad,
        grads[None],
        left_new[None],
        right_new[None],
        new_weights[None],
        norm_grads,
        state_new,
        norm_new,
    )


def solution(mesh):
    blocks = P("head", None, "dp", None, None)
    rows = P(("dp", "head"), None)
    return jax.shard_map(
        per_device,
        mesh=mesh,
        in_specs=(rows, rows, P("dp"), P("dp", "head"), P(), P(), blocks, blocks, blocks),
        out_specs=(rows, rows, blocks, blocks, blocks, blocks, P(), P(), P()),
        check_vma=False,
    )
```

```python
import math

import jax
import jax.numpy as jnp
from jax import lax
from jax.experimental import pallas as pl
from jax.experimental.pallas import tpu as pltpu
from jax.sharding import Mesh, PartitionSpec as P

D = 384
HEAD_DIM = 64
MLP = 1536
S = 256
ITERS = 8
PAIR = 2 * HEAD_DIM
PAIRS = D // PAIR
HALF = D // 2
SLABS = 16
INNER = 4
PACK = 4
WIDE = 64
ROOT_HALF = 0.7071067811865476
DENSITY_FACTOR = 0.3989422804014327
BF = jnp.bfloat16
F32 = jnp.float32
VMEM_LIMIT = 56 << 20


def nn(left, right):
    return jnp.dot(left, right, preferred_element_type=F32)


def nt(left, right):
    return lax.dot_general(left, right, (((1,), (1,)), ((), ())), preferred_element_type=F32)


def tn(left, right):
    return lax.dot_general(left, right, (((0,), (0,)), ((), ())), preferred_element_type=F32)


def normalize(values):
    centered = values - jnp.mean(values, axis=-1, keepdims=True)
    variance = jnp.mean(centered * centered, axis=-1, keepdims=True)
    inverse_std = lax.rsqrt(variance + 1e-06)
    return centered * inverse_std, inverse_std


def norm_backward(grad_out, normed, inverse_std, gain):
    grad_normed = grad_out * gain
    mean_first = jnp.mean(grad_normed, axis=-1, keepdims=True)
    mean_second = jnp.mean(grad_normed * normed, axis=-1, keepdims=True)
    grad_in = inverse_std * (grad_normed - mean_first - normed * mean_second)
    gain_grad = jnp.sum(grad_out * normed, axis=0, keepdims=True)
    shift_grad = jnp.sum(grad_out, axis=0, keepdims=True)
    return grad_in, jnp.concatenate([gain_grad, shift_grad], axis=0)


def slab_at(owner):
    return (owner % INNER) * (SLABS // INNER) + owner // INNER


def lane_halves():
    lane = lax.broadcasted_iota(jnp.int32, (1, PAIR), 1)
    first = (lane < HEAD_DIM).astype(BF)
    return first, (1 - first).astype(BF)


def stacked(values, first, second):
    return jnp.concatenate([values * first, values * second], axis=0)


def attn_forward_kernel(
    counts_ref, x_ref, mask_ref, norm_ref, own_ref, other_ref,
    prob_ref, qkv_ref, out_ref, middle_ref, wqkv_ref, wo_ref,
):
    step = pl.program_id(0)

    @pl.when(step == 0)
    def _():
        slabs = (own_ref, other_ref)
        for row in range(D // 48):
            for part in range(3):
                pieces = []
                for ref in slabs:
                    slab, side = divmod(3 * row + part, 2)
                    pieces.append(ref[slab_at(slab)][:, side * HALF : (side + 1) * HALF])
                joined = jnp.concatenate(pieces, axis=1)
                if part == 0:
                    joined = joined * 0.125
                wqkv_ref[48 * row : 48 * row + 48, D * part : D * part + D] = joined
        for side, ref in enumerate(slabs):
            for row in range(HALF // 48):
                start = side * HALF + 48 * row
                wo_ref[start : start + 48, :] = ref[slab_at(12 + row)]

    x = x_ref[...].astype(F32)
    normed, _ = normalize(x)
    rows = (normed * norm_ref[0:1, :] + norm_ref[1:2, :]).astype(BF)
    qkv_ref[...] = nn(rows, wqkv_ref[...]).astype(BF)
    first, second = lane_halves()
    count = counts_ref[step]
    column = lax.broadcasted_iota(jnp.int32, (1, S), 1)
    valid = column < count
    for pair in range(PAIRS):
        lanes = slice(PAIR * pair, PAIR * (pair + 1))
        queries = qkv_ref[:, lanes]
        keys = qkv_ref[:, D + PAIR * pair : D + PAIR * (pair + 1)]
        values = qkv_ref[:, 2 * D + PAIR * pair : 2 * D + PAIR * (pair + 1)]
        scores = nt(stacked(queries, first, second), keys)
        scores = jnp.where(valid, scores, -1e30)
        top = jnp.max(scores, axis=-1, keepdims=True)
        exp_scores = jnp.exp(scores - top)
        total = jnp.sum(exp_scores, axis=-1, keepdims=True)
        prob = (exp_scores * (1.0 / total)).astype(BF)
        prob_ref[0, pair] = prob
        head_out = nn(prob[:S], values * first) + nn(prob[S:], values * second)
        out_ref[:, lanes] = (head_out * mask_ref[0, :, lanes]).astype(BF)
    middle_ref[...] = x + nn(out_ref[...], wo_ref[...])


def attn_forward(counts, tokens, mask_lanes, norm_params, own, other):
    rows = tokens.shape[0]
    images = rows // S
    return pl.pallas_call(
        attn_forward_kernel,
        grid=(images,),
        in_specs=[
            pl.BlockSpec(memory_space=pltpu.SMEM),
            pl.BlockSpec((S, D), lambda i: (i, 0)),
            pl.BlockSpec((1, 1, D), lambda i: (i, 0, 0)),
            pl.BlockSpec((4, D), lambda i: (0, 0)),
            pl.BlockSpec((SLABS, 48, D), lambda i: (0, 0, 0)),
            pl.BlockSpec((SLABS, 48, D), lambda i: (0, 0, 0)),
        ],
        out_specs=[
            pl.BlockSpec((1, PAIRS, 2 * S, S), lambda i: (i, 0, 0, 0)),
            pl.BlockSpec((S, 3 * D), lambda i: (i, 0)),
            pl.BlockSpec((S, D), lambda i: (i, 0)),
            pl.BlockSpec((S, D), lambda i: (i, 0)),
            pl.BlockSpec((D, 3 * D), lambda i: (0, 0)),
            pl.BlockSpec((D, D), lambda i: (0, 0)),
        ],
        out_shape=[
            jax.ShapeDtypeStruct((images, PAIRS, 2 * S, S), BF),
            jax.ShapeDtypeStruct((rows, 3 * D), BF),
            jax.ShapeDtypeStruct((rows, D), BF),
            jax.ShapeDtypeStruct((rows, D), F32),
            jax.ShapeDtypeStruct((D, 3 * D), BF),
            jax.ShapeDtypeStruct((D, D), BF),
        ],
        compiler_params=pltpu.CompilerParams(vmem_limit_bytes=VMEM_LIMIT),
        cost_estimate=pl.CostEstimate(
            flops=rows * D * (8 * D + 16 * S), bytes_accessed=16 << 20, transcendentals=rows * 6 * S
        ),
        name="attn_forward",
    )(counts, tokens, mask_lanes, norm_params, own, other)


def mlp_kernel(
    middle_ref, cot_ref, norm_ref, own_ref, other_ref,
    out_ref, grad_ref, own_grad_ref, sent_grad_ref, norm_grad_ref, other_grad_ref,
):
    step = pl.program_id(0)

    @pl.when(step == 0)
    def _():
        own_grad_ref[...] = jnp.zeros_like(own_grad_ref)
        other_grad_ref[...] = jnp.zeros_like(other_grad_ref)
        norm_grad_ref[...] = jnp.zeros_like(norm_grad_ref)

    middle = middle_ref[...]
    normed, inverse_std = normalize(middle)
    rows = (normed * norm_ref[2:3, :] + norm_ref[3:4, :]).astype(BF)
    cot = cot_ref[...]
    total = middle
    back = None
    for ref, grads in ((own_ref, own_grad_ref), (other_ref, other_grad_ref)):
        for part in range(2):
            up_at = [slab_at(2 * r + part) for r in range(8)]
            down_at = [slab_at(8 * part + r) for r in range(8)]
            up = jnp.concatenate([ref[at, 0] for at in up_at], axis=0)
            down = jnp.concatenate([ref[at, 1] for at in down_at], axis=0)
            pre = nn(rows, up)
            cumulative = 0.5 * (1.0 + lax.erf(pre * ROOT_HALF))
            density = jnp.exp(-0.5 * pre * pre) * DENSITY_FACTOR
            act = (pre * cumulative).astype(BF)
            total = total + nn(act, down)
            act_grad = nt(cot, down)
            pre_grad = (act_grad * (cumulative + pre * density)).astype(BF)
            down_part = tn(act, cot)
            up_part = tn(rows, pre_grad)
            for r in range(8):
                grads[up_at[r], 0] += up_part[48 * r : 48 * r + 48]
                grads[down_at[r], 1] += down_part[48 * r : 48 * r + 48]
            term = nt(pre_grad, up)
            back = term if back is None else back + term
    out_ref[...] = total
    grad_in, norm_part = norm_backward(back, normed, inverse_std, norm_ref[2:3, :])
    norm_grad_ref[...] += norm_part
    grad_ref[...] = cot.astype(F32) + grad_in

    @pl.when(step == pl.num_programs(0) - 1)
    def _():
        sent_grad_ref[...] = other_grad_ref[...].astype(BF)


def mlp(middle, cotangent, norm_params, own, other):
    rows = middle.shape[0]
    slabs = (SLABS, 2, 48, D)
    slab = pl.BlockSpec(slabs, lambda i: (0, 0, 0, 0))
    tile = pl.BlockSpec((S, D), lambda i: (i, 0))
    return pl.pallas_call(
        mlp_kernel,
        grid=(rows // S,),
        in_specs=[tile, tile, pl.BlockSpec((4, D), lambda i: (0, 0)), slab, slab],
        out_specs=[tile, tile, slab, slab, pl.BlockSpec((2, D), lambda i: (0, 0))],
        out_shape=[
            jax.ShapeDtypeStruct((rows, D), F32),
            jax.ShapeDtypeStruct((rows, D), F32),
            jax.ShapeDtypeStruct(slabs, F32),
            jax.ShapeDtypeStruct(slabs, BF),
            jax.ShapeDtypeStruct((2, D), F32),
        ],
        scratch_shapes=[pltpu.VMEM(slabs, F32)],
        compiler_params=pltpu.CompilerParams(vmem_limit_bytes=VMEM_LIMIT),
        cost_estimate=pl.CostEstimate(
            flops=12 * rows * D * MLP, bytes_accessed=20 << 20, transcendentals=2 * rows * MLP
        ),
        name="mlp",
    )(middle, cotangent, norm_params, own, other)


def attn_backward_kernel(
    x_ref, grad_ref, prob_ref, qkv_ref, out_ref, mask_ref, norm_ref, wqkv_ref, wo_ref,
    in_grad_ref, own_grad_ref, sent_grad_ref, norm_grad_ref, dqkv_ref, wqkv_grad_ref, wo_grad_ref,
):
    step = pl.program_id(0)

    @pl.when(step == 0)
    def _():
        wqkv_grad_ref[...] = jnp.zeros_like(wqkv_grad_ref)
        wo_grad_ref[...] = jnp.zeros_like(wo_grad_ref)
        norm_grad_ref[...] = jnp.zeros_like(norm_grad_ref)

    x = x_ref[...].astype(F32)
    normed, inverse_std = normalize(x)
    rows = (normed * norm_ref[0:1, :] + norm_ref[1:2, :]).astype(BF)
    grad = grad_ref[...]
    low_grad = grad.astype(BF)
    head_out = out_ref[...]
    wo_grad_ref[...] += tn(head_out, low_grad)
    out_grad = (nt(low_grad, wo_ref[...]).astype(BF) * mask_ref[0].astype(BF))
    first, second = lane_halves()
    for pair in range(PAIRS):
        lanes = slice(PAIR * pair, PAIR * (pair + 1))
        key_lanes = slice(D + PAIR * pair, D + PAIR * (pair + 1))
        value_lanes = slice(2 * D + PAIR * pair, 2 * D + PAIR * (pair + 1))
        queries = qkv_ref[:, lanes]
        keys = qkv_ref[:, key_lanes]
        values = qkv_ref[:, value_lanes]
        prob = prob_ref[0, pair]
        pair_grad = stacked(out_grad[:, lanes], first, second)
        dots = out_grad[:, lanes].astype(F32) * head_out[:, lanes].astype(F32)
        row_dot = jnp.concatenate(
            [
                jnp.sum(dots * first.astype(F32), axis=-1, keepdims=True),
                jnp.sum(dots * second.astype(F32), axis=-1, keepdims=True),
            ],
            axis=0,
        )
        prob_grad = nt(pair_grad, values)
        score_grad = (prob.astype(F32) * (prob_grad - row_dot)).astype(BF)
        dqkv_ref[:, lanes] = (
            nn(score_grad[:S], keys * first) + nn(score_grad[S:], keys * second)
        ).astype(BF)
        dqkv_ref[:, key_lanes] = tn(score_grad, stacked(queries, first, second)).astype(BF)
        dqkv_ref[:, value_lanes] = tn(prob, pair_grad).astype(BF)
    dqkv = dqkv_ref[...]
    wqkv_grad_ref[...] += tn(rows, dqkv)
    back = nt(dqkv, wqkv_ref[...])
    grad_in, norm_part = norm_backward(back, normed, inverse_std, norm_ref[0:1, :])
    norm_grad_ref[...] += norm_part
    in_grad_ref[...] = grad + grad_in

    @pl.when(step == pl.num_programs(0) - 1)
    def _():
        for side, slab_grads in enumerate((own_grad_ref, sent_grad_ref)):
            for slab in range(12):
                pieces = []
                for unit in (2 * slab, 2 * slab + 1):
                    row, part = divmod(unit, 3)
                    piece = wqkv_grad_ref[48 * row : 48 * row + 48, D * part : D * part + D]
                    piece = piece[:, HALF * side : HALF * side + HALF]
                    pieces.append(piece * 0.125 if part == 0 else piece)
                joined = jnp.concatenate(pieces, axis=1)
                slab_grads[slab_at(slab)] = joined.astype(slab_grads.dtype)
            for row in range(HALF // 48):
                start = HALF * side + 48 * row
                joined = wo_grad_ref[start : start + 48, :]
                slab_grads[slab_at(12 + row)] = joined.astype(slab_grads.dtype)


def attn_backward(tokens, grad, prob, qkv, out, mask_lanes, norm_params, wqkv, wo):
    rows = tokens.shape[0]
    images = rows // S
    tile = pl.BlockSpec((S, D), lambda i: (i, 0))
    slab = pl.BlockSpec((SLABS, 48, D), lambda i: (0, 0, 0))
    return pl.pallas_call(
        attn_backward_kernel,
        grid=(images,),
        in_specs=[
            tile,
            tile,
            pl.BlockSpec((1, PAIRS, 2 * S, S), lambda i: (i, 0, 0, 0)),
            pl.BlockSpec((S, 3 * D), lambda i: (i, 0)),
            tile,
            pl.BlockSpec((1, 1, D), lambda i: (i, 0, 0)),
            pl.BlockSpec((4, D), lambda i: (0, 0)),
            pl.BlockSpec((D, 3 * D), lambda i: (0, 0)),
            pl.BlockSpec((D, D), lambda i: (0, 0)),
        ],
        out_specs=[
            tile,
            slab,
            slab,
            pl.BlockSpec((2, D), lambda i: (0, 0)),
        ],
        out_shape=[
            jax.ShapeDtypeStruct((rows, D), F32),
            jax.ShapeDtypeStruct((SLABS, 48, D), F32),
            jax.ShapeDtypeStruct((SLABS, 48, D), BF),
            jax.ShapeDtypeStruct((2, D), F32),
        ],
        scratch_shapes=[
            pltpu.VMEM((S, 3 * D), BF),
            pltpu.VMEM((D, 3 * D), F32),
            pltpu.VMEM((D, D), F32),
        ],
        compiler_params=pltpu.CompilerParams(vmem_limit_bytes=VMEM_LIMIT),
        cost_estimate=pl.CostEstimate(
            flops=rows * D * (16 * D + 32 * S), bytes_accessed=20 << 20, transcendentals=0
        ),
        name="attn_backward",
    )(tokens, grad, prob, qkv, out, mask_lanes, norm_params, wqkv, wo)


def split(values):
    high = values.astype(BF)
    return high, (values - high.astype(F32)).astype(BF)


def product(left, right):
    left_high, left_low = left
    right_high, right_low = right
    both = nn(jnp.concatenate([left_high, left_low], axis=0), right_high)
    edge = left_high.shape[0]
    return both[:edge] + (both[edge:] + nn(left_high, right_low))


def shampoo_kernel(
    scale, grad_ref, weight_ref, left_ref, right_ref, *refs
):
    out_grad_ref, left_new_ref, right_new_ref, new_weight_ref, root_ref, power_ref = refs[-6:]
    count, edge = weight_ref.shape[1], weight_ref.shape[2]
    pack = min(PACK, count)
    width = pack * WIDE
    row = lax.broadcasted_iota(jnp.int32, (WIDE, width), 0)
    lane = lax.broadcasted_iota(jnp.int32, (WIDE, width), 1)
    identity = (lane % WIDE == row).astype(F32)
    row = lax.broadcasted_iota(jnp.int32, (width, width), 0)
    lane = lax.broadcasted_iota(jnp.int32, (width, width), 1)
    same = (row // WIDE == lane // WIDE).astype(BF)
    lane = lax.broadcasted_iota(jnp.int32, (1, width), 1)

    def wide(block):
        block = jnp.concatenate([block, jnp.zeros((edge, WIDE - edge), block.dtype)], axis=1)
        return jnp.concatenate([block, jnp.zeros((WIDE - edge, WIDE), block.dtype)], axis=0)

    def spread(pieces):
        return tuple(jnp.concatenate([piece] * pack, axis=0) * same for piece in pieces)

    def cut(packed, index):
        return packed[:edge, WIDE * index : WIDE * index + edge]

    whole = grad_ref[0] * scale
    packs = count // pack
    grads = []
    for number in range(packs):
        blocks = []
        for index in range(pack):
            block = pack * number + index
            grad = whole[:, edge * block : edge * block + edge]
            out_grad_ref[0, block] = grad
            blocks.append(wide(grad))
        grad = jnp.concatenate(blocks, axis=1)
        grad_t = jnp.concatenate([jnp.transpose(block) for block in blocks], axis=1)
        one, two = split(grad), split(grad_t)
        one_diagonal, two_diagonal = spread(one), spread(two)
        grads.append(one_diagonal)
        for kind, (old_ref, new_ref, gram) in enumerate(
            (
                (left_ref, left_new_ref, product(one, two_diagonal)),
                (right_ref, right_new_ref, product(two, one_diagonal)),
            )
        ):
            old = jnp.concatenate([wide(old_ref[0, pack * number + i]) for i in range(pack)], axis=1)
            new = 0.5 * old + 0.5 * gram
            for index in range(pack):
                new_ref[0, pack * number + index] = cut(new, index)
            columns = jnp.sum(new * new, axis=0, keepdims=True)
            squares = jnp.zeros((1, width), F32)
            for index in range(pack):
                inside = lane // WIDE == index
                part = jnp.sum(jnp.where(inside, columns, 0.0), axis=1, keepdims=True)
                squares = jnp.where(inside, part, squares)
            factor = 2.5 / jnp.sqrt(squares)
            root_ref[2 * number + kind] = jnp.sqrt(jnp.sqrt(factor)) * identity
            power_ref[2 * number + kind] = factor * new

    def iteration(_, carry):
        for index in range(2 * packs):
            power = power_ref[index]
            middle = split((5.0 * identity - power) * 0.25)
            right = spread(middle)
            root_ref[index] = product(split(root_ref[index]), right)
            square = split(product(middle, right))
            fourth = split(product(square, spread(square)))
            power_ref[index] = product(fourth, spread(split(power)))
        return carry

    lax.fori_loop(0, ITERS, iteration, 0)
    for number in range(packs):
        step = product(split(root_ref[2 * number]), grads[number])
        step = product(split(step), spread(split(root_ref[2 * number + 1])))
        for index in range(pack):
            block = pack * number + index
            new_weight_ref[0, block] = weight_ref[0, block] - 0.25 * cut(step, index)


def shampoo(grads, weights, stat_left, stat_right, scale, first, earlier=()):
    groups, edge, _ = grads.shape
    _, count, _, _ = weights.shape
    packs = count // min(PACK, count)
    width = min(PACK, count) * WIDE
    block = pl.BlockSpec((1, count, edge, edge), lambda i: (i + first, 0, 0, 0))
    shape = jax.ShapeDtypeStruct(weights.shape, F32)
    return pl.pallas_call(
        lambda *refs: shampoo_kernel(scale, *refs),
        grid=(groups,),
        in_specs=[
            pl.BlockSpec((1, edge, count * edge), lambda i: (i, 0, 0)), block, block, block,
            *[pl.BlockSpec(memory_space=pl.ANY) for _ in earlier],
        ],
        out_specs=[block] * 4,
        out_shape=[shape] * 4,
        scratch_shapes=[
            pltpu.VMEM((2 * packs, WIDE, width), F32),
            pltpu.VMEM((2 * packs, WIDE, width), F32),
        ],
        input_output_aliases={4 + i: i for i in range(len(earlier))},
        compiler_params=pltpu.CompilerParams(vmem_limit_bytes=VMEM_LIMIT),
        cost_estimate=pl.CostEstimate(
            flops=groups * (3 << 30), bytes_accessed=4 << 20, transcendentals=0
        ),
        name="shampoo",
    )(grads, weights, stat_left, stat_right, *earlier)


def swap_heads(values):
    return lax.ppermute(values, "head", [(0, 1), (1, 0)])


def to_all(values, axis):
    return lax.all_to_all(values, axis, 0, 0)


def copies(values, number):
    return jnp.broadcast_to(values[None], (number,) + values.shape)


def gather_slabs(local):
    groups, edge, _ = local.shape
    slabs = local if groups > 1 else local[0]
    slabs = to_all(copies(slabs, lax.axis_size("outer")), "outer")
    slabs = to_all(copies(slabs, lax.axis_size("inner")), "inner")
    return slabs.reshape((SLABS,) + slabs.shape[2:])


def gather_blocks(local):
    groups, _, edge, _ = local.shape
    blocks = lax.all_gather(local, ("outer", "inner"), axis=1, tiled=True)
    blocks = blocks.reshape(groups, SLABS // INNER, INNER, D // edge, edge, edge)
    slabs = blocks.transpose(2, 1, 0, 4, 3, 5).reshape(SLABS, groups, edge, D)
    return slabs if groups > 1 else slabs[:, 0]


def scatter_blocks(slabs, count, edge):
    groups = slabs.shape[1]
    blocks = slabs.reshape(INNER, SLABS // INNER, groups, edge, D // edge, edge)
    blocks = blocks.transpose(2, 1, 0, 4, 3, 5).reshape(groups, SLABS * (D // edge), edge, edge)
    owned = lax.psum_scatter(blocks, ("outer", "inner"), scatter_dimension=1, tiled=True)
    return owned.transpose(0, 2, 1, 3).reshape(groups, edge, count * edge)


def scatter_slabs(slabs):
    groups = slabs.shape[1]
    inner, outer = lax.axis_size("inner"), lax.axis_size("outer")
    shape = (outer, groups, 48, D)
    received = to_all(slabs.reshape((inner,) + shape), "inner")
    partial = jnp.sum(received.astype(F32), axis=0).astype(BF)
    return jnp.sum(to_all(partial, "outer").astype(F32), axis=0)


def with_norms(slabs, norms):
    high, low = split(norms)
    rows = jnp.concatenate([high, low, jnp.zeros_like(high), jnp.zeros_like(high)], axis=0)
    return jnp.concatenate([slabs, copies(rows, slabs.shape[0])], axis=1)


def scatter_with_norms(slabs, norms):
    inner, outer = lax.axis_size("inner"), lax.axis_size("outer")
    sent = with_norms(slabs.reshape(inner, outer * 48, D), norms)
    received = jnp.sum(to_all(sent, "inner").astype(F32), axis=0)
    edge = outer * 48
    norms = received[edge : edge + 4] + received[edge + 4 : edge + 8]
    sent = with_norms(received[:edge].reshape(outer, 48, D).astype(BF), norms)
    received = jnp.sum(to_all(sent, "outer").astype(F32), axis=0)
    return received[None, :48], received[48:52] + received[52:56]


def per_device(
    tokens,
    cotangent,
    token_counts,
    head_mask,
    norm_params,
    norm_state,
    weights,
    stat_left,
    stat_right,
):
    weights, stat_left, stat_right = weights[0], stat_left[0], stat_right[0]
    _, count, edge, _ = weights.shape
    whole_slabs = count * edge == D
    images = tokens.shape[0] // S
    half = lax.axis_index("head")
    counts = lax.dynamic_slice_in_dim(token_counts, half * images, images)
    own_mask = lax.dynamic_slice_in_dim(head_mask, half * images, images)
    sent_mask = lax.dynamic_slice_in_dim(head_mask, (1 - half) * images, images)
    mask = jnp.concatenate([own_mask, swap_heads(sent_mask)], axis=1)
    mask_lanes = jnp.repeat(mask.astype(F32), HEAD_DIM, axis=1)[:, None, :]

    local = weights.astype(BF)
    if whole_slabs:
        local = local.transpose(0, 2, 1, 3).reshape(-1, edge, D)
        early, late = gather_slabs(local[:1]), gather_slabs(local[1:])
    else:
        early, late = gather_blocks(local[:1]), gather_blocks(local[1:])
    prob, qkv, out, middle, wqkv, wo = attn_forward(
        counts, tokens, mask_lanes, norm_params, early, swap_heads(early)
    )
    block_out, middle_grad, own_late, sent_late, norm_two = mlp(
        middle, cotangent, norm_params, late, swap_heads(late)
    )
    late_slabs = (own_late + swap_heads(sent_late).astype(F32)).astype(BF)
    input_grad, own_early, sent_early, norm_one = attn_backward(
        tokens, middle_grad, prob, qkv, out, mask_lanes, norm_params, wqkv, wo
    )
    early_slabs = (own_early + swap_heads(sent_early).astype(F32)).astype(BF)
    norms = jnp.concatenate([norm_one, norm_two], axis=0)
    if whole_slabs:
        late_owned = scatter_slabs(late_slabs)
        early_owned, norm_total = scatter_with_norms(early_slabs, norms + swap_heads(norms))
    else:
        late_owned = scatter_blocks(late_slabs, count, edge).astype(F32)
        early_owned = scatter_blocks(early_slabs[:, None], count, edge).astype(F32)
        norm_total = lax.psum(norms, ("outer", "inner", "head"))
    devices = lax.axis_size("outer") * lax.axis_size("inner") * lax.axis_size("head")
    scale = 1.0 / math.sqrt(tokens.shape[0] * devices)
    state = (weights, stat_left, stat_right, scale)
    results = shampoo(late_owned, *state, 1)
    grads, left_new, right_new, new_weights = shampoo(early_owned, *state, 0, results)
    norm_grads = norm_total * scale
    state_new = 0.5 * norm_state + 0.5 * norm_grads * norm_grads
    norm_new = norm_params - 0.2 * norm_grads / jnp.sqrt(state_new)
    return (
        block_out,
        input_grad,
        grads[None],
        left_new[None],
        right_new[None],
        new_weights[None],
        norm_grads,
        state_new,
        norm_new,
    )


def solution(mesh):
    shape = (mesh.shape["dp"] // INNER, INNER, mesh.shape["head"])
    split_mesh = Mesh(mesh.devices.reshape(shape), ("outer", "inner", "head"))
    group = ("outer", "inner")
    blocks = P("head", None, group, None, None)
    rows = P(group + ("head",), None)
    return jax.shard_map(
        per_device,
        mesh=split_mesh,
        in_specs=(rows, rows, P(group), P(group, "head"), P(), P(), blocks, blocks, blocks),
        out_specs=(rows, rows, blocks, blocks, blocks, blocks, P(), P(), P()),
        check_vma=False,
    )
```

```python
import math

import jax
import jax.numpy as jnp
from jax import lax
from jax.experimental import pallas as pl
from jax.experimental.pallas import tpu as pltpu
from jax.sharding import Mesh, PartitionSpec as P

D = 384
HEAD_DIM = 64
MLP = 1536
S = 256
ITERS = 8
PAIR = 2 * HEAD_DIM
PAIRS = D // PAIR
HALF = D // 2
SLABS = 16
INNER = 4
TILE = 512
HIDDEN = 768
PACK = 2
ROOT_HALF = 0.7071067811865476
DENSITY_FACTOR = 0.3989422804014327
BF = jnp.bfloat16
F32 = jnp.float32
VMEM_LIMIT = 56 << 20


def nn(left, right):
    return jnp.dot(left, right, preferred_element_type=F32)


def nt(left, right):
    return lax.dot_general(left, right, (((1,), (1,)), ((), ())), preferred_element_type=F32)


def tn(left, right):
    return lax.dot_general(left, right, (((0,), (0,)), ((), ())), preferred_element_type=F32)


def normalize(values):
    centered = values - jnp.mean(values, axis=-1, keepdims=True)
    variance = jnp.mean(centered * centered, axis=-1, keepdims=True)
    inverse_std = lax.rsqrt(variance + 1e-06)
    return centered * inverse_std, inverse_std


def norm_backward(grad_out, normed, inverse_std, gain):
    grad_normed = grad_out * gain
    mean_first = jnp.mean(grad_normed, axis=-1, keepdims=True)
    mean_second = jnp.mean(grad_normed * normed, axis=-1, keepdims=True)
    grad_in = inverse_std * (grad_normed - mean_first - normed * mean_second)
    gain_grad = jnp.sum(grad_out * normed, axis=0, keepdims=True)
    shift_grad = jnp.sum(grad_out, axis=0, keepdims=True)
    return grad_in, jnp.concatenate([gain_grad, shift_grad], axis=0)


def slab_at(owner):
    return (owner % INNER) * (SLABS // INNER) + owner // INNER


def lane_halves():
    lane = lax.broadcasted_iota(jnp.int32, (1, PAIR), 1)
    first = (lane < HEAD_DIM).astype(BF)
    return first, (1 - first).astype(BF)


def stacked(values, first, second):
    return jnp.concatenate([values * first, values * second], axis=0)


def attn_forward_kernel(
    counts_ref, x_ref, mask_ref, norm_ref, own_ref, other_ref,
    prob_ref, qkv_ref, out_ref, middle_ref, wqkv_ref, wo_ref,
):
    step = pl.program_id(0)

    @pl.when(step == 0)
    def _():
        slabs = (own_ref, other_ref)
        for row in range(D // 48):
            for part in range(3):
                pieces = []
                for ref in slabs:
                    slab, side = divmod(3 * row + part, 2)
                    pieces.append(ref[slab_at(slab)][:, side * HALF : (side + 1) * HALF])
                joined = jnp.concatenate(pieces, axis=1)
                if part == 0:
                    joined = joined * 0.125
                wqkv_ref[48 * row : 48 * row + 48, D * part : D * part + D] = joined
        for side, ref in enumerate(slabs):
            for row in range(HALF // 48):
                start = side * HALF + 48 * row
                wo_ref[start : start + 48, :] = ref[slab_at(12 + row)]

    x = x_ref[...].astype(F32)
    normed, _ = normalize(x)
    rows = (normed * norm_ref[0:1, :] + norm_ref[1:2, :]).astype(BF)
    qkv_ref[...] = nn(rows, wqkv_ref[...]).astype(BF)
    first, second = lane_halves()
    count = counts_ref[step]
    column = lax.broadcasted_iota(jnp.int32, (1, S), 1)
    valid = column < count
    for pair in range(PAIRS):
        lanes = slice(PAIR * pair, PAIR * (pair + 1))
        queries = qkv_ref[:, lanes]
        keys = qkv_ref[:, D + PAIR * pair : D + PAIR * (pair + 1)]
        values = qkv_ref[:, 2 * D + PAIR * pair : 2 * D + PAIR * (pair + 1)]
        scores = nt(stacked(queries, first, second), keys)
        scores = jnp.where(valid, scores, -1e30)
        top = jnp.max(scores, axis=-1, keepdims=True)
        exp_scores = jnp.exp(scores - top)
        total = jnp.sum(exp_scores, axis=-1, keepdims=True)
        prob = (exp_scores * (1.0 / total)).astype(BF)
        prob_ref[0, pair] = prob
        head_out = nn(prob[:S], values * first) + nn(prob[S:], values * second)
        out_ref[:, lanes] = (head_out * mask_ref[0, :, lanes]).astype(BF)
    middle_ref[...] = x + nn(out_ref[...], wo_ref[...])


def attn_forward(counts, tokens, mask_lanes, norm_params, own, other):
    rows = tokens.shape[0]
    images = rows // S
    return pl.pallas_call(
        attn_forward_kernel,
        grid=(images,),
        in_specs=[
            pl.BlockSpec(memory_space=pltpu.SMEM),
            pl.BlockSpec((S, D), lambda i: (i, 0)),
            pl.BlockSpec((1, 1, D), lambda i: (i, 0, 0)),
            pl.BlockSpec((4, D), lambda i: (0, 0)),
            pl.BlockSpec((SLABS, 48, D), lambda i: (0, 0, 0)),
            pl.BlockSpec((SLABS, 48, D), lambda i: (0, 0, 0)),
        ],
        out_specs=[
            pl.BlockSpec((1, PAIRS, 2 * S, S), lambda i: (i, 0, 0, 0)),
            pl.BlockSpec((S, 3 * D), lambda i: (i, 0)),
            pl.BlockSpec((S, D), lambda i: (i, 0)),
            pl.BlockSpec((S, D), lambda i: (i, 0)),
            pl.BlockSpec((D, 3 * D), lambda i: (0, 0)),
            pl.BlockSpec((D, D), lambda i: (0, 0)),
        ],
        out_shape=[
            jax.ShapeDtypeStruct((images, PAIRS, 2 * S, S), BF),
            jax.ShapeDtypeStruct((rows, 3 * D), BF),
            jax.ShapeDtypeStruct((rows, D), BF),
            jax.ShapeDtypeStruct((rows, D), F32),
            jax.ShapeDtypeStruct((D, 3 * D), BF),
            jax.ShapeDtypeStruct((D, D), BF),
        ],
        compiler_params=pltpu.CompilerParams(vmem_limit_bytes=VMEM_LIMIT),
        cost_estimate=pl.CostEstimate(
            flops=rows * D * (8 * D + 16 * S), bytes_accessed=16 << 20, transcendentals=rows * 6 * S
        ),
        name="attn_forward",
    )(counts, tokens, mask_lanes, norm_params, own, other)


def mlp_kernel(
    middle_ref, cot_ref, norm_ref, own_ref, other_ref,
    out_ref, grad_ref, own_grad_ref, sent_grad_ref, norm_grad_ref,
    up_ref, down_ref, up_grad_ref, down_grad_ref,
):
    step = pl.program_id(0)
    sides = ((own_ref, own_grad_ref), (other_ref, sent_grad_ref))
    places = [
        (side, part, MLP // 2 * side + D * part, row)
        for side in range(2)
        for part in range(2)
        for row in range(8)
    ]

    @pl.when(step == 0)
    def _():
        up_grad_ref[...] = jnp.zeros_like(up_grad_ref)
        down_grad_ref[...] = jnp.zeros_like(down_grad_ref)
        norm_grad_ref[...] = jnp.zeros_like(norm_grad_ref)
        for side, part, start, row in places:
            up = sides[side][0][slab_at(2 * row + part), 0]
            up_ref[48 * row : 48 * row + 48, start : start + D] = up
            down = sides[side][0][slab_at(8 * part + row), 1]
            down_ref[start + 48 * row : start + 48 * row + 48, :] = down

    middle = middle_ref[...]
    normed, inverse_std = normalize(middle)
    rows = (normed * norm_ref[2:3, :] + norm_ref[3:4, :]).astype(BF)
    cot = cot_ref[...]
    total = middle
    back = None
    for start in range(0, MLP, HIDDEN):
        hidden = slice(start, start + HIDDEN)
        up, down = up_ref[:, hidden], down_ref[hidden, :]
        pre = nn(rows, up)
        act_grad = nt(cot, down)
        cumulative = 0.5 * (1.0 + lax.erf(pre * ROOT_HALF))
        density = jnp.exp(-0.5 * pre * pre) * DENSITY_FACTOR
        act = (pre * cumulative).astype(BF)
        pre_grad = (act_grad * (cumulative + pre * density)).astype(BF)
        total = total + nn(act, down)
        term = nt(pre_grad, up)
        back = term if back is None else back + term
        down_grad_ref[hidden, :] += tn(act, cot)
        up_grad_ref[:, hidden] += tn(rows, pre_grad)
    out_ref[...] = total
    grad_in, norm_part = norm_backward(back, normed, inverse_std, norm_ref[2:3, :])
    norm_grad_ref[...] += norm_part
    grad_ref[...] = cot.astype(F32) + grad_in

    @pl.when(step == pl.num_programs(0) - 1)
    def _():
        for side, part, start, row in places:
            ref = sides[side][1]
            up = up_grad_ref[48 * row : 48 * row + 48, start : start + D]
            ref[slab_at(2 * row + part), 0] = up.astype(ref.dtype)
            down = down_grad_ref[start + 48 * row : start + 48 * row + 48, :]
            ref[slab_at(8 * part + row), 1] = down.astype(ref.dtype)


def mlp(middle, cotangent, norm_params, own, other):
    rows = middle.shape[0]
    slabs = (SLABS, 2, 48, D)
    slab = pl.BlockSpec(slabs, lambda i: (0, 0, 0, 0))
    tile = pl.BlockSpec((TILE, D), lambda i: (i, 0))
    return pl.pallas_call(
        mlp_kernel,
        grid=(rows // TILE,),
        in_specs=[tile, tile, pl.BlockSpec((4, D), lambda i: (0, 0)), slab, slab],
        out_specs=[tile, tile, slab, slab, pl.BlockSpec((2, D), lambda i: (0, 0))],
        out_shape=[
            jax.ShapeDtypeStruct((rows, D), F32),
            jax.ShapeDtypeStruct((rows, D), F32),
            jax.ShapeDtypeStruct(slabs, F32),
            jax.ShapeDtypeStruct(slabs, BF),
            jax.ShapeDtypeStruct((2, D), F32),
        ],
        scratch_shapes=[
            pltpu.VMEM((D, MLP), BF),
            pltpu.VMEM((MLP, D), BF),
            pltpu.VMEM((D, MLP), F32),
            pltpu.VMEM((MLP, D), F32),
        ],
        compiler_params=pltpu.CompilerParams(vmem_limit_bytes=VMEM_LIMIT),
        cost_estimate=pl.CostEstimate(
            flops=12 * rows * D * MLP, bytes_accessed=20 << 20, transcendentals=2 * rows * MLP
        ),
        name="mlp",
    )(middle, cotangent, norm_params, own, other)


def attn_backward_kernel(
    x_ref, grad_ref, prob_ref, qkv_ref, out_ref, mask_ref, norm_ref, wqkv_ref, wo_ref,
    in_grad_ref, own_grad_ref, sent_grad_ref, norm_grad_ref, dqkv_ref, wqkv_grad_ref, wo_grad_ref,
):
    step = pl.program_id(0)

    @pl.when(step == 0)
    def _():
        wqkv_grad_ref[...] = jnp.zeros_like(wqkv_grad_ref)
        wo_grad_ref[...] = jnp.zeros_like(wo_grad_ref)
        norm_grad_ref[...] = jnp.zeros_like(norm_grad_ref)

    x = x_ref[...].astype(F32)
    normed, inverse_std = normalize(x)
    rows = (normed * norm_ref[0:1, :] + norm_ref[1:2, :]).astype(BF)
    grad = grad_ref[...]
    low_grad = grad.astype(BF)
    head_out = out_ref[...]
    wo_grad_ref[...] += tn(head_out, low_grad)
    out_grad = (nt(low_grad, wo_ref[...]).astype(BF) * mask_ref[0].astype(BF))
    first, second = lane_halves()
    for pair in range(PAIRS):
        lanes = slice(PAIR * pair, PAIR * (pair + 1))
        key_lanes = slice(D + PAIR * pair, D + PAIR * (pair + 1))
        value_lanes = slice(2 * D + PAIR * pair, 2 * D + PAIR * (pair + 1))
        queries = qkv_ref[:, lanes]
        keys = qkv_ref[:, key_lanes]
        values = qkv_ref[:, value_lanes]
        prob = prob_ref[0, pair]
        pair_grad = stacked(out_grad[:, lanes], first, second)
        dots = out_grad[:, lanes].astype(F32) * head_out[:, lanes].astype(F32)
        row_dot = jnp.concatenate(
            [
                jnp.sum(dots * first.astype(F32), axis=-1, keepdims=True),
                jnp.sum(dots * second.astype(F32), axis=-1, keepdims=True),
            ],
            axis=0,
        )
        prob_grad = nt(pair_grad, values)
        score_grad = (prob.astype(F32) * (prob_grad - row_dot)).astype(BF)
        dqkv_ref[:, lanes] = (
            nn(score_grad[:S], keys * first) + nn(score_grad[S:], keys * second)
        ).astype(BF)
        dqkv_ref[:, key_lanes] = tn(score_grad, stacked(queries, first, second)).astype(BF)
        dqkv_ref[:, value_lanes] = tn(prob, pair_grad).astype(BF)
    dqkv = dqkv_ref[...]
    wqkv_grad_ref[...] += tn(rows, dqkv)
    back = nt(dqkv, wqkv_ref[...])
    grad_in, norm_part = norm_backward(back, normed, inverse_std, norm_ref[0:1, :])
    norm_grad_ref[...] += norm_part
    in_grad_ref[...] = grad + grad_in

    @pl.when(step == pl.num_programs(0) - 1)
    def _():
        for side, slab_grads in enumerate((own_grad_ref, sent_grad_ref)):
            for slab in range(12):
                pieces = []
                for unit in (2 * slab, 2 * slab + 1):
                    row, part = divmod(unit, 3)
                    piece = wqkv_grad_ref[48 * row : 48 * row + 48, D * part : D * part + D]
                    piece = piece[:, HALF * side : HALF * side + HALF]
                    pieces.append(piece * 0.125 if part == 0 else piece)
                joined = jnp.concatenate(pieces, axis=1)
                slab_grads[slab_at(slab)] = joined.astype(slab_grads.dtype)
            for row in range(HALF // 48):
                start = HALF * side + 48 * row
                joined = wo_grad_ref[start : start + 48, :]
                slab_grads[slab_at(12 + row)] = joined.astype(slab_grads.dtype)


def attn_backward(tokens, grad, prob, qkv, out, mask_lanes, norm_params, wqkv, wo):
    rows = tokens.shape[0]
    images = rows // S
    tile = pl.BlockSpec((S, D), lambda i: (i, 0))
    slab = pl.BlockSpec((SLABS, 48, D), lambda i: (0, 0, 0))
    return pl.pallas_call(
        attn_backward_kernel,
        grid=(images,),
        in_specs=[
            tile,
            tile,
            pl.BlockSpec((1, PAIRS, 2 * S, S), lambda i: (i, 0, 0, 0)),
            pl.BlockSpec((S, 3 * D), lambda i: (i, 0)),
            tile,
            pl.BlockSpec((1, 1, D), lambda i: (i, 0, 0)),
            pl.BlockSpec((4, D), lambda i: (0, 0)),
            pl.BlockSpec((D, 3 * D), lambda i: (0, 0)),
            pl.BlockSpec((D, D), lambda i: (0, 0)),
        ],
        out_specs=[
            tile,
            slab,
            slab,
            pl.BlockSpec((2, D), lambda i: (0, 0)),
        ],
        out_shape=[
            jax.ShapeDtypeStruct((rows, D), F32),
            jax.ShapeDtypeStruct((SLABS, 48, D), F32),
            jax.ShapeDtypeStruct((SLABS, 48, D), BF),
            jax.ShapeDtypeStruct((2, D), F32),
        ],
        scratch_shapes=[
            pltpu.VMEM((S, 3 * D), BF),
            pltpu.VMEM((D, 3 * D), F32),
            pltpu.VMEM((D, D), F32),
        ],
        compiler_params=pltpu.CompilerParams(vmem_limit_bytes=VMEM_LIMIT),
        cost_estimate=pl.CostEstimate(
            flops=rows * D * (16 * D + 32 * S), bytes_accessed=20 << 20, transcendentals=0
        ),
        name="attn_backward",
    )(tokens, grad, prob, qkv, out, mask_lanes, norm_params, wqkv, wo)


def split(values):
    high = values.astype(BF)
    return high, (values - high.astype(F32)).astype(BF)


def stack(*pieces):
    return jnp.concatenate(pieces, axis=0)


def cut_rows(values, number):
    edge = values.shape[0] // number
    return [values[edge * i : edge * i + edge] for i in range(number)]


def product(left, right):
    high, low = left
    right_high, right_low = right
    one, two = cut_rows(nn(stack(high, low), right_high), 2)
    return one + (two + nn(high, right_low))


def two_products(left, middle, right):
    right_high, right_low = right
    both = cut_rows(nn(stack(left[0], middle[0], left[1], middle[1]), right_high), 4)
    high = cut_rows(nn(stack(left[0], middle[0]), right_low), 2)
    return both[0] + (both[2] + high[0]), both[1] + (both[3] + high[1])


def shampoo_kernel(scale, grad_ref, weight_ref, left_ref, right_ref, *refs):
    out_grad_ref, left_new_ref, right_new_ref, new_weight_ref, root_ref, power_ref = refs[-6:]
    count, edge = weight_ref.shape[1], weight_ref.shape[2]
    pack = min(PACK, count)
    packs = count // pack
    width = pack * edge

    def block_of(shape, dim):
        return lax.broadcasted_iota(jnp.int32, shape, dim) // edge

    row = lax.broadcasted_iota(jnp.int32, (edge, width), 0)
    lane = lax.broadcasted_iota(jnp.int32, (edge, width), 1)
    identity = (lane % edge == row).astype(F32)
    same = (block_of((width, width), 0) == block_of((width, width), 1)).astype(BF)
    lane_block = block_of((1, width), 1)

    def spread(pieces):
        return tuple(stack(*[piece] * pack) * same for piece in pieces)

    def cut(packed, index):
        return packed[:, edge * index : edge * index + edge]

    def beside(ref, number):
        return jnp.concatenate([ref[0, pack * number + i] for i in range(pack)], axis=1)

    grads, parts = [], []
    for number in range(packs):
        grad = grad_ref[0, :, width * number : width * number + width] * scale
        blocks = [cut(grad, index) for index in range(pack)]
        for index in range(pack):
            out_grad_ref[0, pack * number + index] = blocks[index]
        grad_t = jnp.concatenate([jnp.transpose(block) for block in blocks], axis=1)
        one, two = split(grad), split(grad_t)
        one_diagonal, two_diagonal = spread(one), spread(two)
        grads.append(one_diagonal)
        parts.append((left_ref, left_new_ref, one, two_diagonal))
        parts.append((right_ref, right_new_ref, two, one_diagonal))
    grams = [product(left, right) for _, _, left, right in parts]
    for slot, (old_ref, new_ref, _, _) in enumerate(parts):
        new = 0.5 * beside(old_ref, slot // 2) + 0.5 * grams[slot]
        for index in range(pack):
            new_ref[0, pack * (slot // 2) + index] = cut(new, index)
        columns = jnp.sum(new * new, axis=0, keepdims=True)
        squares = jnp.zeros((1, width), F32)
        for index in range(pack):
            inside = lane_block == index
            part = jnp.sum(jnp.where(inside, columns, 0.0), axis=1, keepdims=True)
            squares = jnp.where(inside, part, squares)
        factor = 2.5 / jnp.sqrt(squares)
        root_ref[slot] = jnp.broadcast_to(jnp.sqrt(jnp.sqrt(factor)), (edge, width))
        power_ref[slot] = factor * new
    slots = range(2 * packs)

    def advance(first):
        powers = [power_ref[slot] for slot in slots]
        middles = [split((5.0 * identity - power) * 0.25) for power in powers]
        rights = [spread(middle) for middle in middles]
        powers = [split(power) for power in powers]
        if first:
            squares = [product(middles[s], rights[s]) for s in slots]
            for slot in slots:
                root_ref[slot] *= (5.0 * identity - power_ref[slot]) * 0.25
        else:
            roots = [split(root_ref[slot]) for slot in slots]
            both = [two_products(roots[s], middles[s], rights[s]) for s in slots]
            squares = [pair[1] for pair in both]
            for slot in slots:
                root_ref[slot] = both[slot][0]
        rights = [spread(split(square)) for square in squares]
        powers = [split(product(powers[s], rights[s])) for s in slots]
        for slot in slots:
            power_ref[slot] = product(powers[slot], rights[slot])

    advance(True)
    lax.fori_loop(0, ITERS - 2, lambda _, carry: advance(False) or carry, 0)
    rights = [spread(split((5.0 * identity - power_ref[slot]) * 0.25)) for slot in slots]
    for slot in slots:
        root_ref[slot] = product(split(root_ref[slot]), rights[slot])
    steps = [product(split(root_ref[2 * n]), grads[n]) for n in range(packs)]
    rights = [spread(split(root_ref[2 * n + 1])) for n in range(packs)]
    steps = [product(split(steps[n]), rights[n]) for n in range(packs)]
    for number in range(packs):
        for index in range(pack):
            block = pack * number + index
            new_weight_ref[0, block] = weight_ref[0, block] - 0.25 * cut(steps[number], index)


def shampoo(grads, weights, stat_left, stat_right, scale, first, earlier=()):
    groups, edge, _ = grads.shape
    _, count, _, _ = weights.shape
    packs = count // min(PACK, count)
    width = min(PACK, count) * edge
    block = pl.BlockSpec((1, count, edge, edge), lambda i: (i + first, 0, 0, 0))
    shape = jax.ShapeDtypeStruct(weights.shape, F32)
    return pl.pallas_call(
        lambda *refs: shampoo_kernel(scale, *refs),
        grid=(groups,),
        in_specs=[
            pl.BlockSpec((1, edge, count * edge), lambda i: (i, 0, 0)), block, block, block,
            *[pl.BlockSpec(memory_space=pl.ANY) for _ in earlier],
        ],
        out_specs=[block] * 4,
        out_shape=[shape] * 4,
        scratch_shapes=[
            pltpu.VMEM((2 * packs, edge, width), F32),
            pltpu.VMEM((2 * packs, edge, width), F32),
        ],
        input_output_aliases={4 + i: i for i in range(len(earlier))},
        compiler_params=pltpu.CompilerParams(vmem_limit_bytes=VMEM_LIMIT),
        cost_estimate=pl.CostEstimate(
            flops=groups * (3 << 30), bytes_accessed=4 << 20, transcendentals=0
        ),
        name="shampoo",
    )(grads, weights, stat_left, stat_right, *earlier)


def swap_heads(values):
    return lax.ppermute(values, "head", [(0, 1), (1, 0)])


def to_all(values, axis):
    return lax.all_to_all(values, axis, 0, 0)


def copies(values, number):
    return jnp.broadcast_to(values[None], (number,) + values.shape)


def gather_slabs(local):
    inner, outer = lax.axis_size("inner"), lax.axis_size("outer")
    column = to_all(copies(local, outer), "outer")
    early = to_all(copies(column[:, 0], inner), "inner")
    early = early.reshape((SLABS,) + early.shape[2:])
    column, early = lax.optimization_barrier((column, early))
    late = to_all(copies(column[:, 1:], inner), "inner")
    return early, late.reshape((SLABS,) + late.shape[2:])


def gather_blocks(local):
    groups, _, edge, _ = local.shape
    blocks = lax.all_gather(local, ("outer", "inner"), axis=1, tiled=True)
    blocks = blocks.reshape(groups, SLABS // INNER, INNER, D // edge, edge, edge)
    slabs = blocks.transpose(2, 1, 0, 4, 3, 5).reshape(SLABS, groups, edge, D)
    return slabs if groups > 1 else slabs[:, 0]


def scatter_blocks(slabs, count, edge):
    groups = slabs.shape[1]
    blocks = slabs.reshape(INNER, SLABS // INNER, groups, edge, D // edge, edge)
    blocks = blocks.transpose(2, 1, 0, 4, 3, 5).reshape(groups, SLABS * (D // edge), edge, edge)
    owned = lax.psum_scatter(blocks, ("outer", "inner"), scatter_dimension=1, tiled=True)
    return owned.transpose(0, 2, 1, 3).reshape(groups, edge, count * edge)


def with_norms(slabs, norms):
    high, low = split(norms)
    rows = jnp.concatenate([high, low, jnp.zeros_like(high), jnp.zeros_like(high)], axis=0)
    return jnp.concatenate([slabs, copies(rows, SLABS)], axis=1)


def per_device(
    tokens,
    cotangent,
    token_counts,
    head_mask,
    norm_params,
    norm_state,
    weights,
    stat_left,
    stat_right,
):
    weights, stat_left, stat_right = weights[0], stat_left[0], stat_right[0]
    _, count, edge, _ = weights.shape
    whole_slabs = count * edge == D
    images = tokens.shape[0] // S
    half = lax.axis_index("head")
    counts = lax.dynamic_slice_in_dim(token_counts, half * images, images)
    own_mask = lax.dynamic_slice_in_dim(head_mask, half * images, images)
    sent_mask = lax.dynamic_slice_in_dim(head_mask, (1 - half) * images, images)
    mask = jnp.concatenate([own_mask, swap_heads(sent_mask)], axis=1)
    mask_lanes = jnp.repeat(mask.astype(F32), HEAD_DIM, axis=1)[:, None, :]

    local = weights.astype(BF)
    if whole_slabs:
        local = local.transpose(0, 2, 1, 3).reshape(-1, edge, D)
        early, late = gather_slabs(local)
    else:
        early, late = gather_blocks(local[:1]), gather_blocks(local[1:])
    prob, qkv, out, middle, wqkv, wo = attn_forward(
        counts, tokens, mask_lanes, norm_params, early, swap_heads(early)
    )
    late, middle = lax.optimization_barrier((late, middle))
    block_out, middle_grad, own_late, sent_late, norm_two = mlp(
        middle, cotangent, norm_params, late, swap_heads(late)
    )
    late_slabs = (own_late + swap_heads(sent_late).astype(F32)).astype(BF)
    late_slabs, middle_grad = lax.optimization_barrier((late_slabs, middle_grad))
    input_grad, own_early, sent_early, norm_one = attn_backward(
        tokens, middle_grad, prob, qkv, out, mask_lanes, norm_params, wqkv, wo
    )
    early_slabs = (own_early + swap_heads(sent_early).astype(F32)).astype(BF)
    norms = jnp.concatenate([norm_one, norm_two], axis=0)
    if whole_slabs:
        late_received = to_all(late_slabs, ("inner", "outer"))
        sent = with_norms(early_slabs, norms + swap_heads(norms))
        late_received, sent = lax.optimization_barrier((late_received, sent))
        late_owned = jnp.sum(late_received.astype(F32), axis=0)
        received = jnp.sum(to_all(sent, ("inner", "outer")).astype(F32), axis=0)
        early_owned, norm_total = received[None, :48], received[48:52] + received[52:56]
    else:
        late_owned = scatter_blocks(late_slabs, count, edge).astype(F32)
        early_owned = scatter_blocks(early_slabs[:, None], count, edge).astype(F32)
        norm_total = lax.psum(norms, ("outer", "inner", "head"))
    devices = lax.axis_size("outer") * lax.axis_size("inner") * lax.axis_size("head")
    scale = 1.0 / math.sqrt(tokens.shape[0] * devices)
    state = (weights, stat_left, stat_right, scale)
    results = shampoo(late_owned, *state, 1)
    grads, left_new, right_new, new_weights = shampoo(early_owned, *state, 0, results)
    norm_grads = norm_total * scale
    state_new = 0.5 * norm_state + 0.5 * norm_grads * norm_grads
    norm_new = norm_params - 0.2 * norm_grads / jnp.sqrt(state_new)
    return (
        block_out,
        input_grad,
        grads[None],
        left_new[None],
        right_new[None],
        new_weights[None],
        norm_grads,
        state_new,
        norm_new,
    )


def solution(mesh):
    shape = (mesh.shape["dp"] // INNER, INNER, mesh.shape["head"])
    split_mesh = Mesh(mesh.devices.reshape(shape), ("outer", "inner", "head"))
    group = ("outer", "inner")
    blocks = P("head", None, group, None, None)
    rows = P(group + ("head",), None)
    return jax.shard_map(
        per_device,
        mesh=split_mesh,
        in_specs=(rows, rows, P(group), P(group, "head"), P(), P(), blocks, blocks, blocks),
        out_specs=(rows, rows, blocks, blocks, blocks, blocks, P(), P(), P()),
        check_vma=False,
    )
```

```python
import math

import jax
import jax.numpy as jnp
from jax import lax
from jax.experimental import pallas as pl
from jax.experimental.pallas import tpu as pltpu
from jax.sharding import Mesh, PartitionSpec as P

D = 384
HEAD_DIM = 64
MLP = 1536
S = 256
ITERS = 8
PAIR = 2 * HEAD_DIM
PAIRS = D // PAIR
HALF = D // 2
SLABS = 16
INNER = 4
TILE = 512
IMAGES = TILE // S
NORM_ROWS = 8
HIDDEN = 768
PACK = 2
ROOT_HALF = 0.7071067811865476
DENSITY_FACTOR = 0.3989422804014327
BF = jnp.bfloat16
F32 = jnp.float32
VMEM_LIMIT = 40 << 20
SMALL_VMEM = 8 << 20


def nn(left, right):
    return jnp.dot(left, right, preferred_element_type=F32)


def nt(left, right):
    return lax.dot_general(left, right, (((1,), (1,)), ((), ())), preferred_element_type=F32)


def tn(left, right):
    return lax.dot_general(left, right, (((0,), (0,)), ((), ())), preferred_element_type=F32)


def normalize(values):
    centered = values - jnp.mean(values, axis=-1, keepdims=True)
    variance = jnp.mean(centered * centered, axis=-1, keepdims=True)
    inverse_std = lax.rsqrt(variance + 1e-06)
    return centered * inverse_std, inverse_std


def norm_backward(grad_out, normed, inverse_std, gain):
    grad_normed = grad_out * gain
    mean_first = jnp.mean(grad_normed, axis=-1, keepdims=True)
    mean_second = jnp.mean(grad_normed * normed, axis=-1, keepdims=True)
    grad_in = inverse_std * (grad_normed - mean_first - normed * mean_second)
    gain_grad = jnp.sum(grad_out * normed, axis=0, keepdims=True)
    shift_grad = jnp.sum(grad_out, axis=0, keepdims=True)
    return grad_in, jnp.concatenate([gain_grad, shift_grad], axis=0)


def slab_at(owner):
    return (owner % INNER) * (SLABS // INNER) + owner // INNER


def lane_halves():
    lane = lax.broadcasted_iota(jnp.int32, (1, PAIR), 1)
    first = (lane < HEAD_DIM).astype(BF)
    return first, (1 - first).astype(BF)


def stacked(values, first, second):
    return jnp.concatenate([values * first, values * second], axis=0)


def mask_lanes(half_ref, own_ref, other_ref, image, pair):
    image = half_ref[0] * (own_ref.shape[0] // 2) + image
    heads = own_ref.shape[1]
    on = [
        own_ref[image, head] if head < heads else other_ref[image, head - heads]
        for head in (2 * pair, 2 * pair + 1)
    ]
    lane = lax.broadcasted_iota(jnp.int32, (1, PAIR), 1)
    return jnp.where(lane < HEAD_DIM, on[0], on[1]).astype(F32)


def attn_forward_kernel(
    half_ref, counts_ref, own_mask_ref, other_mask_ref, x_ref, norm_ref, own_ref, other_ref,
    prob_ref, qkv_ref, out_ref, middle_ref, wqkv_ref, wo_ref,
):
    step = pl.program_id(0)

    @pl.when(step == 0)
    def _():
        slabs = (own_ref, other_ref)
        for row in range(D // 48):
            for part in range(3):
                pieces = []
                for ref in slabs:
                    slab, side = divmod(3 * row + part, 2)
                    pieces.append(ref[slab_at(slab)][:, side * HALF : (side + 1) * HALF])
                joined = jnp.concatenate(pieces, axis=1)
                if part == 0:
                    joined = joined * 0.125
                wqkv_ref[48 * row : 48 * row + 48, D * part : D * part + D] = joined
        for side, ref in enumerate(slabs):
            for row in range(HALF // 48):
                start = side * HALF + 48 * row
                wo_ref[start : start + 48, :] = ref[slab_at(12 + row)]

    x = x_ref[...].astype(F32)
    normed, _ = normalize(x)
    rows = (normed * norm_ref[0:1, :] + norm_ref[1:2, :]).astype(BF)
    qkv_ref[...] = nn(rows, wqkv_ref[...]).astype(BF)
    first, second = lane_halves()
    column = lax.broadcasted_iota(jnp.int32, (1, S), 1)
    tasks = [(image, pair) for image in range(IMAGES) for pair in range(PAIRS)]

    def places(task):
        image, pair = task
        here = slice(S * image, S * image + S)
        return here, *(slice(D * t + PAIR * pair, D * t + PAIR * (pair + 1)) for t in range(3))

    def get_scores(task):
        here, query_lanes, key_lanes, _ = places(task)
        return nt(stacked(qkv_ref[here, query_lanes], first, second), qkv_ref[here, key_lanes])

    def get_prob(task, scores):
        image = half_ref[0] * (counts_ref.shape[0] // 2) + IMAGES * step + task[0]
        scores = jnp.where(column < counts_ref[image], scores, -1e30)
        top = jnp.max(scores, axis=-1, keepdims=True)
        exp_scores = jnp.exp(scores - top)
        total = jnp.sum(exp_scores, axis=-1, keepdims=True)
        prob = (exp_scores * (1.0 / total)).astype(BF)
        prob_ref[task] = prob
        return prob

    all_scores = [get_scores(task) for task in tasks]
    probs = [get_prob(task, scores) for task, scores in zip(tasks, all_scores)]
    for task, prob in zip(tasks, probs):
        here, lanes, _, value_lanes = places(task)
        values = qkv_ref[here, value_lanes]
        head_out = nn(prob[:S], values * first) + nn(prob[S:], values * second)
        mask = mask_lanes(half_ref, own_mask_ref, other_mask_ref, IMAGES * step + task[0], task[1])
        out_ref[here, lanes] = (head_out * mask).astype(BF)
    middle_ref[...] = x + nn(out_ref[...], wo_ref[...])


def attn_forward(half, counts, own_mask, other_mask, tokens, norm_params, own, other):
    rows = tokens.shape[0]
    images = rows // S
    tile = pl.BlockSpec((TILE, D), lambda i: (i, 0))
    slab = pl.BlockSpec((SLABS, 48, D), lambda i: (0, 0, 0))
    smem = pl.BlockSpec(memory_space=pltpu.SMEM)
    return pl.pallas_call(
        attn_forward_kernel,
        grid=(rows // TILE,),
        in_specs=[smem] * 4 + [tile, pl.BlockSpec((4, D), lambda i: (0, 0)), slab, slab],
        out_specs=[
            pl.BlockSpec((IMAGES, PAIRS, 2 * S, S), lambda i: (i, 0, 0, 0)),
            pl.BlockSpec((TILE, 3 * D), lambda i: (i, 0)),
            tile,
            tile,
            pl.BlockSpec((D, 3 * D), lambda i: (0, 0)),
            pl.BlockSpec((D, D), lambda i: (0, 0)),
        ],
        out_shape=[
            jax.ShapeDtypeStruct((images, PAIRS, 2 * S, S), BF),
            jax.ShapeDtypeStruct((rows, 3 * D), BF),
            jax.ShapeDtypeStruct((rows, D), BF),
            jax.ShapeDtypeStruct((rows, D), F32),
            jax.ShapeDtypeStruct((D, 3 * D), BF),
            jax.ShapeDtypeStruct((D, D), BF),
        ],
        compiler_params=pltpu.CompilerParams(vmem_limit_bytes=VMEM_LIMIT),
        cost_estimate=pl.CostEstimate(
            flops=rows * D * (8 * D + 16 * S), bytes_accessed=16 << 20, transcendentals=rows * 6 * S
        ),
        name="attn_forward",
    )(half, counts, own_mask, other_mask, tokens, norm_params, own, other)


def mlp_kernel(
    middle_ref, cot_ref, norm_ref, own_ref, other_ref,
    out_ref, grad_ref, own_grad_ref, sent_grad_ref, norm_grad_ref,
    up_ref, down_ref, up_grad_ref, down_grad_ref,
):
    step = pl.program_id(0)
    sides = ((own_ref, own_grad_ref), (other_ref, sent_grad_ref))
    places = [
        (side, part, MLP // 2 * side + D * part, row)
        for side in range(2)
        for part in range(2)
        for row in range(8)
    ]

    @pl.when(step == 0)
    def _():
        up_grad_ref[...] = jnp.zeros_like(up_grad_ref)
        down_grad_ref[...] = jnp.zeros_like(down_grad_ref)
        norm_grad_ref[...] = jnp.zeros_like(norm_grad_ref)
        for side, part, start, row in places:
            up = sides[side][0][slab_at(2 * row + part), 0]
            up_ref[48 * row : 48 * row + 48, start : start + D] = up
            down = sides[side][0][slab_at(8 * part + row), 1]
            down_ref[start + 48 * row : start + 48 * row + 48, :] = down

    middle = middle_ref[...]
    normed, inverse_std = normalize(middle)
    rows = (normed * norm_ref[2:3, :] + norm_ref[3:4, :]).astype(BF)
    cot = cot_ref[...]
    total = middle
    back = None
    for start in range(0, MLP, HIDDEN):
        hidden = slice(start, start + HIDDEN)
        up, down = up_ref[:, hidden], down_ref[hidden, :]
        pre = nn(rows, up)
        act_grad = nt(cot, down)
        cumulative = 0.5 * (1.0 + lax.erf(pre * ROOT_HALF))
        density = jnp.exp(-0.5 * pre * pre) * DENSITY_FACTOR
        act = (pre * cumulative).astype(BF)
        pre_grad = (act_grad * (cumulative + pre * density)).astype(BF)
        total = total + nn(act, down)
        term = nt(pre_grad, up)
        back = term if back is None else back + term
        down_grad_ref[hidden, :] += tn(act, cot)
        up_grad_ref[:, hidden] += tn(rows, pre_grad)
    out_ref[...] = total
    grad_in, norm_part = norm_backward(back, normed, inverse_std, norm_ref[2:3, :])
    norm_grad_ref[...] += norm_part
    grad_ref[...] = cot.astype(F32) + grad_in

    @pl.when(step == pl.num_programs(0) - 1)
    def _():
        for side, part, start, row in places:
            ref = sides[side][1]
            up = up_grad_ref[48 * row : 48 * row + 48, start : start + D]
            ref[slab_at(2 * row + part), 0] = up.astype(ref.dtype)
            down = down_grad_ref[start + 48 * row : start + 48 * row + 48, :]
            ref[slab_at(8 * part + row), 1] = down.astype(ref.dtype)


def mlp(middle, cotangent, norm_params, own, other):
    rows = middle.shape[0]
    slabs = (SLABS, 2, 48, D)
    slab = pl.BlockSpec(slabs, lambda i: (0, 0, 0, 0))
    tile = pl.BlockSpec((TILE, D), lambda i: (i, 0))
    return pl.pallas_call(
        mlp_kernel,
        grid=(rows // TILE,),
        in_specs=[tile, tile, pl.BlockSpec((4, D), lambda i: (0, 0)), slab, slab],
        out_specs=[tile, tile, slab, slab, pl.BlockSpec((2, D), lambda i: (0, 0))],
        out_shape=[
            jax.ShapeDtypeStruct((rows, D), F32),
            jax.ShapeDtypeStruct((rows, D), F32),
            jax.ShapeDtypeStruct(slabs, BF),
            jax.ShapeDtypeStruct(slabs, BF),
            jax.ShapeDtypeStruct((2, D), F32),
        ],
        scratch_shapes=[
            pltpu.VMEM((D, MLP), BF),
            pltpu.VMEM((MLP, D), BF),
            pltpu.VMEM((D, MLP), F32),
            pltpu.VMEM((MLP, D), F32),
        ],
        compiler_params=pltpu.CompilerParams(vmem_limit_bytes=VMEM_LIMIT),
        cost_estimate=pl.CostEstimate(
            flops=12 * rows * D * MLP, bytes_accessed=20 << 20, transcendentals=2 * rows * MLP
        ),
        name="mlp",
    )(middle, cotangent, norm_params, own, other)


def attn_backward_kernel(
    half_ref, own_mask_ref, other_mask_ref, x_ref, grad_ref, prob_ref, qkv_ref, out_ref,
    norm_ref, later_norm_ref, wqkv_ref, wo_ref,
    in_grad_ref, own_grad_ref, sent_grad_ref, norm_grad_ref,
    dqkv_ref, wqkv_grad_ref, wo_grad_ref,
):
    step = pl.program_id(0)

    @pl.when(step == 0)
    def _():
        wqkv_grad_ref[...] = jnp.zeros_like(wqkv_grad_ref)
        wo_grad_ref[...] = jnp.zeros_like(wo_grad_ref)
        norm_grad_ref[0:2, :] = jnp.zeros((2, D), F32)
        norm_grad_ref[2:4, :] = later_norm_ref[...]

    x = x_ref[...].astype(F32)
    normed, inverse_std = normalize(x)
    rows = (normed * norm_ref[0:1, :] + norm_ref[1:2, :]).astype(BF)
    grad = grad_ref[...]
    low_grad = grad.astype(BF)
    head_out = out_ref[...]
    wo_grad_ref[...] += tn(head_out, low_grad)
    whole_grad = nt(low_grad, wo_ref[...]).astype(BF)
    first, second = lane_halves()
    first_wide, second_wide = first.astype(F32), second.astype(F32)
    tasks = [(image, pair) for image in range(IMAGES) for pair in range(PAIRS)]

    def places(task):
        image, pair = task
        here = slice(S * image, S * image + S)
        return here, *(slice(D * t + PAIR * pair, D * t + PAIR * (pair + 1)) for t in range(3))

    def get_pair_grad(task):
        here, lanes, _, _ = places(task)
        mask = mask_lanes(half_ref, own_mask_ref, other_mask_ref, IMAGES * step + task[0], task[1])
        grad = whole_grad[here, lanes] * mask.astype(BF)
        dots = grad.astype(F32) * head_out[here, lanes].astype(F32)
        first_dot = jnp.sum(dots * first_wide, axis=-1, keepdims=True)
        second_dot = jnp.sum(dots * second_wide, axis=-1, keepdims=True)
        return stacked(grad, first, second), jnp.concatenate([first_dot, second_dot], axis=0)

    pair_grads = [get_pair_grad(task) for task in tasks]
    prob_grads = [
        nt(pair_grad[0], qkv_ref[places(task)[0], places(task)[3]])
        for task, pair_grad in zip(tasks, pair_grads)
    ]
    score_grads = [
        (prob_ref[task].astype(F32) * (prob_grad - pair_grad[1])).astype(BF)
        for task, prob_grad, pair_grad in zip(tasks, prob_grads, pair_grads)
    ]
    for task, score_grad, (pair_grad, _) in zip(tasks, score_grads, pair_grads):
        here, query_lanes, key_lanes, value_lanes = places(task)
        keys = qkv_ref[here, key_lanes]
        queries = stacked(qkv_ref[here, query_lanes], first, second)
        query_grad = nn(score_grad[:S], keys * first) + nn(score_grad[S:], keys * second)
        key_grad = nn(jnp.transpose(queries), score_grad)
        value_grad = nn(jnp.transpose(pair_grad), prob_ref[task])
        dqkv_ref[here, query_lanes] = query_grad.astype(BF)
        dqkv_ref[here, key_lanes] = jnp.transpose(key_grad).astype(BF)
        dqkv_ref[here, value_lanes] = jnp.transpose(value_grad).astype(BF)
    dqkv = dqkv_ref[...]
    wqkv_grad_ref[...] += tn(rows, dqkv)
    back = nt(dqkv, wqkv_ref[...])
    grad_in, norm_part = norm_backward(back, normed, inverse_std, norm_ref[0:1, :])
    norm_grad_ref[0:2, :] += norm_part
    in_grad_ref[...] = grad + grad_in

    @pl.when(step == pl.num_programs(0) - 1)
    def _():
        for side, slab_grads in enumerate((own_grad_ref, sent_grad_ref)):
            for slab in range(12):
                pieces = []
                for unit in (2 * slab, 2 * slab + 1):
                    row, part = divmod(unit, 3)
                    piece = wqkv_grad_ref[48 * row : 48 * row + 48, D * part : D * part + D]
                    piece = piece[:, HALF * side : HALF * side + HALF]
                    pieces.append(piece * 0.125 if part == 0 else piece)
                slab_grads[slab_at(slab)] = jnp.concatenate(pieces, axis=1).astype(BF)
            for row in range(HALF // 48):
                start = HALF * side + 48 * row
                slab_grads[slab_at(12 + row)] = wo_grad_ref[start : start + 48, :].astype(BF)
        sent_grad_ref[SLABS, :NORM_ROWS] = jnp.concatenate(split(norm_grad_ref[...]), axis=0)
        sent_grad_ref[SLABS, NORM_ROWS:] = jnp.zeros((48 - NORM_ROWS, D), BF)


def attn_backward(
    half, own_mask, other_mask, tokens, grad, prob, qkv, out, norm_params, later_norms, wqkv, wo
):
    rows = tokens.shape[0]
    tile = pl.BlockSpec((TILE, D), lambda i: (i, 0))
    smem = pl.BlockSpec(memory_space=pltpu.SMEM)
    return pl.pallas_call(
        attn_backward_kernel,
        grid=(rows // TILE,),
        in_specs=[
            smem,
            smem,
            smem,
            tile,
            tile,
            pl.BlockSpec((IMAGES, PAIRS, 2 * S, S), lambda i: (i, 0, 0, 0)),
            pl.BlockSpec((TILE, 3 * D), lambda i: (i, 0)),
            tile,
            pl.BlockSpec((4, D), lambda i: (0, 0)),
            pl.BlockSpec((2, D), lambda i: (0, 0)),
            pl.BlockSpec((D, 3 * D), lambda i: (0, 0)),
            pl.BlockSpec((D, D), lambda i: (0, 0)),
        ],
        out_specs=[
            tile,
            pl.BlockSpec((SLABS, 48, D), lambda i: (0, 0, 0)),
            pl.BlockSpec((SLABS + 1, 48, D), lambda i: (0, 0, 0)),
            pl.BlockSpec((4, D), lambda i: (0, 0)),
        ],
        out_shape=[
            jax.ShapeDtypeStruct((rows, D), F32),
            jax.ShapeDtypeStruct((SLABS, 48, D), BF),
            jax.ShapeDtypeStruct((SLABS + 1, 48, D), BF),
            jax.ShapeDtypeStruct((4, D), F32),
        ],
        scratch_shapes=[
            pltpu.VMEM((TILE, 3 * D), BF),
            pltpu.VMEM((D, 3 * D), F32),
            pltpu.VMEM((D, D), F32),
        ],
        compiler_params=pltpu.CompilerParams(vmem_limit_bytes=VMEM_LIMIT),
        cost_estimate=pl.CostEstimate(
            flops=rows * D * (16 * D + 32 * S), bytes_accessed=20 << 20, transcendentals=0
        ),
        name="attn_backward",
    )(half, own_mask, other_mask, tokens, grad, prob, qkv, out, norm_params, later_norms, wqkv, wo)


def pack_kernel(weight_ref, early_ref, late_ref):
    groups, count, _, _ = weight_ref.shape
    for group in range(groups):
        blocks = [weight_ref[group, block] for block in range(count)]
        slab = jnp.concatenate(blocks, axis=1).astype(BF)
        for copy in range(early_ref.shape[0]):
            if group == 0:
                early_ref[copy] = slab
            else:
                late_ref[copy, group - 1] = slab


def pack(weights, number):
    groups, count, edge, _ = weights.shape
    return pl.pallas_call(
        pack_kernel,
        out_shape=[
            jax.ShapeDtypeStruct((number, edge, count * edge), BF),
            jax.ShapeDtypeStruct((number, groups - 1, edge, count * edge), BF),
        ],
        compiler_params=pltpu.CompilerParams(vmem_limit_bytes=SMALL_VMEM),
        name="pack",
    )(weights)


def add_kernel(one_ref, two_ref, out_ref):
    out_ref[...] = (one_ref[...].astype(F32) + two_ref[...].astype(F32)).astype(BF)


def add_slabs(one, two):
    block = pl.BlockSpec((4,) + one.shape[1:], lambda i: (i, 0, 0, 0))
    return pl.pallas_call(
        add_kernel,
        grid=(one.shape[0] // 4,),
        in_specs=[block, block],
        out_specs=block,
        out_shape=jax.ShapeDtypeStruct(one.shape, BF),
        compiler_params=pltpu.CompilerParams(vmem_limit_bytes=SMALL_VMEM),
        name="add_slabs",
    )(one, two)


def combine_kernel(own_ref, received_ref, norm_ref, out_ref):
    slabs = own_ref.shape[0]
    total = own_ref[...].astype(F32) + received_ref[:slabs].astype(F32)
    out_ref[:, :48] = total.astype(BF)
    norms = received_ref[slabs, :NORM_ROWS].astype(F32)
    norms = norm_ref[...] + (norms[:4] + norms[4:])
    rows = jnp.concatenate(split(norms), axis=0)
    out_ref[:, 48:] = jnp.broadcast_to(rows[None], (slabs, NORM_ROWS, D))


def combine(own, received, norms):
    return pl.pallas_call(
        combine_kernel,
        out_shape=jax.ShapeDtypeStruct((SLABS, 48 + NORM_ROWS, D), BF),
        compiler_params=pltpu.CompilerParams(vmem_limit_bytes=SMALL_VMEM),
        name="combine",
    )(own, received, norms)


def split(values):
    high = values.astype(BF)
    return high, (values - high.astype(F32)).astype(BF)


def stack(*pieces):
    return jnp.concatenate(pieces, axis=0)


def cut_rows(values, number):
    edge = values.shape[0] // number
    return [values[edge * i : edge * i + edge] for i in range(number)]


def product(left, right):
    high, low = left
    right_high, right_low = right
    one, two = cut_rows(nn(stack(high, low), right_high), 2)
    return one + (two + nn(high, right_low))


def two_products(left, middle, right):
    right_high, right_low = right
    both = cut_rows(nn(stack(left[0], middle[0], left[1], middle[1]), right_high), 4)
    high = cut_rows(nn(stack(left[0], middle[0]), right_low), 2)
    return both[0] + (both[2] + high[0]), both[1] + (both[3] + high[1])


def update_norms(scale, total, param_ref, state_ref, grad_ref, new_state_ref, new_ref):
    grads = total * scale
    state = 0.5 * state_ref[...] + 0.5 * grads * grads
    grad_ref[...] = grads
    new_state_ref[...] = state
    new_ref[...] = param_ref[...] - 0.2 * grads / jnp.sqrt(state)


def shampoo_kernel(scale, with_norms, received_ref, weight_ref, left_ref, right_ref, *refs):
    if with_norms:
        norm_ins, norm_outs, refs = refs[:2], refs[-5:-2], refs[:-5] + refs[-2:]
    out_grad_ref, left_new_ref, right_new_ref, new_weight_ref, root_ref, power_ref = refs[-6:]
    count, edge = weight_ref.shape[1], weight_ref.shape[2]
    received = received_ref[0].astype(F32)
    for number in range(1, received_ref.shape[0]):
        received = received + received_ref[number].astype(F32)
    received = received.reshape(received.shape[-2:])
    if with_norms:
        total = received[edge : edge + 4] + received[edge + 4 : edge + NORM_ROWS]
        update_norms(scale, total, *norm_ins, *norm_outs)
    pack = min(PACK, count)
    packs = count // pack
    width = pack * edge

    def block_of(shape, dim):
        return lax.broadcasted_iota(jnp.int32, shape, dim) // edge

    row = lax.broadcasted_iota(jnp.int32, (edge, width), 0)
    lane = lax.broadcasted_iota(jnp.int32, (edge, width), 1)
    identity = (lane % edge == row).astype(F32)
    same = (block_of((width, width), 0) == block_of((width, width), 1)).astype(BF)
    lane_block = block_of((1, width), 1)

    def spread(pieces):
        return tuple(stack(*[piece] * pack) * same for piece in pieces)

    def cut(packed, index):
        return packed[:, edge * index : edge * index + edge]

    def beside(ref, number):
        return jnp.concatenate([ref[0, pack * number + i] for i in range(pack)], axis=1)

    grads, parts = [], []
    for number in range(packs):
        grad = received[:edge, width * number : width * number + width] * scale
        blocks = [cut(grad, index) for index in range(pack)]
        for index in range(pack):
            out_grad_ref[0, pack * number + index] = blocks[index]
        grad_t = jnp.concatenate([jnp.transpose(block) for block in blocks], axis=1)
        one, two = split(grad), split(grad_t)
        one_diagonal, two_diagonal = spread(one), spread(two)
        grads.append(one_diagonal)
        parts.append((left_ref, left_new_ref, one, two_diagonal))
        parts.append((right_ref, right_new_ref, two, one_diagonal))
    grams = [product(left, right) for _, _, left, right in parts]
    for slot, (old_ref, new_ref, _, _) in enumerate(parts):
        new = 0.5 * beside(old_ref, slot // 2) + 0.5 * grams[slot]
        for index in range(pack):
            new_ref[0, pack * (slot // 2) + index] = cut(new, index)
        columns = jnp.sum(new * new, axis=0, keepdims=True)
        squares = jnp.zeros((1, width), F32)
        for index in range(pack):
            inside = lane_block == index
            part = jnp.sum(jnp.where(inside, columns, 0.0), axis=1, keepdims=True)
            squares = jnp.where(inside, part, squares)
        factor = 2.5 / jnp.sqrt(squares)
        root_ref[slot] = jnp.broadcast_to(jnp.sqrt(jnp.sqrt(factor)), (edge, width))
        power_ref[slot] = factor * new
    slots = range(2 * packs)

    def advance(first):
        powers = [power_ref[slot] for slot in slots]
        middles = [split((5.0 * identity - power) * 0.25) for power in powers]
        rights = [spread(middle) for middle in middles]
        powers = [split(power) for power in powers]
        if first:
            squares = [product(middles[s], rights[s]) for s in slots]
            for slot in slots:
                root_ref[slot] *= (5.0 * identity - power_ref[slot]) * 0.25
        else:
            roots = [split(root_ref[slot]) for slot in slots]
            both = [two_products(roots[s], middles[s], rights[s]) for s in slots]
            squares = [pair[1] for pair in both]
            for slot in slots:
                root_ref[slot] = both[slot][0]
        rights = [spread(split(square)) for square in squares]
        powers = [split(product(powers[s], rights[s])) for s in slots]
        for slot in slots:
            power_ref[slot] = product(powers[slot], rights[slot])

    advance(True)
    lax.fori_loop(0, ITERS - 2, lambda _, carry: advance(False) or carry, 0)
    rights = [spread(split((5.0 * identity - power_ref[slot]) * 0.25)) for slot in slots]
    for slot in slots:
        root_ref[slot] = product(split(root_ref[slot]), rights[slot])
    steps = [product(split(root_ref[2 * n]), grads[n]) for n in range(packs)]
    rights = [spread(split(root_ref[2 * n + 1])) for n in range(packs)]
    steps = [product(split(steps[n]), rights[n]) for n in range(packs)]
    for number in range(packs):
        for index in range(pack):
            block = pack * number + index
            new_weight_ref[0, block] = weight_ref[0, block] - 0.25 * cut(steps[number], index)


def shampoo(received, weights, stat_left, stat_right, scale, first, earlier=(), norms=()):
    sources, groups, rows, lanes = received.shape
    _, count, edge, _ = weights.shape
    packs = count // min(PACK, count)
    width = min(PACK, count) * edge
    block = pl.BlockSpec((1, count, edge, edge), lambda i: (i + first, 0, 0, 0))
    shape = jax.ShapeDtypeStruct(weights.shape, F32)
    norm = pl.BlockSpec((4, D), lambda i: (0, 0))
    norm_outs = 3 if norms else 0
    ins = 4 + len(norms)
    return pl.pallas_call(
        lambda *refs: shampoo_kernel(scale, bool(norms), *refs),
        grid=(groups,),
        in_specs=[
            pl.BlockSpec((sources, 1, rows, lanes), lambda i: (0, i, 0, 0)),
            *[block] * 3,
            *[norm] * len(norms),
            *[pl.BlockSpec(memory_space=pl.ANY)] * len(earlier),
        ],
        out_specs=[block] * 4 + [norm] * norm_outs,
        out_shape=[shape] * 4 + [jax.ShapeDtypeStruct((4, D), F32)] * norm_outs,
        scratch_shapes=[
            pltpu.VMEM((2 * packs, edge, width), F32),
            pltpu.VMEM((2 * packs, edge, width), F32),
        ],
        input_output_aliases={ins + i: i for i in range(len(earlier))},
        compiler_params=pltpu.CompilerParams(vmem_limit_bytes=SMALL_VMEM),
        cost_estimate=pl.CostEstimate(
            flops=groups * (3 << 30), bytes_accessed=4 << 20, transcendentals=0
        ),
        name="shampoo",
    )(received, weights, stat_left, stat_right, *norms, *earlier)


def swap_heads(values):
    return lax.ppermute(values, "head", [(0, 1), (1, 0)])


def to_all(values, axis):
    return lax.all_to_all(values, axis, 0, 0)


def copies(values, number):
    return jnp.broadcast_to(values[None], (number,) + values.shape)


def flat(slabs):
    return slabs.reshape((SLABS,) + slabs.shape[2:])


def gather_slabs(weights, other_mask):
    inner, outer = lax.axis_size("inner"), lax.axis_size("outer")
    early, late = pack(weights, outer)
    early = to_all(early, "outer")
    early, late = lax.optimization_barrier((early, late))
    early = to_all(copies(early, inner), "inner")
    late = copies(to_all(late, "outer"), inner)
    early, late, other_mask = lax.optimization_barrier((early, late, other_mask))
    return flat(early), flat(to_all(late, "inner")), other_mask


def gather_blocks(local):
    groups, _, edge, _ = local.shape
    blocks = lax.all_gather(local, ("outer", "inner"), axis=1, tiled=True)
    blocks = blocks.reshape(groups, SLABS // INNER, INNER, D // edge, edge, edge)
    slabs = blocks.transpose(2, 1, 0, 4, 3, 5).reshape(SLABS, groups, edge, D)
    return slabs if groups > 1 else slabs[:, 0]


def scatter_blocks(slabs, count, edge):
    groups = slabs.shape[1]
    blocks = slabs.reshape(INNER, SLABS // INNER, groups, edge, D // edge, edge)
    blocks = blocks.transpose(2, 1, 0, 4, 3, 5).reshape(groups, SLABS * (D // edge), edge, edge)
    owned = lax.psum_scatter(blocks, ("outer", "inner"), scatter_dimension=1, tiled=True)
    return owned.transpose(0, 2, 1, 3).reshape(groups, edge, count * edge)


def per_device(
    tokens,
    cotangent,
    token_counts,
    head_mask,
    norm_params,
    norm_state,
    weights,
    stat_left,
    stat_right,
):
    weights, stat_left, stat_right = weights[0], stat_left[0], stat_right[0]
    _, count, edge, _ = weights.shape
    whole_slabs = count * edge == D
    half = lax.axis_index("head").reshape(1)
    other_mask = swap_heads(head_mask)
    if whole_slabs:
        early, late, other_mask = gather_slabs(weights, other_mask)
    else:
        local = weights.astype(BF)
        early, late = gather_blocks(local[:1]), gather_blocks(local[1:])
    masks = (head_mask, other_mask)
    prob, qkv, out, middle, wqkv, wo = attn_forward(
        half, token_counts, *masks, tokens, norm_params, early, swap_heads(early)
    )
    late, middle = lax.optimization_barrier((late, middle))
    block_out, middle_grad, own_late, sent_late, norm_two = mlp(
        middle, cotangent, norm_params, late, swap_heads(late)
    )
    late_slabs = add_slabs(own_late, swap_heads(sent_late))
    late_slabs, middle_grad = lax.optimization_barrier((late_slabs, middle_grad))
    input_grad, own_early, sent_early, norm_sums = attn_backward(
        half, *masks, tokens, middle_grad, prob, qkv, out, norm_params, norm_two, wqkv, wo
    )
    early_slabs = combine(own_early, swap_heads(sent_early), norm_sums)
    devices = lax.axis_size("outer") * lax.axis_size("inner") * lax.axis_size("head")
    scale = 1.0 / math.sqrt(tokens.shape[0] * devices)
    state = (weights, stat_left, stat_right, scale)
    norms = (norm_params, norm_state)
    if whole_slabs:
        late_received = to_all(late_slabs, ("inner", "outer"))
        late_received, early_slabs = lax.optimization_barrier((late_received, early_slabs))
        results = shampoo(late_received, *state, 1)
        early_received = to_all(early_slabs, ("inner", "outer"))[:, None]
        results = shampoo(early_received, *state, 0, results, norms)
    else:
        late_received = scatter_blocks(late_slabs, count, edge)[None]
        early_received = scatter_blocks(early_slabs[:, None, :48], count, edge)[None]
        norm_total = lax.psum(norm_sums, ("outer", "inner", "head"))
        results = shampoo(late_received, *state, 1)
        results = list(shampoo(early_received, *state, 0, results))
        norm_grads = norm_total * scale
        state_new = 0.5 * norm_state + 0.5 * norm_grads * norm_grads
        results += [norm_grads, state_new, norm_params - 0.2 * norm_grads / jnp.sqrt(state_new)]
    return (block_out, input_grad, *[result[None] for result in results[:4]], *results[4:])


def solution(mesh):
    shape = (mesh.shape["dp"] // INNER, INNER, mesh.shape["head"])
    split_mesh = Mesh(mesh.devices.reshape(shape), ("outer", "inner", "head"))
    group = ("outer", "inner")
    blocks = P("head", None, group, None, None)
    rows = P(group + ("head",), None)
    return jax.shard_map(
        per_device,
        mesh=split_mesh,
        in_specs=(rows, rows, P(group), P(group, "head"), P(), P(), blocks, blocks, blocks),
        out_specs=(rows, rows, blocks, blocks, blocks, blocks, P(), P(), P()),
        check_vma=False,
    )
```

```python
import math

import jax
import jax.numpy as jnp
from jax import lax
from jax.experimental import pallas as pl
from jax.experimental.pallas import tpu as pltpu
from jax.sharding import Mesh, PartitionSpec as P

D = 384
HEAD_DIM = 64
MLP = 1536
S = 256
ITERS = 8
PAIR = 2 * HEAD_DIM
PAIRS = D // PAIR
HALF = D // 2
SLABS = 16
INNER = 4
TILE = 512
IMAGES = TILE // S
NORM_ROWS = 8
HIDDEN = 768
PACK = 2
ROOT_HALF = 0.7071067811865476
DENSITY_FACTOR = 0.3989422804014327
BF = jnp.bfloat16
F32 = jnp.float32
VMEM_LIMIT = 40 << 20
SMALL_VMEM = 8 << 20


def in_hbm(values):
    return pltpu.with_memory_space_constraint(values, pltpu.HBM)


def nn(left, right):
    return jnp.dot(left, right, preferred_element_type=F32)


def nt(left, right):
    return lax.dot_general(left, right, (((1,), (1,)), ((), ())), preferred_element_type=F32)


def tn(left, right):
    return lax.dot_general(left, right, (((0,), (0,)), ((), ())), preferred_element_type=F32)


def normalize(values):
    centered = values - jnp.mean(values, axis=-1, keepdims=True)
    variance = jnp.mean(centered * centered, axis=-1, keepdims=True)
    inverse_std = lax.rsqrt(variance + 1e-06)
    return centered * inverse_std, inverse_std


def norm_backward(grad_out, normed, inverse_std, gain):
    grad_normed = grad_out * gain
    mean_first = jnp.mean(grad_normed, axis=-1, keepdims=True)
    mean_second = jnp.mean(grad_normed * normed, axis=-1, keepdims=True)
    grad_in = inverse_std * (grad_normed - mean_first - normed * mean_second)
    gain_grad = jnp.sum(grad_out * normed, axis=0, keepdims=True)
    shift_grad = jnp.sum(grad_out, axis=0, keepdims=True)
    return grad_in, jnp.concatenate([gain_grad, shift_grad], axis=0)


def slab_at(owner):
    return (owner % INNER) * (SLABS // INNER) + owner // INNER


def lane_halves():
    lane = lax.broadcasted_iota(jnp.int32, (1, PAIR), 1)
    first = (lane < HEAD_DIM).astype(BF)
    return first, (1 - first).astype(BF)


def stacked(values, first, second):
    return jnp.concatenate([values * first, values * second], axis=0)


def mask_lanes(half_ref, own_ref, other_ref, image, pair):
    image = half_ref[0] * (own_ref.shape[0] // 2) + image
    heads = own_ref.shape[1]
    on = [
        own_ref[image, head] if head < heads else other_ref[image, head - heads]
        for head in (2 * pair, 2 * pair + 1)
    ]
    lane = lax.broadcasted_iota(jnp.int32, (1, PAIR), 1)
    return jnp.where(lane < HEAD_DIM, on[0], on[1]).astype(F32)


def attn_forward_kernel(
    half_ref, counts_ref, own_mask_ref, other_mask_ref, x_ref, norm_ref, own_ref, other_ref,
    prob_ref, qkv_ref, out_ref, middle_ref, wqkv_ref, wo_ref,
):
    step = pl.program_id(0)

    @pl.when(step == 0)
    def _():
        slabs = (own_ref, other_ref)
        for row in range(D // 48):
            for part in range(3):
                pieces = []
                for ref in slabs:
                    slab, side = divmod(3 * row + part, 2)
                    pieces.append(ref[slab_at(slab)][:, side * HALF : (side + 1) * HALF])
                joined = jnp.concatenate(pieces, axis=1)
                if part == 0:
                    joined = joined * 0.125
                wqkv_ref[48 * row : 48 * row + 48, D * part : D * part + D] = joined
        for side, ref in enumerate(slabs):
            for row in range(HALF // 48):
                start = side * HALF + 48 * row
                wo_ref[start : start + 48, :] = ref[slab_at(12 + row)]

    x = x_ref[...].astype(F32)
    normed, _ = normalize(x)
    rows = (normed * norm_ref[0:1, :] + norm_ref[1:2, :]).astype(BF)
    qkv_ref[...] = nn(rows, wqkv_ref[...]).astype(BF)
    first, second = lane_halves()
    column = lax.broadcasted_iota(jnp.int32, (1, S), 1)
    tasks = [(image, pair) for image in range(IMAGES) for pair in range(PAIRS)]

    def places(task):
        image, pair = task
        here = slice(S * image, S * image + S)
        return here, *(slice(D * t + PAIR * pair, D * t + PAIR * (pair + 1)) for t in range(3))

    def get_scores(task):
        here, query_lanes, key_lanes, _ = places(task)
        return nt(stacked(qkv_ref[here, query_lanes], first, second), qkv_ref[here, key_lanes])

    def get_prob(task, scores):
        image = half_ref[0] * (counts_ref.shape[0] // 2) + IMAGES * step + task[0]
        scores = jnp.where(column < counts_ref[image], scores, -1e30)
        top = jnp.max(scores, axis=-1, keepdims=True)
        exp_scores = jnp.exp(scores - top)
        total = jnp.sum(exp_scores, axis=-1, keepdims=True)
        prob = (exp_scores * (1.0 / total)).astype(BF)
        prob_ref[task] = prob
        return prob

    all_scores = [get_scores(task) for task in tasks]
    probs = [get_prob(task, scores) for task, scores in zip(tasks, all_scores)]
    for task, prob in zip(tasks, probs):
        here, lanes, _, value_lanes = places(task)
        values = qkv_ref[here, value_lanes]
        head_out = nn(prob[:S], values * first) + nn(prob[S:], values * second)
        mask = mask_lanes(half_ref, own_mask_ref, other_mask_ref, IMAGES * step + task[0], task[1])
        out_ref[here, lanes] = (head_out * mask).astype(BF)
    middle_ref[...] = x + nn(out_ref[...], wo_ref[...])


def attn_forward(half, counts, own_mask, other_mask, tokens, norm_params, own, other):
    rows = tokens.shape[0]
    images = rows // S
    tile = pl.BlockSpec((TILE, D), lambda i: (i, 0))
    slab = pl.BlockSpec((SLABS, 48, D), lambda i: (0, 0, 0))
    smem = pl.BlockSpec(memory_space=pltpu.SMEM)
    return pl.pallas_call(
        attn_forward_kernel,
        grid=(rows // TILE,),
        in_specs=[smem] * 4 + [tile, pl.BlockSpec((4, D), lambda i: (0, 0)), slab, slab],
        out_specs=[
            pl.BlockSpec((IMAGES, PAIRS, 2 * S, S), lambda i: (i, 0, 0, 0)),
            pl.BlockSpec((TILE, 3 * D), lambda i: (i, 0)),
            tile,
            tile,
            pl.BlockSpec((D, 3 * D), lambda i: (0, 0)),
            pl.BlockSpec((D, D), lambda i: (0, 0)),
        ],
        out_shape=[
            pltpu.HBM((images, PAIRS, 2 * S, S), BF),
            pltpu.HBM((rows, 3 * D), BF),
            pltpu.HBM((rows, D), BF),
            pltpu.HBM((rows, D), F32),
            pltpu.HBM((D, 3 * D), BF),
            pltpu.HBM((D, D), BF),
        ],
        compiler_params=pltpu.CompilerParams(vmem_limit_bytes=VMEM_LIMIT),
        cost_estimate=pl.CostEstimate(
            flops=rows * D * (8 * D + 16 * S), bytes_accessed=16 << 20, transcendentals=rows * 6 * S
        ),
        name="attn_forward",
    )(half, counts, own_mask, other_mask, in_hbm(tokens), in_hbm(norm_params), own, other)


def mlp_kernel(
    middle_ref, cot_ref, norm_ref, own_ref, other_ref,
    out_ref, grad_ref, own_grad_ref, sent_grad_ref, norm_grad_ref,
    up_ref, down_ref, up_grad_ref, down_grad_ref,
):
    step = pl.program_id(0)
    sides = ((own_ref, own_grad_ref), (other_ref, sent_grad_ref))
    places = [
        (side, part, MLP // 2 * side + D * part, row)
        for side in range(2)
        for part in range(2)
        for row in range(8)
    ]

    @pl.when(step == 0)
    def _():
        up_grad_ref[...] = jnp.zeros_like(up_grad_ref)
        down_grad_ref[...] = jnp.zeros_like(down_grad_ref)
        norm_grad_ref[...] = jnp.zeros_like(norm_grad_ref)
        for side, part, start, row in places:
            up = sides[side][0][slab_at(2 * row + part), 0]
            up_ref[48 * row : 48 * row + 48, start : start + D] = up
            down = sides[side][0][slab_at(8 * part + row), 1]
            down_ref[start + 48 * row : start + 48 * row + 48, :] = down

    middle = middle_ref[...]
    normed, inverse_std = normalize(middle)
    rows = (normed * norm_ref[2:3, :] + norm_ref[3:4, :]).astype(BF)
    cot = cot_ref[...]
    total = middle
    back = None
    for start in range(0, MLP, HIDDEN):
        hidden = slice(start, start + HIDDEN)
        up, down = up_ref[:, hidden], down_ref[hidden, :]
        pre = nn(rows, up)
        act_grad = nt(cot, down)
        cumulative = 0.5 * (1.0 + lax.erf(pre * ROOT_HALF))
        density = jnp.exp(-0.5 * pre * pre) * DENSITY_FACTOR
        act = (pre * cumulative).astype(BF)
        pre_grad = (act_grad * (cumulative + pre * density)).astype(BF)
        total = total + nn(act, down)
        term = nt(pre_grad, up)
        back = term if back is None else back + term
        down_grad_ref[hidden, :] += tn(act, cot)
        up_grad_ref[:, hidden] += tn(rows, pre_grad)
    out_ref[...] = total
    grad_in, norm_part = norm_backward(back, normed, inverse_std, norm_ref[2:3, :])
    norm_grad_ref[...] += norm_part
    grad_ref[...] = cot.astype(F32) + grad_in

    @pl.when(step == pl.num_programs(0) - 1)
    def _():
        for side, part, start, row in places:
            ref = sides[side][1]
            up = up_grad_ref[48 * row : 48 * row + 48, start : start + D]
            ref[slab_at(2 * row + part), 0] = up.astype(ref.dtype)
            down = down_grad_ref[start + 48 * row : start + 48 * row + 48, :]
            ref[slab_at(8 * part + row), 1] = down.astype(ref.dtype)


def mlp(middle, cotangent, norm_params, own, other):
    rows = middle.shape[0]
    slabs = (SLABS, 2, 48, D)
    slab = pl.BlockSpec(slabs, lambda i: (0, 0, 0, 0))
    tile = pl.BlockSpec((TILE, D), lambda i: (i, 0))
    return pl.pallas_call(
        mlp_kernel,
        grid=(rows // TILE,),
        in_specs=[tile, tile, pl.BlockSpec((4, D), lambda i: (0, 0)), slab, slab],
        out_specs=[tile, tile, slab, slab, pl.BlockSpec((2, D), lambda i: (0, 0))],
        out_shape=[
            jax.ShapeDtypeStruct((rows, D), F32),
            pltpu.HBM((rows, D), F32),
            jax.ShapeDtypeStruct(slabs, BF),
            jax.ShapeDtypeStruct(slabs, BF),
            jax.ShapeDtypeStruct((2, D), F32),
        ],
        scratch_shapes=[
            pltpu.VMEM((D, MLP), BF),
            pltpu.VMEM((MLP, D), BF),
            pltpu.VMEM((D, MLP), F32),
            pltpu.VMEM((MLP, D), F32),
        ],
        compiler_params=pltpu.CompilerParams(vmem_limit_bytes=VMEM_LIMIT),
        cost_estimate=pl.CostEstimate(
            flops=12 * rows * D * MLP, bytes_accessed=20 << 20, transcendentals=2 * rows * MLP
        ),
        name="mlp",
    )(in_hbm(middle), in_hbm(cotangent), in_hbm(norm_params), own, other)


def attn_backward_kernel(
    half_ref, own_mask_ref, other_mask_ref, x_ref, grad_ref, prob_ref, qkv_ref, out_ref,
    norm_ref, later_norm_ref, wqkv_ref, wo_ref,
    in_grad_ref, own_grad_ref, sent_grad_ref, norm_grad_ref,
    dqkv_ref, wqkv_grad_ref, wo_grad_ref,
):
    step = pl.program_id(0)

    @pl.when(step == 0)
    def _():
        wqkv_grad_ref[...] = jnp.zeros_like(wqkv_grad_ref)
        wo_grad_ref[...] = jnp.zeros_like(wo_grad_ref)
        norm_grad_ref[0:2, :] = jnp.zeros((2, D), F32)
        norm_grad_ref[2:4, :] = later_norm_ref[...]

    x = x_ref[...].astype(F32)
    normed, inverse_std = normalize(x)
    rows = (normed * norm_ref[0:1, :] + norm_ref[1:2, :]).astype(BF)
    grad = grad_ref[...]
    low_grad = grad.astype(BF)
    head_out = out_ref[...]
    wo_grad_ref[...] += tn(head_out, low_grad)
    whole_grad = nt(low_grad, wo_ref[...]).astype(BF)
    first, second = lane_halves()
    first_wide, second_wide = first.astype(F32), second.astype(F32)
    tasks = [(image, pair) for image in range(IMAGES) for pair in range(PAIRS)]

    def places(task):
        image, pair = task
        here = slice(S * image, S * image + S)
        return here, *(slice(D * t + PAIR * pair, D * t + PAIR * (pair + 1)) for t in range(3))

    def get_pair_grad(task):
        here, lanes, _, _ = places(task)
        mask = mask_lanes(half_ref, own_mask_ref, other_mask_ref, IMAGES * step + task[0], task[1])
        grad = whole_grad[here, lanes] * mask.astype(BF)
        dots = grad.astype(F32) * head_out[here, lanes].astype(F32)
        first_dot = jnp.sum(dots * first_wide, axis=-1, keepdims=True)
        second_dot = jnp.sum(dots * second_wide, axis=-1, keepdims=True)
        return stacked(grad, first, second), jnp.concatenate([first_dot, second_dot], axis=0)

    pair_grads = [get_pair_grad(task) for task in tasks]
    prob_grads = [
        nt(pair_grad[0], qkv_ref[places(task)[0], places(task)[3]])
        for task, pair_grad in zip(tasks, pair_grads)
    ]
    score_grads = [
        (prob_ref[task].astype(F32) * (prob_grad - pair_grad[1])).astype(BF)
        for task, prob_grad, pair_grad in zip(tasks, prob_grads, pair_grads)
    ]
    for task, score_grad, (pair_grad, _) in zip(tasks, score_grads, pair_grads):
        here, query_lanes, key_lanes, value_lanes = places(task)
        keys = qkv_ref[here, key_lanes]
        queries = stacked(qkv_ref[here, query_lanes], first, second)
        query_grad = nn(score_grad[:S], keys * first) + nn(score_grad[S:], keys * second)
        key_grad = nn(jnp.transpose(queries), score_grad)
        value_grad = nn(jnp.transpose(pair_grad), prob_ref[task])
        dqkv_ref[here, query_lanes] = query_grad.astype(BF)
        dqkv_ref[here, key_lanes] = jnp.transpose(key_grad).astype(BF)
        dqkv_ref[here, value_lanes] = jnp.transpose(value_grad).astype(BF)
    dqkv = dqkv_ref[...]
    wqkv_grad_ref[...] += tn(rows, dqkv)
    back = nt(dqkv, wqkv_ref[...])
    grad_in, norm_part = norm_backward(back, normed, inverse_std, norm_ref[0:1, :])
    norm_grad_ref[0:2, :] += norm_part
    in_grad_ref[...] = grad + grad_in

    @pl.when(step == pl.num_programs(0) - 1)
    def _():
        for side, slab_grads in enumerate((own_grad_ref, sent_grad_ref)):
            for slab in range(12):
                pieces = []
                for unit in (2 * slab, 2 * slab + 1):
                    row, part = divmod(unit, 3)
                    piece = wqkv_grad_ref[48 * row : 48 * row + 48, D * part : D * part + D]
                    piece = piece[:, HALF * side : HALF * side + HALF]
                    pieces.append(piece * 0.125 if part == 0 else piece)
                slab_grads[slab_at(slab)] = jnp.concatenate(pieces, axis=1).astype(BF)
            for row in range(HALF // 48):
                start = HALF * side + 48 * row
                slab_grads[slab_at(12 + row)] = wo_grad_ref[start : start + 48, :].astype(BF)
        sent_grad_ref[SLABS, :NORM_ROWS] = jnp.concatenate(split(norm_grad_ref[...]), axis=0)
        sent_grad_ref[SLABS, NORM_ROWS:] = jnp.zeros((48 - NORM_ROWS, D), BF)


def attn_backward(
    half, own_mask, other_mask, tokens, grad, prob, qkv, out, norm_params, later_norms, wqkv, wo
):
    rows = tokens.shape[0]
    tile = pl.BlockSpec((TILE, D), lambda i: (i, 0))
    smem = pl.BlockSpec(memory_space=pltpu.SMEM)
    return pl.pallas_call(
        attn_backward_kernel,
        grid=(rows // TILE,),
        in_specs=[
            smem,
            smem,
            smem,
            tile,
            tile,
            pl.BlockSpec((IMAGES, PAIRS, 2 * S, S), lambda i: (i, 0, 0, 0)),
            pl.BlockSpec((TILE, 3 * D), lambda i: (i, 0)),
            tile,
            pl.BlockSpec((4, D), lambda i: (0, 0)),
            pl.BlockSpec((2, D), lambda i: (0, 0)),
            pl.BlockSpec((D, 3 * D), lambda i: (0, 0)),
            pl.BlockSpec((D, D), lambda i: (0, 0)),
        ],
        out_specs=[
            tile,
            pl.BlockSpec((SLABS, 48, D), lambda i: (0, 0, 0)),
            pl.BlockSpec((SLABS + 1, 48, D), lambda i: (0, 0, 0)),
            pl.BlockSpec((4, D), lambda i: (0, 0)),
        ],
        out_shape=[
            jax.ShapeDtypeStruct((rows, D), F32),
            jax.ShapeDtypeStruct((SLABS, 48, D), BF),
            jax.ShapeDtypeStruct((SLABS + 1, 48, D), BF),
            jax.ShapeDtypeStruct((4, D), F32),
        ],
        scratch_shapes=[
            pltpu.VMEM((TILE, 3 * D), BF),
            pltpu.VMEM((D, 3 * D), F32),
            pltpu.VMEM((D, D), F32),
        ],
        compiler_params=pltpu.CompilerParams(vmem_limit_bytes=VMEM_LIMIT),
        cost_estimate=pl.CostEstimate(
            flops=rows * D * (16 * D + 32 * S), bytes_accessed=20 << 20, transcendentals=0
        ),
        name="attn_backward",
    )(
        half, own_mask, other_mask,
        *map(in_hbm, (tokens, grad, prob, qkv, out, norm_params, later_norms, wqkv, wo)),
    )


def pack_kernel(weight_ref, early_ref, late_ref):
    groups, count, _, _ = weight_ref.shape
    for group in range(groups):
        blocks = [weight_ref[group, block] for block in range(count)]
        slab = jnp.concatenate(blocks, axis=1).astype(BF)
        for copy in range(early_ref.shape[0]):
            if group == 0:
                early_ref[copy] = slab
            else:
                late_ref[copy, group - 1] = slab


def pack(weights, number):
    groups, count, edge, _ = weights.shape
    return pl.pallas_call(
        pack_kernel,
        out_shape=[
            jax.ShapeDtypeStruct((number, edge, count * edge), BF),
            jax.ShapeDtypeStruct((number, groups - 1, edge, count * edge), BF),
        ],
        compiler_params=pltpu.CompilerParams(vmem_limit_bytes=SMALL_VMEM),
        name="pack",
    )(weights)


def add_kernel(one_ref, two_ref, out_ref):
    out_ref[...] = (one_ref[...].astype(F32) + two_ref[...].astype(F32)).astype(BF)


def add_slabs(one, two):
    block = pl.BlockSpec((4,) + one.shape[1:], lambda i: (i, 0, 0, 0))
    return pl.pallas_call(
        add_kernel,
        grid=(one.shape[0] // 4,),
        in_specs=[block, block],
        out_specs=block,
        out_shape=jax.ShapeDtypeStruct(one.shape, BF),
        compiler_params=pltpu.CompilerParams(vmem_limit_bytes=SMALL_VMEM),
        name="add_slabs",
    )(one, two)


def combine_kernel(own_ref, received_ref, norm_ref, out_ref):
    slabs = own_ref.shape[0]
    total = own_ref[...].astype(F32) + received_ref[:slabs].astype(F32)
    out_ref[:, :48] = total.astype(BF)
    norms = received_ref[slabs, :NORM_ROWS].astype(F32)
    norms = norm_ref[...] + (norms[:4] + norms[4:])
    rows = jnp.concatenate(split(norms), axis=0)
    out_ref[:, 48:] = jnp.broadcast_to(rows[None], (slabs, NORM_ROWS, D))


def combine(own, received, norms):
    return pl.pallas_call(
        combine_kernel,
        out_shape=jax.ShapeDtypeStruct((SLABS, 48 + NORM_ROWS, D), BF),
        compiler_params=pltpu.CompilerParams(vmem_limit_bytes=SMALL_VMEM),
        name="combine",
    )(own, received, norms)


def split(values):
    high = values.astype(BF)
    return high, (values - high.astype(F32)).astype(BF)


def stack(*pieces):
    return jnp.concatenate(pieces, axis=0)


def cut_rows(values, number):
    edge = values.shape[0] // number
    return [values[edge * i : edge * i + edge] for i in range(number)]


def product(left, right):
    high, low = left
    right_high, right_low = right
    one, two = cut_rows(nn(stack(high, low), right_high), 2)
    return one + (two + nn(high, right_low))


def two_products(left, middle, right):
    right_high, right_low = right
    both = cut_rows(nn(stack(left[0], middle[0], left[1], middle[1]), right_high), 4)
    high = cut_rows(nn(stack(left[0], middle[0]), right_low), 2)
    return both[0] + (both[2] + high[0]), both[1] + (both[3] + high[1])


def update_norms(scale, total, param_ref, state_ref, grad_ref, new_state_ref, new_ref):
    grads = total * scale
    state = 0.5 * state_ref[...] + 0.5 * grads * grads
    grad_ref[...] = grads
    new_state_ref[...] = state
    new_ref[...] = param_ref[...] - 0.2 * grads / jnp.sqrt(state)


def shampoo_kernel(scale, with_norms, received_ref, weight_ref, left_ref, right_ref, *refs):
    if with_norms:
        norm_ins, norm_outs, refs = refs[:2], refs[-5:-2], refs[:-5] + refs[-2:]
    out_grad_ref, left_new_ref, right_new_ref, new_weight_ref, root_ref, power_ref = refs[-6:]
    count, edge = weight_ref.shape[1], weight_ref.shape[2]
    received = received_ref[0].astype(F32)
    for number in range(1, received_ref.shape[0]):
        received = received + received_ref[number].astype(F32)
    received = received.reshape(received.shape[-2:])
    if with_norms:
        total = received[edge : edge + 4] + received[edge + 4 : edge + NORM_ROWS]
        update_norms(scale, total, *norm_ins, *norm_outs)
    pack = min(PACK, count)
    packs = count // pack
    width = pack * edge

    def block_of(shape, dim):
        return lax.broadcasted_iota(jnp.int32, shape, dim) // edge

    row = lax.broadcasted_iota(jnp.int32, (edge, width), 0)
    lane = lax.broadcasted_iota(jnp.int32, (edge, width), 1)
    identity = (lane % edge == row).astype(F32)
    same = (block_of((width, width), 0) == block_of((width, width), 1)).astype(BF)
    lane_block = block_of((1, width), 1)

    def spread(pieces):
        return tuple(stack(*[piece] * pack) * same for piece in pieces)

    def cut(packed, index):
        return packed[:, edge * index : edge * index + edge]

    def beside(ref, number):
        return jnp.concatenate([ref[0, pack * number + i] for i in range(pack)], axis=1)

    grads, parts = [], []
    for number in range(packs):
        grad = received[:edge, width * number : width * number + width] * scale
        blocks = [cut(grad, index) for index in range(pack)]
        for index in range(pack):
            out_grad_ref[0, pack * number + index] = blocks[index]
        grad_t = jnp.concatenate([jnp.transpose(block) for block in blocks], axis=1)
        one, two = split(grad), split(grad_t)
        one_diagonal, two_diagonal = spread(one), spread(two)
        grads.append(one_diagonal)
        parts.append((left_ref, left_new_ref, one, two_diagonal))
        parts.append((right_ref, right_new_ref, two, one_diagonal))
    grams = [product(left, right) for _, _, left, right in parts]
    for slot, (old_ref, new_ref, _, _) in enumerate(parts):
        new = 0.5 * beside(old_ref, slot // 2) + 0.5 * grams[slot]
        for index in range(pack):
            new_ref[0, pack * (slot // 2) + index] = cut(new, index)
        columns = jnp.sum(new * new, axis=0, keepdims=True)
        squares = jnp.zeros((1, width), F32)
        for index in range(pack):
            inside = lane_block == index
            part = jnp.sum(jnp.where(inside, columns, 0.0), axis=1, keepdims=True)
            squares = jnp.where(inside, part, squares)
        factor = 2.5 / jnp.sqrt(squares)
        root_ref[slot] = jnp.broadcast_to(jnp.sqrt(jnp.sqrt(factor)), (edge, width))
        power_ref[slot] = factor * new
    slots = range(2 * packs)

    def advance(first):
        powers = [power_ref[slot] for slot in slots]
        middles = [split((5.0 * identity - power) * 0.25) for power in powers]
        rights = [spread(middle) for middle in middles]
        powers = [split(power) for power in powers]
        if first:
            squares = [product(middles[s], rights[s]) for s in slots]
            for slot in slots:
                root_ref[slot] *= (5.0 * identity - power_ref[slot]) * 0.25
        else:
            roots = [split(root_ref[slot]) for slot in slots]
            both = [two_products(roots[s], middles[s], rights[s]) for s in slots]
            squares = [pair[1] for pair in both]
            for slot in slots:
                root_ref[slot] = both[slot][0]
        rights = [spread(split(square)) for square in squares]
        powers = [split(product(powers[s], rights[s])) for s in slots]
        for slot in slots:
            power_ref[slot] = product(powers[slot], rights[slot])

    advance(True)
    lax.fori_loop(0, ITERS - 2, lambda _, carry: advance(False) or carry, 0)
    rights = [spread(split((5.0 * identity - power_ref[slot]) * 0.25)) for slot in slots]
    for slot in slots:
        root_ref[slot] = product(split(root_ref[slot]), rights[slot])
    steps = [product(split(root_ref[2 * n]), grads[n]) for n in range(packs)]
    rights = [spread(split(root_ref[2 * n + 1])) for n in range(packs)]
    steps = [product(split(steps[n]), rights[n]) for n in range(packs)]
    for number in range(packs):
        for index in range(pack):
            block = pack * number + index
            new_weight_ref[0, block] = weight_ref[0, block] - 0.25 * cut(steps[number], index)


def shampoo(received, weights, stat_left, stat_right, scale, first, earlier=(), norms=()):
    sources, groups, rows, lanes = received.shape
    _, count, edge, _ = weights.shape
    packs = count // min(PACK, count)
    width = min(PACK, count) * edge
    block = pl.BlockSpec((1, count, edge, edge), lambda i: (i + first, 0, 0, 0))
    shape = jax.ShapeDtypeStruct(weights.shape, F32)
    norm = pl.BlockSpec((4, D), lambda i: (0, 0))
    norm_outs = 3 if norms else 0
    ins = 4 + len(norms)
    return pl.pallas_call(
        lambda *refs: shampoo_kernel(scale, bool(norms), *refs),
        grid=(groups,),
        in_specs=[
            pl.BlockSpec((sources, 1, rows, lanes), lambda i: (0, i, 0, 0)),
            *[block] * 3,
            *[norm] * len(norms),
            *[pl.BlockSpec(memory_space=pl.ANY)] * len(earlier),
        ],
        out_specs=[block] * 4 + [norm] * norm_outs,
        out_shape=[shape] * 4 + [jax.ShapeDtypeStruct((4, D), F32)] * norm_outs,
        scratch_shapes=[
            pltpu.VMEM((2 * packs, edge, width), F32),
            pltpu.VMEM((2 * packs, edge, width), F32),
        ],
        input_output_aliases={ins + i: i for i in range(len(earlier))},
        compiler_params=pltpu.CompilerParams(vmem_limit_bytes=SMALL_VMEM),
        cost_estimate=pl.CostEstimate(
            flops=groups * (3 << 30), bytes_accessed=4 << 20, transcendentals=0
        ),
        name="shampoo",
    )(received, in_hbm(weights), in_hbm(stat_left), in_hbm(stat_right), *map(in_hbm, norms), *earlier)


def swap_heads(values):
    return lax.ppermute(values, "head", [(0, 1), (1, 0)])


def to_all(values, axis):
    return lax.all_to_all(values, axis, 0, 0)


def copies(values, number):
    return jnp.broadcast_to(values[None], (number,) + values.shape)


def flat(slabs):
    return slabs.reshape((SLABS,) + slabs.shape[2:])


def gather_slabs(weights, other_mask):
    inner, outer = lax.axis_size("inner"), lax.axis_size("outer")
    early, late = pack(weights, outer)
    early = to_all(early, "outer")
    early, late = lax.optimization_barrier((early, late))
    early = to_all(copies(early, inner), "inner")
    late = copies(to_all(late, "outer"), inner)
    early, late, other_mask = lax.optimization_barrier((early, late, other_mask))
    return flat(early), flat(to_all(late, "inner")), other_mask


def gather_blocks(local):
    groups, _, edge, _ = local.shape
    blocks = lax.all_gather(local, ("outer", "inner"), axis=1, tiled=True)
    blocks = blocks.reshape(groups, SLABS // INNER, INNER, D // edge, edge, edge)
    slabs = blocks.transpose(2, 1, 0, 4, 3, 5).reshape(SLABS, groups, edge, D)
    return slabs if groups > 1 else slabs[:, 0]


def scatter_blocks(slabs, count, edge):
    groups = slabs.shape[1]
    blocks = slabs.reshape(INNER, SLABS // INNER, groups, edge, D // edge, edge)
    blocks = blocks.transpose(2, 1, 0, 4, 3, 5).reshape(groups, SLABS * (D // edge), edge, edge)
    owned = lax.psum_scatter(blocks, ("outer", "inner"), scatter_dimension=1, tiled=True)
    return owned.transpose(0, 2, 1, 3).reshape(groups, edge, count * edge)


def per_device(
    tokens,
    cotangent,
    token_counts,
    head_mask,
    norm_params,
    norm_state,
    weights,
    stat_left,
    stat_right,
):
    weights, stat_left, stat_right = weights[0], stat_left[0], stat_right[0]
    _, count, edge, _ = weights.shape
    whole_slabs = count * edge == D
    half = lax.axis_index("head").reshape(1)
    other_mask = swap_heads(head_mask)
    if whole_slabs:
        early, late, other_mask = gather_slabs(weights, other_mask)
    else:
        local = weights.astype(BF)
        early, late = gather_blocks(local[:1]), gather_blocks(local[1:])
    masks = (head_mask, other_mask)
    prob, qkv, out, middle, wqkv, wo = attn_forward(
        half, token_counts, *masks, tokens, norm_params, early, swap_heads(early)
    )
    late, middle = lax.optimization_barrier((late, middle))
    block_out, middle_grad, own_late, sent_late, norm_two = mlp(
        middle, cotangent, norm_params, late, swap_heads(late)
    )
    late_slabs = add_slabs(own_late, swap_heads(sent_late))
    late_slabs, middle_grad = lax.optimization_barrier((late_slabs, middle_grad))
    input_grad, own_early, sent_early, norm_sums = attn_backward(
        half, *masks, tokens, middle_grad, prob, qkv, out, norm_params, norm_two, wqkv, wo
    )
    early_slabs = combine(own_early, swap_heads(sent_early), norm_sums)
    devices = lax.axis_size("outer") * lax.axis_size("inner") * lax.axis_size("head")
    scale = 1.0 / math.sqrt(tokens.shape[0] * devices)
    state = (weights, stat_left, stat_right, scale)
    norms = (norm_params, norm_state)
    if whole_slabs:
        late_received = to_all(late_slabs, ("inner", "outer"))
        late_received, early_slabs = lax.optimization_barrier((late_received, early_slabs))
        results = shampoo(late_received, *state, 1)
        early_received = to_all(early_slabs, ("inner", "outer"))[:, None]
        results = shampoo(early_received, *state, 0, results, norms)
    else:
        late_received = scatter_blocks(late_slabs, count, edge)[None]
        early_received = scatter_blocks(early_slabs[:, None, :48], count, edge)[None]
        norm_total = lax.psum(norm_sums, ("outer", "inner", "head"))
        results = shampoo(late_received, *state, 1)
        results = list(shampoo(early_received, *state, 0, results))
        norm_grads = norm_total * scale
        state_new = 0.5 * norm_state + 0.5 * norm_grads * norm_grads
        results += [norm_grads, state_new, norm_params - 0.2 * norm_grads / jnp.sqrt(state_new)]
    return (block_out, input_grad, *[result[None] for result in results[:4]], *results[4:])


def solution(mesh):
    shape = (mesh.shape["dp"] // INNER, INNER, mesh.shape["head"])
    split_mesh = Mesh(mesh.devices.reshape(shape), ("outer", "inner", "head"))
    group = ("outer", "inner")
    blocks = P("head", None, group, None, None)
    rows = P(group + ("head",), None)
    return jax.shard_map(
        per_device,
        mesh=split_mesh,
        in_specs=(rows, rows, P(group), P(group, "head"), P(), P(), blocks, blocks, blocks),
        out_specs=(rows, rows, blocks, blocks, blocks, blocks, P(), P(), P()),
        check_vma=False,
    )
```

```python
import math

import jax
import jax.numpy as jnp
from jax import lax
from jax.experimental import pallas as pl
from jax.experimental.pallas import tpu as pltpu
from jax.sharding import Mesh, PartitionSpec as P

D = 384
HEAD_DIM = 64
MLP = 1536
S = 256
ITERS = 8
PAIR = 2 * HEAD_DIM
PAIRS = D // PAIR
HALF = D // 2
SLABS = 16
INNER = 4
OUTER = SLABS // INNER
TILE = 512
IMAGES = TILE // S
NORM_ROWS = 8
PACK = 2
ROOT_HALF = 0.7071067811865476
DENSITY_FACTOR = 0.3989422804014327
BF = jnp.bfloat16
F32 = jnp.float32
VMEM_LIMIT = 40 << 20
SMALL_VMEM = 8 << 20
SHAMPOO_VMEM = 24 << 20


def in_hbm(values):
    return pltpu.with_memory_space_constraint(values, pltpu.HBM)


def nn(left, right):
    return jnp.dot(left, right, preferred_element_type=F32)


def nt(left, right):
    return lax.dot_general(left, right, (((1,), (1,)), ((), ())), preferred_element_type=F32)


def tn(left, right):
    return lax.dot_general(left, right, (((0,), (0,)), ((), ())), preferred_element_type=F32)


def normalize(values):
    centered = values - jnp.mean(values, axis=-1, keepdims=True)
    variance = jnp.mean(centered * centered, axis=-1, keepdims=True)
    inverse_std = lax.rsqrt(variance + 1e-06)
    return centered * inverse_std, inverse_std


def norm_backward(grad_out, normed, inverse_std, gain):
    grad_normed = grad_out * gain
    mean_first = jnp.mean(grad_normed, axis=-1, keepdims=True)
    mean_second = jnp.mean(grad_normed * normed, axis=-1, keepdims=True)
    grad_in = inverse_std * (grad_normed - mean_first - normed * mean_second)
    gain_grad = jnp.sum(grad_out * normed, axis=0, keepdims=True)
    shift_grad = jnp.sum(grad_out, axis=0, keepdims=True)
    return grad_in, jnp.concatenate([gain_grad, shift_grad], axis=0)


def slab_at(owner):
    return (owner % INNER) * OUTER + owner // INNER


def lane_halves():
    lane = lax.broadcasted_iota(jnp.int32, (1, PAIR), 1)
    first = (lane < HEAD_DIM).astype(BF)
    return first, (1 - first).astype(BF)


def stacked(values, first, second):
    return jnp.concatenate([values * first, values * second], axis=0)


def mask_lanes(place_ref, own_ref, other_ref, image, pair):
    image = place_ref[0] * (own_ref.shape[0] // 2) + image
    heads = own_ref.shape[1]
    on = [
        own_ref[image, head] if head < heads else other_ref[image, head - heads]
        for head in (2 * pair, 2 * pair + 1)
    ]
    lane = lax.broadcasted_iota(jnp.int32, (1, PAIR), 1)
    return jnp.where(lane < HEAD_DIM, on[0], on[1]).astype(F32)


def attn_forward_kernel(
    place_ref, counts_ref, own_mask_ref, other_mask_ref, x_ref, norm_ref, *refs
):
    slab_refs, refs = refs[: 2 * INNER], refs[2 * INNER :]
    prob_ref, qkv_ref, out_ref, middle_ref, wqkv_ref, wo_ref, held_ref = refs
    step = pl.program_id(0)

    @pl.when(step == 0)
    def _():
        for number, ref in enumerate(slab_refs):
            side, apart = divmod(number, INNER)
            held_ref[side, place_ref[1] ^ apart] = ref[...]

        def slab_of(side, owner):
            return held_ref[side, owner % INNER, owner // INNER]

        for row in range(D // 48):
            for part in range(3):
                pieces = []
                for number in range(2):
                    slab, side = divmod(3 * row + part, 2)
                    piece = slab_of(number, slab)[:, side * HALF : (side + 1) * HALF]
                    pieces.append(piece)
                joined = jnp.concatenate(pieces, axis=1)
                if part == 0:
                    joined = joined * 0.125
                wqkv_ref[48 * row : 48 * row + 48, D * part : D * part + D] = joined
        for side in range(2):
            for row in range(HALF // 48):
                start = side * HALF + 48 * row
                wo_ref[start : start + 48, :] = slab_of(side, 12 + row)

    x = x_ref[...].astype(F32)
    normed, _ = normalize(x)
    rows = (normed * norm_ref[0:1, :] + norm_ref[1:2, :]).astype(BF)
    qkv_ref[...] = nn(rows, wqkv_ref[...]).astype(BF)
    first, second = lane_halves()
    column = lax.broadcasted_iota(jnp.int32, (1, S), 1)
    tasks = [(image, pair) for image in range(IMAGES) for pair in range(PAIRS)]

    def places(task):
        image, pair = task
        here = slice(S * image, S * image + S)
        return here, *(slice(D * t + PAIR * pair, D * t + PAIR * (pair + 1)) for t in range(3))

    def get_scores(task):
        here, query_lanes, key_lanes, _ = places(task)
        return nt(stacked(qkv_ref[here, query_lanes], first, second), qkv_ref[here, key_lanes])

    def get_prob(task, scores):
        image = place_ref[0] * (counts_ref.shape[0] // 2) + IMAGES * step + task[0]
        scores = jnp.where(column < counts_ref[image], scores, -1e30)
        top = jnp.max(scores, axis=-1, keepdims=True)
        exp_scores = jnp.exp(scores - top)
        total = jnp.sum(exp_scores, axis=-1, keepdims=True)
        prob = (exp_scores * (1.0 / total)).astype(BF)
        prob_ref[task] = prob
        return prob

    all_scores = [get_scores(task) for task in tasks]
    probs = [get_prob(task, scores) for task, scores in zip(tasks, all_scores)]
    for task, prob in zip(tasks, probs):
        here, lanes, _, value_lanes = places(task)
        values = qkv_ref[here, value_lanes]
        head_out = nn(prob[:S], values * first) + nn(prob[S:], values * second)
        mask = mask_lanes(place_ref, own_mask_ref, other_mask_ref, IMAGES * step + task[0], task[1])
        out_ref[here, lanes] = (head_out * mask).astype(BF)
    middle_ref[...] = x + nn(out_ref[...], wo_ref[...])


def attn_forward(place, counts, own_mask, other_mask, tokens, norm_params, slabs):
    rows = tokens.shape[0]
    images = rows // S
    tile = pl.BlockSpec((TILE, D), lambda i: (i, 0))
    slab = pl.BlockSpec((OUTER, 48, D), lambda i: (0, 0, 0))
    smem = pl.BlockSpec(memory_space=pltpu.SMEM)
    return pl.pallas_call(
        attn_forward_kernel,
        grid=(rows // TILE,),
        in_specs=[smem] * 4 + [tile, pl.BlockSpec((4, D), lambda i: (0, 0))] + [slab] * 2 * INNER,
        out_specs=[
            pl.BlockSpec((IMAGES, PAIRS, 2 * S, S), lambda i: (i, 0, 0, 0)),
            pl.BlockSpec((TILE, 3 * D), lambda i: (i, 0)),
            tile,
            tile,
            pl.BlockSpec((D, 3 * D), lambda i: (0, 0)),
            pl.BlockSpec((D, D), lambda i: (0, 0)),
        ],
        out_shape=[
            pltpu.HBM((images, PAIRS, 2 * S, S), BF),
            pltpu.HBM((rows, 3 * D), BF),
            pltpu.HBM((rows, D), BF),
            pltpu.HBM((rows, D), F32),
            pltpu.HBM((D, 3 * D), BF),
            pltpu.HBM((D, D), BF),
        ],
        scratch_shapes=[pltpu.VMEM((2, INNER, OUTER, 48, D), BF)],
        compiler_params=pltpu.CompilerParams(vmem_limit_bytes=VMEM_LIMIT),
        cost_estimate=pl.CostEstimate(
            flops=rows * D * (8 * D + 16 * S), bytes_accessed=16 << 20, transcendentals=rows * 6 * S
        ),
        name="attn_forward",
    )(place, counts, own_mask, other_mask, in_hbm(tokens), in_hbm(norm_params), *slabs)


def mlp_kernel(place_ref, middle_ref, cot_ref, norm_ref, *refs):
    slab_refs, refs = refs[: 2 * INNER], refs[2 * INNER :]
    out_ref, grad_ref, norm_grad_ref, *refs = refs
    sent_refs, (up_ref, down_ref, up_grad_ref, down_grad_ref) = refs[:INNER], refs[INNER:]
    step = pl.program_id(0)
    half = MLP // 2

    def places(apart, outer):
        inner = place_ref[1] ^ apart
        row = pl.multiple_of(48 * (2 * outer + inner // 2), 16)
        lane = pl.multiple_of(D * (inner % 2), 128)
        down_row = pl.multiple_of(48 * (INNER * outer + inner), 16)
        return row, lane, down_row

    @pl.when(step == 0)
    def _():
        up_grad_ref[...] = jnp.zeros_like(up_grad_ref)
        down_grad_ref[...] = jnp.zeros_like(down_grad_ref)
        norm_grad_ref[...] = jnp.zeros_like(norm_grad_ref)
        for number, ref in enumerate(slab_refs):
            side, apart = divmod(number, INNER)
            for outer in range(OUTER):
                row, lane, down_row = places(apart, outer)
                up_ref[side, pl.ds(row, 48), pl.ds(lane, D)] = ref[outer, 0]
                down_ref[side, pl.ds(down_row, 48), :] = ref[outer, 1]

    middle = middle_ref[...]
    normed, inverse_std = normalize(middle)
    rows = (normed * norm_ref[2:3, :] + norm_ref[3:4, :]).astype(BF)
    cot = cot_ref[...]
    total = middle
    back = None
    for side in range(2):
        up, down = up_ref[side], down_ref[side]
        pre = nn(rows, up)
        act_grad = nt(cot, down)
        cumulative = 0.5 * (1.0 + lax.erf(pre * ROOT_HALF))
        density = jnp.exp(-0.5 * pre * pre) * DENSITY_FACTOR
        act = (pre * cumulative).astype(BF)
        pre_grad = (act_grad * (cumulative + pre * density)).astype(BF)
        total = total + nn(act, down)
        term = nt(pre_grad, up)
        back = term if back is None else back + term
        down_grad_ref[side] += tn(act, cot)
        up_grad_ref[side] += tn(rows, pre_grad)
    out_ref[...] = total
    grad_in, norm_part = norm_backward(back, normed, inverse_std, norm_ref[2:3, :])
    norm_grad_ref[...] += norm_part
    grad_ref[...] = cot.astype(F32) + grad_in

    @pl.when(step == pl.num_programs(0) - 1)
    def _():
        for apart, ref in enumerate(sent_refs):
            for outer in range(OUTER):
                row, lane, down_row = places(apart, outer)
                for side in range(2):
                    up = up_grad_ref[side, pl.ds(row, 48), pl.ds(lane, D)]
                    ref[side, outer, 0] = up.astype(BF)
                    ref[side, outer, 1] = down_grad_ref[side, pl.ds(down_row, 48), :].astype(BF)


def mlp(place, middle, cotangent, norm_params, slabs):
    rows = middle.shape[0]
    slab = pl.BlockSpec((OUTER, 2, 48, D), lambda i: (0, 0, 0, 0))
    sent = pl.BlockSpec((2, OUTER, 2, 48, D), lambda i: (0, 0, 0, 0, 0))
    tile = pl.BlockSpec((TILE, D), lambda i: (i, 0))
    return pl.pallas_call(
        mlp_kernel,
        grid=(rows // TILE,),
        in_specs=[
            pl.BlockSpec(memory_space=pltpu.SMEM),
            tile,
            tile,
            pl.BlockSpec((4, D), lambda i: (0, 0)),
            *[slab] * 2 * INNER,
        ],
        out_specs=[tile, tile, pl.BlockSpec((2, D), lambda i: (0, 0)), *[sent] * INNER],
        out_shape=[
            jax.ShapeDtypeStruct((rows, D), F32),
            pltpu.HBM((rows, D), F32),
            jax.ShapeDtypeStruct((2, D), F32),
            *[jax.ShapeDtypeStruct((2, OUTER, 2, 48, D), BF)] * INNER,
        ],
        scratch_shapes=[
            pltpu.VMEM((2, D, MLP // 2), BF),
            pltpu.VMEM((2, MLP // 2, D), BF),
            pltpu.VMEM((2, D, MLP // 2), F32),
            pltpu.VMEM((2, MLP // 2, D), F32),
        ],
        compiler_params=pltpu.CompilerParams(vmem_limit_bytes=VMEM_LIMIT),
        cost_estimate=pl.CostEstimate(
            flops=12 * rows * D * MLP, bytes_accessed=20 << 20, transcendentals=2 * rows * MLP
        ),
        name="mlp",
    )(place, in_hbm(middle), in_hbm(cotangent), in_hbm(norm_params), *slabs)


def attn_backward_kernel(
    place_ref, own_mask_ref, other_mask_ref, x_ref, grad_ref, prob_ref, qkv_ref, out_ref,
    norm_ref, later_norm_ref, wqkv_ref, wo_ref,
    in_grad_ref, own_grad_ref, sent_grad_ref, norm_grad_ref,
    dqkv_ref, wqkv_grad_ref, wo_grad_ref,
):
    step = pl.program_id(0)

    @pl.when(step == 0)
    def _():
        wqkv_grad_ref[...] = jnp.zeros_like(wqkv_grad_ref)
        wo_grad_ref[...] = jnp.zeros_like(wo_grad_ref)
        norm_grad_ref[0:2, :] = jnp.zeros((2, D), F32)
        norm_grad_ref[2:4, :] = later_norm_ref[...]

    x = x_ref[...].astype(F32)
    normed, inverse_std = normalize(x)
    rows = (normed * norm_ref[0:1, :] + norm_ref[1:2, :]).astype(BF)
    grad = grad_ref[...]
    low_grad = grad.astype(BF)
    head_out = out_ref[...]
    wo_grad_ref[...] += tn(head_out, low_grad)
    whole_grad = nt(low_grad, wo_ref[...]).astype(BF)
    first, second = lane_halves()
    first_wide, second_wide = first.astype(F32), second.astype(F32)
    tasks = [(image, pair) for image in range(IMAGES) for pair in range(PAIRS)]

    def places(task):
        image, pair = task
        here = slice(S * image, S * image + S)
        return here, *(slice(D * t + PAIR * pair, D * t + PAIR * (pair + 1)) for t in range(3))

    def get_pair_grad(task):
        here, lanes, _, _ = places(task)
        mask = mask_lanes(place_ref, own_mask_ref, other_mask_ref, IMAGES * step + task[0], task[1])
        grad = whole_grad[here, lanes] * mask.astype(BF)
        dots = grad.astype(F32) * head_out[here, lanes].astype(F32)
        first_dot = jnp.sum(dots * first_wide, axis=-1, keepdims=True)
        second_dot = jnp.sum(dots * second_wide, axis=-1, keepdims=True)
        return stacked(grad, first, second), jnp.concatenate([first_dot, second_dot], axis=0)

    pair_grads = [get_pair_grad(task) for task in tasks]
    prob_grads = [
        nt(pair_grad[0], qkv_ref[places(task)[0], places(task)[3]])
        for task, pair_grad in zip(tasks, pair_grads)
    ]
    score_grads = [
        (prob_ref[task].astype(F32) * (prob_grad - pair_grad[1])).astype(BF)
        for task, prob_grad, pair_grad in zip(tasks, prob_grads, pair_grads)
    ]
    for task, score_grad, (pair_grad, _) in zip(tasks, score_grads, pair_grads):
        here, query_lanes, key_lanes, value_lanes = places(task)
        keys = qkv_ref[here, key_lanes]
        queries = stacked(qkv_ref[here, query_lanes], first, second)
        query_grad = nn(score_grad[:S], keys * first) + nn(score_grad[S:], keys * second)
        key_grad = nn(jnp.transpose(queries), score_grad)
        value_grad = nn(jnp.transpose(pair_grad), prob_ref[task])
        dqkv_ref[here, query_lanes] = query_grad.astype(BF)
        dqkv_ref[here, key_lanes] = jnp.transpose(key_grad).astype(BF)
        dqkv_ref[here, value_lanes] = jnp.transpose(value_grad).astype(BF)
    dqkv = dqkv_ref[...]
    wqkv_grad_ref[...] += tn(rows, dqkv)
    back = nt(dqkv, wqkv_ref[...])
    grad_in, norm_part = norm_backward(back, normed, inverse_std, norm_ref[0:1, :])
    norm_grad_ref[0:2, :] += norm_part
    in_grad_ref[...] = grad + grad_in

    @pl.when(step == pl.num_programs(0) - 1)
    def _():
        for side, slab_grads in enumerate((own_grad_ref, sent_grad_ref)):
            for slab in range(12):
                pieces = []
                for unit in (2 * slab, 2 * slab + 1):
                    row, part = divmod(unit, 3)
                    piece = wqkv_grad_ref[48 * row : 48 * row + 48, D * part : D * part + D]
                    piece = piece[:, HALF * side : HALF * side + HALF]
                    pieces.append(piece * 0.125 if part == 0 else piece)
                slab_grads[slab_at(slab)] = jnp.concatenate(pieces, axis=1).astype(BF)
            for row in range(HALF // 48):
                start = HALF * side + 48 * row
                slab_grads[slab_at(12 + row)] = wo_grad_ref[start : start + 48, :].astype(BF)
        sent_grad_ref[SLABS, :NORM_ROWS] = jnp.concatenate(split(norm_grad_ref[...]), axis=0)
        sent_grad_ref[SLABS, NORM_ROWS:] = jnp.zeros((48 - NORM_ROWS, D), BF)


def attn_backward(
    place, own_mask, other_mask, tokens, grad, prob, qkv, out, norm_params, later_norms, wqkv, wo
):
    rows = tokens.shape[0]
    tile = pl.BlockSpec((TILE, D), lambda i: (i, 0))
    smem = pl.BlockSpec(memory_space=pltpu.SMEM)
    return pl.pallas_call(
        attn_backward_kernel,
        grid=(rows // TILE,),
        in_specs=[
            smem,
            smem,
            smem,
            tile,
            tile,
            pl.BlockSpec((IMAGES, PAIRS, 2 * S, S), lambda i: (i, 0, 0, 0)),
            pl.BlockSpec((TILE, 3 * D), lambda i: (i, 0)),
            tile,
            pl.BlockSpec((4, D), lambda i: (0, 0)),
            pl.BlockSpec((2, D), lambda i: (0, 0)),
            pl.BlockSpec((D, 3 * D), lambda i: (0, 0)),
            pl.BlockSpec((D, D), lambda i: (0, 0)),
        ],
        out_specs=[
            tile,
            pl.BlockSpec((SLABS, 48, D), lambda i: (0, 0, 0)),
            pl.BlockSpec((SLABS + 1, 48, D), lambda i: (0, 0, 0)),
            pl.BlockSpec((4, D), lambda i: (0, 0)),
        ],
        out_shape=[
            jax.ShapeDtypeStruct((rows, D), F32),
            jax.ShapeDtypeStruct((SLABS, 48, D), BF),
            jax.ShapeDtypeStruct((SLABS + 1, 48, D), BF),
            jax.ShapeDtypeStruct((4, D), F32),
        ],
        scratch_shapes=[
            pltpu.VMEM((TILE, 3 * D), BF),
            pltpu.VMEM((D, 3 * D), F32),
            pltpu.VMEM((D, D), F32),
        ],
        compiler_params=pltpu.CompilerParams(vmem_limit_bytes=VMEM_LIMIT),
        cost_estimate=pl.CostEstimate(
            flops=rows * D * (16 * D + 32 * S), bytes_accessed=20 << 20, transcendentals=0
        ),
        name="attn_backward",
    )(
        place, own_mask, other_mask,
        *map(in_hbm, (tokens, grad, prob, qkv, out, norm_params, later_norms, wqkv, wo)),
    )


def pack_kernel(weight_ref, early_ref, late_ref):
    groups, count, _, _ = weight_ref.shape
    for group in range(groups):
        blocks = [weight_ref[group, block] for block in range(count)]
        slab = jnp.concatenate(blocks, axis=1).astype(BF)
        for copy in range(early_ref.shape[0]):
            if group == 0:
                early_ref[copy] = slab
            else:
                late_ref[copy, group - 1] = slab


def pack(weights, number):
    groups, count, edge, _ = weights.shape
    return pl.pallas_call(
        pack_kernel,
        out_shape=[
            jax.ShapeDtypeStruct((number, edge, count * edge), BF),
            jax.ShapeDtypeStruct((number, groups - 1, edge, count * edge), BF),
        ],
        compiler_params=pltpu.CompilerParams(vmem_limit_bytes=SMALL_VMEM),
        name="pack",
    )(weights)


def sum_kernel(*refs):
    *in_refs, kept_ref, sent_ref = refs
    for side, out_ref in enumerate((kept_ref, sent_ref)):
        total = in_refs[0][side].astype(F32)
        for ref in in_refs[1:]:
            total = total + ref[side].astype(F32)
        out_ref[...] = total.astype(out_ref.dtype)


def sum_late(pieces):
    shape = pieces[0].shape[1:]
    return pl.pallas_call(
        sum_kernel,
        out_shape=[jax.ShapeDtypeStruct(shape, F32), jax.ShapeDtypeStruct(shape, BF)],
        compiler_params=pltpu.CompilerParams(vmem_limit_bytes=SMALL_VMEM),
        name="sum_late",
    )(*pieces)


def combine_kernel(place_ref, own_ref, received_ref, norm_ref, *out_refs):
    norms = received_ref[SLABS, :NORM_ROWS].astype(F32)
    norms = norm_ref[...] + (norms[:4] + norms[4:])
    rows = jnp.concatenate(split(norms), axis=0)
    for apart, out_ref in enumerate(out_refs):
        start = OUTER * (place_ref[1] ^ apart)
        for outer in range(OUTER):
            total = own_ref[start + outer].astype(F32) + received_ref[start + outer].astype(F32)
            out_ref[48 * outer : 48 * outer + 48, :] = total.astype(BF)
        out_ref[48 * OUTER :, :] = rows


def combine(place, own, received, norms):
    vmem = pl.BlockSpec(memory_space=pltpu.VMEM)
    shape = jax.ShapeDtypeStruct((48 * OUTER + NORM_ROWS, D), BF)
    return pl.pallas_call(
        combine_kernel,
        in_specs=[pl.BlockSpec(memory_space=pltpu.SMEM), vmem, vmem, vmem],
        out_shape=[shape] * INNER,
        compiler_params=pltpu.CompilerParams(vmem_limit_bytes=SMALL_VMEM),
        name="combine",
    )(place, own, received, norms)


def join_kernel(*refs):
    *early_refs, kept_ref, received_ref, out_ref = refs
    total = early_refs[0][...].astype(F32)
    for ref in early_refs[1:]:
        total = total + ref[...].astype(F32)
    norms = total[48 * OUTER : 48 * OUTER + 4] + total[48 * OUTER + 4 :]
    late = kept_ref[...] + received_ref[...].astype(F32)
    for outer in range(OUTER):
        out_ref[outer, :48] = total[48 * outer : 48 * outer + 48].astype(BF)
        for group in range(late.shape[1]):
            out_ref[outer, 48 * group + 48 : 48 * group + 96] = late[outer, group].astype(BF)
        out_ref[outer, 144:] = jnp.concatenate(split(norms), axis=0)


def join(early, kept, received):
    return pl.pallas_call(
        join_kernel,
        out_shape=jax.ShapeDtypeStruct((OUTER, 144 + NORM_ROWS, D), BF),
        compiler_params=pltpu.CompilerParams(vmem_limit_bytes=SMALL_VMEM),
        name="join",
    )(*early, kept, received)


def split(values):
    high = values.astype(BF)
    return high, (values - high.astype(F32)).astype(BF)


def stack(*pieces):
    return jnp.concatenate(pieces, axis=0)


def cut_rows(values, number):
    edge = values.shape[0] // number
    return [values[edge * i : edge * i + edge] for i in range(number)]


def product(left, right):
    high, low = left
    right_high, right_low = right
    one, two = cut_rows(nn(stack(high, low), right_high), 2)
    return one + (two + nn(high, right_low))


def two_products(left, middle, right):
    right_high, right_low = right
    both = cut_rows(nn(stack(left[0], middle[0], left[1], middle[1]), right_high), 4)
    high = cut_rows(nn(stack(left[0], middle[0]), right_low), 2)
    return both[0] + (both[2] + high[0]), both[1] + (both[3] + high[1])


def update_norms(scale, total, param_ref, state_ref, grad_ref, new_state_ref, new_ref):
    grads = total * scale
    state = 0.5 * state_ref[...] + 0.5 * grads * grads
    grad_ref[...] = grads
    new_state_ref[...] = state
    new_ref[...] = param_ref[...] - 0.2 * grads / jnp.sqrt(state)


def shampoo_kernel(scale, with_norms, received_ref, weight_ref, left_ref, right_ref, *refs):
    if with_norms:
        norm_ins, norm_outs, refs = refs[:2], refs[6:9], refs[2:6] + refs[9:]
    out_grad_ref, left_new_ref, right_new_ref, new_weight_ref, root_ref, power_ref = refs
    groups, count, edge = weight_ref.shape[:3]
    received = received_ref[0].astype(F32)
    for number in range(1, received_ref.shape[0]):
        received = received + received_ref[number].astype(F32)
    if with_norms:
        norms = received[groups * edge :]
        update_norms(scale, norms[:4] + norms[4:], *norm_ins, *norm_outs)
    pack = min(PACK, count)
    width = pack * edge
    places = [(g, pack * n) for g in range(groups) for n in range(count // pack)]
    packs = len(places)

    def block_of(shape, dim):
        return lax.broadcasted_iota(jnp.int32, shape, dim) // edge

    row = lax.broadcasted_iota(jnp.int32, (edge, width), 0)
    lane = lax.broadcasted_iota(jnp.int32, (edge, width), 1)
    identity = (lane % edge == row).astype(F32)
    same = (block_of((width, width), 0) == block_of((width, width), 1)).astype(BF)
    lane_block = block_of((1, width), 1)

    def spread(pieces):
        return tuple(stack(*[piece] * pack) * same for piece in pieces)

    def cut(packed, index):
        return packed[:, edge * index : edge * index + edge]

    def beside(ref, place):
        return jnp.concatenate([ref[place[0], place[1] + i] for i in range(pack)], axis=1)

    grads, parts = [], []
    for group, start in places:
        rows = received[edge * group : edge * group + edge]
        grad = rows[:, edge * start : edge * start + width] * scale
        blocks = [cut(grad, index) for index in range(pack)]
        for index in range(pack):
            out_grad_ref[group, start + index] = blocks[index]
        grad_t = jnp.concatenate([jnp.transpose(block) for block in blocks], axis=1)
        one, two = split(grad), split(grad_t)
        one_diagonal, two_diagonal = spread(one), spread(two)
        grads.append(one_diagonal)
        parts.append((left_ref, left_new_ref, one, two_diagonal))
        parts.append((right_ref, right_new_ref, two, one_diagonal))
    grams = [product(left, right) for _, _, left, right in parts]
    for slot, (old_ref, new_ref, _, _) in enumerate(parts):
        group, start = places[slot // 2]
        new = 0.5 * beside(old_ref, places[slot // 2]) + 0.5 * grams[slot]
        for index in range(pack):
            new_ref[group, start + index] = cut(new, index)
        columns = jnp.sum(new * new, axis=0, keepdims=True)
        squares = jnp.zeros((1, width), F32)
        for index in range(pack):
            inside = lane_block == index
            part = jnp.sum(jnp.where(inside, columns, 0.0), axis=1, keepdims=True)
            squares = jnp.where(inside, part, squares)
        factor = 2.5 / jnp.sqrt(squares)
        root_ref[slot] = jnp.broadcast_to(jnp.sqrt(jnp.sqrt(factor)), (edge, width))
        power_ref[slot] = factor * new
    slots = range(2 * packs)

    def advance(first):
        powers = [power_ref[slot] for slot in slots]
        middles = [split((5.0 * identity - power) * 0.25) for power in powers]
        rights = [spread(middle) for middle in middles]
        powers = [split(power) for power in powers]
        if first:
            squares = [product(middles[s], rights[s]) for s in slots]
            for slot in slots:
                root_ref[slot] *= (5.0 * identity - power_ref[slot]) * 0.25
        else:
            roots = [split(root_ref[slot]) for slot in slots]
            both = [two_products(roots[s], middles[s], rights[s]) for s in slots]
            squares = [pair[1] for pair in both]
            for slot in slots:
                root_ref[slot] = both[slot][0]
        rights = [spread(split(square)) for square in squares]
        powers = [split(product(powers[s], rights[s])) for s in slots]
        for slot in slots:
            power_ref[slot] = product(powers[slot], rights[slot])

    advance(True)
    lax.fori_loop(0, ITERS - 2, lambda _, carry: advance(False) or carry, 0)
    rights = [spread(split((5.0 * identity - power_ref[slot]) * 0.25)) for slot in slots]
    for slot in slots:
        root_ref[slot] = product(split(root_ref[slot]), rights[slot])
    steps = [product(split(root_ref[2 * n]), grads[n]) for n in range(packs)]
    rights = [spread(split(root_ref[2 * n + 1])) for n in range(packs)]
    steps = [product(split(steps[n]), rights[n]) for n in range(packs)]
    for number, (group, start) in enumerate(places):
        for index in range(pack):
            step = 0.25 * cut(steps[number], index)
            new_weight_ref[group, start + index] = weight_ref[group, start + index] - step


def shampoo(received, weights, stat_left, stat_right, scale, norms=()):
    groups, count, edge, _ = weights.shape
    slots = 2 * groups * count // min(PACK, count)
    width = min(PACK, count) * edge
    shape = jax.ShapeDtypeStruct(weights.shape, F32)
    norm_shapes = [jax.ShapeDtypeStruct((4, D), F32)] * (3 if norms else 0)
    return pl.pallas_call(
        lambda *refs: shampoo_kernel(scale, bool(norms), *refs),
        out_shape=[shape] * 4 + norm_shapes,
        scratch_shapes=[
            pltpu.VMEM((slots, edge, width), F32),
            pltpu.VMEM((slots, edge, width), F32),
        ],
        compiler_params=pltpu.CompilerParams(vmem_limit_bytes=SHAMPOO_VMEM),
        cost_estimate=pl.CostEstimate(flops=9 << 30, bytes_accessed=4 << 20, transcendentals=0),
        name="shampoo",
    )(received, weights, stat_left, stat_right, *norms)


def swap_heads(values):
    return lax.ppermute(values, "head", [(0, 1), (1, 0)])


def to_all(values, axis):
    return lax.all_to_all(values, axis, 0, 0)


def across(values, apart):
    pairs = [(i, i ^ apart) for i in range(INNER)]
    return lax.ppermute(values, "inner", pairs)


def from_all(values):
    return [values] + [across(values, apart) for apart in range(1, INNER)]


def gather_slabs(weights, other_mask):
    early, late = pack(weights, OUTER)
    early = to_all(early, "outer")
    early, late = lax.optimization_barrier((early, late))
    late = to_all(late, "outer")
    early, late, other_mask = lax.optimization_barrier((from_all(early), late, other_mask))
    return early, from_all(late), other_mask


def gather_blocks(local):
    groups, _, edge, _ = local.shape
    blocks = lax.all_gather(local, ("outer", "inner"), axis=1, tiled=True)
    blocks = blocks.reshape(groups, SLABS // INNER, INNER, D // edge, edge, edge)
    slabs = blocks.transpose(2, 1, 0, 4, 3, 5).reshape(SLABS, groups, edge, D)
    return slabs if groups > 1 else slabs[:, 0]


def scatter_blocks(slabs, count, edge):
    groups = slabs.shape[1]
    blocks = slabs.reshape(INNER, SLABS // INNER, groups, edge, D // edge, edge)
    blocks = blocks.transpose(2, 1, 0, 4, 3, 5).reshape(groups, SLABS * (D // edge), edge, edge)
    owned = lax.psum_scatter(blocks, ("outer", "inner"), scatter_dimension=1, tiled=True)
    return owned.transpose(0, 2, 1, 3).reshape(groups, edge, count * edge)


def per_device(
    tokens,
    cotangent,
    token_counts,
    head_mask,
    norm_params,
    norm_state,
    weights,
    stat_left,
    stat_right,
):
    weights, stat_left, stat_right = weights[0], stat_left[0], stat_right[0]
    _, count, edge, _ = weights.shape
    whole_slabs = count * edge == D
    other_mask = swap_heads(head_mask)
    if whole_slabs:
        place = jnp.stack([lax.axis_index("head"), lax.axis_index("inner")])
        early, late, other_mask = gather_slabs(weights, other_mask)
    else:
        place = jnp.stack([lax.axis_index("head"), 0])
        local = weights.astype(BF)
        early = jnp.split(gather_blocks(local[:1]), INNER)
        late = jnp.split(gather_blocks(local[1:]), INNER)
    early, late = list(early), list(late)
    masks = (head_mask, other_mask)
    early += [swap_heads(piece) for piece in early]
    prob, qkv, out, middle, wqkv, wo = attn_forward(
        place, token_counts, *masks, tokens, norm_params, early
    )
    late, middle = lax.optimization_barrier((late, middle))
    late = [*late, *[swap_heads(piece) for piece in late]]
    block_out, middle_grad, norm_two, *late_grads = mlp(place, middle, cotangent, norm_params, late)
    if whole_slabs:
        late_grads[1:] = [across(late_grads[apart], apart) for apart in range(1, INNER)]
    input_grad, own_early, sent_early, norm_sums = attn_backward(
        place, *masks, tokens, middle_grad, prob, qkv, out, norm_params, norm_two, wqkv, wo
    )
    late_grads, sent_early = lax.optimization_barrier((late_grads, sent_early))
    early_received = swap_heads(sent_early)
    devices = lax.axis_size("outer") * lax.axis_size("inner") * lax.axis_size("head")
    scale = 1.0 / math.sqrt(tokens.shape[0] * devices)
    state = (weights, stat_left, stat_right, scale)
    if whole_slabs:
        kept, sent_late = sum_late(late_grads)
        early_grads = list(combine(place, own_early, early_received, norm_sums))
        early_grads[1:] = [across(early_grads[apart], apart) for apart in range(1, INNER)]
        received = to_all(join(early_grads, kept, swap_heads(sent_late)), "outer")
        results = shampoo(received, *state, (norm_params, norm_state))
    else:
        early_slabs = own_early.astype(F32) + early_received[:SLABS].astype(F32)
        late_slabs = jnp.concatenate([grad[0].astype(F32) for grad in late_grads])
        late_slabs += jnp.concatenate([swap_heads(grad[1]).astype(F32) for grad in late_grads])
        slabs = jnp.concatenate([early_slabs[:, None], late_slabs], axis=1).astype(BF)
        owned = scatter_blocks(slabs, count, edge)
        results = list(shampoo(owned.reshape(1, -1, count * edge), *state))
        norm_grads = lax.psum(norm_sums, ("outer", "inner", "head")) * scale
        state_new = 0.5 * norm_state + 0.5 * norm_grads * norm_grads
        results += [norm_grads, state_new, norm_params - 0.2 * norm_grads / jnp.sqrt(state_new)]
    return (block_out, input_grad, *[result[None] for result in results[:4]], *results[4:])


def solution(mesh):
    shape = (mesh.shape["dp"] // INNER, INNER, mesh.shape["head"])
    split_mesh = Mesh(mesh.devices.reshape(shape), ("outer", "inner", "head"))
    group = ("outer", "inner")
    blocks = P("head", None, group, None, None)
    rows = P(group + ("head",), None)
    return jax.shard_map(
        per_device,
        mesh=split_mesh,
        in_specs=(rows, rows, P(group), P(group, "head"), P(), P(), blocks, blocks, blocks),
        out_specs=(rows, rows, blocks, blocks, blocks, blocks, P(), P(), P()),
        check_vma=False,
    )
```

```python
import math

import jax
import jax.numpy as jnp
from jax import lax
from jax.experimental import pallas as pl
from jax.experimental.pallas import tpu as pltpu
from jax.sharding import Mesh, PartitionSpec as P

D = 384
HEAD_DIM = 64
MLP = 1536
S = 256
ITERS = 8
PAIR = 2 * HEAD_DIM
PAIRS = D // PAIR
HALF = D // 2
SLABS = 16
INNER = 4
OUTER = SLABS // INNER
TILE = 512
IMAGES = TILE // S
NORM_ROWS = 8
PACK = 2
ROOT_HALF = 0.7071067811865476
DENSITY_FACTOR = 0.3989422804014327
BF = jnp.bfloat16
F32 = jnp.float32
VMEM_LIMIT = 40 << 20
SMALL_VMEM = 8 << 20
SHAMPOO_VMEM = 24 << 20


def in_hbm(values):
    return pltpu.with_memory_space_constraint(values, pltpu.HBM)


def nn(left, right):
    return jnp.dot(left, right, preferred_element_type=F32)


def nt(left, right):
    return lax.dot_general(left, right, (((1,), (1,)), ((), ())), preferred_element_type=F32)


def tn(left, right):
    return lax.dot_general(left, right, (((0,), (0,)), ((), ())), preferred_element_type=F32)


def normalize(values):
    centered = values - jnp.mean(values, axis=-1, keepdims=True)
    variance = jnp.mean(centered * centered, axis=-1, keepdims=True)
    inverse_std = lax.rsqrt(variance + 1e-06)
    return centered * inverse_std, inverse_std


def norm_backward(grad_out, normed, inverse_std, gain):
    grad_normed = grad_out * gain
    mean_first = jnp.mean(grad_normed, axis=-1, keepdims=True)
    mean_second = jnp.mean(grad_normed * normed, axis=-1, keepdims=True)
    grad_in = inverse_std * (grad_normed - mean_first - normed * mean_second)
    gain_grad = jnp.sum(grad_out * normed, axis=0, keepdims=True)
    shift_grad = jnp.sum(grad_out, axis=0, keepdims=True)
    return grad_in, jnp.concatenate([gain_grad, shift_grad], axis=0)


def slab_at(owner):
    return (owner % INNER) * OUTER + owner // INNER


def lane_halves():
    lane = lax.broadcasted_iota(jnp.int32, (1, PAIR), 1)
    first = (lane < HEAD_DIM).astype(BF)
    return first, (1 - first).astype(BF)


def stacked(values, first, second):
    return jnp.concatenate([values * first, values * second], axis=0)


def mask_lanes(place_ref, own_ref, other_ref, image, pair):
    image = place_ref[0] * (own_ref.shape[0] // 2) + image
    heads = own_ref.shape[1]
    on = [
        own_ref[image, head] if head < heads else other_ref[image, head - heads]
        for head in (2 * pair, 2 * pair + 1)
    ]
    lane = lax.broadcasted_iota(jnp.int32, (1, PAIR), 1)
    return jnp.where(lane < HEAD_DIM, on[0], on[1]).astype(F32)


def attn_forward_kernel(
    place_ref, counts_ref, own_mask_ref, other_mask_ref, x_ref, norm_ref, *refs
):
    slab_refs, refs = refs[: 2 * INNER], refs[2 * INNER :]
    prob_ref, qkv_ref, out_ref, middle_ref, wqkv_ref, wo_ref, held_ref = refs
    step = pl.program_id(0)

    @pl.when(step == 0)
    def _():
        for number, ref in enumerate(slab_refs):
            side, apart = divmod(number, INNER)
            held_ref[side, place_ref[1] ^ apart] = ref[...]

        def slab_of(side, owner):
            return held_ref[side, owner % INNER, owner // INNER]

        for row in range(D // 48):
            for part in range(3):
                pieces = []
                for number in range(2):
                    slab, side = divmod(3 * row + part, 2)
                    piece = slab_of(number, slab)[:, side * HALF : (side + 1) * HALF]
                    pieces.append(piece)
                joined = jnp.concatenate(pieces, axis=1)
                if part == 0:
                    joined = joined * 0.125
                wqkv_ref[48 * row : 48 * row + 48, D * part : D * part + D] = joined
        for side in range(2):
            for row in range(HALF // 48):
                start = side * HALF + 48 * row
                wo_ref[start : start + 48, :] = slab_of(side, 12 + row)

    x = x_ref[...].astype(F32)
    normed, _ = normalize(x)
    rows = (normed * norm_ref[0:1, :] + norm_ref[1:2, :]).astype(BF)
    qkv_ref[...] = nn(rows, wqkv_ref[...]).astype(BF)
    first, second = lane_halves()
    column = lax.broadcasted_iota(jnp.int32, (1, S), 1)
    tasks = [(image, pair) for image in range(IMAGES) for pair in range(PAIRS)]

    def places(task):
        image, pair = task
        here = slice(S * image, S * image + S)
        return here, *(slice(D * t + PAIR * pair, D * t + PAIR * (pair + 1)) for t in range(3))

    def get_scores(task):
        here, query_lanes, key_lanes, _ = places(task)
        return nt(stacked(qkv_ref[here, query_lanes], first, second), qkv_ref[here, key_lanes])

    def get_prob(task, scores):
        image = place_ref[0] * (counts_ref.shape[0] // 2) + IMAGES * step + task[0]
        scores = jnp.where(column < counts_ref[image], scores, -1e30)
        top = jnp.max(scores, axis=-1, keepdims=True)
        exp_scores = jnp.exp(scores - top)
        total = jnp.sum(exp_scores, axis=-1, keepdims=True)
        prob = (exp_scores * (1.0 / total)).astype(BF)
        prob_ref[task] = prob
        return prob

    all_scores = [get_scores(task) for task in tasks]
    probs = [get_prob(task, scores) for task, scores in zip(tasks, all_scores)]
    for task, prob in zip(tasks, probs):
        here, lanes, _, value_lanes = places(task)
        values = qkv_ref[here, value_lanes]
        head_out = nn(prob[:S], values * first) + nn(prob[S:], values * second)
        mask = mask_lanes(place_ref, own_mask_ref, other_mask_ref, IMAGES * step + task[0], task[1])
        out_ref[here, lanes] = (head_out * mask).astype(BF)
    middle_ref[...] = x + nn(out_ref[...], wo_ref[...])


def attn_forward(place, counts, own_mask, other_mask, tokens, norm_params, slabs):
    rows = tokens.shape[0]
    images = rows // S
    tile = pl.BlockSpec((TILE, D), lambda i: (i, 0))
    slab = pl.BlockSpec((OUTER, 48, D), lambda i: (0, 0, 0))
    smem = pl.BlockSpec(memory_space=pltpu.SMEM)
    return pl.pallas_call(
        attn_forward_kernel,
        grid=(rows // TILE,),
        in_specs=[smem] * 4 + [tile, pl.BlockSpec((4, D), lambda i: (0, 0))] + [slab] * 2 * INNER,
        out_specs=[
            pl.BlockSpec((IMAGES, PAIRS, 2 * S, S), lambda i: (i, 0, 0, 0)),
            pl.BlockSpec((TILE, 3 * D), lambda i: (i, 0)),
            tile,
            tile,
            pl.BlockSpec((D, 3 * D), lambda i: (0, 0)),
            pl.BlockSpec((D, D), lambda i: (0, 0)),
        ],
        out_shape=[
            pltpu.HBM((images, PAIRS, 2 * S, S), BF),
            pltpu.HBM((rows, 3 * D), BF),
            pltpu.HBM((rows, D), BF),
            pltpu.HBM((rows, D), F32),
            pltpu.HBM((D, 3 * D), BF),
            pltpu.HBM((D, D), BF),
        ],
        scratch_shapes=[pltpu.VMEM((2, INNER, OUTER, 48, D), BF)],
        compiler_params=pltpu.CompilerParams(vmem_limit_bytes=VMEM_LIMIT),
        cost_estimate=pl.CostEstimate(
            flops=rows * D * (8 * D + 16 * S), bytes_accessed=16 << 20, transcendentals=rows * 6 * S
        ),
        name="attn_forward",
    )(place, counts, own_mask, other_mask, in_hbm(tokens), in_hbm(norm_params), *slabs)


def mlp_kernel(place_ref, middle_ref, cot_ref, norm_ref, *refs):
    slab_refs, refs = refs[: 2 * INNER], refs[2 * INNER :]
    out_ref, grad_ref, norm_grad_ref, *refs = refs
    own_ref, sent_ref, up_ref, down_ref, up_grad_ref, down_grad_ref = refs
    step = pl.program_id(0)
    half = MLP // 2

    def places(apart, outer):
        inner = place_ref[1] ^ apart
        row = pl.multiple_of(48 * (2 * outer + inner // 2), 16)
        lane = pl.multiple_of(D * (inner % 2), 128)
        down_row = pl.multiple_of(48 * (INNER * outer + inner), 16)
        return row, lane, down_row

    @pl.when(step == 0)
    def _():
        up_grad_ref[...] = jnp.zeros_like(up_grad_ref)
        down_grad_ref[...] = jnp.zeros_like(down_grad_ref)
        norm_grad_ref[...] = jnp.zeros_like(norm_grad_ref)
        for number, ref in enumerate(slab_refs):
            side, apart = divmod(number, INNER)
            for outer in range(OUTER):
                row, lane, down_row = places(apart, outer)
                up_ref[side, pl.ds(row, 48), pl.ds(lane, D)] = ref[outer, 0]
                down_ref[side, pl.ds(down_row, 48), :] = ref[outer, 1]

    middle = middle_ref[...]
    normed, inverse_std = normalize(middle)
    rows = (normed * norm_ref[2:3, :] + norm_ref[3:4, :]).astype(BF)
    cot = cot_ref[...]
    total = middle
    back = None
    for side in range(2):
        up, down = up_ref[side], down_ref[side]
        pre = nn(rows, up)
        act_grad = nt(cot, down)
        cumulative = 0.5 * (1.0 + lax.erf(pre * ROOT_HALF))
        density = jnp.exp(-0.5 * pre * pre) * DENSITY_FACTOR
        act = (pre * cumulative).astype(BF)
        pre_grad = (act_grad * (cumulative + pre * density)).astype(BF)
        total = total + nn(act, down)
        term = nt(pre_grad, up)
        back = term if back is None else back + term
        down_grad_ref[side] += tn(act, cot)
        up_grad_ref[side] += tn(rows, pre_grad)
    out_ref[...] = total
    grad_in, norm_part = norm_backward(back, normed, inverse_std, norm_ref[2:3, :])
    norm_grad_ref[...] += norm_part
    grad_ref[...] = cot.astype(F32) + grad_in

    @pl.when(step == pl.num_programs(0) - 1)
    def _():
        for apart in range(INNER):
            for outer in range(OUTER):
                row, lane, down_row = places(apart, outer)
                for side, ref in enumerate((own_ref, sent_ref)):
                    up = up_grad_ref[side, pl.ds(row, 48), pl.ds(lane, D)]
                    down = down_grad_ref[side, pl.ds(down_row, 48), :]
                    ref[apart, outer, 0] = up.astype(BF)
                    ref[apart, outer, 1] = down.astype(BF)


def mlp(place, middle, cotangent, norm_params, slabs):
    rows = middle.shape[0]
    slab = pl.BlockSpec((OUTER, 2, 48, D), lambda i: (0, 0, 0, 0))
    grads = (INNER, OUTER, 2, 48, D)
    grad = pl.BlockSpec(grads, lambda i: (0, 0, 0, 0, 0))
    tile = pl.BlockSpec((TILE, D), lambda i: (i, 0))
    return pl.pallas_call(
        mlp_kernel,
        grid=(rows // TILE,),
        in_specs=[
            pl.BlockSpec(memory_space=pltpu.SMEM),
            tile,
            tile,
            pl.BlockSpec((4, D), lambda i: (0, 0)),
            *[slab] * 2 * INNER,
        ],
        out_specs=[tile, tile, pl.BlockSpec((2, D), lambda i: (0, 0)), grad, grad],
        out_shape=[
            jax.ShapeDtypeStruct((rows, D), F32),
            pltpu.HBM((rows, D), F32),
            jax.ShapeDtypeStruct((2, D), F32),
            *[jax.ShapeDtypeStruct(grads, BF)] * 2,
        ],
        scratch_shapes=[
            pltpu.VMEM((2, D, MLP // 2), BF),
            pltpu.VMEM((2, MLP // 2, D), BF),
            pltpu.VMEM((2, D, MLP // 2), F32),
            pltpu.VMEM((2, MLP // 2, D), F32),
        ],
        compiler_params=pltpu.CompilerParams(vmem_limit_bytes=VMEM_LIMIT),
        cost_estimate=pl.CostEstimate(
            flops=12 * rows * D * MLP, bytes_accessed=20 << 20, transcendentals=2 * rows * MLP
        ),
        name="mlp",
    )(place, in_hbm(middle), in_hbm(cotangent), in_hbm(norm_params), *slabs)


def attn_backward_kernel(
    place_ref, own_mask_ref, other_mask_ref, x_ref, grad_ref, prob_ref, qkv_ref, out_ref,
    norm_ref, later_norm_ref, wqkv_ref, wo_ref,
    in_grad_ref, own_grad_ref, sent_grad_ref, norm_grad_ref,
    dqkv_ref, wqkv_grad_ref, wo_grad_ref,
):
    step = pl.program_id(0)

    @pl.when(step == 0)
    def _():
        wqkv_grad_ref[...] = jnp.zeros_like(wqkv_grad_ref)
        wo_grad_ref[...] = jnp.zeros_like(wo_grad_ref)
        norm_grad_ref[0:2, :] = jnp.zeros((2, D), F32)
        norm_grad_ref[2:4, :] = later_norm_ref[...]

    x = x_ref[...].astype(F32)
    normed, inverse_std = normalize(x)
    rows = (normed * norm_ref[0:1, :] + norm_ref[1:2, :]).astype(BF)
    grad = grad_ref[...]
    low_grad = grad.astype(BF)
    head_out = out_ref[...]
    wo_grad_ref[...] += tn(head_out, low_grad)
    whole_grad = nt(low_grad, wo_ref[...]).astype(BF)
    first, second = lane_halves()
    first_wide, second_wide = first.astype(F32), second.astype(F32)
    tasks = [(image, pair) for image in range(IMAGES) for pair in range(PAIRS)]

    def places(task):
        image, pair = task
        here = slice(S * image, S * image + S)
        return here, *(slice(D * t + PAIR * pair, D * t + PAIR * (pair + 1)) for t in range(3))

    def get_pair_grad(task):
        here, lanes, _, _ = places(task)
        mask = mask_lanes(place_ref, own_mask_ref, other_mask_ref, IMAGES * step + task[0], task[1])
        grad = whole_grad[here, lanes] * mask.astype(BF)
        dots = grad.astype(F32) * head_out[here, lanes].astype(F32)
        first_dot = jnp.sum(dots * first_wide, axis=-1, keepdims=True)
        second_dot = jnp.sum(dots * second_wide, axis=-1, keepdims=True)
        return stacked(grad, first, second), jnp.concatenate([first_dot, second_dot], axis=0)

    pair_grads = [get_pair_grad(task) for task in tasks]
    prob_grads = [
        nt(pair_grad[0], qkv_ref[places(task)[0], places(task)[3]])
        for task, pair_grad in zip(tasks, pair_grads)
    ]
    score_grads = [
        (prob_ref[task].astype(F32) * (prob_grad - pair_grad[1])).astype(BF)
        for task, prob_grad, pair_grad in zip(tasks, prob_grads, pair_grads)
    ]
    for task, score_grad, (pair_grad, _) in zip(tasks, score_grads, pair_grads):
        here, query_lanes, key_lanes, value_lanes = places(task)
        keys = qkv_ref[here, key_lanes]
        queries = stacked(qkv_ref[here, query_lanes], first, second)
        query_grad = nn(score_grad[:S], keys * first) + nn(score_grad[S:], keys * second)
        key_grad = nn(jnp.transpose(queries), score_grad)
        value_grad = nn(jnp.transpose(pair_grad), prob_ref[task])
        dqkv_ref[here, query_lanes] = query_grad.astype(BF)
        dqkv_ref[here, key_lanes] = jnp.transpose(key_grad).astype(BF)
        dqkv_ref[here, value_lanes] = jnp.transpose(value_grad).astype(BF)
    dqkv = dqkv_ref[...]
    wqkv_grad_ref[...] += tn(rows, dqkv)
    back = nt(dqkv, wqkv_ref[...])
    grad_in, norm_part = norm_backward(back, normed, inverse_std, norm_ref[0:1, :])
    norm_grad_ref[0:2, :] += norm_part
    in_grad_ref[...] = grad + grad_in

    @pl.when(step == pl.num_programs(0) - 1)
    def _():
        for side, slab_grads in enumerate((own_grad_ref, sent_grad_ref)):
            for slab in range(12):
                pieces = []
                for unit in (2 * slab, 2 * slab + 1):
                    row, part = divmod(unit, 3)
                    piece = wqkv_grad_ref[48 * row : 48 * row + 48, D * part : D * part + D]
                    piece = piece[:, HALF * side : HALF * side + HALF]
                    pieces.append(piece * 0.125 if part == 0 else piece)
                slab_grads[slab_at(slab)] = jnp.concatenate(pieces, axis=1).astype(BF)
            for row in range(HALF // 48):
                start = HALF * side + 48 * row
                slab_grads[slab_at(12 + row)] = wo_grad_ref[start : start + 48, :].astype(BF)
        sent_grad_ref[SLABS, :NORM_ROWS] = jnp.concatenate(split(norm_grad_ref[...]), axis=0)
        sent_grad_ref[SLABS, NORM_ROWS:] = jnp.zeros((48 - NORM_ROWS, D), BF)


def attn_backward(
    place, own_mask, other_mask, tokens, grad, prob, qkv, out, norm_params, later_norms, wqkv, wo
):
    rows = tokens.shape[0]
    tile = pl.BlockSpec((TILE, D), lambda i: (i, 0))
    smem = pl.BlockSpec(memory_space=pltpu.SMEM)
    return pl.pallas_call(
        attn_backward_kernel,
        grid=(rows // TILE,),
        in_specs=[
            smem,
            smem,
            smem,
            tile,
            tile,
            pl.BlockSpec((IMAGES, PAIRS, 2 * S, S), lambda i: (i, 0, 0, 0)),
            pl.BlockSpec((TILE, 3 * D), lambda i: (i, 0)),
            tile,
            pl.BlockSpec((4, D), lambda i: (0, 0)),
            pl.BlockSpec((2, D), lambda i: (0, 0)),
            pl.BlockSpec((D, 3 * D), lambda i: (0, 0)),
            pl.BlockSpec((D, D), lambda i: (0, 0)),
        ],
        out_specs=[
            tile,
            pl.BlockSpec((SLABS, 48, D), lambda i: (0, 0, 0)),
            pl.BlockSpec((SLABS + 1, 48, D), lambda i: (0, 0, 0)),
            pl.BlockSpec((4, D), lambda i: (0, 0)),
        ],
        out_shape=[
            jax.ShapeDtypeStruct((rows, D), F32),
            jax.ShapeDtypeStruct((SLABS, 48, D), BF),
            jax.ShapeDtypeStruct((SLABS + 1, 48, D), BF),
            jax.ShapeDtypeStruct((4, D), F32),
        ],
        scratch_shapes=[
            pltpu.VMEM((TILE, 3 * D), BF),
            pltpu.VMEM((D, 3 * D), F32),
            pltpu.VMEM((D, D), F32),
        ],
        compiler_params=pltpu.CompilerParams(vmem_limit_bytes=VMEM_LIMIT),
        cost_estimate=pl.CostEstimate(
            flops=rows * D * (16 * D + 32 * S), bytes_accessed=20 << 20, transcendentals=0
        ),
        name="attn_backward",
    )(
        place, own_mask, other_mask,
        *map(in_hbm, (tokens, grad, prob, qkv, out, norm_params, later_norms, wqkv, wo)),
    )


def pack_kernel(weight_ref, early_ref, late_ref):
    groups, count, _, _ = weight_ref.shape
    for group in range(groups):
        blocks = [weight_ref[group, block] for block in range(count)]
        slab = jnp.concatenate(blocks, axis=1).astype(BF)
        for copy in range(early_ref.shape[0]):
            if group == 0:
                early_ref[copy] = slab
            else:
                late_ref[copy, group - 1] = slab


def pack(weights, number):
    groups, count, edge, _ = weights.shape
    return pl.pallas_call(
        pack_kernel,
        out_shape=[
            jax.ShapeDtypeStruct((number, edge, count * edge), BF),
            jax.ShapeDtypeStruct((number, groups - 1, edge, count * edge), BF),
        ],
        compiler_params=pltpu.CompilerParams(vmem_limit_bytes=SMALL_VMEM),
        name="pack",
    )(weights)


def add_kernel(own_ref, received_ref, *out_refs):
    for apart, out_ref in enumerate(out_refs):
        total = own_ref[apart].astype(F32) + received_ref[apart].astype(F32)
        out_ref[...] = total.astype(BF)


def add_late(own, received):
    return pl.pallas_call(
        add_kernel,
        out_shape=[jax.ShapeDtypeStruct(own.shape[1:], BF)] * own.shape[0],
        compiler_params=pltpu.CompilerParams(vmem_limit_bytes=SMALL_VMEM),
        name="add_late",
    )(own, received)


def sum_kernel(*refs):
    *in_refs, out_ref = refs
    total = in_refs[0][...].astype(F32)
    for ref in in_refs[1:]:
        total = total + ref[...].astype(F32)
    out_ref[...] = total.astype(BF)


def sum_late(pieces):
    return pl.pallas_call(
        sum_kernel,
        out_shape=jax.ShapeDtypeStruct(pieces[0].shape, BF),
        compiler_params=pltpu.CompilerParams(vmem_limit_bytes=SMALL_VMEM),
        name="sum_late",
    )(*pieces)


def combine_kernel(place_ref, own_ref, received_ref, norm_ref, *out_refs):
    norms = received_ref[SLABS, :NORM_ROWS].astype(F32)
    norms = norm_ref[...] + (norms[:4] + norms[4:])
    rows = jnp.concatenate(split(norms), axis=0)
    for apart, out_ref in enumerate(out_refs):
        start = OUTER * (place_ref[1] ^ apart)
        for outer in range(OUTER):
            total = own_ref[start + outer].astype(F32) + received_ref[start + outer].astype(F32)
            out_ref[48 * outer : 48 * outer + 48, :] = total.astype(BF)
        out_ref[48 * OUTER :, :] = rows


def combine(place, own, received, norms):
    vmem = pl.BlockSpec(memory_space=pltpu.VMEM)
    shape = jax.ShapeDtypeStruct((48 * OUTER + NORM_ROWS, D), BF)
    return pl.pallas_call(
        combine_kernel,
        in_specs=[pl.BlockSpec(memory_space=pltpu.SMEM), vmem, vmem, vmem],
        out_shape=[shape] * INNER,
        compiler_params=pltpu.CompilerParams(vmem_limit_bytes=SMALL_VMEM),
        name="combine",
    )(place, own, received, norms)


def join_kernel(*refs):
    *early_refs, out_ref = refs
    total = early_refs[0][...].astype(F32)
    for ref in early_refs[1:]:
        total = total + ref[...].astype(F32)
    norms = total[48 * OUTER : 48 * OUTER + 4] + total[48 * OUTER + 4 :]
    for outer in range(OUTER):
        out_ref[outer, :48] = total[48 * outer : 48 * outer + 48].astype(BF)
        out_ref[outer, 48:] = jnp.concatenate(split(norms), axis=0)


def join(early):
    return pl.pallas_call(
        join_kernel,
        out_shape=jax.ShapeDtypeStruct((OUTER, 48 + NORM_ROWS, D), BF),
        compiler_params=pltpu.CompilerParams(vmem_limit_bytes=SMALL_VMEM),
        name="join",
    )(*early)


def split(values):
    high = values.astype(BF)
    return high, (values - high.astype(F32)).astype(BF)


def stack(*pieces):
    return jnp.concatenate(pieces, axis=0)


def cut_rows(values, number):
    edge = values.shape[0] // number
    return [values[edge * i : edge * i + edge] for i in range(number)]


def product(left, right):
    high, low = left
    right_high, right_low = right
    one, two = cut_rows(nn(stack(high, low), right_high), 2)
    return one + (two + nn(high, right_low))


def two_products(left, middle, right):
    right_high, right_low = right
    both = cut_rows(nn(stack(left[0], middle[0], left[1], middle[1]), right_high), 4)
    high = cut_rows(nn(stack(left[0], middle[0]), right_low), 2)
    return both[0] + (both[2] + high[0]), both[1] + (both[3] + high[1])


def update_norms(scale, total, param_ref, state_ref, grad_ref, new_state_ref, new_ref):
    grads = total * scale
    state = 0.5 * state_ref[...] + 0.5 * grads * grads
    grad_ref[...] = grads
    new_state_ref[...] = state
    new_ref[...] = param_ref[...] - 0.2 * grads / jnp.sqrt(state)


def shampoo_kernel(scale, with_norms, early_ref, late_ref, weight_ref, left_ref, right_ref, *refs):
    if with_norms:
        norm_ins, norm_outs, refs = refs[:2], refs[6:9], refs[2:6] + refs[9:]
    out_grad_ref, left_new_ref, right_new_ref, new_weight_ref, root_ref, power_ref = refs
    groups, count, edge = weight_ref.shape[:3]

    def total_of(ref):
        total = ref[0].astype(F32)
        for number in range(1, ref.shape[0]):
            total = total + ref[number].astype(F32)
        return total

    early, late = total_of(early_ref), total_of(late_ref)
    received = [early[:edge], *[late[group] for group in range(groups - 1)]]
    if with_norms:
        norms = early[edge:]
        update_norms(scale, norms[:4] + norms[4:], *norm_ins, *norm_outs)
    pack = min(PACK, count)
    width = pack * edge
    places = [(g, pack * n) for g in range(groups) for n in range(count // pack)]
    packs = len(places)

    def block_of(shape, dim):
        return lax.broadcasted_iota(jnp.int32, shape, dim) // edge

    row = lax.broadcasted_iota(jnp.int32, (edge, width), 0)
    lane = lax.broadcasted_iota(jnp.int32, (edge, width), 1)
    identity = (lane % edge == row).astype(F32)
    same = (block_of((width, width), 0) == block_of((width, width), 1)).astype(BF)
    lane_block = block_of((1, width), 1)

    def spread(pieces):
        return tuple(stack(*[piece] * pack) * same for piece in pieces)

    def cut(packed, index):
        return packed[:, edge * index : edge * index + edge]

    def beside(ref, place):
        return jnp.concatenate([ref[place[0], place[1] + i] for i in range(pack)], axis=1)

    grads, parts = [], []
    for group, start in places:
        grad = received[group][:, edge * start : edge * start + width] * scale
        blocks = [cut(grad, index) for index in range(pack)]
        for index in range(pack):
            out_grad_ref[group, start + index] = blocks[index]
        grad_t = jnp.concatenate([jnp.transpose(block) for block in blocks], axis=1)
        one, two = split(grad), split(grad_t)
        one_diagonal, two_diagonal = spread(one), spread(two)
        grads.append(one_diagonal)
        parts.append((left_ref, left_new_ref, one, two_diagonal))
        parts.append((right_ref, right_new_ref, two, one_diagonal))
    grams = [product(left, right) for _, _, left, right in parts]
    for slot, (old_ref, new_ref, _, _) in enumerate(parts):
        group, start = places[slot // 2]
        new = 0.5 * beside(old_ref, places[slot // 2]) + 0.5 * grams[slot]
        for index in range(pack):
            new_ref[group, start + index] = cut(new, index)
        columns = jnp.sum(new * new, axis=0, keepdims=True)
        squares = jnp.zeros((1, width), F32)
        for index in range(pack):
            inside = lane_block == index
            part = jnp.sum(jnp.where(inside, columns, 0.0), axis=1, keepdims=True)
            squares = jnp.where(inside, part, squares)
        factor = 2.5 / jnp.sqrt(squares)
        root_ref[slot] = jnp.broadcast_to(jnp.sqrt(jnp.sqrt(factor)), (edge, width))
        power_ref[slot] = factor * new
    slots = range(2 * packs)

    def advance(first):
        powers = [power_ref[slot] for slot in slots]
        middles = [split((5.0 * identity - power) * 0.25) for power in powers]
        rights = [spread(middle) for middle in middles]
        powers = [split(power) for power in powers]
        if first:
            squares = [product(middles[s], rights[s]) for s in slots]
            for slot in slots:
                root_ref[slot] *= (5.0 * identity - power_ref[slot]) * 0.25
        else:
            roots = [split(root_ref[slot]) for slot in slots]
            both = [two_products(roots[s], middles[s], rights[s]) for s in slots]
            squares = [pair[1] for pair in both]
            for slot in slots:
                root_ref[slot] = both[slot][0]
        rights = [spread(split(square)) for square in squares]
        powers = [split(product(powers[s], rights[s])) for s in slots]
        for slot in slots:
            power_ref[slot] = product(powers[slot], rights[slot])

    advance(True)
    lax.fori_loop(0, ITERS - 2, lambda _, carry: advance(False) or carry, 0)
    rights = [spread(split((5.0 * identity - power_ref[slot]) * 0.25)) for slot in slots]
    for slot in slots:
        root_ref[slot] = product(split(root_ref[slot]), rights[slot])
    steps = [product(split(root_ref[2 * n]), grads[n]) for n in range(packs)]
    rights = [spread(split(root_ref[2 * n + 1])) for n in range(packs)]
    steps = [product(split(steps[n]), rights[n]) for n in range(packs)]
    for number, (group, start) in enumerate(places):
        for index in range(pack):
            step = 0.25 * cut(steps[number], index)
            new_weight_ref[group, start + index] = weight_ref[group, start + index] - step


def shampoo(early, late, weights, stat_left, stat_right, scale, norms=()):
    groups, count, edge, _ = weights.shape
    slots = 2 * groups * count // min(PACK, count)
    width = min(PACK, count) * edge
    shape = jax.ShapeDtypeStruct(weights.shape, F32)
    norm_shapes = [jax.ShapeDtypeStruct((4, D), F32)] * (3 if norms else 0)
    return pl.pallas_call(
        lambda *refs: shampoo_kernel(scale, bool(norms), *refs),
        out_shape=[shape] * 4 + norm_shapes,
        scratch_shapes=[
            pltpu.VMEM((slots, edge, width), F32),
            pltpu.VMEM((slots, edge, width), F32),
        ],
        compiler_params=pltpu.CompilerParams(vmem_limit_bytes=SHAMPOO_VMEM),
        cost_estimate=pl.CostEstimate(flops=9 << 30, bytes_accessed=4 << 20, transcendentals=0),
        name="shampoo",
    )(early, late, weights, stat_left, stat_right, *norms)


def swap_heads(values):
    return lax.ppermute(values, "head", [(0, 1), (1, 0)])


def to_all(values, axis):
    return lax.all_to_all(values, axis, 0, 0)


def across(values, apart):
    pairs = [(i, i ^ apart) for i in range(INNER)]
    return lax.ppermute(values, "inner", pairs)


def from_all(values):
    return [values] + [across(values, apart) for apart in range(1, INNER)]


def gather_slabs(weights, other_mask):
    early, late = pack(weights, OUTER)
    early = to_all(early, "outer")
    early, late = lax.optimization_barrier((early, late))
    late = to_all(late, "outer")
    early = from_all(early)
    early[-1], late, other_mask = lax.optimization_barrier((early[-1], late, other_mask))
    return early, from_all(late), other_mask


def gather_blocks(local):
    groups, _, edge, _ = local.shape
    blocks = lax.all_gather(local, ("outer", "inner"), axis=1, tiled=True)
    blocks = blocks.reshape(groups, SLABS // INNER, INNER, D // edge, edge, edge)
    slabs = blocks.transpose(2, 1, 0, 4, 3, 5).reshape(SLABS, groups, edge, D)
    return slabs if groups > 1 else slabs[:, 0]


def scatter_blocks(slabs, count, edge):
    groups = slabs.shape[1]
    blocks = slabs.reshape(INNER, SLABS // INNER, groups, edge, D // edge, edge)
    blocks = blocks.transpose(2, 1, 0, 4, 3, 5).reshape(groups, SLABS * (D // edge), edge, edge)
    owned = lax.psum_scatter(blocks, ("outer", "inner"), scatter_dimension=1, tiled=True)
    return owned.transpose(0, 2, 1, 3).reshape(groups, edge, count * edge)


def per_device(
    tokens,
    cotangent,
    token_counts,
    head_mask,
    norm_params,
    norm_state,
    weights,
    stat_left,
    stat_right,
):
    weights, stat_left, stat_right = weights[0], stat_left[0], stat_right[0]
    _, count, edge, _ = weights.shape
    whole_slabs = count * edge == D
    other_mask = swap_heads(head_mask)
    if whole_slabs:
        place = jnp.stack([lax.axis_index("head"), lax.axis_index("inner")])
        early, late, other_mask = gather_slabs(weights, other_mask)
    else:
        place = jnp.stack([lax.axis_index("head"), 0])
        local = weights.astype(BF)
        early = jnp.split(gather_blocks(local[:1]), INNER)
        late = jnp.split(gather_blocks(local[1:]), INNER)
    early, late = list(early), list(late)
    masks = (head_mask, other_mask)
    early += [swap_heads(piece) for piece in early]
    prob, qkv, out, middle, wqkv, wo = attn_forward(
        place, token_counts, *masks, tokens, norm_params, early
    )
    late[1:], middle = lax.optimization_barrier((late[1:], middle))
    late += [swap_heads(piece) for piece in late]
    block_out, middle_grad, norm_two, own_late, sent_late = mlp(
        place, middle, cotangent, norm_params, late
    )
    late_received = swap_heads(sent_late)
    if whole_slabs:
        late_grads = list(add_late(own_late, late_received))
        late_grads, middle_grad = lax.optimization_barrier((late_grads, middle_grad))
        late_grads[1:] = [across(late_grads[apart], apart) for apart in range(1, INNER)]
    input_grad, own_early, sent_early, norm_sums = attn_backward(
        place, *masks, tokens, middle_grad, prob, qkv, out, norm_params, norm_two, wqkv, wo
    )
    if whole_slabs:
        late_grads, sent_early = lax.optimization_barrier((late_grads, sent_early))
    early_received = swap_heads(sent_early)
    devices = lax.axis_size("outer") * lax.axis_size("inner") * lax.axis_size("head")
    scale = 1.0 / math.sqrt(tokens.shape[0] * devices)
    state = (weights, stat_left, stat_right, scale)
    if whole_slabs:
        late_grads = to_all(sum_late(late_grads), "outer")
        early_grads = list(combine(place, own_early, early_received, norm_sums))
        early_grads[1:] = [across(early_grads[apart], apart) for apart in range(1, INNER)]
        joined, late_grads = lax.optimization_barrier((join(early_grads), late_grads))
        results = shampoo(to_all(joined, "outer"), late_grads, *state, (norm_params, norm_state))
    else:
        early_slabs = own_early.astype(F32) + early_received[:SLABS].astype(F32)
        late_slabs = own_late.astype(F32) + late_received.astype(F32)
        late_slabs = late_slabs.reshape(SLABS, 2, edge, D)
        slabs = jnp.concatenate([early_slabs[:, None], late_slabs], axis=1).astype(BF)
        owned = scatter_blocks(slabs, count, edge)
        results = list(shampoo(owned[:1], owned[None, 1:], *state))
        norm_grads = lax.psum(norm_sums, ("outer", "inner", "head")) * scale
        state_new = 0.5 * norm_state + 0.5 * norm_grads * norm_grads
        results += [norm_grads, state_new, norm_params - 0.2 * norm_grads / jnp.sqrt(state_new)]
    return (block_out, input_grad, *[result[None] for result in results[:4]], *results[4:])


def solution(mesh):
    shape = (mesh.shape["dp"] // INNER, INNER, mesh.shape["head"])
    split_mesh = Mesh(mesh.devices.reshape(shape), ("outer", "inner", "head"))
    group = ("outer", "inner")
    blocks = P("head", None, group, None, None)
    rows = P(group + ("head",), None)
    return jax.shard_map(
        per_device,
        mesh=split_mesh,
        in_specs=(rows, rows, P(group), P(group, "head"), P(), P(), blocks, blocks, blocks),
        out_specs=(rows, rows, blocks, blocks, blocks, blocks, P(), P(), P()),
        check_vma=False,
    )
```

```python
import math

import jax
import jax.numpy as jnp
from jax import lax
from jax.experimental import pallas as pl
from jax.experimental.pallas import tpu as pltpu
from jax.sharding import Mesh, PartitionSpec as P

D = 384
HEAD_DIM = 64
MLP = 1536
S = 256
ITERS = 8
PAIR = 2 * HEAD_DIM
PAIRS = D // PAIR
HALF = D // 2
SLABS = 16
INNER = 4
OUTER = SLABS // INNER
TILE = 512
IMAGES = TILE // S
NORM_ROWS = 8
PACK = 2
ROOT_HALF = 0.7071067811865476
DENSITY_FACTOR = 0.3989422804014327
BF = jnp.bfloat16
F32 = jnp.float32
VMEM_LIMIT = 40 << 20
SMALL_VMEM = 8 << 20
SHAMPOO_VMEM = 24 << 20


def in_hbm(values):
    return pltpu.with_memory_space_constraint(values, pltpu.HBM)


def nn(left, right):
    return jnp.dot(left, right, preferred_element_type=F32)


def nt(left, right):
    return lax.dot_general(left, right, (((1,), (1,)), ((), ())), preferred_element_type=F32)


def tn(left, right):
    return lax.dot_general(left, right, (((0,), (0,)), ((), ())), preferred_element_type=F32)


def normalize(values):
    centered = values - jnp.mean(values, axis=-1, keepdims=True)
    variance = jnp.mean(centered * centered, axis=-1, keepdims=True)
    inverse_std = lax.rsqrt(variance + 1e-06)
    return centered * inverse_std, inverse_std


def norm_backward(grad_out, normed, inverse_std, gain):
    grad_normed = grad_out * gain
    mean_first = jnp.mean(grad_normed, axis=-1, keepdims=True)
    mean_second = jnp.mean(grad_normed * normed, axis=-1, keepdims=True)
    grad_in = inverse_std * (grad_normed - mean_first - normed * mean_second)
    gain_grad = jnp.sum(grad_out * normed, axis=0, keepdims=True)
    shift_grad = jnp.sum(grad_out, axis=0, keepdims=True)
    return grad_in, jnp.concatenate([gain_grad, shift_grad], axis=0)


def slab_at(owner):
    return (owner % INNER) * OUTER + owner // INNER


def lane_halves():
    lane = lax.broadcasted_iota(jnp.int32, (1, PAIR), 1)
    first = (lane < HEAD_DIM).astype(BF)
    return first, (1 - first).astype(BF)


def stacked(values, first, second):
    return jnp.concatenate([values * first, values * second], axis=0)


def mask_lanes(place_ref, own_ref, other_ref, image, pair):
    image = place_ref[0] * (own_ref.shape[0] // 2) + image
    heads = own_ref.shape[1]
    on = [
        own_ref[image, head] if head < heads else other_ref[image, head - heads]
        for head in (2 * pair, 2 * pair + 1)
    ]
    lane = lax.broadcasted_iota(jnp.int32, (1, PAIR), 1)
    return jnp.where(lane < HEAD_DIM, on[0], on[1]).astype(F32)


def attn_forward_kernel(
    place_ref, own_mask_ref, other_mask_ref, x_ref, norm_ref, *refs
):
    slab_refs, refs = refs[: 2 * INNER], refs[2 * INNER :]
    prob_ref, qkv_ref, out_ref, middle_ref, wqkv_ref, wo_ref, held_ref = refs
    step = pl.program_id(0)

    @pl.when(step == 0)
    def _():
        for number, ref in enumerate(slab_refs):
            side, apart = divmod(number, INNER)
            held_ref[side, place_ref[1] ^ apart] = ref[...]

        def slab_of(side, owner):
            return held_ref[side, owner % INNER, owner // INNER]

        for row in range(D // 48):
            for part in range(3):
                pieces = []
                for number in range(2):
                    slab, side = divmod(3 * row + part, 2)
                    piece = slab_of(number, slab)[:, side * HALF : (side + 1) * HALF]
                    pieces.append(piece)
                joined = jnp.concatenate(pieces, axis=1)
                if part == 0:
                    joined = joined * 0.125
                wqkv_ref[48 * row : 48 * row + 48, D * part : D * part + D] = joined
        for side in range(2):
            for row in range(HALF // 48):
                start = side * HALF + 48 * row
                wo_ref[start : start + 48, :] = slab_of(side, 12 + row)

    x = x_ref[...].astype(F32)
    normed, _ = normalize(x)
    rows = (normed * norm_ref[0:1, :] + norm_ref[1:2, :]).astype(BF)
    qkv_ref[...] = nn(rows, wqkv_ref[...]).astype(BF)
    first, second = lane_halves()
    column = lax.broadcasted_iota(jnp.int32, (1, S), 1)
    tasks = [(image, pair) for image in range(IMAGES) for pair in range(PAIRS)]

    def places(task):
        image, pair = task
        here = slice(S * image, S * image + S)
        return here, *(slice(D * t + PAIR * pair, D * t + PAIR * (pair + 1)) for t in range(3))

    def get_scores(task):
        here, query_lanes, key_lanes, _ = places(task)
        return nt(stacked(qkv_ref[here, query_lanes], first, second), qkv_ref[here, key_lanes])

    def get_prob(task, scores):
        image = place_ref[0] * (own_mask_ref.shape[0] // 2) + IMAGES * step + task[0]
        scores = jnp.where(column < place_ref[2 + image], scores, -1e30)
        top = jnp.max(scores, axis=-1, keepdims=True)
        exp_scores = jnp.exp(scores - top)
        total = jnp.sum(exp_scores, axis=-1, keepdims=True)
        prob = (exp_scores * (1.0 / total)).astype(BF)
        prob_ref[task] = prob
        return prob

    all_scores = [get_scores(task) for task in tasks]
    probs = [get_prob(task, scores) for task, scores in zip(tasks, all_scores)]
    for task, prob in zip(tasks, probs):
        here, lanes, _, value_lanes = places(task)
        values = qkv_ref[here, value_lanes]
        head_out = nn(prob[:S], values * first) + nn(prob[S:], values * second)
        mask = mask_lanes(place_ref, own_mask_ref, other_mask_ref, IMAGES * step + task[0], task[1])
        out_ref[here, lanes] = (head_out * mask).astype(BF)
    middle_ref[...] = x + nn(out_ref[...], wo_ref[...])


def attn_forward(place, own_mask, other_mask, tokens, norm_params, slabs):
    rows = tokens.shape[0]
    images = rows // S
    tile = pl.BlockSpec((TILE, D), lambda i: (i, 0))
    slab = pl.BlockSpec((OUTER, 48, D), lambda i: (0, 0, 0))
    smem = pl.BlockSpec(memory_space=pltpu.SMEM)
    return pl.pallas_call(
        attn_forward_kernel,
        grid=(rows // TILE,),
        in_specs=[smem] * 3 + [tile, pl.BlockSpec((4, D), lambda i: (0, 0))] + [slab] * 2 * INNER,
        out_specs=[
            pl.BlockSpec((IMAGES, PAIRS, 2 * S, S), lambda i: (i, 0, 0, 0)),
            pl.BlockSpec((TILE, 3 * D), lambda i: (i, 0)),
            tile,
            tile,
            pl.BlockSpec((D, 3 * D), lambda i: (0, 0)),
            pl.BlockSpec((D, D), lambda i: (0, 0)),
        ],
        out_shape=[
            pltpu.HBM((images, PAIRS, 2 * S, S), BF),
            pltpu.HBM((rows, 3 * D), BF),
            pltpu.HBM((rows, D), BF),
            pltpu.HBM((rows, D), F32),
            pltpu.HBM((D, 3 * D), BF),
            pltpu.HBM((D, D), BF),
        ],
        scratch_shapes=[pltpu.VMEM((2, INNER, OUTER, 48, D), BF)],
        compiler_params=pltpu.CompilerParams(vmem_limit_bytes=VMEM_LIMIT),
        cost_estimate=pl.CostEstimate(
            flops=rows * D * (8 * D + 16 * S), bytes_accessed=16 << 20, transcendentals=rows * 6 * S
        ),
        name="attn_forward",
    )(place, own_mask, other_mask, in_hbm(tokens), in_hbm(norm_params), *slabs)


def mlp_kernel(place_ref, middle_ref, cot_ref, norm_ref, *refs):
    slab_refs, refs = refs[: 2 * INNER], refs[2 * INNER :]
    out_ref, grad_ref, norm_grad_ref, *refs = refs
    own_ref, sent_ref, up_ref, down_ref, up_grad_ref, down_grad_ref = refs
    step = pl.program_id(0)
    half = MLP // 2

    def places(apart, outer):
        inner = place_ref[1] ^ apart
        row = pl.multiple_of(48 * (2 * outer + inner // 2), 16)
        lane = pl.multiple_of(D * (inner % 2), 128)
        down_row = pl.multiple_of(48 * (INNER * outer + inner), 16)
        return row, lane, down_row

    @pl.when(step == 0)
    def _():
        up_grad_ref[...] = jnp.zeros_like(up_grad_ref)
        down_grad_ref[...] = jnp.zeros_like(down_grad_ref)
        norm_grad_ref[...] = jnp.zeros_like(norm_grad_ref)
        for number, ref in enumerate(slab_refs):
            side, apart = divmod(number, INNER)
            for outer in range(OUTER):
                row, lane, down_row = places(apart, outer)
                up_ref[side, pl.ds(row, 48), pl.ds(lane, D)] = ref[outer, 0]
                down_ref[side, pl.ds(down_row, 48), :] = ref[outer, 1]

    middle = middle_ref[...]
    normed, inverse_std = normalize(middle)
    rows = (normed * norm_ref[2:3, :] + norm_ref[3:4, :]).astype(BF)
    cot = cot_ref[...]
    total = middle
    back = None
    for side in range(2):
        up, down = up_ref[side], down_ref[side]
        pre = nn(rows, up)
        act_grad = nt(cot, down)
        cumulative = 0.5 * (1.0 + lax.erf(pre * ROOT_HALF))
        density = jnp.exp(-0.5 * pre * pre) * DENSITY_FACTOR
        act = (pre * cumulative).astype(BF)
        pre_grad = (act_grad * (cumulative + pre * density)).astype(BF)
        total = total + nn(act, down)
        term = nt(pre_grad, up)
        back = term if back is None else back + term
        down_grad_ref[side] += tn(act, cot)
        up_grad_ref[side] += tn(rows, pre_grad)
    out_ref[...] = total
    grad_in, norm_part = norm_backward(back, normed, inverse_std, norm_ref[2:3, :])
    norm_grad_ref[...] += norm_part
    grad_ref[...] = cot.astype(F32) + grad_in

    @pl.when(step == pl.num_programs(0) - 1)
    def _():
        for apart in range(INNER):
            for outer in range(OUTER):
                row, lane, down_row = places(apart, outer)
                for side, ref in enumerate((own_ref, sent_ref)):
                    up = up_grad_ref[side, pl.ds(row, 48), pl.ds(lane, D)]
                    down = down_grad_ref[side, pl.ds(down_row, 48), :]
                    ref[apart, outer, 0] = up.astype(BF)
                    ref[apart, outer, 1] = down.astype(BF)


def mlp(place, middle, cotangent, norm_params, slabs):
    rows = middle.shape[0]
    slab = pl.BlockSpec((OUTER, 2, 48, D), lambda i: (0, 0, 0, 0))
    grads = (INNER, OUTER, 2, 48, D)
    grad = pl.BlockSpec(grads, lambda i: (0, 0, 0, 0, 0))
    tile = pl.BlockSpec((TILE, D), lambda i: (i, 0))
    return pl.pallas_call(
        mlp_kernel,
        grid=(rows // TILE,),
        in_specs=[
            pl.BlockSpec(memory_space=pltpu.SMEM),
            tile,
            tile,
            pl.BlockSpec((4, D), lambda i: (0, 0)),
            *[slab] * 2 * INNER,
        ],
        out_specs=[tile, tile, pl.BlockSpec((2, D), lambda i: (0, 0)), grad, grad],
        out_shape=[
            jax.ShapeDtypeStruct((rows, D), F32),
            pltpu.HBM((rows, D), F32),
            jax.ShapeDtypeStruct((2, D), F32),
            *[jax.ShapeDtypeStruct(grads, BF)] * 2,
        ],
        scratch_shapes=[
            pltpu.VMEM((2, D, MLP // 2), BF),
            pltpu.VMEM((2, MLP // 2, D), BF),
            pltpu.VMEM((2, D, MLP // 2), F32),
            pltpu.VMEM((2, MLP // 2, D), F32),
        ],
        compiler_params=pltpu.CompilerParams(vmem_limit_bytes=VMEM_LIMIT),
        cost_estimate=pl.CostEstimate(
            flops=12 * rows * D * MLP, bytes_accessed=20 << 20, transcendentals=2 * rows * MLP
        ),
        name="mlp",
    )(place, in_hbm(middle), in_hbm(cotangent), in_hbm(norm_params), *slabs)


def attn_backward_kernel(
    place_ref, own_mask_ref, other_mask_ref, x_ref, grad_ref, prob_ref, qkv_ref, out_ref,
    norm_ref, later_norm_ref, wqkv_ref, wo_ref,
    in_grad_ref, own_grad_ref, sent_grad_ref, norm_grad_ref,
    dqkv_ref, wqkv_grad_ref, wo_grad_ref,
):
    step = pl.program_id(0)

    @pl.when(step == 0)
    def _():
        wqkv_grad_ref[...] = jnp.zeros_like(wqkv_grad_ref)
        wo_grad_ref[...] = jnp.zeros_like(wo_grad_ref)
        norm_grad_ref[0:2, :] = jnp.zeros((2, D), F32)
        norm_grad_ref[2:4, :] = later_norm_ref[...]

    x = x_ref[...].astype(F32)
    normed, inverse_std = normalize(x)
    rows = (normed * norm_ref[0:1, :] + norm_ref[1:2, :]).astype(BF)
    grad = grad_ref[...]
    low_grad = grad.astype(BF)
    head_out = out_ref[...]
    wo_grad_ref[...] += tn(head_out, low_grad)
    whole_grad = nt(low_grad, wo_ref[...]).astype(BF)
    first, second = lane_halves()
    first_wide, second_wide = first.astype(F32), second.astype(F32)
    tasks = [(image, pair) for image in range(IMAGES) for pair in range(PAIRS)]

    def places(task):
        image, pair = task
        here = slice(S * image, S * image + S)
        return here, *(slice(D * t + PAIR * pair, D * t + PAIR * (pair + 1)) for t in range(3))

    def get_pair_grad(task):
        here, lanes, _, _ = places(task)
        mask = mask_lanes(place_ref, own_mask_ref, other_mask_ref, IMAGES * step + task[0], task[1])
        grad = whole_grad[here, lanes] * mask.astype(BF)
        dots = grad.astype(F32) * head_out[here, lanes].astype(F32)
        first_dot = jnp.sum(dots * first_wide, axis=-1, keepdims=True)
        second_dot = jnp.sum(dots * second_wide, axis=-1, keepdims=True)
        return stacked(grad, first, second), jnp.concatenate([first_dot, second_dot], axis=0)

    pair_grads = [get_pair_grad(task) for task in tasks]
    prob_grads = [
        nt(pair_grad[0], qkv_ref[places(task)[0], places(task)[3]])
        for task, pair_grad in zip(tasks, pair_grads)
    ]
    score_grads = [
        (prob_ref[task].astype(F32) * (prob_grad - pair_grad[1])).astype(BF)
        for task, prob_grad, pair_grad in zip(tasks, prob_grads, pair_grads)
    ]
    for task, score_grad, (pair_grad, _) in zip(tasks, score_grads, pair_grads):
        here, query_lanes, key_lanes, value_lanes = places(task)
        keys = qkv_ref[here, key_lanes]
        queries = stacked(qkv_ref[here, query_lanes], first, second)
        query_grad = nn(score_grad[:S], keys * first) + nn(score_grad[S:], keys * second)
        key_grad = nn(jnp.transpose(queries), score_grad)
        value_grad = nn(jnp.transpose(pair_grad), prob_ref[task])
        dqkv_ref[here, query_lanes] = query_grad.astype(BF)
        dqkv_ref[here, key_lanes] = jnp.transpose(key_grad).astype(BF)
        dqkv_ref[here, value_lanes] = jnp.transpose(value_grad).astype(BF)
    dqkv = dqkv_ref[...]
    wqkv_grad_ref[...] += tn(rows, dqkv)
    back = nt(dqkv, wqkv_ref[...])
    grad_in, norm_part = norm_backward(back, normed, inverse_std, norm_ref[0:1, :])
    norm_grad_ref[0:2, :] += norm_part
    in_grad_ref[...] = grad + grad_in

    @pl.when(step == pl.num_programs(0) - 1)
    def _():
        for side, slab_grads in enumerate((own_grad_ref, sent_grad_ref)):
            for slab in range(12):
                pieces = []
                for unit in (2 * slab, 2 * slab + 1):
                    row, part = divmod(unit, 3)
                    piece = wqkv_grad_ref[48 * row : 48 * row + 48, D * part : D * part + D]
                    piece = piece[:, HALF * side : HALF * side + HALF]
                    pieces.append(piece * 0.125 if part == 0 else piece)
                slab_grads[slab_at(slab)] = jnp.concatenate(pieces, axis=1).astype(BF)
            for row in range(HALF // 48):
                start = HALF * side + 48 * row
                slab_grads[slab_at(12 + row)] = wo_grad_ref[start : start + 48, :].astype(BF)
        sent_grad_ref[SLABS, :NORM_ROWS] = jnp.concatenate(split(norm_grad_ref[...]), axis=0)
        sent_grad_ref[SLABS, NORM_ROWS:] = jnp.zeros((48 - NORM_ROWS, D), BF)


def attn_backward(
    place, own_mask, other_mask, tokens, grad, prob, qkv, out, norm_params, later_norms, wqkv, wo
):
    rows = tokens.shape[0]
    tile = pl.BlockSpec((TILE, D), lambda i: (i, 0))
    smem = pl.BlockSpec(memory_space=pltpu.SMEM)
    return pl.pallas_call(
        attn_backward_kernel,
        grid=(rows // TILE,),
        in_specs=[
            smem,
            smem,
            smem,
            tile,
            tile,
            pl.BlockSpec((IMAGES, PAIRS, 2 * S, S), lambda i: (i, 0, 0, 0)),
            pl.BlockSpec((TILE, 3 * D), lambda i: (i, 0)),
            tile,
            pl.BlockSpec((4, D), lambda i: (0, 0)),
            pl.BlockSpec((2, D), lambda i: (0, 0)),
            pl.BlockSpec((D, 3 * D), lambda i: (0, 0)),
            pl.BlockSpec((D, D), lambda i: (0, 0)),
        ],
        out_specs=[
            tile,
            pl.BlockSpec((SLABS, 48, D), lambda i: (0, 0, 0)),
            pl.BlockSpec((SLABS + 1, 48, D), lambda i: (0, 0, 0)),
            pl.BlockSpec((4, D), lambda i: (0, 0)),
        ],
        out_shape=[
            jax.ShapeDtypeStruct((rows, D), F32),
            jax.ShapeDtypeStruct((SLABS, 48, D), BF),
            jax.ShapeDtypeStruct((SLABS + 1, 48, D), BF),
            jax.ShapeDtypeStruct((4, D), F32),
        ],
        scratch_shapes=[
            pltpu.VMEM((TILE, 3 * D), BF),
            pltpu.VMEM((D, 3 * D), F32),
            pltpu.VMEM((D, D), F32),
        ],
        compiler_params=pltpu.CompilerParams(vmem_limit_bytes=VMEM_LIMIT),
        cost_estimate=pl.CostEstimate(
            flops=rows * D * (16 * D + 32 * S), bytes_accessed=20 << 20, transcendentals=0
        ),
        name="attn_backward",
    )(
        place, own_mask, other_mask,
        *map(in_hbm, (tokens, grad, prob, qkv, out, norm_params, later_norms, wqkv, wo)),
    )


def pack_kernel(weight_ref, early_ref, late_ref):
    groups, count, _, _ = weight_ref.shape
    for group in range(groups):
        blocks = [weight_ref[group, block] for block in range(count)]
        slab = jnp.concatenate(blocks, axis=1).astype(BF)
        for copy in range(early_ref.shape[0]):
            if group == 0:
                early_ref[copy] = slab
            else:
                late_ref[copy, group - 1] = slab


def pack(weights, number):
    groups, count, edge, _ = weights.shape
    return pl.pallas_call(
        pack_kernel,
        out_shape=[
            jax.ShapeDtypeStruct((number, edge, count * edge), BF),
            jax.ShapeDtypeStruct((number, groups - 1, edge, count * edge), BF),
        ],
        compiler_params=pltpu.CompilerParams(vmem_limit_bytes=SMALL_VMEM),
        name="pack",
    )(in_hbm(weights))


def add_kernel(own_ref, received_ref, *out_refs):
    for apart, out_ref in enumerate(out_refs):
        total = own_ref[apart].astype(F32) + received_ref[apart].astype(F32)
        out_ref[...] = total.astype(BF)


def add_late(own, received):
    return pl.pallas_call(
        add_kernel,
        out_shape=[jax.ShapeDtypeStruct(own.shape[1:], BF)] * own.shape[0],
        compiler_params=pltpu.CompilerParams(vmem_limit_bytes=SMALL_VMEM),
        name="add_late",
    )(own, received)


def sum_kernel(*refs):
    *in_refs, out_ref = refs
    total = in_refs[0][...].astype(F32)
    for ref in in_refs[1:]:
        total = total + ref[...].astype(F32)
    out_ref[...] = total.astype(BF)


def sum_late(pieces):
    return pl.pallas_call(
        sum_kernel,
        out_shape=jax.ShapeDtypeStruct(pieces[0].shape, BF),
        compiler_params=pltpu.CompilerParams(vmem_limit_bytes=SMALL_VMEM),
        name="sum_late",
    )(*pieces)


def combine_kernel(place_ref, own_ref, received_ref, norm_ref, *out_refs):
    norms = received_ref[SLABS, :NORM_ROWS].astype(F32)
    norms = norm_ref[...] + (norms[:4] + norms[4:])
    rows = jnp.concatenate(split(norms), axis=0)
    for apart, out_ref in enumerate(out_refs):
        start = OUTER * (place_ref[1] ^ apart)
        for outer in range(OUTER):
            total = own_ref[start + outer].astype(F32) + received_ref[start + outer].astype(F32)
            out_ref[48 * outer : 48 * outer + 48, :] = total.astype(BF)
        out_ref[48 * OUTER :, :] = rows


def combine(place, own, received, norms):
    vmem = pl.BlockSpec(memory_space=pltpu.VMEM)
    shape = jax.ShapeDtypeStruct((48 * OUTER + NORM_ROWS, D), BF)
    return pl.pallas_call(
        combine_kernel,
        in_specs=[pl.BlockSpec(memory_space=pltpu.SMEM), vmem, vmem, vmem],
        out_shape=[shape] * INNER,
        compiler_params=pltpu.CompilerParams(vmem_limit_bytes=SMALL_VMEM),
        name="combine",
    )(place, own, received, norms)


def join_kernel(*refs):
    *early_refs, out_ref = refs
    total = early_refs[0][...].astype(F32)
    for ref in early_refs[1:]:
        total = total + ref[...].astype(F32)
    norms = total[48 * OUTER : 48 * OUTER + 4] + total[48 * OUTER + 4 :]
    for outer in range(OUTER):
        out_ref[outer, :48] = total[48 * outer : 48 * outer + 48].astype(BF)
        out_ref[outer, 48:] = jnp.concatenate(split(norms), axis=0)


def join(early):
    return pl.pallas_call(
        join_kernel,
        out_shape=jax.ShapeDtypeStruct((OUTER, 48 + NORM_ROWS, D), BF),
        compiler_params=pltpu.CompilerParams(vmem_limit_bytes=SMALL_VMEM),
        name="join",
    )(*early)


def split(values):
    high = values.astype(BF)
    return high, (values - high.astype(F32)).astype(BF)


def stack(*pieces):
    return jnp.concatenate(pieces, axis=0)


def cut_rows(values, number):
    edge = values.shape[0] // number
    return [values[edge * i : edge * i + edge] for i in range(number)]


def product(left, right):
    high, low = left
    right_high, right_low = right
    one, two = cut_rows(nn(stack(high, low), right_high), 2)
    return one + (two + nn(high, right_low))


def two_products(left, middle, right):
    right_high, right_low = right
    both = cut_rows(nn(stack(left[0], middle[0], left[1], middle[1]), right_high), 4)
    high = cut_rows(nn(stack(left[0], middle[0]), right_low), 2)
    return both[0] + (both[2] + high[0]), both[1] + (both[3] + high[1])


def update_norms(scale, total, param_ref, state_ref, grad_ref, new_state_ref, new_ref):
    grads = total * scale
    state = 0.5 * state_ref[...] + 0.5 * grads * grads
    grad_ref[...] = grads
    new_state_ref[...] = state
    new_ref[...] = param_ref[...] - 0.2 * grads / jnp.sqrt(state)


def shampoo_kernel(scale, with_norms, received_ref, weight_ref, left_ref, right_ref, *refs):
    if with_norms:
        norm_ins, norm_outs, refs = refs[:2], refs[-5:-2], refs[:-5] + refs[-2:]
    out_grad_ref, left_new_ref, right_new_ref, new_weight_ref, root_ref, power_ref = refs[-6:]
    groups, count, edge = weight_ref.shape[:3]

    received = received_ref[0].astype(F32)
    for number in range(1, received_ref.shape[0]):
        received = received + received_ref[number].astype(F32)
    if with_norms:
        norms = received[0, edge:]
        update_norms(scale, norms[:4] + norms[4:], *norm_ins, *norm_outs)
    pack = min(PACK, count)
    width = pack * edge
    places = [(g, pack * n) for g in range(groups) for n in range(count // pack)]
    packs = len(places)

    def block_of(shape, dim):
        return lax.broadcasted_iota(jnp.int32, shape, dim) // edge

    row = lax.broadcasted_iota(jnp.int32, (edge, width), 0)
    lane = lax.broadcasted_iota(jnp.int32, (edge, width), 1)
    identity = (lane % edge == row).astype(F32)
    same = (block_of((width, width), 0) == block_of((width, width), 1)).astype(BF)
    lane_block = block_of((1, width), 1)

    def spread(pieces):
        return tuple(stack(*[piece] * pack) * same for piece in pieces)

    def cut(packed, index):
        return packed[:, edge * index : edge * index + edge]

    def beside(ref, place):
        return jnp.concatenate([ref[place[0], place[1] + i] for i in range(pack)], axis=1)

    grads, parts = [], []
    for group, start in places:
        grad = received[group, :edge, edge * start : edge * start + width] * scale
        blocks = [cut(grad, index) for index in range(pack)]
        for index in range(pack):
            out_grad_ref[group, start + index] = blocks[index]
        grad_t = jnp.concatenate([jnp.transpose(block) for block in blocks], axis=1)
        one, two = split(grad), split(grad_t)
        one_diagonal, two_diagonal = spread(one), spread(two)
        grads.append(one_diagonal)
        parts.append((left_ref, left_new_ref, one, two_diagonal))
        parts.append((right_ref, right_new_ref, two, one_diagonal))
    grams = [product(left, right) for _, _, left, right in parts]
    for slot, (old_ref, new_ref, _, _) in enumerate(parts):
        group, start = places[slot // 2]
        new = 0.5 * beside(old_ref, places[slot // 2]) + 0.5 * grams[slot]
        for index in range(pack):
            new_ref[group, start + index] = cut(new, index)
        columns = jnp.sum(new * new, axis=0, keepdims=True)
        squares = jnp.zeros((1, width), F32)
        for index in range(pack):
            inside = lane_block == index
            part = jnp.sum(jnp.where(inside, columns, 0.0), axis=1, keepdims=True)
            squares = jnp.where(inside, part, squares)
        factor = 2.5 / jnp.sqrt(squares)
        root_ref[slot] = jnp.broadcast_to(jnp.sqrt(jnp.sqrt(factor)), (edge, width))
        power_ref[slot] = factor * new
    slots = range(2 * packs)

    def advance(first):
        powers = [power_ref[slot] for slot in slots]
        middles = [split((5.0 * identity - power) * 0.25) for power in powers]
        rights = [spread(middle) for middle in middles]
        powers = [split(power) for power in powers]
        if first:
            squares = [product(middles[s], rights[s]) for s in slots]
            for slot in slots:
                root_ref[slot] *= (5.0 * identity - power_ref[slot]) * 0.25
        else:
            roots = [split(root_ref[slot]) for slot in slots]
            both = [two_products(roots[s], middles[s], rights[s]) for s in slots]
            squares = [pair[1] for pair in both]
            for slot in slots:
                root_ref[slot] = both[slot][0]
        rights = [spread(split(square)) for square in squares]
        powers = [split(product(powers[s], rights[s])) for s in slots]
        for slot in slots:
            power_ref[slot] = product(powers[slot], rights[slot])

    advance(True)
    lax.fori_loop(0, ITERS - 2, lambda _, carry: advance(False) or carry, 0)
    rights = [spread(split((5.0 * identity - power_ref[slot]) * 0.25)) for slot in slots]
    for slot in slots:
        root_ref[slot] = product(split(root_ref[slot]), rights[slot])
    steps = [product(split(root_ref[2 * n]), grads[n]) for n in range(packs)]
    rights = [spread(split(root_ref[2 * n + 1])) for n in range(packs)]
    steps = [product(split(steps[n]), rights[n]) for n in range(packs)]
    for number, (group, start) in enumerate(places):
        for index in range(pack):
            step = 0.25 * cut(steps[number], index)
            new_weight_ref[group, start + index] = weight_ref[group, start + index] - step


def shampoo(received, weights, stat_left, stat_right, scale, first, earlier=(), norms=()):
    groups = received.shape[1]
    _, count, edge, _ = weights.shape
    slots = 2 * groups * count // min(PACK, count)
    width = min(PACK, count) * edge
    block = pl.BlockSpec(
        (pl.Element(groups), pl.Element(count), pl.Element(edge), pl.Element(edge)),
        lambda i: (first, 0, 0, 0),
    )
    shape = jax.ShapeDtypeStruct(weights.shape, F32)
    norm = pl.BlockSpec((4, D), lambda i: (0, 0))
    norm_outs = 3 if norms else 0
    ins = 4 + len(norms)
    return pl.pallas_call(
        lambda *refs: shampoo_kernel(scale, bool(norms), *refs),
        grid=(1,),
        in_specs=[
            pl.BlockSpec(received.shape, lambda i: (0, 0, 0, 0)),
            *[block] * 3,
            *[norm] * len(norms),
            *[pl.BlockSpec(memory_space=pl.ANY)] * len(earlier),
        ],
        out_specs=[block] * 4 + [norm] * norm_outs,
        out_shape=[shape] * 4 + [jax.ShapeDtypeStruct((4, D), F32)] * norm_outs,
        scratch_shapes=[
            pltpu.VMEM((slots, edge, width), F32),
            pltpu.VMEM((slots, edge, width), F32),
        ],
        input_output_aliases={ins + i: i for i in range(len(earlier))},
        compiler_params=pltpu.CompilerParams(vmem_limit_bytes=SHAMPOO_VMEM),
        cost_estimate=pl.CostEstimate(
            flops=groups * (3 << 30), bytes_accessed=4 << 20, transcendentals=0
        ),
        name="shampoo",
    )(received, in_hbm(weights), in_hbm(stat_left), in_hbm(stat_right), *map(in_hbm, norms), *earlier)


def swap_heads(values):
    return lax.ppermute(values, "head", [(0, 1), (1, 0)])


def to_all(values, axis):
    return lax.all_to_all(values, axis, 0, 0)


def across(values, apart):
    pairs = [(i, i ^ apart) for i in range(INNER)]
    return lax.ppermute(values, "inner", pairs)


def from_all(values):
    return [values] + [across(values, apart) for apart in range(1, INNER)]


def gather_slabs(weights, other_mask):
    early, late = pack(weights, OUTER)
    early = to_all(early, "outer")
    early, late = lax.optimization_barrier((early, late))
    late = to_all(late, "outer")
    early = from_all(early)
    early[-1], late, other_mask = lax.optimization_barrier((early[-1], late, other_mask))
    return early, from_all(late), other_mask


def gather_blocks(local):
    groups, _, edge, _ = local.shape
    blocks = lax.all_gather(local, ("outer", "inner"), axis=1, tiled=True)
    blocks = blocks.reshape(groups, SLABS // INNER, INNER, D // edge, edge, edge)
    slabs = blocks.transpose(2, 1, 0, 4, 3, 5).reshape(SLABS, groups, edge, D)
    return slabs if groups > 1 else slabs[:, 0]


def scatter_blocks(slabs, count, edge):
    groups = slabs.shape[1]
    blocks = slabs.reshape(INNER, SLABS // INNER, groups, edge, D // edge, edge)
    blocks = blocks.transpose(2, 1, 0, 4, 3, 5).reshape(groups, SLABS * (D // edge), edge, edge)
    owned = lax.psum_scatter(blocks, ("outer", "inner"), scatter_dimension=1, tiled=True)
    return owned.transpose(0, 2, 1, 3).reshape(groups, edge, count * edge)


def per_device(
    tokens,
    cotangent,
    token_counts,
    head_mask,
    norm_params,
    norm_state,
    weights,
    stat_left,
    stat_right,
):
    weights, stat_left, stat_right = weights[0], stat_left[0], stat_right[0]
    _, count, edge, _ = weights.shape
    whole_slabs = count * edge == D
    other_mask = swap_heads(head_mask)
    inner = lax.axis_index("inner") if whole_slabs else 0
    place = jnp.concatenate([jnp.stack([lax.axis_index("head"), inner]), token_counts])
    if whole_slabs:
        early, late, other_mask = gather_slabs(weights, other_mask)
    else:
        local = weights.astype(BF)
        early = jnp.split(gather_blocks(local[:1]), INNER)
        late = jnp.split(gather_blocks(local[1:]), INNER)
    early, late = list(early), list(late)
    masks = (head_mask, other_mask)
    early += [swap_heads(piece) for piece in early]
    prob, qkv, out, middle, wqkv, wo = attn_forward(
        place, *masks, tokens, norm_params, early
    )
    late[1:], middle = lax.optimization_barrier((late[1:], middle))
    late += [swap_heads(piece) for piece in late]
    block_out, middle_grad, norm_two, own_late, sent_late = mlp(
        place, middle, cotangent, norm_params, late
    )
    late_received = swap_heads(sent_late)
    if whole_slabs:
        late_grads = list(add_late(own_late, late_received))
        late_grads, middle_grad = lax.optimization_barrier((late_grads, middle_grad))
        late_grads[1:] = [across(late_grads[apart], apart) for apart in range(1, INNER)]
    input_grad, own_early, sent_early, norm_sums = attn_backward(
        place, *masks, tokens, middle_grad, prob, qkv, out, norm_params, norm_two, wqkv, wo
    )
    if whole_slabs:
        late_grads, sent_early = lax.optimization_barrier((late_grads, sent_early))
    early_received = swap_heads(sent_early)
    devices = lax.axis_size("outer") * lax.axis_size("inner") * lax.axis_size("head")
    scale = 1.0 / math.sqrt(tokens.shape[0] * devices)
    state = (weights, stat_left, stat_right, scale)
    if whole_slabs:
        late_grads = to_all(sum_late(late_grads), "outer")
        early_grads = list(combine(place, own_early, early_received, norm_sums))
        early_grads[1:] = [across(early_grads[apart], apart) for apart in range(1, INNER)]
        joined, late_grads = lax.optimization_barrier((join(early_grads), late_grads))
        joined = to_all(joined, "outer")[:, None]
        results = shampoo(late_grads, *state, 1)
        results = shampoo(joined, *state, 0, results, (norm_params, norm_state))
    else:
        early_slabs = own_early.astype(F32) + early_received[:SLABS].astype(F32)
        late_slabs = own_late.astype(F32) + late_received.astype(F32)
        late_slabs = late_slabs.reshape(SLABS, 2, edge, D)
        slabs = jnp.concatenate([early_slabs[:, None], late_slabs], axis=1).astype(BF)
        owned = scatter_blocks(slabs, count, edge)
        results = list(shampoo(owned[None], *state, 0))
        norm_grads = lax.psum(norm_sums, ("outer", "inner", "head")) * scale
        state_new = 0.5 * norm_state + 0.5 * norm_grads * norm_grads
        results += [norm_grads, state_new, norm_params - 0.2 * norm_grads / jnp.sqrt(state_new)]
    return (block_out, input_grad, *[result[None] for result in results[:4]], *results[4:])


def solution(mesh):
    shape = (mesh.shape["dp"] // INNER, INNER, mesh.shape["head"])
    split_mesh = Mesh(mesh.devices.reshape(shape), ("outer", "inner", "head"))
    group = ("outer", "inner")
    blocks = P("head", None, group, None, None)
    rows = P(group + ("head",), None)
    return jax.shard_map(
        per_device,
        mesh=split_mesh,
        in_specs=(rows, rows, P(group), P(group, "head"), P(), P(), blocks, blocks, blocks),
        out_specs=(rows, rows, blocks, blocks, blocks, blocks, P(), P(), P()),
        check_vma=False,
    )
```

```python
import math

import jax
import jax.numpy as jnp
from jax import lax
from jax.experimental import pallas as pl
from jax.experimental.pallas import tpu as pltpu
from jax.sharding import Mesh, PartitionSpec as P

D = 384
HEAD_DIM = 64
MLP = 1536
S = 256
ITERS = 8
PAIR = 2 * HEAD_DIM
PAIRS = D // PAIR
HALF = D // 2
SLABS = 16
INNER = 4
OUTER = SLABS // INNER
TILE = 512
IMAGES = TILE // S
NORM_ROWS = 8
PACK = 2
ROOT_HALF = 0.7071067811865476
DENSITY_FACTOR = 0.3989422804014327
BF = jnp.bfloat16
F32 = jnp.float32
VMEM_LIMIT = 40 << 20
SMALL_VMEM = 8 << 20
SHAMPOO_VMEM = 24 << 20


def in_hbm(values):
    return pltpu.with_memory_space_constraint(values, pltpu.HBM)


def nn(left, right):
    return jnp.dot(left, right, preferred_element_type=F32)


def nt(left, right):
    return lax.dot_general(left, right, (((1,), (1,)), ((), ())), preferred_element_type=F32)


def tn(left, right):
    return lax.dot_general(left, right, (((0,), (0,)), ((), ())), preferred_element_type=F32)


def normalize(values):
    centered = values - jnp.mean(values, axis=-1, keepdims=True)
    variance = jnp.mean(centered * centered, axis=-1, keepdims=True)
    inverse_std = lax.rsqrt(variance + 1e-06)
    return centered * inverse_std, inverse_std


def norm_backward(grad_out, normed, inverse_std, gain):
    grad_normed = grad_out * gain
    mean_first = jnp.mean(grad_normed, axis=-1, keepdims=True)
    mean_second = jnp.mean(grad_normed * normed, axis=-1, keepdims=True)
    grad_in = inverse_std * (grad_normed - mean_first - normed * mean_second)
    gain_grad = jnp.sum(grad_out * normed, axis=0, keepdims=True)
    shift_grad = jnp.sum(grad_out, axis=0, keepdims=True)
    return grad_in, jnp.concatenate([gain_grad, shift_grad], axis=0)


def slab_at(owner):
    return (owner % INNER) * OUTER + owner // INNER


def lane_halves():
    lane = lax.broadcasted_iota(jnp.int32, (1, PAIR), 1)
    first = (lane < HEAD_DIM).astype(BF)
    return first, (1 - first).astype(BF)


def stacked(values, first, second):
    return jnp.concatenate([values * first, values * second], axis=0)


def mask_lanes(place_ref, own_ref, other_ref, image, pair):
    image = place_ref[0] * (own_ref.shape[0] // 2) + image
    heads = own_ref.shape[1]
    on = [
        own_ref[image, head] if head < heads else other_ref[image, head - heads]
        for head in (2 * pair, 2 * pair + 1)
    ]
    lane = lax.broadcasted_iota(jnp.int32, (1, PAIR), 1)
    return jnp.where(lane < HEAD_DIM, on[0], on[1]).astype(F32)


def attn_forward_kernel(
    place_ref, own_mask_ref, other_mask_ref, x_ref, norm_ref, *refs
):
    slab_refs, refs = refs[: 2 * INNER], refs[2 * INNER :]
    prob_ref, qkv_ref, out_ref, middle_ref, wqkv_ref, wo_ref, held_ref = refs
    step = pl.program_id(0)

    @pl.when(step == 0)
    def _():
        for number, ref in enumerate(slab_refs):
            side, apart = divmod(number, INNER)
            held_ref[side, place_ref[1] ^ apart] = ref[...]

        def slab_of(side, owner):
            return held_ref[side, owner % INNER, owner // INNER]

        for row in range(D // 48):
            for part in range(3):
                pieces = []
                for number in range(2):
                    slab, side = divmod(3 * row + part, 2)
                    piece = slab_of(number, slab)[:, side * HALF : (side + 1) * HALF]
                    pieces.append(piece)
                joined = jnp.concatenate(pieces, axis=1)
                if part == 0:
                    joined = joined * 0.125
                wqkv_ref[48 * row : 48 * row + 48, D * part : D * part + D] = joined
        for side in range(2):
            for row in range(HALF // 48):
                start = side * HALF + 48 * row
                wo_ref[start : start + 48, :] = slab_of(side, 12 + row)

    x = x_ref[...].astype(F32)
    normed, _ = normalize(x)
    rows = (normed * norm_ref[0:1, :] + norm_ref[1:2, :]).astype(BF)
    qkv_ref[...] = nn(rows, wqkv_ref[...]).astype(BF)
    first, second = lane_halves()
    column = lax.broadcasted_iota(jnp.int32, (1, S), 1)
    tasks = [(image, pair) for image in range(IMAGES) for pair in range(PAIRS)]

    def places(task):
        image, pair = task
        here = slice(S * image, S * image + S)
        return here, *(slice(D * t + PAIR * pair, D * t + PAIR * (pair + 1)) for t in range(3))

    def get_scores(task):
        here, query_lanes, key_lanes, _ = places(task)
        return nt(stacked(qkv_ref[here, query_lanes], first, second), qkv_ref[here, key_lanes])

    def get_prob(task, scores):
        image = place_ref[0] * (own_mask_ref.shape[0] // 2) + IMAGES * step + task[0]
        scores = jnp.where(column < place_ref[2 + image], scores, -1e30)
        top = jnp.max(scores, axis=-1, keepdims=True)
        exp_scores = jnp.exp(scores - top)
        total = jnp.sum(exp_scores, axis=-1, keepdims=True)
        prob = (exp_scores * (1.0 / total)).astype(BF)
        prob_ref[task] = prob
        return prob

    all_scores = [get_scores(task) for task in tasks]
    probs = [get_prob(task, scores) for task, scores in zip(tasks, all_scores)]
    for task, prob in zip(tasks, probs):
        here, lanes, _, value_lanes = places(task)
        values = qkv_ref[here, value_lanes]
        head_out = nn(prob[:S], values * first) + nn(prob[S:], values * second)
        mask = mask_lanes(place_ref, own_mask_ref, other_mask_ref, IMAGES * step + task[0], task[1])
        out_ref[here, lanes] = (head_out * mask).astype(BF)
    middle_ref[...] = x + nn(out_ref[...], wo_ref[...])


def attn_forward(place, own_mask, other_mask, tokens, norm_params, slabs):
    rows = tokens.shape[0]
    images = rows // S
    tile = pl.BlockSpec((TILE, D), lambda i: (i, 0))
    slab = pl.BlockSpec((OUTER, 48, D), lambda i: (0, 0, 0))
    smem = pl.BlockSpec(memory_space=pltpu.SMEM)
    return pl.pallas_call(
        attn_forward_kernel,
        grid=(rows // TILE,),
        in_specs=[smem] * 3 + [tile, pl.BlockSpec((4, D), lambda i: (0, 0))] + [slab] * 2 * INNER,
        out_specs=[
            pl.BlockSpec((IMAGES, PAIRS, 2 * S, S), lambda i: (i, 0, 0, 0)),
            pl.BlockSpec((TILE, 3 * D), lambda i: (i, 0)),
            tile,
            tile,
            pl.BlockSpec((D, 3 * D), lambda i: (0, 0)),
            pl.BlockSpec((D, D), lambda i: (0, 0)),
        ],
        out_shape=[
            pltpu.HBM((images, PAIRS, 2 * S, S), BF),
            pltpu.HBM((rows, 3 * D), BF),
            pltpu.HBM((rows, D), BF),
            pltpu.HBM((rows, D), F32),
            pltpu.HBM((D, 3 * D), BF),
            pltpu.HBM((D, D), BF),
        ],
        scratch_shapes=[pltpu.VMEM((2, INNER, OUTER, 48, D), BF)],
        compiler_params=pltpu.CompilerParams(vmem_limit_bytes=VMEM_LIMIT),
        cost_estimate=pl.CostEstimate(
            flops=rows * D * (8 * D + 16 * S), bytes_accessed=16 << 20, transcendentals=rows * 6 * S
        ),
        name="attn_forward",
    )(place, own_mask, other_mask, in_hbm(tokens), in_hbm(norm_params), *slabs)


def mlp_kernel(place_ref, middle_ref, cot_ref, norm_ref, *refs):
    slab_refs, refs = refs[: 2 * INNER], refs[2 * INNER :]
    out_ref, grad_ref, norm_grad_ref, *refs = refs
    own_ref, sent_ref, up_ref, down_ref, up_grad_ref, down_grad_ref = refs
    step = pl.program_id(0)
    half = MLP // 2

    def places(apart, outer):
        inner = place_ref[1] ^ apart
        row = pl.multiple_of(48 * (2 * outer + inner // 2), 16)
        lane = pl.multiple_of(D * (inner % 2), 128)
        down_row = pl.multiple_of(48 * (INNER * outer + inner), 16)
        return row, lane, down_row

    @pl.when(step == 0)
    def _():
        up_grad_ref[...] = jnp.zeros_like(up_grad_ref)
        down_grad_ref[...] = jnp.zeros_like(down_grad_ref)
        norm_grad_ref[...] = jnp.zeros_like(norm_grad_ref)
        for number, ref in enumerate(slab_refs):
            side, apart = divmod(number, INNER)
            for outer in range(OUTER):
                row, lane, down_row = places(apart, outer)
                up_ref[side, pl.ds(row, 48), pl.ds(lane, D)] = ref[outer, 0]
                down_ref[side, pl.ds(down_row, 48), :] = ref[outer, 1]

    middle = middle_ref[...]
    normed, inverse_std = normalize(middle)
    rows = (normed * norm_ref[2:3, :] + norm_ref[3:4, :]).astype(BF)
    cot = cot_ref[...]
    total = middle
    back = None
    for side in range(2):
        up, down = up_ref[side], down_ref[side]
        pre = nn(rows, up)
        act_grad = nt(cot, down)
        cumulative = 0.5 * (1.0 + lax.erf(pre * ROOT_HALF))
        density = jnp.exp(-0.5 * pre * pre) * DENSITY_FACTOR
        act = (pre * cumulative).astype(BF)
        pre_grad = (act_grad * (cumulative + pre * density)).astype(BF)
        total = total + nn(act, down)
        term = nt(pre_grad, up)
        back = term if back is None else back + term
        down_grad_ref[side] += tn(act, cot)
        up_grad_ref[side] += tn(rows, pre_grad)
    out_ref[...] = total
    grad_in, norm_part = norm_backward(back, normed, inverse_std, norm_ref[2:3, :])
    norm_grad_ref[...] += norm_part
    grad_ref[...] = cot.astype(F32) + grad_in

    @pl.when(step == pl.num_programs(0) - 1)
    def _():
        for apart in range(INNER):
            for outer in range(OUTER):
                row, lane, down_row = places(apart, outer)
                for side, ref in enumerate((own_ref, sent_ref)):
                    up = up_grad_ref[side, pl.ds(row, 48), pl.ds(lane, D)]
                    down = down_grad_ref[side, pl.ds(down_row, 48), :]
                    ref[apart, outer, 0] = up.astype(BF)
                    ref[apart, outer, 1] = down.astype(BF)


def mlp(place, middle, cotangent, norm_params, slabs):
    rows = middle.shape[0]
    slab = pl.BlockSpec((OUTER, 2, 48, D), lambda i: (0, 0, 0, 0))
    grads = (INNER, OUTER, 2, 48, D)
    grad = pl.BlockSpec(grads, lambda i: (0, 0, 0, 0, 0))
    tile = pl.BlockSpec((TILE, D), lambda i: (i, 0))
    return pl.pallas_call(
        mlp_kernel,
        grid=(rows // TILE,),
        in_specs=[
            pl.BlockSpec(memory_space=pltpu.SMEM),
            tile,
            tile,
            pl.BlockSpec((4, D), lambda i: (0, 0)),
            *[slab] * 2 * INNER,
        ],
        out_specs=[tile, tile, pl.BlockSpec((2, D), lambda i: (0, 0)), grad, grad],
        out_shape=[
            jax.ShapeDtypeStruct((rows, D), F32),
            pltpu.HBM((rows, D), F32),
            jax.ShapeDtypeStruct((2, D), F32),
            *[jax.ShapeDtypeStruct(grads, BF)] * 2,
        ],
        scratch_shapes=[
            pltpu.VMEM((2, D, MLP // 2), BF),
            pltpu.VMEM((2, MLP // 2, D), BF),
            pltpu.VMEM((2, D, MLP // 2), F32),
            pltpu.VMEM((2, MLP // 2, D), F32),
        ],
        compiler_params=pltpu.CompilerParams(vmem_limit_bytes=VMEM_LIMIT),
        cost_estimate=pl.CostEstimate(
            flops=12 * rows * D * MLP, bytes_accessed=20 << 20, transcendentals=2 * rows * MLP
        ),
        name="mlp",
    )(place, in_hbm(middle), in_hbm(cotangent), in_hbm(norm_params), *slabs)


def attn_backward_kernel(
    place_ref, own_mask_ref, other_mask_ref, x_ref, grad_ref, prob_ref, qkv_ref, out_ref,
    norm_ref, later_norm_ref, wqkv_ref, wo_ref,
    dqkv_ref, own_grad_ref, sent_grad_ref, norm_grad_ref,
    cross_ref, column_ref, wo_grad_ref,
):
    step = pl.program_id(0)

    @pl.when(step == 0)
    def _():
        cross_ref[...] = jnp.zeros_like(cross_ref)
        column_ref[...] = jnp.zeros_like(column_ref)
        wo_grad_ref[...] = jnp.zeros_like(wo_grad_ref)

    normed, _ = normalize(x_ref[...].astype(F32))
    low_grad = grad_ref[...].astype(BF)
    head_out = out_ref[...]
    wo_grad_ref[...] += tn(head_out, low_grad)
    whole_grad = nt(low_grad, wo_ref[...]).astype(BF)
    first, second = lane_halves()
    first_wide, second_wide = first.astype(F32), second.astype(F32)
    tasks = [(image, pair) for image in range(IMAGES) for pair in range(PAIRS)]

    def places(task):
        image, pair = task
        here = slice(S * image, S * image + S)
        return here, *(slice(D * t + PAIR * pair, D * t + PAIR * (pair + 1)) for t in range(3))

    def get_pair_grad(task):
        here, lanes, _, _ = places(task)
        mask = mask_lanes(place_ref, own_mask_ref, other_mask_ref, IMAGES * step + task[0], task[1])
        grad = whole_grad[here, lanes] * mask.astype(BF)
        dots = grad.astype(F32) * head_out[here, lanes].astype(F32)
        first_dot = jnp.sum(dots * first_wide, axis=-1, keepdims=True)
        second_dot = jnp.sum(dots * second_wide, axis=-1, keepdims=True)
        return stacked(grad, first, second), jnp.concatenate([first_dot, second_dot], axis=0)

    pair_grads = [get_pair_grad(task) for task in tasks]
    prob_grads = [
        nt(pair_grad[0], qkv_ref[places(task)[0], places(task)[3]])
        for task, pair_grad in zip(tasks, pair_grads)
    ]
    score_grads = [
        (prob_ref[task].astype(F32) * (prob_grad - pair_grad[1])).astype(BF)
        for task, prob_grad, pair_grad in zip(tasks, prob_grads, pair_grads)
    ]
    for task, score_grad, (pair_grad, _) in zip(tasks, score_grads, pair_grads):
        here, query_lanes, key_lanes, value_lanes = places(task)
        keys = qkv_ref[here, key_lanes]
        queries = stacked(qkv_ref[here, query_lanes], first, second)
        query_grad = nn(score_grad[:S], keys * first) + nn(score_grad[S:], keys * second)
        key_grad = nn(jnp.transpose(queries), score_grad)
        value_grad = nn(jnp.transpose(pair_grad), prob_ref[task])
        dqkv_ref[here, query_lanes] = query_grad.astype(BF)
        dqkv_ref[here, key_lanes] = jnp.transpose(key_grad).astype(BF)
        dqkv_ref[here, value_lanes] = jnp.transpose(value_grad).astype(BF)
    dqkv = dqkv_ref[...]
    cross_ref[...] += tn(normed.astype(BF), dqkv)
    column_ref[...] += jnp.sum(dqkv.astype(F32), axis=0, keepdims=True)

    @pl.when(step == pl.num_programs(0) - 1)
    def _():
        wqkv = wqkv_ref[...]
        products = wqkv.astype(F32) * cross_ref[...]
        gain_grad = jnp.sum(products, axis=1, keepdims=True)
        gain_grad = jnp.transpose(jnp.broadcast_to(gain_grad, (D, 128)))
        columns = column_ref[...]
        shift_grad = nt(jnp.concatenate(split(jnp.broadcast_to(columns, (8, 3 * D)))), wqkv)
        norm_grad_ref[0:1, :] = gain_grad[0:1]
        norm_grad_ref[1:2, :] = shift_grad[0:1] + shift_grad[8:9]
        norm_grad_ref[2:4, :] = later_norm_ref[...]
        gain = jnp.transpose(jnp.broadcast_to(norm_ref[0:1, :], (128, D)))[:, :1]
        shift = jnp.transpose(jnp.broadcast_to(norm_ref[1:2, :], (128, D)))[:, :1]
        cross_ref[...] = cross_ref[...] * gain + shift * columns
        for side, slab_grads in enumerate((own_grad_ref, sent_grad_ref)):
            for slab in range(12):
                pieces = []
                for unit in (2 * slab, 2 * slab + 1):
                    row, part = divmod(unit, 3)
                    piece = cross_ref[48 * row : 48 * row + 48, D * part : D * part + D]
                    piece = piece[:, HALF * side : HALF * side + HALF]
                    pieces.append(piece * 0.125 if part == 0 else piece)
                slab_grads[slab_at(slab)] = jnp.concatenate(pieces, axis=1).astype(BF)
            for row in range(HALF // 48):
                start = HALF * side + 48 * row
                slab_grads[slab_at(12 + row)] = wo_grad_ref[start : start + 48, :].astype(BF)
        sent_grad_ref[SLABS, :NORM_ROWS] = jnp.concatenate(split(norm_grad_ref[...]), axis=0)
        sent_grad_ref[SLABS, NORM_ROWS:] = jnp.zeros((48 - NORM_ROWS, D), BF)


def attn_backward(
    place, own_mask, other_mask, tokens, grad, prob, qkv, out, norm_params, later_norms, wqkv, wo
):
    rows = tokens.shape[0]
    tile = pl.BlockSpec((TILE, D), lambda i: (i, 0))
    smem = pl.BlockSpec(memory_space=pltpu.SMEM)
    return pl.pallas_call(
        attn_backward_kernel,
        grid=(rows // TILE,),
        in_specs=[
            smem,
            smem,
            smem,
            tile,
            tile,
            pl.BlockSpec((IMAGES, PAIRS, 2 * S, S), lambda i: (i, 0, 0, 0)),
            pl.BlockSpec((TILE, 3 * D), lambda i: (i, 0)),
            tile,
            pl.BlockSpec((4, D), lambda i: (0, 0)),
            pl.BlockSpec((2, D), lambda i: (0, 0)),
            pl.BlockSpec((D, 3 * D), lambda i: (0, 0)),
            pl.BlockSpec((D, D), lambda i: (0, 0)),
        ],
        out_specs=[
            pl.BlockSpec((TILE, 3 * D), lambda i: (i, 0)),
            pl.BlockSpec((SLABS, 48, D), lambda i: (0, 0, 0)),
            pl.BlockSpec((SLABS + 1, 48, D), lambda i: (0, 0, 0)),
            pl.BlockSpec((4, D), lambda i: (0, 0)),
        ],
        out_shape=[
            pltpu.HBM((rows, 3 * D), BF),
            jax.ShapeDtypeStruct((SLABS, 48, D), BF),
            jax.ShapeDtypeStruct((SLABS + 1, 48, D), BF),
            jax.ShapeDtypeStruct((4, D), F32),
        ],
        scratch_shapes=[
            pltpu.VMEM((D, 3 * D), F32),
            pltpu.VMEM((1, 3 * D), F32),
            pltpu.VMEM((D, D), F32),
        ],
        compiler_params=pltpu.CompilerParams(vmem_limit_bytes=VMEM_LIMIT),
        cost_estimate=pl.CostEstimate(
            flops=rows * D * (10 * D + 32 * S), bytes_accessed=20 << 20, transcendentals=0
        ),
        name="attn_backward",
    )(
        place, own_mask, other_mask,
        *map(in_hbm, (tokens, grad, prob, qkv, out, norm_params, later_norms, wqkv, wo)),
    )


def input_grad_kernel(x_ref, grad_ref, dqkv_ref, norm_ref, wqkv_ref, out_ref):
    normed, inverse_std = normalize(x_ref[...].astype(F32))
    back = nt(dqkv_ref[...], wqkv_ref[...]) * norm_ref[0:1, :]
    mean_first = jnp.mean(back, axis=-1, keepdims=True)
    mean_second = jnp.mean(back * normed, axis=-1, keepdims=True)
    out_ref[...] = grad_ref[...] + inverse_std * (back - mean_first - normed * mean_second)


def input_gradient(tokens, grad, dqkv, norm_params, wqkv):
    rows = tokens.shape[0]
    tile = pl.BlockSpec((TILE, D), lambda i: (i, 0))
    return pl.pallas_call(
        input_grad_kernel,
        grid=(rows // TILE,),
        in_specs=[
            tile,
            tile,
            pl.BlockSpec((TILE, 3 * D), lambda i: (i, 0)),
            pl.BlockSpec((4, D), lambda i: (0, 0)),
            pl.BlockSpec((D, 3 * D), lambda i: (0, 0)),
        ],
        out_specs=tile,
        out_shape=jax.ShapeDtypeStruct((rows, D), F32),
        compiler_params=pltpu.CompilerParams(vmem_limit_bytes=VMEM_LIMIT),
        cost_estimate=pl.CostEstimate(
            flops=rows * D * 6 * D, bytes_accessed=10 << 20, transcendentals=0
        ),
        name="input_gradient",
    )(*map(in_hbm, (tokens, grad, dqkv, norm_params, wqkv)))


def pack_kernel(weight_ref, early_ref, late_ref):
    groups, count, _, _ = weight_ref.shape
    for group in range(groups):
        blocks = [weight_ref[group, block] for block in range(count)]
        slab = jnp.concatenate(blocks, axis=1).astype(BF)
        for copy in range(early_ref.shape[0]):
            if group == 0:
                early_ref[copy] = slab
            else:
                late_ref[copy, group - 1] = slab


def pack(weights, number):
    groups, count, edge, _ = weights.shape
    return pl.pallas_call(
        pack_kernel,
        out_shape=[
            jax.ShapeDtypeStruct((number, edge, count * edge), BF),
            jax.ShapeDtypeStruct((number, groups - 1, edge, count * edge), BF),
        ],
        compiler_params=pltpu.CompilerParams(vmem_limit_bytes=SMALL_VMEM),
        name="pack",
    )(in_hbm(weights))


def add_kernel(own_ref, received_ref, *out_refs):
    for apart, out_ref in enumerate(out_refs):
        total = own_ref[apart].astype(F32) + received_ref[apart].astype(F32)
        out_ref[...] = total.astype(BF)


def add_late(own, received):
    return pl.pallas_call(
        add_kernel,
        out_shape=[jax.ShapeDtypeStruct(own.shape[1:], BF)] * own.shape[0],
        compiler_params=pltpu.CompilerParams(vmem_limit_bytes=SMALL_VMEM),
        name="add_late",
    )(own, received)


def sum_kernel(*refs):
    *in_refs, out_ref = refs
    total = in_refs[0][...].astype(F32)
    for ref in in_refs[1:]:
        total = total + ref[...].astype(F32)
    out_ref[...] = total.astype(BF)


def sum_late(pieces):
    return pl.pallas_call(
        sum_kernel,
        out_shape=jax.ShapeDtypeStruct(pieces[0].shape, BF),
        compiler_params=pltpu.CompilerParams(vmem_limit_bytes=SMALL_VMEM),
        name="sum_late",
    )(*pieces)


def combine_kernel(place_ref, own_ref, received_ref, norm_ref, *out_refs):
    norms = received_ref[SLABS, :NORM_ROWS].astype(F32)
    norms = norm_ref[...] + (norms[:4] + norms[4:])
    rows = jnp.concatenate(split(norms), axis=0)
    for apart, out_ref in enumerate(out_refs):
        start = OUTER * (place_ref[1] ^ apart)
        for outer in range(OUTER):
            total = own_ref[start + outer].astype(F32) + received_ref[start + outer].astype(F32)
            out_ref[48 * outer : 48 * outer + 48, :] = total.astype(BF)
        out_ref[48 * OUTER :, :] = rows


def combine(place, own, received, norms):
    vmem = pl.BlockSpec(memory_space=pltpu.VMEM)
    shape = jax.ShapeDtypeStruct((48 * OUTER + NORM_ROWS, D), BF)
    return pl.pallas_call(
        combine_kernel,
        in_specs=[pl.BlockSpec(memory_space=pltpu.SMEM), vmem, vmem, vmem],
        out_shape=[shape] * INNER,
        compiler_params=pltpu.CompilerParams(vmem_limit_bytes=SMALL_VMEM),
        name="combine",
    )(place, own, received, norms)


def join_kernel(*refs):
    *early_refs, out_ref = refs
    total = early_refs[0][...].astype(F32)
    for ref in early_refs[1:]:
        total = total + ref[...].astype(F32)
    norms = total[48 * OUTER : 48 * OUTER + 4] + total[48 * OUTER + 4 :]
    for outer in range(OUTER):
        out_ref[outer, :48] = total[48 * outer : 48 * outer + 48].astype(BF)
        out_ref[outer, 48:] = jnp.concatenate(split(norms), axis=0)


def join(early):
    return pl.pallas_call(
        join_kernel,
        out_shape=jax.ShapeDtypeStruct((OUTER, 48 + NORM_ROWS, D), BF),
        compiler_params=pltpu.CompilerParams(vmem_limit_bytes=SMALL_VMEM),
        name="join",
    )(*early)


def split(values):
    high = values.astype(BF)
    return high, (values - high.astype(F32)).astype(BF)


def stack(*pieces):
    return jnp.concatenate(pieces, axis=0)


def cut_rows(values, number):
    edge = values.shape[0] // number
    return [values[edge * i : edge * i + edge] for i in range(number)]


def product(left, right):
    high, low = left
    right_high, right_low = right
    one, two = cut_rows(nn(stack(high, low), right_high), 2)
    return one + (two + nn(high, right_low))


def two_products(left, middle, right):
    right_high, right_low = right
    both = cut_rows(nn(stack(left[0], middle[0], left[1], middle[1]), right_high), 4)
    high = cut_rows(nn(stack(left[0], middle[0]), right_low), 2)
    return both[0] + (both[2] + high[0]), both[1] + (both[3] + high[1])


def update_norms(scale, total, param_ref, state_ref, grad_ref, new_state_ref, new_ref):
    grads = total * scale
    state = 0.5 * state_ref[...] + 0.5 * grads * grads
    grad_ref[...] = grads
    new_state_ref[...] = state
    new_ref[...] = param_ref[...] - 0.2 * grads / jnp.sqrt(state)


def shampoo_kernel(scale, with_norms, received_ref, weight_ref, left_ref, right_ref, *refs):
    if with_norms:
        norm_ins, norm_outs, refs = refs[:2], refs[-5:-2], refs[:-5] + refs[-2:]
    out_grad_ref, left_new_ref, right_new_ref, new_weight_ref, root_ref, power_ref = refs[-6:]
    groups, count, edge = weight_ref.shape[:3]

    received = received_ref[0].astype(F32)
    for number in range(1, received_ref.shape[0]):
        received = received + received_ref[number].astype(F32)
    if with_norms:
        norms = received[0, edge:]
        update_norms(scale, norms[:4] + norms[4:], *norm_ins, *norm_outs)
    pack = min(PACK, count)
    width = pack * edge
    places = [(g, pack * n) for g in range(groups) for n in range(count // pack)]
    packs = len(places)

    def block_of(shape, dim):
        return lax.broadcasted_iota(jnp.int32, shape, dim) // edge

    row = lax.broadcasted_iota(jnp.int32, (edge, width), 0)
    lane = lax.broadcasted_iota(jnp.int32, (edge, width), 1)
    identity = (lane % edge == row).astype(F32)
    same = (block_of((width, width), 0) == block_of((width, width), 1)).astype(BF)
    lane_block = block_of((1, width), 1)

    def spread(pieces):
        return tuple(stack(*[piece] * pack) * same for piece in pieces)

    def cut(packed, index):
        return packed[:, edge * index : edge * index + edge]

    def beside(ref, place):
        return jnp.concatenate([ref[place[0], place[1] + i] for i in range(pack)], axis=1)

    grads, parts = [], []
    for group, start in places:
        grad = received[group, :edge, edge * start : edge * start + width] * scale
        blocks = [cut(grad, index) for index in range(pack)]
        for index in range(pack):
            out_grad_ref[group, start + index] = blocks[index]
        grad_t = jnp.concatenate([jnp.transpose(block) for block in blocks], axis=1)
        one, two = split(grad), split(grad_t)
        one_diagonal, two_diagonal = spread(one), spread(two)
        grads.append(one_diagonal)
        parts.append((left_ref, left_new_ref, one, two_diagonal))
        parts.append((right_ref, right_new_ref, two, one_diagonal))
    grams = [product(left, right) for _, _, left, right in parts]
    for slot, (old_ref, new_ref, _, _) in enumerate(parts):
        group, start = places[slot // 2]
        new = 0.5 * beside(old_ref, places[slot // 2]) + 0.5 * grams[slot]
        for index in range(pack):
            new_ref[group, start + index] = cut(new, index)
        columns = jnp.sum(new * new, axis=0, keepdims=True)
        squares = jnp.zeros((1, width), F32)
        for index in range(pack):
            inside = lane_block == index
            part = jnp.sum(jnp.where(inside, columns, 0.0), axis=1, keepdims=True)
            squares = jnp.where(inside, part, squares)
        factor = 2.5 / jnp.sqrt(squares)
        root_ref[slot] = jnp.broadcast_to(jnp.sqrt(jnp.sqrt(factor)), (edge, width))
        power_ref[slot] = factor * new
    slots = range(2 * packs)

    def advance(first):
        powers = [power_ref[slot] for slot in slots]
        middles = [split((5.0 * identity - power) * 0.25) for power in powers]
        rights = [spread(middle) for middle in middles]
        powers = [split(power) for power in powers]
        if first:
            squares = [product(middles[s], rights[s]) for s in slots]
            for slot in slots:
                root_ref[slot] *= (5.0 * identity - power_ref[slot]) * 0.25
        else:
            roots = [split(root_ref[slot]) for slot in slots]
            both = [two_products(roots[s], middles[s], rights[s]) for s in slots]
            squares = [pair[1] for pair in both]
            for slot in slots:
                root_ref[slot] = both[slot][0]
        rights = [spread(split(square)) for square in squares]
        powers = [split(product(powers[s], rights[s])) for s in slots]
        for slot in slots:
            power_ref[slot] = product(powers[slot], rights[slot])

    advance(True)
    lax.fori_loop(0, ITERS - 2, lambda _, carry: advance(False) or carry, 0)
    rights = [spread(split((5.0 * identity - power_ref[slot]) * 0.25)) for slot in slots]
    for slot in slots:
        root_ref[slot] = product(split(root_ref[slot]), rights[slot])
    steps = [product(split(root_ref[2 * n]), grads[n]) for n in range(packs)]
    rights = [spread(split(root_ref[2 * n + 1])) for n in range(packs)]
    steps = [product(split(steps[n]), rights[n]) for n in range(packs)]
    for number, (group, start) in enumerate(places):
        for index in range(pack):
            step = 0.25 * cut(steps[number], index)
            new_weight_ref[group, start + index] = weight_ref[group, start + index] - step


def shampoo(received, weights, stat_left, stat_right, scale, first, earlier=(), norms=()):
    groups = received.shape[1]
    _, count, edge, _ = weights.shape
    slots = 2 * groups * count // min(PACK, count)
    width = min(PACK, count) * edge
    block = pl.BlockSpec(
        (pl.Element(groups), pl.Element(count), pl.Element(edge), pl.Element(edge)),
        lambda i: (first, 0, 0, 0),
    )
    shape = jax.ShapeDtypeStruct(weights.shape, F32)
    norm = pl.BlockSpec((4, D), lambda i: (0, 0))
    norm_outs = 3 if norms else 0
    ins = 4 + len(norms)
    return pl.pallas_call(
        lambda *refs: shampoo_kernel(scale, bool(norms), *refs),
        grid=(1,),
        in_specs=[
            pl.BlockSpec(received.shape, lambda i: (0, 0, 0, 0)),
            *[block] * 3,
            *[norm] * len(norms),
            *[pl.BlockSpec(memory_space=pl.ANY)] * len(earlier),
        ],
        out_specs=[block] * 4 + [norm] * norm_outs,
        out_shape=[shape] * 4 + [jax.ShapeDtypeStruct((4, D), F32)] * norm_outs,
        scratch_shapes=[
            pltpu.VMEM((slots, edge, width), F32),
            pltpu.VMEM((slots, edge, width), F32),
        ],
        input_output_aliases={ins + i: i for i in range(len(earlier))},
        compiler_params=pltpu.CompilerParams(vmem_limit_bytes=SHAMPOO_VMEM),
        cost_estimate=pl.CostEstimate(
            flops=groups * (3 << 30), bytes_accessed=4 << 20, transcendentals=0
        ),
        name="shampoo",
    )(received, weights, stat_left, stat_right, *norms, *earlier)


def swap_heads(values):
    return lax.ppermute(values, "head", [(0, 1), (1, 0)])


def to_all(values, axis):
    return lax.all_to_all(values, axis, 0, 0)


def across(values, apart):
    pairs = [(i, i ^ apart) for i in range(INNER)]
    return lax.ppermute(values, "inner", pairs)


def from_all(values):
    return [values] + [across(values, apart) for apart in range(1, INNER)]


def gather_slabs(weights, small):
    early, late = pack(weights, OUTER)
    early = to_all(early, "outer")
    early, late = lax.optimization_barrier((early, late))
    late = to_all(late, "outer")
    early = from_all(early)
    early[-1], late, small = lax.optimization_barrier((early[-1], late, small))
    return early, from_all(late), small


def gather_blocks(local):
    groups, _, edge, _ = local.shape
    blocks = lax.all_gather(local, ("outer", "inner"), axis=1, tiled=True)
    blocks = blocks.reshape(groups, SLABS // INNER, INNER, D // edge, edge, edge)
    slabs = blocks.transpose(2, 1, 0, 4, 3, 5).reshape(SLABS, groups, edge, D)
    return slabs if groups > 1 else slabs[:, 0]


def scatter_blocks(slabs, count, edge):
    groups = slabs.shape[1]
    blocks = slabs.reshape(INNER, SLABS // INNER, groups, edge, D // edge, edge)
    blocks = blocks.transpose(2, 1, 0, 4, 3, 5).reshape(groups, SLABS * (D // edge), edge, edge)
    owned = lax.psum_scatter(blocks, ("outer", "inner"), scatter_dimension=1, tiled=True)
    return owned.transpose(0, 2, 1, 3).reshape(groups, edge, count * edge)


def per_device(
    tokens,
    cotangent,
    token_counts,
    head_mask,
    norm_params,
    norm_state,
    weights,
    stat_left,
    stat_right,
):
    weights, stat_left, stat_right = weights[0], stat_left[0], stat_right[0]
    _, count, edge, _ = weights.shape
    whole_slabs = count * edge == D
    other_mask = swap_heads(head_mask)
    inner = lax.axis_index("inner") if whole_slabs else 0
    place = jnp.concatenate([jnp.stack([lax.axis_index("head"), inner]), token_counts])
    if whole_slabs:
        early, late, (other_mask, place) = gather_slabs(weights, (other_mask, place))
    else:
        local = weights.astype(BF)
        early = jnp.split(gather_blocks(local[:1]), INNER)
        late = jnp.split(gather_blocks(local[1:]), INNER)
    early, late = list(early), list(late)
    masks = (head_mask, other_mask)
    early += [swap_heads(piece) for piece in early]
    prob, qkv, out, middle, wqkv, wo = attn_forward(
        place, *masks, tokens, norm_params, early
    )
    late[1:], middle = lax.optimization_barrier((late[1:], middle))
    late += [swap_heads(piece) for piece in late]
    block_out, middle_grad, norm_two, own_late, sent_late = mlp(
        place, middle, cotangent, norm_params, late
    )
    late_received = swap_heads(sent_late)
    if whole_slabs:
        late_grads = list(add_late(own_late, late_received))
        late_grads, middle_grad = lax.optimization_barrier((late_grads, middle_grad))
        late_grads[1:] = [across(late_grads[apart], apart) for apart in range(1, INNER)]
    dqkv, own_early, sent_early, norm_sums = attn_backward(
        place, *masks, tokens, middle_grad, prob, qkv, out, norm_params, norm_two, wqkv, wo
    )
    if whole_slabs:
        late_grads, sent_early = lax.optimization_barrier((late_grads, sent_early))
    early_received = swap_heads(sent_early)
    devices = lax.axis_size("outer") * lax.axis_size("inner") * lax.axis_size("head")
    scale = 1.0 / math.sqrt(tokens.shape[0] * devices)
    state = (weights, stat_left, stat_right, scale)
    if whole_slabs:
        late_grads = to_all(sum_late(late_grads), "outer")
        early_grads = list(combine(place, own_early, early_received, norm_sums))
        early_grads, dqkv = lax.optimization_barrier((early_grads, dqkv))
        early_grads[1:] = [across(early_grads[apart], apart) for apart in range(1, INNER)]
        input_grad = input_gradient(tokens, middle_grad, dqkv, norm_params, wqkv)
        early_grads, input_grad = lax.optimization_barrier((early_grads, input_grad))
        joined, late_grads = lax.optimization_barrier((join(early_grads), late_grads))
        joined = to_all(joined, "outer")[:, None]
        results = shampoo(late_grads, *state, 1)
        results = shampoo(joined, *state, 0, results, (norm_params, norm_state))
    else:
        input_grad = input_gradient(tokens, middle_grad, dqkv, norm_params, wqkv)
        early_slabs = own_early.astype(F32) + early_received[:SLABS].astype(F32)
        late_slabs = own_late.astype(F32) + late_received.astype(F32)
        late_slabs = late_slabs.reshape(SLABS, 2, edge, D)
        slabs = jnp.concatenate([early_slabs[:, None], late_slabs], axis=1).astype(BF)
        owned = scatter_blocks(slabs, count, edge)
        results = list(shampoo(owned[None], *state, 0))
        norm_grads = lax.psum(norm_sums, ("outer", "inner", "head")) * scale
        state_new = 0.5 * norm_state + 0.5 * norm_grads * norm_grads
        results += [norm_grads, state_new, norm_params - 0.2 * norm_grads / jnp.sqrt(state_new)]
    return (block_out, input_grad, *[result[None] for result in results[:4]], *results[4:])


def solution(mesh):
    shape = (mesh.shape["dp"] // INNER, INNER, mesh.shape["head"])
    split_mesh = Mesh(mesh.devices.reshape(shape), ("outer", "inner", "head"))
    group = ("outer", "inner")
    blocks = P("head", None, group, None, None)
    rows = P(group + ("head",), None)
    return jax.shard_map(
        per_device,
        mesh=split_mesh,
        in_specs=(rows, rows, P(group), P(group, "head"), P(), P(), blocks, blocks, blocks),
        out_specs=(rows, rows, blocks, blocks, blocks, blocks, P(), P(), P()),
        check_vma=False,
    )
```

```python
import math

import jax
import jax.numpy as jnp
from jax import lax
from jax.experimental import pallas as pl
from jax.experimental.pallas import tpu as pltpu
from jax.sharding import Mesh, PartitionSpec as P

D = 384
HEAD_DIM = 64
MLP = 1536
S = 256
ITERS = 8
PAIR = 2 * HEAD_DIM
PAIRS = D // PAIR
HALF = D // 2
SLABS = 16
INNER = 4
OUTER = SLABS // INNER
TILE = 512
INPUT_TILE = 768
IMAGES = TILE // S
NORM_ROWS = 8
PACK = 2
ROOT_HALF = 0.7071067811865476
DENSITY_FACTOR = 0.3989422804014327
BF = jnp.bfloat16
F32 = jnp.float32
VMEM_LIMIT = 40 << 20
SMALL_VMEM = 8 << 20
SHAMPOO_VMEM = 24 << 20


def in_hbm(values):
    return pltpu.with_memory_space_constraint(values, pltpu.HBM)


def nn(left, right):
    return jnp.dot(left, right, preferred_element_type=F32)


def nt(left, right):
    return lax.dot_general(left, right, (((1,), (1,)), ((), ())), preferred_element_type=F32)


def tn(left, right):
    return lax.dot_general(left, right, (((0,), (0,)), ((), ())), preferred_element_type=F32)


def normalize(values):
    centered = values - jnp.mean(values, axis=-1, keepdims=True)
    variance = jnp.mean(centered * centered, axis=-1, keepdims=True)
    inverse_std = lax.rsqrt(variance + 1e-06)
    return centered * inverse_std, inverse_std


def norm_backward(grad_out, normed, inverse_std, gain):
    grad_normed = grad_out * gain
    mean_first = jnp.mean(grad_normed, axis=-1, keepdims=True)
    mean_second = jnp.mean(grad_normed * normed, axis=-1, keepdims=True)
    grad_in = inverse_std * (grad_normed - mean_first - normed * mean_second)
    gain_grad = jnp.sum(grad_out * normed, axis=0, keepdims=True)
    shift_grad = jnp.sum(grad_out, axis=0, keepdims=True)
    return grad_in, jnp.concatenate([gain_grad, shift_grad], axis=0)


def slab_at(owner):
    return (owner % INNER) * OUTER + owner // INNER


def lane_halves():
    lane = lax.broadcasted_iota(jnp.int32, (1, PAIR), 1)
    first = (lane < HEAD_DIM).astype(BF)
    return first, (1 - first).astype(BF)


def stacked(values, first, second):
    return jnp.concatenate([values * first, values * second], axis=0)


def mask_lanes(place_ref, own_ref, other_ref, image, pair):
    image = place_ref[0] * (own_ref.shape[0] // 2) + image
    heads = own_ref.shape[1]
    on = [
        own_ref[image, head] if head < heads else other_ref[image, head - heads]
        for head in (2 * pair, 2 * pair + 1)
    ]
    lane = lax.broadcasted_iota(jnp.int32, (1, PAIR), 1)
    return jnp.where(lane < HEAD_DIM, on[0], on[1]).astype(F32)


def attn_forward_kernel(
    place_ref, own_mask_ref, other_mask_ref, x_ref, norm_ref, *refs
):
    slab_refs, refs = refs[: 2 * INNER], refs[2 * INNER :]
    prob_ref, qkv_ref, out_ref, middle_ref, wqkv_ref, wo_ref, held_ref = refs
    step = pl.program_id(0)

    @pl.when(step == 0)
    def _():
        for number, ref in enumerate(slab_refs):
            side, apart = divmod(number, INNER)
            held_ref[side, place_ref[1] ^ apart] = ref[...]

        def slab_of(side, owner):
            return held_ref[side, owner % INNER, owner // INNER]

        for row in range(D // 48):
            for part in range(3):
                pieces = []
                for number in range(2):
                    slab, side = divmod(3 * row + part, 2)
                    piece = slab_of(number, slab)[:, side * HALF : (side + 1) * HALF]
                    pieces.append(piece)
                joined = jnp.concatenate(pieces, axis=1)
                if part == 0:
                    joined = joined * 0.125
                wqkv_ref[48 * row : 48 * row + 48, D * part : D * part + D] = joined
        for side in range(2):
            for row in range(HALF // 48):
                start = side * HALF + 48 * row
                wo_ref[start : start + 48, :] = slab_of(side, 12 + row)

    x = x_ref[...].astype(F32)
    normed, _ = normalize(x)
    rows = (normed * norm_ref[0:1, :] + norm_ref[1:2, :]).astype(BF)
    qkv_ref[...] = nn(rows, wqkv_ref[...]).astype(BF)
    first, second = lane_halves()
    column = lax.broadcasted_iota(jnp.int32, (1, S), 1)
    tasks = [(image, pair) for image in range(IMAGES) for pair in range(PAIRS)]

    def places(task):
        image, pair = task
        here = slice(S * image, S * image + S)
        return here, *(slice(D * t + PAIR * pair, D * t + PAIR * (pair + 1)) for t in range(3))

    def get_scores(task):
        here, query_lanes, key_lanes, _ = places(task)
        return nt(stacked(qkv_ref[here, query_lanes], first, second), qkv_ref[here, key_lanes])

    def get_prob(task, scores):
        image = place_ref[0] * (own_mask_ref.shape[0] // 2) + IMAGES * step + task[0]
        scores = jnp.where(column < place_ref[2 + image], scores, -1e30)
        top = jnp.max(scores, axis=-1, keepdims=True)
        exp_scores = jnp.exp(scores - top)
        total = jnp.sum(exp_scores, axis=-1, keepdims=True)
        prob = (exp_scores * (1.0 / total)).astype(BF)
        prob_ref[task] = prob
        return prob

    all_scores = [get_scores(task) for task in tasks]
    probs = [get_prob(task, scores) for task, scores in zip(tasks, all_scores)]
    for task, prob in zip(tasks, probs):
        here, lanes, _, value_lanes = places(task)
        values = qkv_ref[here, value_lanes]
        head_out = nn(prob[:S], values * first) + nn(prob[S:], values * second)
        mask = mask_lanes(place_ref, own_mask_ref, other_mask_ref, IMAGES * step + task[0], task[1])
        out_ref[here, lanes] = (head_out * mask).astype(BF)
    middle_ref[...] = x + nn(out_ref[...], wo_ref[...])


def attn_forward(place, own_mask, other_mask, tokens, norm_params, slabs):
    rows = tokens.shape[0]
    images = rows // S
    tile = pl.BlockSpec((TILE, D), lambda i: (i, 0))
    slab = pl.BlockSpec((OUTER, 48, D), lambda i: (0, 0, 0))
    smem = pl.BlockSpec(memory_space=pltpu.SMEM)
    return pl.pallas_call(
        attn_forward_kernel,
        grid=(rows // TILE,),
        in_specs=[smem] * 3 + [tile, pl.BlockSpec((4, D), lambda i: (0, 0))] + [slab] * 2 * INNER,
        out_specs=[
            pl.BlockSpec((IMAGES, PAIRS, 2 * S, S), lambda i: (i, 0, 0, 0)),
            pl.BlockSpec((TILE, 3 * D), lambda i: (i, 0)),
            tile,
            tile,
            pl.BlockSpec((D, 3 * D), lambda i: (0, 0)),
            pl.BlockSpec((D, D), lambda i: (0, 0)),
        ],
        out_shape=[
            pltpu.HBM((images, PAIRS, 2 * S, S), BF),
            pltpu.HBM((rows, 3 * D), BF),
            pltpu.HBM((rows, D), BF),
            pltpu.HBM((rows, D), F32),
            pltpu.HBM((D, 3 * D), BF),
            pltpu.HBM((D, D), BF),
        ],
        scratch_shapes=[pltpu.VMEM((2, INNER, OUTER, 48, D), BF)],
        compiler_params=pltpu.CompilerParams(vmem_limit_bytes=VMEM_LIMIT),
        cost_estimate=pl.CostEstimate(
            flops=rows * D * (8 * D + 16 * S), bytes_accessed=16 << 20, transcendentals=rows * 6 * S
        ),
        name="attn_forward",
    )(place, own_mask, other_mask, in_hbm(tokens), in_hbm(norm_params), *slabs)


def mlp_kernel(place_ref, middle_ref, cot_ref, norm_ref, *refs):
    slab_refs, refs = refs[: 2 * INNER], refs[2 * INNER :]
    out_ref, grad_ref, norm_grad_ref, *refs = refs
    own_refs, sent_refs, refs = refs[:2], refs[2:4], refs[4:]
    up_ref, down_ref, up_grad_ref, down_grad_ref = refs
    step = pl.program_id(0)
    half = MLP // 2

    def places(apart, outer):
        inner = place_ref[1] ^ apart
        row = pl.multiple_of(48 * (2 * outer + inner // 2), 16)
        lane = pl.multiple_of(D * (inner % 2), 128)
        down_row = pl.multiple_of(48 * (INNER * outer + inner), 16)
        return row, lane, down_row

    @pl.when(step == 0)
    def _():
        up_grad_ref[...] = jnp.zeros_like(up_grad_ref)
        down_grad_ref[...] = jnp.zeros_like(down_grad_ref)
        norm_grad_ref[...] = jnp.zeros_like(norm_grad_ref)
        for number, ref in enumerate(slab_refs):
            side, apart = divmod(number, INNER)
            for outer in range(OUTER):
                row, lane, down_row = places(apart, outer)
                up_ref[side, pl.ds(row, 48), pl.ds(lane, D)] = ref[outer, 0]
                down_ref[side, pl.ds(down_row, 48), :] = ref[outer, 1]

    middle = middle_ref[...]
    normed, inverse_std = normalize(middle)
    rows = (normed * norm_ref[2:3, :] + norm_ref[3:4, :]).astype(BF)
    cot = cot_ref[...]
    total = middle
    back = None
    for side in range(2):
        up, down = up_ref[side], down_ref[side]
        pre = nn(rows, up)
        act_grad = nt(cot, down)
        cumulative = 0.5 * (1.0 + lax.erf(pre * ROOT_HALF))
        density = jnp.exp(-0.5 * pre * pre) * DENSITY_FACTOR
        act = (pre * cumulative).astype(BF)
        pre_grad = (act_grad * (cumulative + pre * density)).astype(BF)
        total = total + nn(act, down)
        term = nt(pre_grad, up)
        back = term if back is None else back + term
        down_grad_ref[side] += tn(act, cot)
        up_grad_ref[side] += tn(rows, pre_grad)
    out_ref[...] = total
    grad_in, norm_part = norm_backward(back, normed, inverse_std, norm_ref[2:3, :])
    norm_grad_ref[...] += norm_part
    grad_ref[...] = cot.astype(F32) + grad_in

    @pl.when(step == pl.num_programs(0) - 1)
    def _():
        for apart in range(INNER):
            for outer in range(OUTER):
                row, lane, down_row = places(apart, outer)
                for side, halves in enumerate((own_refs, sent_refs)):
                    ref = halves[apart // 2]
                    up = up_grad_ref[side, pl.ds(row, 48), pl.ds(lane, D)]
                    down = down_grad_ref[side, pl.ds(down_row, 48), :]
                    ref[apart % 2, outer, 0] = up.astype(BF)
                    ref[apart % 2, outer, 1] = down.astype(BF)


def mlp(place, middle, cotangent, norm_params, slabs):
    rows = middle.shape[0]
    slab = pl.BlockSpec((OUTER, 2, 48, D), lambda i: (0, 0, 0, 0))
    grads = (INNER // 2, OUTER, 2, 48, D)
    grad = pl.BlockSpec(grads, lambda i: (0, 0, 0, 0, 0))
    tile = pl.BlockSpec((TILE, D), lambda i: (i, 0))
    return pl.pallas_call(
        mlp_kernel,
        grid=(rows // TILE,),
        in_specs=[
            pl.BlockSpec(memory_space=pltpu.SMEM),
            tile,
            tile,
            pl.BlockSpec((4, D), lambda i: (0, 0)),
            *[slab] * 2 * INNER,
        ],
        out_specs=[tile, tile, pl.BlockSpec((2, D), lambda i: (0, 0)), *[grad] * 4],
        out_shape=[
            jax.ShapeDtypeStruct((rows, D), F32),
            pltpu.HBM((rows, D), F32),
            jax.ShapeDtypeStruct((2, D), F32),
            *[jax.ShapeDtypeStruct(grads, BF)] * 4,
        ],
        scratch_shapes=[
            pltpu.VMEM((2, D, MLP // 2), BF),
            pltpu.VMEM((2, MLP // 2, D), BF),
            pltpu.VMEM((2, D, MLP // 2), F32),
            pltpu.VMEM((2, MLP // 2, D), F32),
        ],
        compiler_params=pltpu.CompilerParams(vmem_limit_bytes=VMEM_LIMIT),
        cost_estimate=pl.CostEstimate(
            flops=12 * rows * D * MLP, bytes_accessed=20 << 20, transcendentals=2 * rows * MLP
        ),
        name="mlp",
    )(place, in_hbm(middle), in_hbm(cotangent), in_hbm(norm_params), *slabs)


def attn_backward_kernel(
    place_ref, own_mask_ref, other_mask_ref, x_ref, grad_ref, prob_ref, qkv_ref, out_ref,
    norm_ref, later_norm_ref, wqkv_ref, wo_ref,
    dqkv_ref, own_grad_ref, sent_grad_ref, norm_grad_ref,
    cross_ref, column_ref, wo_grad_ref,
):
    step = pl.program_id(0)

    @pl.when(step == 0)
    def _():
        cross_ref[...] = jnp.zeros_like(cross_ref)
        column_ref[...] = jnp.zeros_like(column_ref)
        wo_grad_ref[...] = jnp.zeros_like(wo_grad_ref)

    normed, _ = normalize(x_ref[...].astype(F32))
    low_grad = grad_ref[...].astype(BF)
    head_out = out_ref[...]
    wo_grad_ref[...] += tn(head_out, low_grad)
    whole_grad = nt(low_grad, wo_ref[...]).astype(BF)
    first, second = lane_halves()
    first_wide, second_wide = first.astype(F32), second.astype(F32)
    tasks = [(image, pair) for image in range(IMAGES) for pair in range(PAIRS)]

    def places(task):
        image, pair = task
        here = slice(S * image, S * image + S)
        return here, *(slice(D * t + PAIR * pair, D * t + PAIR * (pair + 1)) for t in range(3))

    def get_pair_grad(task):
        here, lanes, _, _ = places(task)
        mask = mask_lanes(place_ref, own_mask_ref, other_mask_ref, IMAGES * step + task[0], task[1])
        grad = whole_grad[here, lanes] * mask.astype(BF)
        dots = grad.astype(F32) * head_out[here, lanes].astype(F32)
        first_dot = jnp.sum(dots * first_wide, axis=-1, keepdims=True)
        second_dot = jnp.sum(dots * second_wide, axis=-1, keepdims=True)
        return stacked(grad, first, second), jnp.concatenate([first_dot, second_dot], axis=0)

    pair_grads = [get_pair_grad(task) for task in tasks]
    prob_grads = [
        nt(pair_grad[0], qkv_ref[places(task)[0], places(task)[3]])
        for task, pair_grad in zip(tasks, pair_grads)
    ]
    score_grads = [
        (prob_ref[task].astype(F32) * (prob_grad - pair_grad[1])).astype(BF)
        for task, prob_grad, pair_grad in zip(tasks, prob_grads, pair_grads)
    ]
    for task, score_grad, (pair_grad, _) in zip(tasks, score_grads, pair_grads):
        here, query_lanes, key_lanes, value_lanes = places(task)
        keys = qkv_ref[here, key_lanes]
        queries = stacked(qkv_ref[here, query_lanes], first, second)
        query_grad = nn(score_grad[:S], keys * first) + nn(score_grad[S:], keys * second)
        key_grad = nn(jnp.transpose(queries), score_grad)
        value_grad = nn(jnp.transpose(pair_grad), prob_ref[task])
        dqkv_ref[here, query_lanes] = query_grad.astype(BF)
        dqkv_ref[here, key_lanes] = jnp.transpose(key_grad).astype(BF)
        dqkv_ref[here, value_lanes] = jnp.transpose(value_grad).astype(BF)
    dqkv = dqkv_ref[...]
    cross_ref[...] += tn(normed.astype(BF), dqkv)
    column_ref[...] += jnp.sum(dqkv.astype(F32), axis=0, keepdims=True)

    @pl.when(step == pl.num_programs(0) - 1)
    def _():
        wqkv = wqkv_ref[...]
        products = wqkv.astype(F32) * cross_ref[...]
        gain_grad = jnp.sum(products, axis=1, keepdims=True)
        gain_grad = jnp.transpose(jnp.broadcast_to(gain_grad, (D, 128)))
        columns = column_ref[...]
        shift_grad = nt(jnp.concatenate(split(jnp.broadcast_to(columns, (8, 3 * D)))), wqkv)
        norm_grad_ref[0:1, :] = gain_grad[0:1]
        norm_grad_ref[1:2, :] = shift_grad[0:1] + shift_grad[8:9]
        norm_grad_ref[2:4, :] = later_norm_ref[...]
        gain = jnp.transpose(jnp.broadcast_to(norm_ref[0:1, :], (128, D)))[:, :1]
        shift = jnp.transpose(jnp.broadcast_to(norm_ref[1:2, :], (128, D)))[:, :1]
        cross_ref[...] = cross_ref[...] * gain + shift * columns
        for side, slab_grads in enumerate((own_grad_ref, sent_grad_ref)):
            for slab in range(12):
                pieces = []
                for unit in (2 * slab, 2 * slab + 1):
                    row, part = divmod(unit, 3)
                    piece = cross_ref[48 * row : 48 * row + 48, D * part : D * part + D]
                    piece = piece[:, HALF * side : HALF * side + HALF]
                    pieces.append(piece * 0.125 if part == 0 else piece)
                slab_grads[slab_at(slab)] = jnp.concatenate(pieces, axis=1).astype(BF)
            for row in range(HALF // 48):
                start = HALF * side + 48 * row
                slab_grads[slab_at(12 + row)] = wo_grad_ref[start : start + 48, :].astype(BF)
        sent_grad_ref[SLABS, :NORM_ROWS] = jnp.concatenate(split(norm_grad_ref[...]), axis=0)
        sent_grad_ref[SLABS, NORM_ROWS:] = jnp.zeros((48 - NORM_ROWS, D), BF)


def attn_backward(
    place, own_mask, other_mask, tokens, grad, prob, qkv, out, norm_params, later_norms, wqkv, wo
):
    rows = tokens.shape[0]
    tile = pl.BlockSpec((TILE, D), lambda i: (i, 0))
    smem = pl.BlockSpec(memory_space=pltpu.SMEM)
    return pl.pallas_call(
        attn_backward_kernel,
        grid=(rows // TILE,),
        in_specs=[
            smem,
            smem,
            smem,
            tile,
            tile,
            pl.BlockSpec((IMAGES, PAIRS, 2 * S, S), lambda i: (i, 0, 0, 0)),
            pl.BlockSpec((TILE, 3 * D), lambda i: (i, 0)),
            tile,
            pl.BlockSpec((4, D), lambda i: (0, 0)),
            pl.BlockSpec((2, D), lambda i: (0, 0)),
            pl.BlockSpec((D, 3 * D), lambda i: (0, 0)),
            pl.BlockSpec((D, D), lambda i: (0, 0)),
        ],
        out_specs=[
            pl.BlockSpec((TILE, 3 * D), lambda i: (i, 0)),
            pl.BlockSpec((SLABS, 48, D), lambda i: (0, 0, 0)),
            pl.BlockSpec((SLABS + 1, 48, D), lambda i: (0, 0, 0)),
            pl.BlockSpec((4, D), lambda i: (0, 0)),
        ],
        out_shape=[
            pltpu.HBM((rows, 3 * D), BF),
            jax.ShapeDtypeStruct((SLABS, 48, D), BF),
            jax.ShapeDtypeStruct((SLABS + 1, 48, D), BF),
            jax.ShapeDtypeStruct((4, D), F32),
        ],
        scratch_shapes=[
            pltpu.VMEM((D, 3 * D), F32),
            pltpu.VMEM((1, 3 * D), F32),
            pltpu.VMEM((D, D), F32),
        ],
        compiler_params=pltpu.CompilerParams(vmem_limit_bytes=VMEM_LIMIT),
        cost_estimate=pl.CostEstimate(
            flops=rows * D * (10 * D + 32 * S), bytes_accessed=20 << 20, transcendentals=0
        ),
        name="attn_backward",
    )(
        place, own_mask, other_mask,
        *map(in_hbm, (tokens, grad, prob, qkv, out, norm_params, later_norms, wqkv, wo)),
    )


def input_grad_kernel(x_ref, grad_ref, dqkv_ref, norm_ref, wqkv_ref, out_ref):
    normed, inverse_std = normalize(x_ref[...].astype(F32))
    back = nt(dqkv_ref[...], wqkv_ref[...]) * norm_ref[0:1, :]
    mean_first = jnp.mean(back, axis=-1, keepdims=True)
    mean_second = jnp.mean(back * normed, axis=-1, keepdims=True)
    out_ref[...] = grad_ref[...] + inverse_std * (back - mean_first - normed * mean_second)


def input_gradient(tokens, grad, dqkv, norm_params, wqkv):
    rows = tokens.shape[0]
    tile = pl.BlockSpec((INPUT_TILE, D), lambda i: (i, 0))
    return pl.pallas_call(
        input_grad_kernel,
        grid=(rows // INPUT_TILE,),
        in_specs=[
            tile,
            tile,
            pl.BlockSpec((INPUT_TILE, 3 * D), lambda i: (i, 0)),
            pl.BlockSpec((4, D), lambda i: (0, 0)),
            pl.BlockSpec((D, 3 * D), lambda i: (0, 0)),
        ],
        out_specs=tile,
        out_shape=jax.ShapeDtypeStruct((rows, D), F32),
        compiler_params=pltpu.CompilerParams(vmem_limit_bytes=VMEM_LIMIT),
        cost_estimate=pl.CostEstimate(
            flops=rows * D * 6 * D, bytes_accessed=10 << 20, transcendentals=0
        ),
        name="input_gradient",
    )(*map(in_hbm, (tokens, grad, dqkv, norm_params, wqkv)))


def pack_kernel(weight_ref, out_ref):
    groups, count, _, _ = weight_ref.shape
    for group in range(groups):
        blocks = [weight_ref[group, block] for block in range(count)]
        slab = jnp.concatenate(blocks, axis=1).astype(BF)
        for copy in range(OUTER):
            out_ref[copy, group] = slab


def pack(weights, first, groups):
    _, count, edge, _ = weights.shape
    shape = (OUTER, groups, edge, count * edge)
    return pl.pallas_call(
        pack_kernel,
        grid=(1,),
        in_specs=[
            pl.BlockSpec(
                (pl.Element(groups), pl.Element(count), pl.Element(edge), pl.Element(edge)),
                lambda i: (first, 0, 0, 0),
            )
        ],
        out_specs=pl.BlockSpec(shape, lambda i: (0, 0, 0, 0)),
        out_shape=jax.ShapeDtypeStruct(shape, BF),
        compiler_params=pltpu.CompilerParams(vmem_limit_bytes=SMALL_VMEM),
        name="pack",
    )(in_hbm(weights))


def add_kernel(own_ref, received_ref, *out_refs):
    for apart, out_ref in enumerate(out_refs):
        total = own_ref[apart].astype(F32) + received_ref[apart].astype(F32)
        out_ref[...] = total.astype(BF)


def add_late(own, received):
    return pl.pallas_call(
        add_kernel,
        out_shape=[jax.ShapeDtypeStruct(own.shape[1:], BF)] * own.shape[0],
        compiler_params=pltpu.CompilerParams(vmem_limit_bytes=SMALL_VMEM),
        name="add_late",
    )(own, received)


def sum_kernel(*refs):
    *in_refs, out_ref = refs
    total = in_refs[0][...].astype(F32)
    for ref in in_refs[1:]:
        total = total + ref[...].astype(F32)
    out_ref[...] = total.astype(BF)


def sum_late(pieces):
    return pl.pallas_call(
        sum_kernel,
        out_shape=jax.ShapeDtypeStruct(pieces[0].shape, BF),
        compiler_params=pltpu.CompilerParams(vmem_limit_bytes=SMALL_VMEM),
        name="sum_late",
    )(*pieces)


def combine_kernel(place_ref, own_ref, received_ref, norm_ref, *out_refs):
    norms = received_ref[SLABS, :NORM_ROWS].astype(F32)
    norms = norm_ref[...] + (norms[:4] + norms[4:])
    rows = jnp.concatenate(split(norms), axis=0)
    for apart, out_ref in enumerate(out_refs):
        start = OUTER * (place_ref[1] ^ apart)
        for outer in range(OUTER):
            total = own_ref[start + outer].astype(F32) + received_ref[start + outer].astype(F32)
            out_ref[48 * outer : 48 * outer + 48, :] = total.astype(BF)
        out_ref[48 * OUTER :, :] = rows


def combine(place, own, received, norms):
    vmem = pl.BlockSpec(memory_space=pltpu.VMEM)
    shape = jax.ShapeDtypeStruct((48 * OUTER + NORM_ROWS, D), BF)
    return pl.pallas_call(
        combine_kernel,
        in_specs=[pl.BlockSpec(memory_space=pltpu.SMEM), vmem, vmem, vmem],
        out_shape=[shape] * INNER,
        compiler_params=pltpu.CompilerParams(vmem_limit_bytes=SMALL_VMEM),
        name="combine",
    )(place, own, received, norms)


def join_kernel(*refs):
    *early_refs, out_ref = refs
    total = early_refs[0][...].astype(F32)
    for ref in early_refs[1:]:
        total = total + ref[...].astype(F32)
    norms = total[48 * OUTER : 48 * OUTER + 4] + total[48 * OUTER + 4 :]
    for outer in range(OUTER):
        out_ref[outer, :48] = total[48 * outer : 48 * outer + 48].astype(BF)
        out_ref[outer, 48:] = jnp.concatenate(split(norms), axis=0)


def join(early):
    return pl.pallas_call(
        join_kernel,
        out_shape=jax.ShapeDtypeStruct((OUTER, 48 + NORM_ROWS, D), BF),
        compiler_params=pltpu.CompilerParams(vmem_limit_bytes=SMALL_VMEM),
        name="join",
    )(*early)


def split(values):
    high = values.astype(BF)
    return high, (values - high.astype(F32)).astype(BF)


def stack(*pieces):
    return jnp.concatenate(pieces, axis=0)


def cut_rows(values, number):
    edge = values.shape[0] // number
    return [values[edge * i : edge * i + edge] for i in range(number)]


def product(left, right):
    high, low = left
    right_high, right_low = right
    one, two = cut_rows(nn(stack(high, low), right_high), 2)
    return one + (two + nn(high, right_low))


def two_products(left, middle, right):
    right_high, right_low = right
    both = cut_rows(nn(stack(left[0], middle[0], left[1], middle[1]), right_high), 4)
    high = cut_rows(nn(stack(left[0], middle[0]), right_low), 2)
    return both[0] + (both[2] + high[0]), both[1] + (both[3] + high[1])


def update_norms(scale, total, param_ref, state_ref, grad_ref, new_state_ref, new_ref):
    grads = total * scale
    state = 0.5 * state_ref[...] + 0.5 * grads * grads
    grad_ref[...] = grads
    new_state_ref[...] = state
    new_ref[...] = param_ref[...] - 0.2 * grads / jnp.sqrt(state)


def shampoo_kernel(scale, with_norms, received_ref, weight_ref, left_ref, right_ref, *refs):
    if with_norms:
        norm_ins, norm_outs, refs = refs[:2], refs[-5:-2], refs[:-5] + refs[-2:]
    out_grad_ref, left_new_ref, right_new_ref, new_weight_ref, root_ref, power_ref = refs[-6:]
    groups, count, edge = weight_ref.shape[:3]

    received = received_ref[0].astype(F32)
    for number in range(1, received_ref.shape[0]):
        received = received + received_ref[number].astype(F32)
    if with_norms:
        norms = received[0, edge:]
        update_norms(scale, norms[:4] + norms[4:], *norm_ins, *norm_outs)
    pack = min(PACK, count)
    width = pack * edge
    places = [(g, pack * n) for g in range(groups) for n in range(count // pack)]
    packs = len(places)

    def block_of(shape, dim):
        return lax.broadcasted_iota(jnp.int32, shape, dim) // edge

    row = lax.broadcasted_iota(jnp.int32, (edge, width), 0)
    lane = lax.broadcasted_iota(jnp.int32, (edge, width), 1)
    identity = (lane % edge == row).astype(F32)
    same = (block_of((width, width), 0) == block_of((width, width), 1)).astype(BF)
    lane_block = block_of((1, width), 1)

    def spread(pieces):
        return tuple(stack(*[piece] * pack) * same for piece in pieces)

    def cut(packed, index):
        return packed[:, edge * index : edge * index + edge]

    def beside(ref, place):
        return jnp.concatenate([ref[place[0], place[1] + i] for i in range(pack)], axis=1)

    grads, parts = [], []
    for group, start in places:
        grad = received[group, :edge, edge * start : edge * start + width] * scale
        blocks = [cut(grad, index) for index in range(pack)]
        for index in range(pack):
            out_grad_ref[group, start + index] = blocks[index]
        grad_t = jnp.concatenate([jnp.transpose(block) for block in blocks], axis=1)
        one, two = split(grad), split(grad_t)
        one_diagonal, two_diagonal = spread(one), spread(two)
        grads.append(one_diagonal)
        parts.append((left_ref, left_new_ref, one, two_diagonal))
        parts.append((right_ref, right_new_ref, two, one_diagonal))
    grams = [product(left, right) for _, _, left, right in parts]
    for slot, (old_ref, new_ref, _, _) in enumerate(parts):
        group, start = places[slot // 2]
        new = 0.5 * beside(old_ref, places[slot // 2]) + 0.5 * grams[slot]
        for index in range(pack):
            new_ref[group, start + index] = cut(new, index)
        columns = jnp.sum(new * new, axis=0, keepdims=True)
        squares = jnp.zeros((1, width), F32)
        for index in range(pack):
            inside = lane_block == index
            part = jnp.sum(jnp.where(inside, columns, 0.0), axis=1, keepdims=True)
            squares = jnp.where(inside, part, squares)
        factor = 2.5 / jnp.sqrt(squares)
        root_ref[slot] = jnp.broadcast_to(jnp.sqrt(jnp.sqrt(factor)), (edge, width))
        power_ref[slot] = factor * new
    slots = range(2 * packs)

    def advance(first):
        powers = [power_ref[slot] for slot in slots]
        middles = [split((5.0 * identity - power) * 0.25) for power in powers]
        rights = [spread(middle) for middle in middles]
        powers = [split(power) for power in powers]
        if first:
            squares = [product(middles[s], rights[s]) for s in slots]
            for slot in slots:
                root_ref[slot] *= (5.0 * identity - power_ref[slot]) * 0.25
        else:
            roots = [split(root_ref[slot]) for slot in slots]
            both = [two_products(roots[s], middles[s], rights[s]) for s in slots]
            squares = [pair[1] for pair in both]
            for slot in slots:
                root_ref[slot] = both[slot][0]
        rights = [spread(split(square)) for square in squares]
        powers = [split(product(powers[s], rights[s])) for s in slots]
        for slot in slots:
            power_ref[slot] = product(powers[slot], rights[slot])

    advance(True)
    lax.fori_loop(0, ITERS - 2, lambda _, carry: advance(False) or carry, 0)
    rights = [spread(split((5.0 * identity - power_ref[slot]) * 0.25)) for slot in slots]
    for slot in slots:
        root_ref[slot] = product(split(root_ref[slot]), rights[slot])
    steps = [product(split(root_ref[2 * n]), grads[n]) for n in range(packs)]
    rights = [spread(split(root_ref[2 * n + 1])) for n in range(packs)]
    steps = [product(split(steps[n]), rights[n]) for n in range(packs)]
    for number, (group, start) in enumerate(places):
        for index in range(pack):
            step = 0.25 * cut(steps[number], index)
            new_weight_ref[group, start + index] = weight_ref[group, start + index] - step


def shampoo(received, weights, stat_left, stat_right, scale, first, earlier=(), norms=()):
    groups = received.shape[1]
    _, count, edge, _ = weights.shape
    slots = 2 * groups * count // min(PACK, count)
    width = min(PACK, count) * edge
    block = pl.BlockSpec(
        (pl.Element(groups), pl.Element(count), pl.Element(edge), pl.Element(edge)),
        lambda i: (first, 0, 0, 0),
    )
    shape = jax.ShapeDtypeStruct(weights.shape, F32)
    norm = pl.BlockSpec((4, D), lambda i: (0, 0))
    norm_outs = 3 if norms else 0
    ins = 4 + len(norms)
    return pl.pallas_call(
        lambda *refs: shampoo_kernel(scale, bool(norms), *refs),
        grid=(1,),
        in_specs=[
            pl.BlockSpec(received.shape, lambda i: (0, 0, 0, 0)),
            *[block] * 3,
            *[norm] * len(norms),
            *[pl.BlockSpec(memory_space=pl.ANY)] * len(earlier),
        ],
        out_specs=[block] * 4 + [norm] * norm_outs,
        out_shape=[shape] * 4 + [jax.ShapeDtypeStruct((4, D), F32)] * norm_outs,
        scratch_shapes=[
            pltpu.VMEM((slots, edge, width), F32),
            pltpu.VMEM((slots, edge, width), F32),
        ],
        input_output_aliases={ins + i: i for i in range(len(earlier))},
        compiler_params=pltpu.CompilerParams(vmem_limit_bytes=SHAMPOO_VMEM),
        cost_estimate=pl.CostEstimate(
            flops=groups * (3 << 30), bytes_accessed=4 << 20, transcendentals=0
        ),
        name="shampoo",
    )(received, weights, stat_left, stat_right, *norms, *earlier)


def swap_heads(values):
    return lax.ppermute(values, "head", [(0, 1), (1, 0)])


def to_all(values, axis):
    return lax.all_to_all(values, axis, 0, 0)


def across(values, apart):
    pairs = [(i, i ^ apart) for i in range(INNER)]
    return lax.ppermute(values, "inner", pairs)


def from_all(values):
    return [values] + [across(values, apart) for apart in range(1, INNER)]


def gather_slabs(weights, small):
    early = to_all(pack(weights, 0, 1), "outer")[:, 0]
    early, late = lax.optimization_barrier((early, pack(weights, 1, 2)))
    late = to_all(late, "outer")
    early = from_all(early)
    early[1], late, small = lax.optimization_barrier((early[1], late, small))
    return early, from_all(late), small


def gather_blocks(local):
    groups, _, edge, _ = local.shape
    blocks = lax.all_gather(local, ("outer", "inner"), axis=1, tiled=True)
    blocks = blocks.reshape(groups, SLABS // INNER, INNER, D // edge, edge, edge)
    slabs = blocks.transpose(2, 1, 0, 4, 3, 5).reshape(SLABS, groups, edge, D)
    return slabs if groups > 1 else slabs[:, 0]


def scatter_blocks(slabs, count, edge):
    groups = slabs.shape[1]
    blocks = slabs.reshape(INNER, SLABS // INNER, groups, edge, D // edge, edge)
    blocks = blocks.transpose(2, 1, 0, 4, 3, 5).reshape(groups, SLABS * (D // edge), edge, edge)
    owned = lax.psum_scatter(blocks, ("outer", "inner"), scatter_dimension=1, tiled=True)
    return owned.transpose(0, 2, 1, 3).reshape(groups, edge, count * edge)


def per_device(
    tokens,
    cotangent,
    token_counts,
    head_mask,
    norm_params,
    norm_state,
    weights,
    stat_left,
    stat_right,
):
    weights, stat_left, stat_right = weights[0], stat_left[0], stat_right[0]
    _, count, edge, _ = weights.shape
    whole_slabs = count * edge == D
    other_mask = swap_heads(head_mask)
    inner = lax.axis_index("inner") if whole_slabs else 0
    place = jnp.concatenate([jnp.stack([lax.axis_index("head"), inner]), token_counts])
    if whole_slabs:
        early, late, (other_mask, place) = gather_slabs(weights, (other_mask, place))
    else:
        local = weights.astype(BF)
        early = jnp.split(gather_blocks(local[:1]), INNER)
        late = jnp.split(gather_blocks(local[1:]), INNER)
    early, late = list(early), list(late)
    masks = (head_mask, other_mask)
    early += [swap_heads(piece) for piece in early]
    prob, qkv, out, middle, wqkv, wo = attn_forward(
        place, *masks, tokens, norm_params, early
    )
    late[1:], middle = lax.optimization_barrier((late[1:], middle))
    late += [swap_heads(piece) for piece in late]
    block_out, middle_grad, norm_two, *late_sums = mlp(place, middle, cotangent, norm_params, late)
    own_late, late_received = late_sums[:2], [swap_heads(sent) for sent in late_sums[2:]]
    if whole_slabs:
        far = add_late(own_late[1], late_received[1])
        near = add_late(own_late[0], late_received[0])
        far = [across(far[number], 2 + number) for number in range(2)]
        near, middle_grad = lax.optimization_barrier((list(near), middle_grad))
        late_grads = [near[0], across(near[1], 1), *far]
    dqkv, own_early, sent_early, norm_sums = attn_backward(
        place, *masks, tokens, middle_grad, prob, qkv, out, norm_params, norm_two, wqkv, wo
    )
    if whole_slabs:
        late_grads, sent_early = lax.optimization_barrier((late_grads, sent_early))
    early_received = swap_heads(sent_early)
    devices = lax.axis_size("outer") * lax.axis_size("inner") * lax.axis_size("head")
    scale = 1.0 / math.sqrt(tokens.shape[0] * devices)
    state = (weights, stat_left, stat_right, scale)
    if whole_slabs:
        late_grads = to_all(sum_late(late_grads), "outer")
        early_grads = list(combine(place, own_early, early_received, norm_sums))
        early_grads, dqkv = lax.optimization_barrier((early_grads, dqkv))
        early_grads[1:] = [across(early_grads[apart], apart) for apart in range(1, INNER)]
        input_grad = input_gradient(tokens, middle_grad, dqkv, norm_params, wqkv)
        early_grads, input_grad = lax.optimization_barrier((early_grads, input_grad))
        joined, late_grads = lax.optimization_barrier((join(early_grads), late_grads))
        joined = to_all(joined, "outer")[:, None]
        results = shampoo(late_grads, *state, 1)
        results = shampoo(joined, *state, 0, results, (norm_params, norm_state))
    else:
        input_grad = input_gradient(tokens, middle_grad, dqkv, norm_params, wqkv)
        early_slabs = own_early.astype(F32) + early_received[:SLABS].astype(F32)
        late_slabs = jnp.concatenate(own_late).astype(F32) + jnp.concatenate(late_received)
        late_slabs = late_slabs.reshape(SLABS, 2, edge, D)
        slabs = jnp.concatenate([early_slabs[:, None], late_slabs], axis=1).astype(BF)
        owned = scatter_blocks(slabs, count, edge)
        results = list(shampoo(owned[None], *state, 0))
        norm_grads = lax.psum(norm_sums, ("outer", "inner", "head")) * scale
        state_new = 0.5 * norm_state + 0.5 * norm_grads * norm_grads
        results += [norm_grads, state_new, norm_params - 0.2 * norm_grads / jnp.sqrt(state_new)]
    return (block_out, input_grad, *[result[None] for result in results[:4]], *results[4:])


def solution(mesh):
    shape = (mesh.shape["dp"] // INNER, INNER, mesh.shape["head"])
    split_mesh = Mesh(mesh.devices.reshape(shape), ("outer", "inner", "head"))
    group = ("outer", "inner")
    blocks = P("head", None, group, None, None)
    rows = P(group + ("head",), None)
    return jax.shard_map(
        per_device,
        mesh=split_mesh,
        in_specs=(rows, rows, P(group), P(group, "head"), P(), P(), blocks, blocks, blocks),
        out_specs=(rows, rows, blocks, blocks, blocks, blocks, P(), P(), P()),
        check_vma=False,
    )
```

```python
import math

import jax
import jax.numpy as jnp
from jax import lax
from jax.experimental import pallas as pl
from jax.experimental.pallas import tpu as pltpu
from jax.sharding import Mesh, PartitionSpec as P

D = 384
HEAD_DIM = 64
MLP = 1536
S = 256
ITERS = 8
PAIR = 2 * HEAD_DIM
PAIRS = D // PAIR
HALF = D // 2
SLABS = 16
INNER = 4
OUTER = SLABS // INNER
TILE = 512
INPUT_TILE = 768
IMAGES = TILE // S
NORM_ROWS = 8
PACK = 2
ROOT_HALF = 0.7071067811865476
DENSITY_FACTOR = 0.3989422804014327
BF = jnp.bfloat16
F32 = jnp.float32
VMEM_LIMIT = 40 << 20
SMALL_VMEM = 8 << 20
SHAMPOO_VMEM = 24 << 20


def in_hbm(values):
    return pltpu.with_memory_space_constraint(values, pltpu.HBM)


def nn(left, right):
    return jnp.dot(left, right, preferred_element_type=F32)


def nt(left, right):
    return lax.dot_general(left, right, (((1,), (1,)), ((), ())), preferred_element_type=F32)


def tn(left, right):
    return lax.dot_general(left, right, (((0,), (0,)), ((), ())), preferred_element_type=F32)


def normalize(values):
    centered = values - jnp.mean(values, axis=-1, keepdims=True)
    variance = jnp.mean(centered * centered, axis=-1, keepdims=True)
    inverse_std = lax.rsqrt(variance + 1e-06)
    return centered * inverse_std, inverse_std


def norm_backward(grad_out, normed, inverse_std, gain):
    grad_normed = grad_out * gain
    mean_first = jnp.mean(grad_normed, axis=-1, keepdims=True)
    mean_second = jnp.mean(grad_normed * normed, axis=-1, keepdims=True)
    grad_in = inverse_std * (grad_normed - mean_first - normed * mean_second)
    gain_grad = jnp.sum(grad_out * normed, axis=0, keepdims=True)
    shift_grad = jnp.sum(grad_out, axis=0, keepdims=True)
    return grad_in, jnp.concatenate([gain_grad, shift_grad], axis=0)


def grown(step, total, part):
    return jnp.where(step == 0, part, total + part)


def slab_at(owner):
    return (owner % INNER) * OUTER + owner // INNER


def lane_halves():
    lane = lax.broadcasted_iota(jnp.int32, (1, PAIR), 1)
    first = (lane < HEAD_DIM).astype(BF)
    return first, (1 - first).astype(BF)


def stacked(values, first, second):
    return jnp.concatenate([values * first, values * second], axis=0)


def mask_lanes(place_ref, own_ref, other_ref, image, pair):
    image = place_ref[0] * (own_ref.shape[0] // 2) + image
    heads = own_ref.shape[1]
    on = [
        own_ref[image, head] if head < heads else other_ref[image, head - heads]
        for head in (2 * pair, 2 * pair + 1)
    ]
    lane = lax.broadcasted_iota(jnp.int32, (1, PAIR), 1)
    return jnp.where(lane < HEAD_DIM, on[0], on[1]).astype(F32)


def attn_forward_kernel(
    place_ref, own_mask_ref, other_mask_ref, x_ref, norm_ref, *refs
):
    slab_refs, refs = refs[: 2 * INNER], refs[2 * INNER :]
    prob_ref, qkv_ref, out_ref, middle_ref, wqkv_ref, wo_ref, held_ref = refs
    step = pl.program_id(0)

    @pl.when(step == 0)
    def _():
        for number, ref in enumerate(slab_refs):
            side, apart = divmod(number, INNER)
            held_ref[side, place_ref[1] ^ apart] = ref[...]

        def slab_of(side, owner):
            return held_ref[side, owner % INNER, owner // INNER]

        for row in range(D // 48):
            for part in range(3):
                pieces = []
                for number in range(2):
                    slab, side = divmod(3 * row + part, 2)
                    piece = slab_of(number, slab)[:, side * HALF : (side + 1) * HALF]
                    pieces.append(piece)
                joined = jnp.concatenate(pieces, axis=1)
                if part == 0:
                    joined = joined * 0.125
                wqkv_ref[48 * row : 48 * row + 48, D * part : D * part + D] = joined
        for side in range(2):
            for row in range(HALF // 48):
                start = side * HALF + 48 * row
                wo_ref[start : start + 48, :] = slab_of(side, 12 + row)

    x = x_ref[...].astype(F32)
    normed, _ = normalize(x)
    rows = (normed * norm_ref[0:1, :] + norm_ref[1:2, :]).astype(BF)
    qkv_ref[...] = nn(rows, wqkv_ref[...]).astype(BF)
    first, second = lane_halves()
    column = lax.broadcasted_iota(jnp.int32, (1, S), 1)
    tasks = [(image, pair) for image in range(IMAGES) for pair in range(PAIRS)]

    def places(task):
        image, pair = task
        here = slice(S * image, S * image + S)
        return here, *(slice(D * t + PAIR * pair, D * t + PAIR * (pair + 1)) for t in range(3))

    def get_scores(task):
        here, query_lanes, key_lanes, _ = places(task)
        return nt(stacked(qkv_ref[here, query_lanes], first, second), qkv_ref[here, key_lanes])

    def get_prob(task, scores):
        image = place_ref[0] * (own_mask_ref.shape[0] // 2) + IMAGES * step + task[0]
        scores = jnp.where(column < place_ref[2 + image], scores, -1e30)
        top = jnp.max(scores, axis=-1, keepdims=True)
        exp_scores = jnp.exp(scores - top)
        total = jnp.sum(exp_scores, axis=-1, keepdims=True)
        prob = (exp_scores * (1.0 / total)).astype(BF)
        prob_ref[task] = prob
        return prob

    all_scores = [get_scores(task) for task in tasks]
    probs = [get_prob(task, scores) for task, scores in zip(tasks, all_scores)]
    for task, prob in zip(tasks, probs):
        here, lanes, _, value_lanes = places(task)
        values = qkv_ref[here, value_lanes]
        head_out = nn(prob[:S], values * first) + nn(prob[S:], values * second)
        mask = mask_lanes(place_ref, own_mask_ref, other_mask_ref, IMAGES * step + task[0], task[1])
        out_ref[here, lanes] = (head_out * mask).astype(BF)
    middle_ref[...] = x + nn(out_ref[...], wo_ref[...])


def attn_forward(place, own_mask, other_mask, tokens, norm_params, slabs):
    rows = tokens.shape[0]
    images = rows // S
    tile = pl.BlockSpec((TILE, D), lambda i: (i, 0))
    slab = pl.BlockSpec((OUTER, 48, D), lambda i: (0, 0, 0))
    smem = pl.BlockSpec(memory_space=pltpu.SMEM)
    return pl.pallas_call(
        attn_forward_kernel,
        grid=(rows // TILE,),
        in_specs=[smem] * 3 + [tile, pl.BlockSpec((4, D), lambda i: (0, 0))] + [slab] * 2 * INNER,
        out_specs=[
            pl.BlockSpec((IMAGES, PAIRS, 2 * S, S), lambda i: (i, 0, 0, 0)),
            pl.BlockSpec((TILE, 3 * D), lambda i: (i, 0)),
            tile,
            tile,
            pl.BlockSpec((D, 3 * D), lambda i: (0, 0)),
            pl.BlockSpec((D, D), lambda i: (0, 0)),
        ],
        out_shape=[
            pltpu.HBM((images, PAIRS, 2 * S, S), BF),
            pltpu.HBM((rows, 3 * D), BF),
            pltpu.HBM((rows, D), BF),
            pltpu.HBM((rows, D), F32),
            pltpu.HBM((D, 3 * D), BF),
            pltpu.HBM((D, D), BF),
        ],
        scratch_shapes=[pltpu.VMEM((2, INNER, OUTER, 48, D), BF)],
        compiler_params=pltpu.CompilerParams(vmem_limit_bytes=VMEM_LIMIT),
        cost_estimate=pl.CostEstimate(
            flops=rows * D * (2 * D + 4 * S), bytes_accessed=4 << 20, transcendentals=0
        ),
        name="attn_forward",
    )(place, own_mask, other_mask, in_hbm(tokens), in_hbm(norm_params), *slabs)


def mlp_kernel(place_ref, middle_ref, cot_ref, norm_ref, *refs):
    slab_refs, refs = refs[: 2 * INNER], refs[2 * INNER :]
    out_ref, grad_ref, norm_grad_ref, *refs = refs
    own_refs, sent_refs, refs = refs[:2], refs[2:4], refs[4:]
    up_ref, down_ref, up_grad_ref, down_grad_ref = refs
    step = pl.program_id(0)
    half = MLP // 2

    def places(apart, outer):
        inner = place_ref[1] ^ apart
        row = pl.multiple_of(48 * (2 * outer + inner // 2), 16)
        lane = pl.multiple_of(D * (inner % 2), 128)
        down_row = pl.multiple_of(48 * (INNER * outer + inner), 16)
        return row, lane, down_row

    @pl.when(step == 0)
    def _():
        for number, ref in enumerate(slab_refs):
            side, apart = divmod(number, INNER)
            for outer in range(OUTER):
                row, lane, down_row = places(apart, outer)
                up_ref[side, pl.ds(row, 48), pl.ds(lane, D)] = ref[outer, 0]
                down_ref[side, pl.ds(down_row, 48), :] = ref[outer, 1]

    middle = middle_ref[...]
    normed, inverse_std = normalize(middle)
    rows = (normed * norm_ref[2:3, :] + norm_ref[3:4, :]).astype(BF)
    cot = cot_ref[...]
    total = middle
    back = None
    for side in range(2):
        up, down = up_ref[side], down_ref[side]
        pre = nn(rows, up)
        act_grad = nt(cot, down)
        cumulative = 0.5 * (1.0 + lax.erf(pre * ROOT_HALF))
        density = jnp.exp(-0.5 * pre * pre) * DENSITY_FACTOR
        act = (pre * cumulative).astype(BF)
        pre_grad = (act_grad * (cumulative + pre * density)).astype(BF)
        total = total + nn(act, down)
        term = nt(pre_grad, up)
        back = term if back is None else back + term
        down_grad_ref[side] = grown(step, down_grad_ref[side], tn(act, cot))
        up_grad_ref[side] = grown(step, up_grad_ref[side], tn(rows, pre_grad))
    out_ref[...] = total
    grad_in, norm_part = norm_backward(back, normed, inverse_std, norm_ref[2:3, :])
    norm_grad_ref[...] = grown(step, norm_grad_ref[...], norm_part)
    grad_ref[...] = cot.astype(F32) + grad_in

    @pl.when(step == pl.num_programs(0) - 1)
    def _():
        for apart in range(INNER):
            for outer in range(OUTER):
                row, lane, down_row = places(apart, outer)
                for side, halves in enumerate((own_refs, sent_refs)):
                    ref = halves[apart // 2]
                    up = up_grad_ref[side, pl.ds(row, 48), pl.ds(lane, D)]
                    down = down_grad_ref[side, pl.ds(down_row, 48), :]
                    ref[apart % 2, outer, 0] = up.astype(BF)
                    ref[apart % 2, outer, 1] = down.astype(BF)


def mlp(place, middle, cotangent, norm_params, slabs):
    rows = middle.shape[0]
    slab = pl.BlockSpec((OUTER, 2, 48, D), lambda i: (0, 0, 0, 0))
    grads = (INNER // 2, OUTER, 2, 48, D)
    grad = pl.BlockSpec(grads, lambda i: (0, 0, 0, 0, 0))
    tile = pl.BlockSpec((TILE, D), lambda i: (i, 0))
    return pl.pallas_call(
        mlp_kernel,
        grid=(rows // TILE,),
        in_specs=[
            pl.BlockSpec(memory_space=pltpu.SMEM),
            tile,
            tile,
            pl.BlockSpec((4, D), lambda i: (0, 0)),
            *[slab] * 2 * INNER,
        ],
        out_specs=[tile, tile, pl.BlockSpec((2, D), lambda i: (0, 0)), *[grad] * 4],
        out_shape=[
            jax.ShapeDtypeStruct((rows, D), F32),
            pltpu.HBM((rows, D), F32),
            jax.ShapeDtypeStruct((2, D), F32),
            *[jax.ShapeDtypeStruct(grads, BF)] * 4,
        ],
        scratch_shapes=[
            pltpu.VMEM((2, D, MLP // 2), BF),
            pltpu.VMEM((2, MLP // 2, D), BF),
            pltpu.VMEM((2, D, MLP // 2), F32),
            pltpu.VMEM((2, MLP // 2, D), F32),
        ],
        compiler_params=pltpu.CompilerParams(vmem_limit_bytes=VMEM_LIMIT),
        cost_estimate=pl.CostEstimate(
            flops=12 * rows * D * MLP, bytes_accessed=20 << 20, transcendentals=2 * rows * MLP
        ),
        name="mlp",
    )(place, in_hbm(middle), in_hbm(cotangent), in_hbm(norm_params), *slabs)


def attn_backward_kernel(
    place_ref, own_mask_ref, other_mask_ref, x_ref, grad_ref, prob_ref, qkv_ref, out_ref,
    norm_ref, later_norm_ref, wqkv_ref, wo_ref,
    dqkv_ref, own_grad_ref, sent_grad_ref, norm_grad_ref,
    cross_ref, column_ref, wo_grad_ref,
):
    step = pl.program_id(0)

    normed, _ = normalize(x_ref[...].astype(F32))
    low_grad = grad_ref[...].astype(BF)
    head_out = out_ref[...]
    wo_grad_ref[...] = grown(step, wo_grad_ref[...], tn(head_out, low_grad))
    whole_grad = nt(low_grad, wo_ref[...]).astype(BF)
    first, second = lane_halves()
    first_wide, second_wide = first.astype(F32), second.astype(F32)
    tasks = [(image, pair) for image in range(IMAGES) for pair in range(PAIRS)]

    def places(task):
        image, pair = task
        here = slice(S * image, S * image + S)
        return here, *(slice(D * t + PAIR * pair, D * t + PAIR * (pair + 1)) for t in range(3))

    def get_pair_grad(task):
        here, lanes, _, _ = places(task)
        mask = mask_lanes(place_ref, own_mask_ref, other_mask_ref, IMAGES * step + task[0], task[1])
        grad = whole_grad[here, lanes] * mask.astype(BF)
        dots = grad.astype(F32) * head_out[here, lanes].astype(F32)
        first_dot = jnp.sum(dots * first_wide, axis=-1, keepdims=True)
        second_dot = jnp.sum(dots * second_wide, axis=-1, keepdims=True)
        return stacked(grad, first, second), jnp.concatenate([first_dot, second_dot], axis=0)

    pair_grads = [get_pair_grad(task) for task in tasks]
    prob_grads = [
        nt(pair_grad[0], qkv_ref[places(task)[0], places(task)[3]])
        for task, pair_grad in zip(tasks, pair_grads)
    ]
    score_grads = [
        (prob_ref[task].astype(F32) * (prob_grad - pair_grad[1])).astype(BF)
        for task, prob_grad, pair_grad in zip(tasks, prob_grads, pair_grads)
    ]
    for task, score_grad, (pair_grad, _) in zip(tasks, score_grads, pair_grads):
        here, query_lanes, key_lanes, value_lanes = places(task)
        keys = qkv_ref[here, key_lanes]
        queries = stacked(qkv_ref[here, query_lanes], first, second)
        query_grad = nn(score_grad[:S], keys * first) + nn(score_grad[S:], keys * second)
        key_grad = nn(jnp.transpose(queries), score_grad)
        value_grad = nn(jnp.transpose(pair_grad), prob_ref[task])
        dqkv_ref[here, query_lanes] = query_grad.astype(BF)
        dqkv_ref[here, key_lanes] = jnp.transpose(key_grad).astype(BF)
        dqkv_ref[here, value_lanes] = jnp.transpose(value_grad).astype(BF)
    dqkv = dqkv_ref[...]
    cross_ref[...] = grown(step, cross_ref[...], tn(normed.astype(BF), dqkv))
    columns = jnp.sum(dqkv.astype(F32), axis=0, keepdims=True)
    column_ref[...] = grown(step, column_ref[...], columns)

    @pl.when(step == pl.num_programs(0) - 1)
    def _():
        wqkv = wqkv_ref[...]
        products = wqkv.astype(F32) * cross_ref[...]
        gain_grad = jnp.sum(products, axis=1, keepdims=True)
        gain_grad = jnp.transpose(jnp.broadcast_to(gain_grad, (D, 128)))
        columns = column_ref[...]
        shift_grad = nt(jnp.concatenate(split(jnp.broadcast_to(columns, (8, 3 * D)))), wqkv)
        norm_grad_ref[0:1, :] = gain_grad[0:1]
        norm_grad_ref[1:2, :] = shift_grad[0:1] + shift_grad[8:9]
        norm_grad_ref[2:4, :] = later_norm_ref[...]
        gain = jnp.transpose(jnp.broadcast_to(norm_ref[0:1, :], (128, D)))[:, :1]
        shift = jnp.transpose(jnp.broadcast_to(norm_ref[1:2, :], (128, D)))[:, :1]
        cross_ref[...] = cross_ref[...] * gain + shift * columns
        for side, slab_grads in enumerate((own_grad_ref, sent_grad_ref)):
            for slab in range(12):
                pieces = []
                for unit in (2 * slab, 2 * slab + 1):
                    row, part = divmod(unit, 3)
                    piece = cross_ref[48 * row : 48 * row + 48, D * part : D * part + D]
                    piece = piece[:, HALF * side : HALF * side + HALF]
                    pieces.append(piece * 0.125 if part == 0 else piece)
                slab_grads[slab_at(slab)] = jnp.concatenate(pieces, axis=1).astype(BF)
            for row in range(HALF // 48):
                start = HALF * side + 48 * row
                slab_grads[slab_at(12 + row)] = wo_grad_ref[start : start + 48, :].astype(BF)
        sent_grad_ref[SLABS, :NORM_ROWS] = jnp.concatenate(split(norm_grad_ref[...]), axis=0)
        sent_grad_ref[SLABS, NORM_ROWS:] = jnp.zeros((48 - NORM_ROWS, D), BF)


def attn_backward(
    place, own_mask, other_mask, tokens, grad, prob, qkv, out, norm_params, later_norms, wqkv, wo
):
    rows = tokens.shape[0]
    tile = pl.BlockSpec((TILE, D), lambda i: (i, 0))
    smem = pl.BlockSpec(memory_space=pltpu.SMEM)
    return pl.pallas_call(
        attn_backward_kernel,
        grid=(rows // TILE,),
        in_specs=[
            smem,
            smem,
            smem,
            tile,
            tile,
            pl.BlockSpec((IMAGES, PAIRS, 2 * S, S), lambda i: (i, 0, 0, 0)),
            pl.BlockSpec((TILE, 3 * D), lambda i: (i, 0)),
            tile,
            pl.BlockSpec((4, D), lambda i: (0, 0)),
            pl.BlockSpec((2, D), lambda i: (0, 0)),
            pl.BlockSpec((D, 3 * D), lambda i: (0, 0)),
            pl.BlockSpec((D, D), lambda i: (0, 0)),
        ],
        out_specs=[
            pl.BlockSpec((TILE, 3 * D), lambda i: (i, 0)),
            pl.BlockSpec((SLABS, 48, D), lambda i: (0, 0, 0)),
            pl.BlockSpec((SLABS + 1, 48, D), lambda i: (0, 0, 0)),
            pl.BlockSpec((4, D), lambda i: (0, 0)),
        ],
        out_shape=[
            pltpu.HBM((rows, 3 * D), BF),
            jax.ShapeDtypeStruct((SLABS, 48, D), BF),
            jax.ShapeDtypeStruct((SLABS + 1, 48, D), BF),
            jax.ShapeDtypeStruct((4, D), F32),
        ],
        scratch_shapes=[
            pltpu.VMEM((D, 3 * D), F32),
            pltpu.VMEM((1, 3 * D), F32),
            pltpu.VMEM((D, D), F32),
        ],
        compiler_params=pltpu.CompilerParams(vmem_limit_bytes=VMEM_LIMIT),
        cost_estimate=pl.CostEstimate(
            flops=rows * D * (10 * D + 32 * S), bytes_accessed=20 << 20, transcendentals=0
        ),
        name="attn_backward",
    )(
        place, own_mask, other_mask,
        *map(in_hbm, (tokens, grad, prob, qkv, out, norm_params, later_norms, wqkv, wo)),
    )


def input_grad_kernel(x_ref, grad_ref, dqkv_ref, norm_ref, wqkv_ref, out_ref):
    normed, inverse_std = normalize(x_ref[...].astype(F32))
    back = nt(dqkv_ref[...], wqkv_ref[...]) * norm_ref[0:1, :]
    mean_first = jnp.mean(back, axis=-1, keepdims=True)
    mean_second = jnp.mean(back * normed, axis=-1, keepdims=True)
    out_ref[...] = grad_ref[...] + inverse_std * (back - mean_first - normed * mean_second)


def input_gradient(tokens, grad, dqkv, norm_params, wqkv):
    rows = tokens.shape[0]
    tile = pl.BlockSpec((INPUT_TILE, D), lambda i: (i, 0))
    return pl.pallas_call(
        input_grad_kernel,
        grid=(rows // INPUT_TILE,),
        in_specs=[
            tile,
            tile,
            pl.BlockSpec((INPUT_TILE, 3 * D), lambda i: (i, 0)),
            pl.BlockSpec((4, D), lambda i: (0, 0)),
            pl.BlockSpec((D, 3 * D), lambda i: (0, 0)),
        ],
        out_specs=tile,
        out_shape=jax.ShapeDtypeStruct((rows, D), F32),
        compiler_params=pltpu.CompilerParams(vmem_limit_bytes=VMEM_LIMIT),
        cost_estimate=pl.CostEstimate(
            flops=rows * D * 6 * D, bytes_accessed=10 << 20, transcendentals=0
        ),
        name="input_gradient",
    )(*map(in_hbm, (tokens, grad, dqkv, norm_params, wqkv)))


def pack_kernel(weight_ref, out_ref):
    groups, count, _, _ = weight_ref.shape
    for group in range(groups):
        blocks = [weight_ref[group, block] for block in range(count)]
        slab = jnp.concatenate(blocks, axis=1).astype(BF)
        for copy in range(OUTER):
            out_ref[copy, group] = slab


def pack(weights):
    groups, count, edge, _ = weights.shape
    shape = (OUTER, groups, edge, count * edge)
    return pl.pallas_call(
        pack_kernel,
        out_shape=jax.ShapeDtypeStruct(shape, BF),
        compiler_params=pltpu.CompilerParams(vmem_limit_bytes=SMALL_VMEM),
        name="pack",
    )(in_hbm(weights))


def add_kernel(own_ref, received_ref, *out_refs):
    for apart, out_ref in enumerate(out_refs):
        total = own_ref[apart].astype(F32) + received_ref[apart].astype(F32)
        out_ref[...] = total.astype(BF)


def add_late(own, received):
    return pl.pallas_call(
        add_kernel,
        out_shape=[jax.ShapeDtypeStruct(own.shape[1:], BF)] * own.shape[0],
        compiler_params=pltpu.CompilerParams(vmem_limit_bytes=SMALL_VMEM),
        name="add_late",
    )(own, received)


def sum_kernel(*refs):
    *in_refs, out_ref = refs
    total = in_refs[0][...].astype(F32)
    for ref in in_refs[1:]:
        total = total + ref[...].astype(F32)
    out_ref[...] = total.astype(BF)


def sum_late(pieces):
    return pl.pallas_call(
        sum_kernel,
        out_shape=jax.ShapeDtypeStruct(pieces[0].shape, BF),
        compiler_params=pltpu.CompilerParams(vmem_limit_bytes=SMALL_VMEM),
        name="sum_late",
    )(*pieces)


def combine_kernel(place_ref, own_ref, received_ref, norm_ref, *out_refs):
    norms = received_ref[SLABS, :NORM_ROWS].astype(F32)
    norms = norm_ref[...] + (norms[:4] + norms[4:])
    rows = jnp.concatenate(split(norms), axis=0)
    for apart, out_ref in enumerate(out_refs):
        start = OUTER * (place_ref[1] ^ apart)
        for outer in range(OUTER):
            total = own_ref[start + outer].astype(F32) + received_ref[start + outer].astype(F32)
            out_ref[48 * outer : 48 * outer + 48, :] = total.astype(BF)
        out_ref[48 * OUTER :, :] = rows


def combine(place, own, received, norms):
    vmem = pl.BlockSpec(memory_space=pltpu.VMEM)
    shape = jax.ShapeDtypeStruct((48 * OUTER + NORM_ROWS, D), BF)
    return pl.pallas_call(
        combine_kernel,
        in_specs=[pl.BlockSpec(memory_space=pltpu.SMEM), vmem, vmem, vmem],
        out_shape=[shape] * INNER,
        compiler_params=pltpu.CompilerParams(vmem_limit_bytes=SMALL_VMEM),
        name="combine",
    )(place, own, received, norms)


def join_kernel(*refs):
    *early_refs, out_ref = refs
    total = early_refs[0][...].astype(F32)
    for ref in early_refs[1:]:
        total = total + ref[...].astype(F32)
    norms = total[48 * OUTER : 48 * OUTER + 4] + total[48 * OUTER + 4 :]
    for outer in range(OUTER):
        out_ref[outer, :48] = total[48 * outer : 48 * outer + 48].astype(BF)
        out_ref[outer, 48:] = jnp.concatenate(split(norms), axis=0)


def join(early):
    return pl.pallas_call(
        join_kernel,
        out_shape=jax.ShapeDtypeStruct((OUTER, 48 + NORM_ROWS, D), BF),
        compiler_params=pltpu.CompilerParams(vmem_limit_bytes=SMALL_VMEM),
        name="join",
    )(*early)


def split(values):
    high = values.astype(BF)
    return high, (values - high.astype(F32)).astype(BF)


def stack(*pieces):
    return jnp.concatenate(pieces, axis=0)


def cut_rows(values, number):
    edge = values.shape[0] // number
    return [values[edge * i : edge * i + edge] for i in range(number)]


def product(left, right):
    high, low = left
    right_high, right_low = right
    one, two = cut_rows(nn(stack(high, low), right_high), 2)
    return one + (two + nn(high, right_low))


def two_products(left, middle, right):
    right_high, right_low = right
    both = cut_rows(nn(stack(left[0], middle[0], left[1], middle[1]), right_high), 4)
    high = cut_rows(nn(stack(left[0], middle[0]), right_low), 2)
    return both[0] + (both[2] + high[0]), both[1] + (both[3] + high[1])


def update_norms(scale, total, param_ref, state_ref, grad_ref, new_state_ref, new_ref):
    grads = total * scale
    state = 0.5 * state_ref[...] + 0.5 * grads * grads
    grad_ref[...] = grads
    new_state_ref[...] = state
    new_ref[...] = param_ref[...] - 0.2 * grads / jnp.sqrt(state)


def shampoo_kernel(scale, with_norms, received_ref, weight_ref, left_ref, right_ref, *refs):
    if with_norms:
        norm_ins, norm_outs, refs = refs[:2], refs[-5:-2], refs[:-5] + refs[-2:]
    out_grad_ref, left_new_ref, right_new_ref, new_weight_ref, root_ref, power_ref = refs[-6:]
    groups, count, edge = weight_ref.shape[:3]

    received = received_ref[0].astype(F32)
    for number in range(1, received_ref.shape[0]):
        received = received + received_ref[number].astype(F32)
    if with_norms:
        norms = received[0, edge:]
        update_norms(scale, norms[:4] + norms[4:], *norm_ins, *norm_outs)
    pack = min(PACK, count)
    width = pack * edge
    places = [(g, pack * n) for g in range(groups) for n in range(count // pack)]
    packs = len(places)

    def block_of(shape, dim):
        return lax.broadcasted_iota(jnp.int32, shape, dim) // edge

    row = lax.broadcasted_iota(jnp.int32, (edge, width), 0)
    lane = lax.broadcasted_iota(jnp.int32, (edge, width), 1)
    identity = (lane % edge == row).astype(F32)
    same = (block_of((width, width), 0) == block_of((width, width), 1)).astype(BF)
    lane_block = block_of((1, width), 1)

    def spread(pieces):
        return tuple(stack(*[piece] * pack) * same for piece in pieces)

    def cut(packed, index):
        return packed[:, edge * index : edge * index + edge]

    def beside(ref, place):
        return jnp.concatenate([ref[place[0], place[1] + i] for i in range(pack)], axis=1)

    grads, parts = [], []
    for group, start in places:
        grad = received[group, :edge, edge * start : edge * start + width] * scale
        blocks = [cut(grad, index) for index in range(pack)]
        for index in range(pack):
            out_grad_ref[group, start + index] = blocks[index]
        grad_t = jnp.concatenate([jnp.transpose(block) for block in blocks], axis=1)
        one, two = split(grad), split(grad_t)
        one_diagonal, two_diagonal = spread(one), spread(two)
        grads.append(one_diagonal)
        parts.append((left_ref, left_new_ref, one, two_diagonal))
        parts.append((right_ref, right_new_ref, two, one_diagonal))
    grams = [product(left, right) for _, _, left, right in parts]
    for slot, (old_ref, new_ref, _, _) in enumerate(parts):
        group, start = places[slot // 2]
        new = 0.5 * beside(old_ref, places[slot // 2]) + 0.5 * grams[slot]
        for index in range(pack):
            new_ref[group, start + index] = cut(new, index)
        columns = jnp.sum(new * new, axis=0, keepdims=True)
        squares = jnp.zeros((1, width), F32)
        for index in range(pack):
            inside = lane_block == index
            part = jnp.sum(jnp.where(inside, columns, 0.0), axis=1, keepdims=True)
            squares = jnp.where(inside, part, squares)
        factor = 2.5 / jnp.sqrt(squares)
        root_ref[slot] = jnp.broadcast_to(jnp.sqrt(jnp.sqrt(factor)), (edge, width))
        power_ref[slot] = factor * new
    slots = range(2 * packs)

    def advance(first):
        powers = [power_ref[slot] for slot in slots]
        middles = [split((5.0 * identity - power) * 0.25) for power in powers]
        rights = [spread(middle) for middle in middles]
        powers = [split(power) for power in powers]
        if first:
            squares = [product(middles[s], rights[s]) for s in slots]
            for slot in slots:
                root_ref[slot] *= (5.0 * identity - power_ref[slot]) * 0.25
        else:
            roots = [split(root_ref[slot]) for slot in slots]
            both = [two_products(roots[s], middles[s], rights[s]) for s in slots]
            squares = [pair[1] for pair in both]
            for slot in slots:
                root_ref[slot] = both[slot][0]
        rights = [spread(split(square)) for square in squares]
        powers = [split(product(powers[s], rights[s])) for s in slots]
        for slot in slots:
            power_ref[slot] = product(powers[slot], rights[slot])

    advance(True)
    lax.fori_loop(0, ITERS - 2, lambda _, carry: advance(False) or carry, 0)
    rights = [spread(split((5.0 * identity - power_ref[slot]) * 0.25)) for slot in slots]
    for slot in slots:
        root_ref[slot] = product(split(root_ref[slot]), rights[slot])
    steps = [product(split(root_ref[2 * n]), grads[n]) for n in range(packs)]
    rights = [spread(split(root_ref[2 * n + 1])) for n in range(packs)]
    steps = [product(split(steps[n]), rights[n]) for n in range(packs)]
    for number, (group, start) in enumerate(places):
        for index in range(pack):
            step = 0.25 * cut(steps[number], index)
            new_weight_ref[group, start + index] = weight_ref[group, start + index] - step


def shampoo(received, weights, stat_left, stat_right, scale, first, earlier=(), norms=()):
    groups = received.shape[1]
    _, count, edge, _ = weights.shape
    slots = 2 * groups * count // min(PACK, count)
    width = min(PACK, count) * edge
    block = pl.BlockSpec(
        (pl.Element(groups), pl.Element(count), pl.Element(edge), pl.Element(edge)),
        lambda i: (first, 0, 0, 0),
    )
    shape = jax.ShapeDtypeStruct(weights.shape, F32)
    norm = pl.BlockSpec((4, D), lambda i: (0, 0))
    norm_outs = 3 if norms else 0
    ins = 4 + len(norms)
    return pl.pallas_call(
        lambda *refs: shampoo_kernel(scale, bool(norms), *refs),
        grid=(1,),
        in_specs=[
            pl.BlockSpec(received.shape, lambda i: (0, 0, 0, 0)),
            *[block] * 3,
            *[norm] * len(norms),
            *[pl.BlockSpec(memory_space=pl.ANY)] * len(earlier),
        ],
        out_specs=[block] * 4 + [norm] * norm_outs,
        out_shape=[shape] * 4 + [jax.ShapeDtypeStruct((4, D), F32)] * norm_outs,
        scratch_shapes=[
            pltpu.VMEM((slots, edge, width), F32),
            pltpu.VMEM((slots, edge, width), F32),
        ],
        input_output_aliases={ins + i: i for i in range(len(earlier))},
        compiler_params=pltpu.CompilerParams(vmem_limit_bytes=SHAMPOO_VMEM),
        cost_estimate=pl.CostEstimate(
            flops=groups * (3 << 30), bytes_accessed=4 << 20, transcendentals=0
        ),
        name="shampoo",
    )(received, weights, stat_left, stat_right, *norms, *earlier)


def swap_heads(values):
    return lax.ppermute(values, "head", [(0, 1), (1, 0)])


def to_all(values, axis):
    return lax.all_to_all(values, axis, 0, 0)


def across(values, apart):
    pairs = [(i, i ^ apart) for i in range(INNER)]
    return lax.ppermute(values, "inner", pairs)


def from_all(values):
    return [values] + [across(values, apart) for apart in range(1, INNER)]


def gather_slabs(weights, small):
    column = to_all(pack(weights), "outer")
    early = column[:, 0]
    column, early = lax.optimization_barrier((column, early))
    early = from_all(early)
    late = from_all(column[:, 1:])
    early[-1], small = lax.optimization_barrier((early[-1], small))
    return early, late, small


def gather_blocks(local):
    groups, _, edge, _ = local.shape
    blocks = lax.all_gather(local, ("outer", "inner"), axis=1, tiled=True)
    blocks = blocks.reshape(groups, SLABS // INNER, INNER, D // edge, edge, edge)
    slabs = blocks.transpose(2, 1, 0, 4, 3, 5).reshape(SLABS, groups, edge, D)
    return slabs if groups > 1 else slabs[:, 0]


def scatter_blocks(slabs, count, edge):
    groups = slabs.shape[1]
    blocks = slabs.reshape(INNER, SLABS // INNER, groups, edge, D // edge, edge)
    blocks = blocks.transpose(2, 1, 0, 4, 3, 5).reshape(groups, SLABS * (D // edge), edge, edge)
    owned = lax.psum_scatter(blocks, ("outer", "inner"), scatter_dimension=1, tiled=True)
    return owned.transpose(0, 2, 1, 3).reshape(groups, edge, count * edge)


def per_device(
    tokens,
    cotangent,
    token_counts,
    head_mask,
    norm_params,
    norm_state,
    weights,
    stat_left,
    stat_right,
):
    weights, stat_left, stat_right = weights[0], stat_left[0], stat_right[0]
    _, count, edge, _ = weights.shape
    whole_slabs = count * edge == D
    other_mask = swap_heads(head_mask)
    inner = lax.axis_index("inner") if whole_slabs else 0
    place = jnp.concatenate([jnp.stack([lax.axis_index("head"), inner]), token_counts])
    if whole_slabs:
        early, late, (other_mask, place) = gather_slabs(weights, (other_mask, place))
    else:
        local = weights.astype(BF)
        early = jnp.split(gather_blocks(local[:1]), INNER)
        late = jnp.split(gather_blocks(local[1:]), INNER)
    early, late = list(early), list(late)
    masks = (head_mask, other_mask)
    early += [swap_heads(piece) for piece in early]
    prob, qkv, out, middle, wqkv, wo = attn_forward(
        place, *masks, tokens, norm_params, early
    )
    late[1:], middle = lax.optimization_barrier((late[1:], middle))
    late += [swap_heads(piece) for piece in late]
    block_out, middle_grad, norm_two, *late_sums = mlp(place, middle, cotangent, norm_params, late)
    own_late, late_received = late_sums[:2], [swap_heads(sent) for sent in late_sums[2:]]
    if whole_slabs:
        far = add_late(own_late[1], late_received[1])
        near = add_late(own_late[0], late_received[0])
        far = [across(far[number], 2 + number) for number in range(2)]
        near, middle_grad = lax.optimization_barrier((list(near), middle_grad))
        late_grads = [near[0], across(near[1], 1), *far]
    dqkv, own_early, sent_early, norm_sums = attn_backward(
        place, *masks, tokens, middle_grad, prob, qkv, out, norm_params, norm_two, wqkv, wo
    )
    if whole_slabs:
        late_grads, sent_early = lax.optimization_barrier((late_grads, sent_early))
    early_received = swap_heads(sent_early)
    devices = lax.axis_size("outer") * lax.axis_size("inner") * lax.axis_size("head")
    scale = 1.0 / math.sqrt(tokens.shape[0] * devices)
    state = (weights, stat_left, stat_right, scale)
    if whole_slabs:
        late_grads = to_all(sum_late(late_grads), "outer")
        early_grads = list(combine(place, own_early, early_received, norm_sums))
        early_grads, dqkv = lax.optimization_barrier((early_grads, dqkv))
        early_grads[1:] = [across(early_grads[apart], apart) for apart in range(1, INNER)]
        input_grad = input_gradient(tokens, middle_grad, dqkv, norm_params, wqkv)
        early_grads, input_grad = lax.optimization_barrier((early_grads, input_grad))
        joined, late_grads = lax.optimization_barrier((join(early_grads), late_grads))
        joined = to_all(joined, "outer")[:, None]
        results = shampoo(late_grads, *state, 1)
        results = shampoo(joined, *state, 0, results, (norm_params, norm_state))
    else:
        input_grad = input_gradient(tokens, middle_grad, dqkv, norm_params, wqkv)
        early_slabs = own_early.astype(F32) + early_received[:SLABS].astype(F32)
        late_slabs = jnp.concatenate(own_late).astype(F32) + jnp.concatenate(late_received)
        late_slabs = late_slabs.reshape(SLABS, 2, edge, D)
        slabs = jnp.concatenate([early_slabs[:, None], late_slabs], axis=1).astype(BF)
        owned = scatter_blocks(slabs, count, edge)
        results = list(shampoo(owned[None], *state, 0))
        norm_grads = lax.psum(norm_sums, ("outer", "inner", "head")) * scale
        state_new = 0.5 * norm_state + 0.5 * norm_grads * norm_grads
        results += [norm_grads, state_new, norm_params - 0.2 * norm_grads / jnp.sqrt(state_new)]
    return (block_out, input_grad, *[result[None] for result in results[:4]], *results[4:])


def solution(mesh):
    shape = (mesh.shape["dp"] // INNER, INNER, mesh.shape["head"])
    split_mesh = Mesh(mesh.devices.reshape(shape), ("outer", "inner", "head"))
    group = ("outer", "inner")
    blocks = P("head", None, group, None, None)
    rows = P(group + ("head",), None)
    return jax.shard_map(
        per_device,
        mesh=split_mesh,
        in_specs=(rows, rows, P(group), P(group, "head"), P(), P(), blocks, blocks, blocks),
        out_specs=(rows, rows, blocks, blocks, blocks, blocks, P(), P(), P()),
        check_vma=False,
    )
```

```python
import math

import jax
import jax.numpy as jnp
from jax import lax
from jax.experimental import pallas as pl
from jax.experimental.pallas import tpu as pltpu
from jax.sharding import Mesh, PartitionSpec as P

D = 384
HEAD_DIM = 64
MLP = 1536
S = 256
ITERS = 8
PAIR = 2 * HEAD_DIM
PAIRS = D // PAIR
HALF = D // 2
SLABS = 16
INNER = 4
OUTER = SLABS // INNER
TILE = 512
INPUT_TILE = 768
IMAGES = TILE // S
NORM_ROWS = 8
PACK = 2
ROOT_HALF = 0.7071067811865476
DENSITY_FACTOR = 0.3989422804014327
BF = jnp.bfloat16
F32 = jnp.float32
VMEM_LIMIT = 40 << 20
SMALL_VMEM = 8 << 20
SHAMPOO_VMEM = 24 << 20


def in_hbm(values):
    return pltpu.with_memory_space_constraint(values, pltpu.HBM)


def nn(left, right):
    return jnp.dot(left, right, preferred_element_type=F32)


def nt(left, right):
    return lax.dot_general(left, right, (((1,), (1,)), ((), ())), preferred_element_type=F32)


def tn(left, right):
    return lax.dot_general(left, right, (((0,), (0,)), ((), ())), preferred_element_type=F32)


def normalize(values):
    centered = values - jnp.mean(values, axis=-1, keepdims=True)
    variance = jnp.mean(centered * centered, axis=-1, keepdims=True)
    inverse_std = lax.rsqrt(variance + 1e-06)
    return centered * inverse_std, inverse_std


def norm_backward(grad_out, normed, inverse_std, gain):
    grad_normed = grad_out * gain
    mean_first = jnp.mean(grad_normed, axis=-1, keepdims=True)
    mean_second = jnp.mean(grad_normed * normed, axis=-1, keepdims=True)
    grad_in = inverse_std * (grad_normed - mean_first - normed * mean_second)
    gain_grad = jnp.sum(grad_out * normed, axis=0, keepdims=True)
    shift_grad = jnp.sum(grad_out, axis=0, keepdims=True)
    return grad_in, jnp.concatenate([gain_grad, shift_grad], axis=0)


def grown(step, total, part):
    return jnp.where(step == 0, part, total + part)


def slab_at(owner):
    return (owner % INNER) * OUTER + owner // INNER


def lane_halves():
    lane = lax.broadcasted_iota(jnp.int32, (1, PAIR), 1)
    first = (lane < HEAD_DIM).astype(BF)
    return first, (1 - first).astype(BF)


def stacked(values, first, second):
    return jnp.concatenate([values * first, values * second], axis=0)


def mask_lanes(place_ref, own_ref, other_ref, image, pair):
    image = place_ref[0] * (own_ref.shape[0] // 2) + image
    heads = own_ref.shape[1]
    on = [
        own_ref[image, head] if head < heads else other_ref[image, head - heads]
        for head in (2 * pair, 2 * pair + 1)
    ]
    lane = lax.broadcasted_iota(jnp.int32, (1, PAIR), 1)
    return jnp.where(lane < HEAD_DIM, on[0], on[1]).astype(F32)


def attn_forward_kernel(
    place_ref, own_mask_ref, other_mask_ref, x_ref, norm_ref, *refs
):
    slab_refs, refs = refs[: 2 * INNER], refs[2 * INNER :]
    prob_ref, qkv_ref, out_ref, middle_ref, rows_ref, wqkv_ref, wo_ref, held_ref = refs
    step = pl.program_id(0)

    @pl.when(step == 0)
    def _():
        for number, ref in enumerate(slab_refs):
            side, apart = divmod(number, INNER)
            held_ref[side, place_ref[1] ^ apart] = ref[...]

        def slab_of(side, owner):
            return held_ref[side, owner % INNER, owner // INNER]

        for row in range(D // 48):
            for part in range(3):
                pieces = []
                for number in range(2):
                    slab, side = divmod(3 * row + part, 2)
                    piece = slab_of(number, slab)[:, side * HALF : (side + 1) * HALF]
                    pieces.append(piece)
                joined = jnp.concatenate(pieces, axis=1)
                if part == 0:
                    joined = joined * 0.125
                wqkv_ref[48 * row : 48 * row + 48, D * part : D * part + D] = joined
        for side in range(2):
            for row in range(HALF // 48):
                start = side * HALF + 48 * row
                wo_ref[start : start + 48, :] = slab_of(side, 12 + row)

    x = x_ref[...].astype(F32)
    normed, _ = normalize(x)
    rows = (normed * norm_ref[0:1, :] + norm_ref[1:2, :]).astype(BF)
    qkv_ref[...] = nn(rows, wqkv_ref[...]).astype(BF)
    first, second = lane_halves()
    column = lax.broadcasted_iota(jnp.int32, (1, S), 1)
    tasks = [(image, pair) for image in range(IMAGES) for pair in range(PAIRS)]

    def places(task):
        image, pair = task
        here = slice(S * image, S * image + S)
        return here, *(slice(D * t + PAIR * pair, D * t + PAIR * (pair + 1)) for t in range(3))

    def get_scores(task):
        here, query_lanes, key_lanes, _ = places(task)
        return nt(stacked(qkv_ref[here, query_lanes], first, second), qkv_ref[here, key_lanes])

    def get_prob(task, scores):
        image = place_ref[0] * (own_mask_ref.shape[0] // 2) + IMAGES * step + task[0]
        scores = jnp.where(column < place_ref[2 + image], scores, -1e30)
        top = jnp.max(scores, axis=-1, keepdims=True)
        exp_scores = jnp.exp(scores - top)
        total = jnp.sum(exp_scores, axis=-1, keepdims=True)
        prob = (exp_scores * (1.0 / total)).astype(BF)
        prob_ref[task] = prob
        return prob

    all_scores = [get_scores(task) for task in tasks]
    probs = [get_prob(task, scores) for task, scores in zip(tasks, all_scores)]
    for task, prob in zip(tasks, probs):
        here, lanes, _, value_lanes = places(task)
        values = qkv_ref[here, value_lanes]
        head_out = nn(prob[:S], values * first) + nn(prob[S:], values * second)
        mask = mask_lanes(place_ref, own_mask_ref, other_mask_ref, IMAGES * step + task[0], task[1])
        out_ref[here, lanes] = (head_out * mask).astype(BF)
    middle = x + nn(out_ref[...], wo_ref[...])
    middle_ref[...] = middle
    normed, _ = normalize(middle)
    rows_ref[...] = (normed * norm_ref[2:3, :] + norm_ref[3:4, :]).astype(BF)


def attn_forward(place, own_mask, other_mask, tokens, norm_params, slabs):
    rows = tokens.shape[0]
    images = rows // S
    tile = pl.BlockSpec((TILE, D), lambda i: (i, 0))
    slab = pl.BlockSpec((OUTER, 48, D), lambda i: (0, 0, 0))
    smem = pl.BlockSpec(memory_space=pltpu.SMEM)
    return pl.pallas_call(
        attn_forward_kernel,
        grid=(rows // TILE,),
        in_specs=[smem] * 3 + [tile, pl.BlockSpec((4, D), lambda i: (0, 0))] + [slab] * 2 * INNER,
        out_specs=[
            pl.BlockSpec((IMAGES, PAIRS, 2 * S, S), lambda i: (i, 0, 0, 0)),
            pl.BlockSpec((TILE, 3 * D), lambda i: (i, 0)),
            tile,
            tile,
            tile,
            pl.BlockSpec((D, 3 * D), lambda i: (0, 0)),
            pl.BlockSpec((D, D), lambda i: (0, 0)),
        ],
        out_shape=[
            pltpu.HBM((images, PAIRS, 2 * S, S), BF),
            pltpu.HBM((rows, 3 * D), BF),
            pltpu.HBM((rows, D), BF),
            pltpu.HBM((rows, D), F32),
            pltpu.HBM((rows, D), BF),
            pltpu.HBM((D, 3 * D), BF),
            pltpu.HBM((D, D), BF),
        ],
        scratch_shapes=[pltpu.VMEM((2, INNER, OUTER, 48, D), BF)],
        compiler_params=pltpu.CompilerParams(vmem_limit_bytes=VMEM_LIMIT),
        cost_estimate=pl.CostEstimate(
            flops=rows * D * (8 * D + 16 * S), bytes_accessed=16 << 20, transcendentals=rows * 6 * S
        ),
        name="attn_forward",
    )(place, own_mask, other_mask, in_hbm(tokens), in_hbm(norm_params), *slabs)


def mlp_kernel(place_ref, middle_ref, rows_ref, cot_ref, norm_ref, *refs):
    slab_refs, refs = refs[: 2 * INNER], refs[2 * INNER :]
    out_ref, grad_ref, norm_grad_ref, *refs = refs
    own_refs, sent_refs, refs = refs[:2], refs[2:4], refs[4:]
    up_ref, down_ref, up_grad_ref, down_grad_ref = refs
    step = pl.program_id(0)
    half = MLP // 2

    def places(apart, outer):
        inner = place_ref[1] ^ apart
        row = pl.multiple_of(48 * (2 * outer + inner // 2), 16)
        lane = pl.multiple_of(D * (inner % 2), 128)
        down_row = pl.multiple_of(48 * (INNER * outer + inner), 16)
        return row, lane, down_row

    @pl.when(step == 0)
    def _():
        for number, ref in enumerate(slab_refs):
            side, apart = divmod(number, INNER)
            for outer in range(OUTER):
                row, lane, down_row = places(apart, outer)
                up_ref[side, pl.ds(row, 48), pl.ds(lane, D)] = ref[outer, 0]
                down_ref[side, pl.ds(down_row, 48), :] = ref[outer, 1]

    middle = middle_ref[...]
    normed, inverse_std = normalize(middle)
    rows, cot = rows_ref[...], cot_ref[...]
    total = middle
    back = None
    for side in range(2):
        up, down = up_ref[side], down_ref[side]
        pre = nn(rows, up)
        act_grad = nt(cot, down)
        cumulative = 0.5 * (1.0 + lax.erf(pre * ROOT_HALF))
        density = jnp.exp(-0.5 * pre * pre) * DENSITY_FACTOR
        act = (pre * cumulative).astype(BF)
        pre_grad = (act_grad * (cumulative + pre * density)).astype(BF)
        total = total + nn(act, down)
        term = nt(pre_grad, up)
        back = term if back is None else back + term
        down_grad_ref[side] = grown(step, down_grad_ref[side], tn(act, cot))
        up_grad_ref[side] = grown(step, up_grad_ref[side], tn(rows, pre_grad))
    out_ref[...] = total
    grad_in, norm_part = norm_backward(back, normed, inverse_std, norm_ref[2:3, :])
    norm_grad_ref[...] = grown(step, norm_grad_ref[...], norm_part)
    grad_ref[...] = cot.astype(F32) + grad_in

    @pl.when(step == pl.num_programs(0) - 1)
    def _():
        for apart in range(INNER):
            for outer in range(OUTER):
                row, lane, down_row = places(apart, outer)
                for side, halves in enumerate((own_refs, sent_refs)):
                    ref = halves[apart // 2]
                    up = up_grad_ref[side, pl.ds(row, 48), pl.ds(lane, D)]
                    down = down_grad_ref[side, pl.ds(down_row, 48), :]
                    ref[apart % 2, outer, 0] = up.astype(BF)
                    ref[apart % 2, outer, 1] = down.astype(BF)


def mlp(place, middle, second_rows, cotangent, norm_params, slabs):
    rows = middle.shape[0]
    slab = pl.BlockSpec((OUTER, 2, 48, D), lambda i: (0, 0, 0, 0))
    grads = (INNER // 2, OUTER, 2, 48, D)
    grad = pl.BlockSpec(grads, lambda i: (0, 0, 0, 0, 0))
    tile = pl.BlockSpec((TILE, D), lambda i: (i, 0))
    return pl.pallas_call(
        mlp_kernel,
        grid=(rows // TILE,),
        in_specs=[
            pl.BlockSpec(memory_space=pltpu.SMEM),
            tile,
            tile,
            tile,
            pl.BlockSpec((4, D), lambda i: (0, 0)),
            *[slab] * 2 * INNER,
        ],
        out_specs=[tile, tile, pl.BlockSpec((2, D), lambda i: (0, 0)), *[grad] * 4],
        out_shape=[
            jax.ShapeDtypeStruct((rows, D), F32),
            pltpu.HBM((rows, D), F32),
            jax.ShapeDtypeStruct((2, D), F32),
            *[jax.ShapeDtypeStruct(grads, BF)] * 4,
        ],
        scratch_shapes=[
            pltpu.VMEM((2, D, MLP // 2), BF),
            pltpu.VMEM((2, MLP // 2, D), BF),
            pltpu.VMEM((2, D, MLP // 2), F32),
            pltpu.VMEM((2, MLP // 2, D), F32),
        ],
        compiler_params=pltpu.CompilerParams(vmem_limit_bytes=VMEM_LIMIT),
        cost_estimate=pl.CostEstimate(
            flops=12 * rows * D * MLP, bytes_accessed=20 << 20, transcendentals=2 * rows * MLP
        ),
        name="mlp",
    )(place, *map(in_hbm, (middle, second_rows, cotangent, norm_params)), *slabs)


def attn_backward_kernel(
    place_ref, own_mask_ref, other_mask_ref, x_ref, grad_ref, prob_ref, qkv_ref, out_ref,
    norm_ref, later_norm_ref, wqkv_ref, wo_ref,
    dqkv_ref, own_grad_ref, sent_grad_ref, norm_grad_ref,
    cross_ref, column_ref, wo_grad_ref,
):
    step = pl.program_id(0)

    normed, _ = normalize(x_ref[...].astype(F32))
    low_grad = grad_ref[...].astype(BF)
    head_out = out_ref[...]
    wo_grad_ref[...] = grown(step, wo_grad_ref[...], tn(head_out, low_grad))
    whole_grad = nt(low_grad, wo_ref[...]).astype(BF)
    first, second = lane_halves()
    first_wide, second_wide = first.astype(F32), second.astype(F32)
    tasks = [(image, pair) for image in range(IMAGES) for pair in range(PAIRS)]

    def places(task):
        image, pair = task
        here = slice(S * image, S * image + S)
        return here, *(slice(D * t + PAIR * pair, D * t + PAIR * (pair + 1)) for t in range(3))

    def get_pair_grad(task):
        here, lanes, _, _ = places(task)
        mask = mask_lanes(place_ref, own_mask_ref, other_mask_ref, IMAGES * step + task[0], task[1])
        grad = whole_grad[here, lanes] * mask.astype(BF)
        dots = grad.astype(F32) * head_out[here, lanes].astype(F32)
        first_dot = jnp.sum(dots * first_wide, axis=-1, keepdims=True)
        second_dot = jnp.sum(dots * second_wide, axis=-1, keepdims=True)
        return stacked(grad, first, second), jnp.concatenate([first_dot, second_dot], axis=0)

    pair_grads = [get_pair_grad(task) for task in tasks]
    prob_grads = [
        nt(pair_grad[0], qkv_ref[places(task)[0], places(task)[3]])
        for task, pair_grad in zip(tasks, pair_grads)
    ]
    score_grads = [
        (prob_ref[task].astype(F32) * (prob_grad - pair_grad[1])).astype(BF)
        for task, prob_grad, pair_grad in zip(tasks, prob_grads, pair_grads)
    ]
    for task, score_grad, (pair_grad, _) in zip(tasks, score_grads, pair_grads):
        here, query_lanes, key_lanes, value_lanes = places(task)
        keys = qkv_ref[here, key_lanes]
        queries = stacked(qkv_ref[here, query_lanes], first, second)
        query_grad = nn(score_grad[:S], keys * first) + nn(score_grad[S:], keys * second)
        key_grad = nn(jnp.transpose(queries), score_grad)
        value_grad = nn(jnp.transpose(pair_grad), prob_ref[task])
        dqkv_ref[here, query_lanes] = query_grad.astype(BF)
        dqkv_ref[here, key_lanes] = jnp.transpose(key_grad).astype(BF)
        dqkv_ref[here, value_lanes] = jnp.transpose(value_grad).astype(BF)
    dqkv = dqkv_ref[...]
    cross_ref[...] = grown(step, cross_ref[...], tn(normed.astype(BF), dqkv))
    columns = jnp.sum(dqkv.astype(F32), axis=0, keepdims=True)
    column_ref[...] = grown(step, column_ref[...], columns)

    @pl.when(step == pl.num_programs(0) - 1)
    def _():
        wqkv = wqkv_ref[...]
        products = wqkv.astype(F32) * cross_ref[...]
        gain_grad = jnp.sum(products, axis=1, keepdims=True)
        gain_grad = jnp.transpose(jnp.broadcast_to(gain_grad, (D, 128)))
        columns = column_ref[...]
        shift_grad = nt(jnp.concatenate(split(jnp.broadcast_to(columns, (8, 3 * D)))), wqkv)
        norm_grad_ref[0:1, :] = gain_grad[0:1]
        norm_grad_ref[1:2, :] = shift_grad[0:1] + shift_grad[8:9]
        norm_grad_ref[2:4, :] = later_norm_ref[...]
        gain = jnp.transpose(jnp.broadcast_to(norm_ref[0:1, :], (128, D)))[:, :1]
        shift = jnp.transpose(jnp.broadcast_to(norm_ref[1:2, :], (128, D)))[:, :1]
        cross_ref[...] = cross_ref[...] * gain + shift * columns
        for side, slab_grads in enumerate((own_grad_ref, sent_grad_ref)):
            for slab in range(12):
                pieces = []
                for unit in (2 * slab, 2 * slab + 1):
                    row, part = divmod(unit, 3)
                    piece = cross_ref[48 * row : 48 * row + 48, D * part : D * part + D]
                    piece = piece[:, HALF * side : HALF * side + HALF]
                    pieces.append(piece * 0.125 if part == 0 else piece)
                slab_grads[slab_at(slab)] = jnp.concatenate(pieces, axis=1).astype(BF)
            for row in range(HALF // 48):
                start = HALF * side + 48 * row
                slab_grads[slab_at(12 + row)] = wo_grad_ref[start : start + 48, :].astype(BF)
        sent_grad_ref[SLABS, :NORM_ROWS] = jnp.concatenate(split(norm_grad_ref[...]), axis=0)
        sent_grad_ref[SLABS, NORM_ROWS:] = jnp.zeros((48 - NORM_ROWS, D), BF)


def attn_backward(
    place, own_mask, other_mask, tokens, grad, prob, qkv, out, norm_params, later_norms, wqkv, wo
):
    rows = tokens.shape[0]
    tile = pl.BlockSpec((TILE, D), lambda i: (i, 0))
    smem = pl.BlockSpec(memory_space=pltpu.SMEM)
    return pl.pallas_call(
        attn_backward_kernel,
        grid=(rows // TILE,),
        in_specs=[
            smem,
            smem,
            smem,
            tile,
            tile,
            pl.BlockSpec((IMAGES, PAIRS, 2 * S, S), lambda i: (i, 0, 0, 0)),
            pl.BlockSpec((TILE, 3 * D), lambda i: (i, 0)),
            tile,
            pl.BlockSpec((4, D), lambda i: (0, 0)),
            pl.BlockSpec((2, D), lambda i: (0, 0)),
            pl.BlockSpec((D, 3 * D), lambda i: (0, 0)),
            pl.BlockSpec((D, D), lambda i: (0, 0)),
        ],
        out_specs=[
            pl.BlockSpec((TILE, 3 * D), lambda i: (i, 0)),
            pl.BlockSpec((SLABS, 48, D), lambda i: (0, 0, 0)),
            pl.BlockSpec((SLABS + 1, 48, D), lambda i: (0, 0, 0)),
            pl.BlockSpec((4, D), lambda i: (0, 0)),
        ],
        out_shape=[
            pltpu.HBM((rows, 3 * D), BF),
            jax.ShapeDtypeStruct((SLABS, 48, D), BF),
            jax.ShapeDtypeStruct((SLABS + 1, 48, D), BF),
            jax.ShapeDtypeStruct((4, D), F32),
        ],
        scratch_shapes=[
            pltpu.VMEM((D, 3 * D), F32),
            pltpu.VMEM((1, 3 * D), F32),
            pltpu.VMEM((D, D), F32),
        ],
        compiler_params=pltpu.CompilerParams(vmem_limit_bytes=VMEM_LIMIT),
        cost_estimate=pl.CostEstimate(
            flops=rows * D * (10 * D + 32 * S), bytes_accessed=20 << 20, transcendentals=0
        ),
        name="attn_backward",
    )(
        place, own_mask, other_mask,
        *map(in_hbm, (tokens, grad, prob, qkv, out, norm_params, later_norms, wqkv, wo)),
    )


def input_grad_kernel(x_ref, grad_ref, dqkv_ref, norm_ref, wqkv_ref, out_ref):
    normed, inverse_std = normalize(x_ref[...].astype(F32))
    back = nt(dqkv_ref[...], wqkv_ref[...]) * norm_ref[0:1, :]
    mean_first = jnp.mean(back, axis=-1, keepdims=True)
    mean_second = jnp.mean(back * normed, axis=-1, keepdims=True)
    out_ref[...] = grad_ref[...] + inverse_std * (back - mean_first - normed * mean_second)


def input_gradient(tokens, grad, dqkv, norm_params, wqkv):
    rows = tokens.shape[0]
    tile = pl.BlockSpec((INPUT_TILE, D), lambda i: (i, 0))
    return pl.pallas_call(
        input_grad_kernel,
        grid=(rows // INPUT_TILE,),
        in_specs=[
            tile,
            tile,
            pl.BlockSpec((INPUT_TILE, 3 * D), lambda i: (i, 0)),
            pl.BlockSpec((4, D), lambda i: (0, 0)),
            pl.BlockSpec((D, 3 * D), lambda i: (0, 0)),
        ],
        out_specs=tile,
        out_shape=jax.ShapeDtypeStruct((rows, D), F32),
        compiler_params=pltpu.CompilerParams(vmem_limit_bytes=VMEM_LIMIT),
        cost_estimate=pl.CostEstimate(
            flops=rows * D * 6 * D, bytes_accessed=10 << 20, transcendentals=0
        ),
        name="input_gradient",
    )(*map(in_hbm, (tokens, grad, dqkv, norm_params, wqkv)))


def pack_kernel(weight_ref, out_ref):
    groups, count, _, _ = weight_ref.shape
    for group in range(groups):
        blocks = [weight_ref[group, block] for block in range(count)]
        slab = jnp.concatenate(blocks, axis=1).astype(BF)
        for copy in range(OUTER):
            out_ref[copy, group] = slab


def pack(weights, first, groups):
    _, count, edge, _ = weights.shape
    shape = (OUTER, groups, edge, count * edge)
    return pl.pallas_call(
        pack_kernel,
        grid=(1,),
        in_specs=[
            pl.BlockSpec(
                (pl.Element(groups), pl.Element(count), pl.Element(edge), pl.Element(edge)),
                lambda i: (first, 0, 0, 0),
            )
        ],
        out_specs=pl.BlockSpec(shape, lambda i: (0, 0, 0, 0)),
        out_shape=jax.ShapeDtypeStruct(shape, BF),
        compiler_params=pltpu.CompilerParams(vmem_limit_bytes=SMALL_VMEM),
        name="pack",
    )(in_hbm(weights))


def add_kernel(own_ref, received_ref, *out_refs):
    for apart, out_ref in enumerate(out_refs):
        total = own_ref[apart].astype(F32) + received_ref[apart].astype(F32)
        out_ref[...] = total.astype(BF)


def add_late(own, received):
    return pl.pallas_call(
        add_kernel,
        out_shape=[jax.ShapeDtypeStruct(own.shape[1:], BF)] * own.shape[0],
        compiler_params=pltpu.CompilerParams(vmem_limit_bytes=SMALL_VMEM),
        name="add_late",
    )(own, received)


def sum_kernel(*refs):
    *in_refs, out_ref = refs
    total = in_refs[0][...].astype(F32)
    for ref in in_refs[1:]:
        total = total + ref[...].astype(F32)
    out_ref[...] = total.astype(BF)


def sum_late(pieces):
    return pl.pallas_call(
        sum_kernel,
        out_shape=jax.ShapeDtypeStruct(pieces[0].shape, BF),
        compiler_params=pltpu.CompilerParams(vmem_limit_bytes=SMALL_VMEM),
        name="sum_late",
    )(*pieces)


def combine_kernel(place_ref, own_ref, received_ref, norm_ref, *out_refs):
    norms = received_ref[SLABS, :NORM_ROWS].astype(F32)
    norms = norm_ref[...] + (norms[:4] + norms[4:])
    rows = jnp.concatenate(split(norms), axis=0)
    for apart, out_ref in enumerate(out_refs):
        start = OUTER * (place_ref[1] ^ apart)
        for outer in range(OUTER):
            total = own_ref[start + outer].astype(F32) + received_ref[start + outer].astype(F32)
            out_ref[48 * outer : 48 * outer + 48, :] = total.astype(BF)
        out_ref[48 * OUTER :, :] = rows


def combine(place, own, received, norms):
    vmem = pl.BlockSpec(memory_space=pltpu.VMEM)
    shape = jax.ShapeDtypeStruct((48 * OUTER + NORM_ROWS, D), BF)
    return pl.pallas_call(
        combine_kernel,
        in_specs=[pl.BlockSpec(memory_space=pltpu.SMEM), vmem, vmem, vmem],
        out_shape=[shape] * INNER,
        compiler_params=pltpu.CompilerParams(vmem_limit_bytes=SMALL_VMEM),
        name="combine",
    )(place, own, received, norms)


def join_kernel(*refs):
    *early_refs, out_ref = refs
    total = early_refs[0][...].astype(F32)
    for ref in early_refs[1:]:
        total = total + ref[...].astype(F32)
    norms = total[48 * OUTER : 48 * OUTER + 4] + total[48 * OUTER + 4 :]
    for outer in range(OUTER):
        out_ref[outer, :48] = total[48 * outer : 48 * outer + 48].astype(BF)
        out_ref[outer, 48:] = jnp.concatenate(split(norms), axis=0)


def join(early):
    return pl.pallas_call(
        join_kernel,
        out_shape=jax.ShapeDtypeStruct((OUTER, 48 + NORM_ROWS, D), BF),
        compiler_params=pltpu.CompilerParams(vmem_limit_bytes=SMALL_VMEM),
        name="join",
    )(*early)


def split(values):
    high = values.astype(BF)
    return high, (values - high.astype(F32)).astype(BF)


def stack(*pieces):
    return jnp.concatenate(pieces, axis=0)


def cut_rows(values, number):
    edge = values.shape[0] // number
    return [values[edge * i : edge * i + edge] for i in range(number)]


def product(left, right):
    high, low = left
    right_high, right_low = right
    one, two = cut_rows(nn(stack(high, low), right_high), 2)
    return one + (two + nn(high, right_low))


def two_products(left, middle, right):
    right_high, right_low = right
    both = cut_rows(nn(stack(left[0], middle[0], left[1], middle[1]), right_high), 4)
    high = cut_rows(nn(stack(left[0], middle[0]), right_low), 2)
    return both[0] + (both[2] + high[0]), both[1] + (both[3] + high[1])


def update_norms(scale, total, param_ref, state_ref, grad_ref, new_state_ref, new_ref):
    grads = total * scale
    state = 0.5 * state_ref[...] + 0.5 * grads * grads
    grad_ref[...] = grads
    new_state_ref[...] = state
    new_ref[...] = param_ref[...] - 0.2 * grads / jnp.sqrt(state)


def shampoo_kernel(scale, with_norms, received_ref, weight_ref, left_ref, right_ref, *refs):
    if with_norms:
        norm_ins, norm_outs, refs = refs[:2], refs[-5:-2], refs[:-5] + refs[-2:]
    out_grad_ref, left_new_ref, right_new_ref, new_weight_ref, root_ref, power_ref = refs[-6:]
    groups, count, edge = weight_ref.shape[:3]

    received = received_ref[0].astype(F32)
    for number in range(1, received_ref.shape[0]):
        received = received + received_ref[number].astype(F32)
    if with_norms:
        norms = received[0, edge:]
        update_norms(scale, norms[:4] + norms[4:], *norm_ins, *norm_outs)
    pack = min(PACK, count)
    width = pack * edge
    places = [(g, pack * n) for g in range(groups) for n in range(count // pack)]
    packs = len(places)

    def block_of(shape, dim):
        return lax.broadcasted_iota(jnp.int32, shape, dim) // edge

    row = lax.broadcasted_iota(jnp.int32, (edge, width), 0)
    lane = lax.broadcasted_iota(jnp.int32, (edge, width), 1)
    identity = (lane % edge == row).astype(F32)
    same = (block_of((width, width), 0) == block_of((width, width), 1)).astype(BF)
    lane_block = block_of((1, width), 1)

    def spread(pieces):
        return tuple(stack(*[piece] * pack) * same for piece in pieces)

    def cut(packed, index):
        return packed[:, edge * index : edge * index + edge]

    def beside(ref, place):
        return jnp.concatenate([ref[place[0], place[1] + i] for i in range(pack)], axis=1)

    grads, parts = [], []
    for group, start in places:
        grad = received[group, :edge, edge * start : edge * start + width] * scale
        blocks = [cut(grad, index) for index in range(pack)]
        for index in range(pack):
            out_grad_ref[group, start + index] = blocks[index]
        grad_t = jnp.concatenate([jnp.transpose(block) for block in blocks], axis=1)
        one, two = split(grad), split(grad_t)
        one_diagonal, two_diagonal = spread(one), spread(two)
        grads.append(one_diagonal)
        parts.append((left_ref, left_new_ref, one, two_diagonal))
        parts.append((right_ref, right_new_ref, two, one_diagonal))
    grams = [product(left, right) for _, _, left, right in parts]
    for slot, (old_ref, new_ref, _, _) in enumerate(parts):
        group, start = places[slot // 2]
        new = 0.5 * beside(old_ref, places[slot // 2]) + 0.5 * grams[slot]
        for index in range(pack):
            new_ref[group, start + index] = cut(new, index)
        columns = jnp.sum(new * new, axis=0, keepdims=True)
        squares = jnp.zeros((1, width), F32)
        for index in range(pack):
            inside = lane_block == index
            part = jnp.sum(jnp.where(inside, columns, 0.0), axis=1, keepdims=True)
            squares = jnp.where(inside, part, squares)
        factor = 2.5 / jnp.sqrt(squares)
        root_ref[slot] = jnp.broadcast_to(jnp.sqrt(jnp.sqrt(factor)), (edge, width))
        power_ref[slot] = factor * new
    slots = range(2 * packs)

    def advance(first):
        powers = [power_ref[slot] for slot in slots]
        middles = [split((5.0 * identity - power) * 0.25) for power in powers]
        rights = [spread(middle) for middle in middles]
        powers = [split(power) for power in powers]
        if first:
            squares = [product(middles[s], rights[s]) for s in slots]
            for slot in slots:
                root_ref[slot] *= (5.0 * identity - power_ref[slot]) * 0.25
        else:
            roots = [split(root_ref[slot]) for slot in slots]
            both = [two_products(roots[s], middles[s], rights[s]) for s in slots]
            squares = [pair[1] for pair in both]
            for slot in slots:
                root_ref[slot] = both[slot][0]
        rights = [spread(split(square)) for square in squares]
        powers = [split(product(powers[s], rights[s])) for s in slots]
        for slot in slots:
            power_ref[slot] = product(powers[slot], rights[slot])

    advance(True)
    for _ in range(ITERS - 2):
        advance(False)
    rights = [spread(split((5.0 * identity - power_ref[slot]) * 0.25)) for slot in slots]
    for slot in slots:
        root_ref[slot] = product(split(root_ref[slot]), rights[slot])
    steps = [product(split(root_ref[2 * n]), grads[n]) for n in range(packs)]
    rights = [spread(split(root_ref[2 * n + 1])) for n in range(packs)]
    steps = [product(split(steps[n]), rights[n]) for n in range(packs)]
    for number, (group, start) in enumerate(places):
        for index in range(pack):
            step = 0.25 * cut(steps[number], index)
            new_weight_ref[group, start + index] = weight_ref[group, start + index] - step


def shampoo(received, weights, stat_left, stat_right, scale, first, earlier=(), norms=()):
    groups = received.shape[1]
    _, count, edge, _ = weights.shape
    slots = 2 * groups * count // min(PACK, count)
    width = min(PACK, count) * edge
    block = pl.BlockSpec(
        (pl.Element(groups), pl.Element(count), pl.Element(edge), pl.Element(edge)),
        lambda i: (first, 0, 0, 0),
    )
    shape = jax.ShapeDtypeStruct(weights.shape, F32)
    norm = pl.BlockSpec((4, D), lambda i: (0, 0))
    norm_outs = 3 if norms else 0
    ins = 4 + len(norms)
    return pl.pallas_call(
        lambda *refs: shampoo_kernel(scale, bool(norms), *refs),
        grid=(1,),
        in_specs=[
            pl.BlockSpec(received.shape, lambda i: (0, 0, 0, 0)),
            *[block] * 3,
            *[norm] * len(norms),
            *[pl.BlockSpec(memory_space=pl.ANY)] * len(earlier),
        ],
        out_specs=[block] * 4 + [norm] * norm_outs,
        out_shape=[shape] * 4 + [jax.ShapeDtypeStruct((4, D), F32)] * norm_outs,
        scratch_shapes=[
            pltpu.VMEM((slots, edge, width), F32),
            pltpu.VMEM((slots, edge, width), F32),
        ],
        input_output_aliases={ins + i: i for i in range(len(earlier))},
        compiler_params=pltpu.CompilerParams(vmem_limit_bytes=SHAMPOO_VMEM),
        cost_estimate=pl.CostEstimate(
            flops=groups * (3 << 30), bytes_accessed=4 << 20, transcendentals=0
        ),
        name="shampoo",
    )(received, weights, stat_left, stat_right, *norms, *earlier)


def swap_heads(values):
    return lax.ppermute(values, "head", [(0, 1), (1, 0)])


def to_all(values, axis):
    return lax.all_to_all(values, axis, 0, 0)


def across(values, apart):
    pairs = [(i, i ^ apart) for i in range(INNER)]
    return lax.ppermute(values, "inner", pairs)


def from_all(values):
    return [values] + [across(values, apart) for apart in range(1, INNER)]


def gather_slabs(weights, small):
    early = to_all(pack(weights, 0, 1), "outer")[:, 0]
    early, late = lax.optimization_barrier((early, pack(weights, 1, 2)))
    late = to_all(late, "outer")
    early = from_all(early)
    early[1], late, small = lax.optimization_barrier((early[1], late, small))
    return early, from_all(late), small


def gather_blocks(local):
    groups, _, edge, _ = local.shape
    blocks = lax.all_gather(local, ("outer", "inner"), axis=1, tiled=True)
    blocks = blocks.reshape(groups, SLABS // INNER, INNER, D // edge, edge, edge)
    slabs = blocks.transpose(2, 1, 0, 4, 3, 5).reshape(SLABS, groups, edge, D)
    return slabs if groups > 1 else slabs[:, 0]


def scatter_blocks(slabs, count, edge):
    groups = slabs.shape[1]
    blocks = slabs.reshape(INNER, SLABS // INNER, groups, edge, D // edge, edge)
    blocks = blocks.transpose(2, 1, 0, 4, 3, 5).reshape(groups, SLABS * (D // edge), edge, edge)
    owned = lax.psum_scatter(blocks, ("outer", "inner"), scatter_dimension=1, tiled=True)
    return owned.transpose(0, 2, 1, 3).reshape(groups, edge, count * edge)


def per_device(
    tokens,
    cotangent,
    token_counts,
    head_mask,
    norm_params,
    norm_state,
    weights,
    stat_left,
    stat_right,
):
    weights, stat_left, stat_right = weights[0], stat_left[0], stat_right[0]
    _, count, edge, _ = weights.shape
    whole_slabs = count * edge == D
    other_mask = swap_heads(head_mask)
    inner = lax.axis_index("inner") if whole_slabs else 0
    place = jnp.concatenate([jnp.stack([lax.axis_index("head"), inner]), token_counts])
    if whole_slabs:
        early, late, (other_mask, place) = gather_slabs(weights, (other_mask, place))
    else:
        local = weights.astype(BF)
        early = jnp.split(gather_blocks(local[:1]), INNER)
        late = jnp.split(gather_blocks(local[1:]), INNER)
    early, late = list(early), list(late)
    masks = (head_mask, other_mask)
    early += [swap_heads(piece) for piece in early]
    prob, qkv, out, middle, second_rows, wqkv, wo = attn_forward(
        place, *masks, tokens, norm_params, early
    )
    late[1:], middle = lax.optimization_barrier((late[1:], middle))
    late += [swap_heads(piece) for piece in late]
    block_out, middle_grad, norm_two, *late_sums = mlp(
        place, middle, second_rows, cotangent, norm_params, late
    )
    own_late, late_received = late_sums[:2], [swap_heads(sent) for sent in late_sums[2:]]
    if whole_slabs:
        far = add_late(own_late[1], late_received[1])
        near = add_late(own_late[0], late_received[0])
        far = [across(far[number], 2 + number) for number in range(2)]
        near, middle_grad = lax.optimization_barrier((list(near), middle_grad))
        late_grads = [near[0], across(near[1], 1), *far]
    dqkv, own_early, sent_early, norm_sums = attn_backward(
        place, *masks, tokens, middle_grad, prob, qkv, out, norm_params, norm_two, wqkv, wo
    )
    if whole_slabs:
        late_grads, sent_early = lax.optimization_barrier((late_grads, sent_early))
    early_received = swap_heads(sent_early)
    devices = lax.axis_size("outer") * lax.axis_size("inner") * lax.axis_size("head")
    scale = 1.0 / math.sqrt(tokens.shape[0] * devices)
    state = (weights, stat_left, stat_right, scale)
    if whole_slabs:
        late_grads = to_all(sum_late(late_grads), "outer")
        early_grads = list(combine(place, own_early, early_received, norm_sums))
        early_grads, dqkv = lax.optimization_barrier((early_grads, dqkv))
        early_grads[1:] = [across(early_grads[apart], apart) for apart in range(1, INNER)]
        input_grad = input_gradient(tokens, middle_grad, dqkv, norm_params, wqkv)
        early_grads, input_grad = lax.optimization_barrier((early_grads, input_grad))
        joined, late_grads = lax.optimization_barrier((join(early_grads), late_grads))
        joined = to_all(joined, "outer")[:, None]
        results = shampoo(late_grads, *state, 1)
        results = shampoo(joined, *state, 0, results, (norm_params, norm_state))
    else:
        input_grad = input_gradient(tokens, middle_grad, dqkv, norm_params, wqkv)
        early_slabs = own_early.astype(F32) + early_received[:SLABS].astype(F32)
        late_slabs = jnp.concatenate(own_late).astype(F32) + jnp.concatenate(late_received)
        late_slabs = late_slabs.reshape(SLABS, 2, edge, D)
        slabs = jnp.concatenate([early_slabs[:, None], late_slabs], axis=1).astype(BF)
        owned = scatter_blocks(slabs, count, edge)
        results = list(shampoo(owned[None], *state, 0))
        norm_grads = lax.psum(norm_sums, ("outer", "inner", "head")) * scale
        state_new = 0.5 * norm_state + 0.5 * norm_grads * norm_grads
        results += [norm_grads, state_new, norm_params - 0.2 * norm_grads / jnp.sqrt(state_new)]
    return (block_out, input_grad, *[result[None] for result in results[:4]], *results[4:])


def solution(mesh):
    shape = (mesh.shape["dp"] // INNER, INNER, mesh.shape["head"])
    split_mesh = Mesh(mesh.devices.reshape(shape), ("outer", "inner", "head"))
    group = ("outer", "inner")
    blocks = P("head", None, group, None, None)
    rows = P(group + ("head",), None)
    return jax.shard_map(
        per_device,
        mesh=split_mesh,
        in_specs=(rows, rows, P(group), P(group, "head"), P(), P(), blocks, blocks, blocks),
        out_specs=(rows, rows, blocks, blocks, blocks, blocks, P(), P(), P()),
        check_vma=False,
    )
```

```python
import math

import jax
import jax.numpy as jnp
from jax import lax
from jax.experimental import pallas as pl
from jax.experimental.pallas import tpu as pltpu
from jax.sharding import Mesh, PartitionSpec as P

D = 384
HEAD_DIM = 64
MLP = 1536
S = 256
ITERS = 8
PAIR = 2 * HEAD_DIM
PAIRS = D // PAIR
HALF = D // 2
SLABS = 16
INNER = 4
OUTER = SLABS // INNER
TILE = 512
INPUT_TILE = 768
IMAGES = TILE // S
NORM_ROWS = 8
PACK = 2
ROOT_HALF = 0.7071067811865476
DENSITY_FACTOR = 0.3989422804014327
BF = jnp.bfloat16
F32 = jnp.float32
VMEM_LIMIT = 40 << 20
SMALL_VMEM = 8 << 20
SHAMPOO_VMEM = 24 << 20


def in_hbm(values):
    return pltpu.with_memory_space_constraint(values, pltpu.HBM)


def nn(left, right):
    return jnp.dot(left, right, preferred_element_type=F32)


def nt(left, right):
    return lax.dot_general(left, right, (((1,), (1,)), ((), ())), preferred_element_type=F32)


def tn(left, right):
    return lax.dot_general(left, right, (((0,), (0,)), ((), ())), preferred_element_type=F32)


def normalize(values):
    centered = values - jnp.mean(values, axis=-1, keepdims=True)
    variance = jnp.mean(centered * centered, axis=-1, keepdims=True)
    inverse_std = lax.rsqrt(variance + 1e-06)
    return centered * inverse_std, inverse_std


def norm_backward(grad_out, normed, inverse_std, gain):
    grad_normed = grad_out * gain
    mean_first = jnp.mean(grad_normed, axis=-1, keepdims=True)
    mean_second = jnp.mean(grad_normed * normed, axis=-1, keepdims=True)
    grad_in = inverse_std * (grad_normed - mean_first - normed * mean_second)
    gain_grad = jnp.sum(grad_out * normed, axis=0, keepdims=True)
    shift_grad = jnp.sum(grad_out, axis=0, keepdims=True)
    return grad_in, jnp.concatenate([gain_grad, shift_grad], axis=0)


def grown(step, total, part):
    return jnp.where(step == 0, part, total + part)


def slab_at(owner):
    return (owner % INNER) * OUTER + owner // INNER


def lane_halves():
    lane = lax.broadcasted_iota(jnp.int32, (1, PAIR), 1)
    first = (lane < HEAD_DIM).astype(BF)
    return first, (1 - first).astype(BF)


def stacked(values, first, second):
    return jnp.concatenate([values * first, values * second], axis=0)


def mask_lanes(place_ref, own_ref, other_ref, image, pair):
    image = place_ref[0] * (own_ref.shape[0] // 2) + image
    heads = own_ref.shape[1]
    on = [
        own_ref[image, head] if head < heads else other_ref[image, head - heads]
        for head in (2 * pair, 2 * pair + 1)
    ]
    lane = lax.broadcasted_iota(jnp.int32, (1, PAIR), 1)
    return jnp.where(lane < HEAD_DIM, on[0], on[1]).astype(F32)


def attn_forward_kernel(
    place_ref, own_mask_ref, other_mask_ref, x_ref, norm_ref, *refs
):
    slab_refs, refs = refs[: 2 * INNER], refs[2 * INNER :]
    prob_ref, qkv_ref, out_ref, middle_ref, rows_ref, wqkv_ref, wo_ref, held_ref = refs
    step = pl.program_id(0)

    @pl.when(step == 0)
    def _():
        for number, ref in enumerate(slab_refs):
            side, apart = divmod(number, INNER)
            held_ref[side, place_ref[1] ^ apart] = ref[...]

        def slab_of(side, owner):
            return held_ref[side, owner % INNER, owner // INNER]

        for row in range(D // 48):
            for part in range(3):
                pieces = []
                for number in range(2):
                    slab, side = divmod(3 * row + part, 2)
                    piece = slab_of(number, slab)[:, side * HALF : (side + 1) * HALF]
                    pieces.append(piece)
                joined = jnp.concatenate(pieces, axis=1)
                if part == 0:
                    joined = joined * 0.125
                wqkv_ref[48 * row : 48 * row + 48, D * part : D * part + D] = joined
        for side in range(2):
            for row in range(HALF // 48):
                start = side * HALF + 48 * row
                wo_ref[start : start + 48, :] = slab_of(side, 12 + row)

    x = x_ref[...].astype(F32)
    normed, _ = normalize(x)
    rows = (normed * norm_ref[0:1, :] + norm_ref[1:2, :]).astype(BF)
    qkv_ref[...] = nn(rows, wqkv_ref[...]).astype(BF)
    first, second = lane_halves()
    column = lax.broadcasted_iota(jnp.int32, (1, S), 1)
    tasks = [(image, pair) for image in range(IMAGES) for pair in range(PAIRS)]

    def places(task):
        image, pair = task
        here = slice(S * image, S * image + S)
        return here, *(slice(D * t + PAIR * pair, D * t + PAIR * (pair + 1)) for t in range(3))

    def get_scores(task):
        here, query_lanes, key_lanes, _ = places(task)
        return nt(stacked(qkv_ref[here, query_lanes], first, second), qkv_ref[here, key_lanes])

    def get_prob(task, scores):
        image = place_ref[0] * (own_mask_ref.shape[0] // 2) + IMAGES * step + task[0]
        scores = jnp.where(column < place_ref[2 + image], scores, -1e30)
        top = jnp.max(scores, axis=-1, keepdims=True)
        exp_scores = jnp.exp(scores - top)
        total = jnp.sum(exp_scores, axis=-1, keepdims=True)
        prob = (exp_scores * (1.0 / total)).astype(BF)
        prob_ref[task] = prob
        return prob

    all_scores = [get_scores(task) for task in tasks]
    probs = [get_prob(task, scores) for task, scores in zip(tasks, all_scores)]
    for task, prob in zip(tasks, probs):
        here, lanes, _, value_lanes = places(task)
        values = qkv_ref[here, value_lanes]
        head_out = nn(prob[:S], values * first) + nn(prob[S:], values * second)
        mask = mask_lanes(place_ref, own_mask_ref, other_mask_ref, IMAGES * step + task[0], task[1])
        out_ref[here, lanes] = (head_out * mask).astype(BF)
    middle = x + nn(out_ref[...], wo_ref[...])
    middle_ref[...] = middle
    normed, _ = normalize(middle)
    rows_ref[...] = (normed * norm_ref[2:3, :] + norm_ref[3:4, :]).astype(BF)


def attn_forward(place, own_mask, other_mask, tokens, norm_params, slabs):
    rows = tokens.shape[0]
    images = rows // S
    tile = pl.BlockSpec((TILE, D), lambda i: (i, 0))
    slab = pl.BlockSpec((OUTER, 48, D), lambda i: (0, 0, 0))
    smem = pl.BlockSpec(memory_space=pltpu.SMEM)
    return pl.pallas_call(
        attn_forward_kernel,
        grid=(rows // TILE,),
        in_specs=[smem] * 3 + [tile, pl.BlockSpec((4, D), lambda i: (0, 0))] + [slab] * 2 * INNER,
        out_specs=[
            pl.BlockSpec((IMAGES, PAIRS, 2 * S, S), lambda i: (i, 0, 0, 0)),
            pl.BlockSpec((TILE, 3 * D), lambda i: (i, 0)),
            tile,
            tile,
            tile,
            pl.BlockSpec((D, 3 * D), lambda i: (0, 0)),
            pl.BlockSpec((D, D), lambda i: (0, 0)),
        ],
        out_shape=[
            pltpu.HBM((images, PAIRS, 2 * S, S), BF),
            pltpu.HBM((rows, 3 * D), BF),
            pltpu.HBM((rows, D), BF),
            jax.ShapeDtypeStruct((rows, D), F32),
            jax.ShapeDtypeStruct((rows, D), BF),
            pltpu.HBM((D, 3 * D), BF),
            pltpu.HBM((D, D), BF),
        ],
        scratch_shapes=[pltpu.VMEM((2, INNER, OUTER, 48, D), BF)],
        compiler_params=pltpu.CompilerParams(vmem_limit_bytes=VMEM_LIMIT),
        cost_estimate=pl.CostEstimate(
            flops=rows * D * (8 * D + 16 * S), bytes_accessed=16 << 20, transcendentals=rows * 6 * S
        ),
        name="attn_forward",
    )(place, own_mask, other_mask, in_hbm(tokens), in_hbm(norm_params), *slabs)


def mlp_kernel(place_ref, middle_ref, rows_ref, cot_ref, norm_ref, *refs):
    slab_refs, refs = refs[: 2 * INNER], refs[2 * INNER :]
    out_ref, grad_ref, norm_grad_ref, *refs = refs
    own_refs, sent_refs, refs = refs[:2], refs[2:4], refs[4:]
    up_ref, down_ref, up_grad_ref, down_grad_ref = refs
    step = pl.program_id(0)
    half = MLP // 2

    def places(apart, outer):
        inner = place_ref[1] ^ apart
        row = pl.multiple_of(48 * (2 * outer + inner // 2), 16)
        lane = pl.multiple_of(D * (inner % 2), 128)
        down_row = pl.multiple_of(48 * (INNER * outer + inner), 16)
        return row, lane, down_row

    @pl.when(step == 0)
    def _():
        for number, ref in enumerate(slab_refs):
            side, apart = divmod(number, INNER)
            for outer in range(OUTER):
                row, lane, down_row = places(apart, outer)
                up_ref[side, pl.ds(row, 48), pl.ds(lane, D)] = ref[outer, 0]
                down_ref[side, pl.ds(down_row, 48), :] = ref[outer, 1]

    middle = middle_ref[...]
    normed, inverse_std = normalize(middle)
    rows, cot = rows_ref[...], cot_ref[...]
    total = middle
    back = None
    for side in range(2):
        up, down = up_ref[side], down_ref[side]
        pre = nn(rows, up)
        act_grad = nt(cot, down)
        cumulative = 0.5 * (1.0 + lax.erf(pre * ROOT_HALF))
        density = jnp.exp(-0.5 * pre * pre) * DENSITY_FACTOR
        act = (pre * cumulative).astype(BF)
        pre_grad = (act_grad * (cumulative + pre * density)).astype(BF)
        total = total + nn(act, down)
        term = nt(pre_grad, up)
        back = term if back is None else back + term
        down_grad_ref[side] = grown(step, down_grad_ref[side], tn(act, cot))
        up_grad_ref[side] = grown(step, up_grad_ref[side], tn(rows, pre_grad))
    out_ref[...] = total
    grad_in, norm_part = norm_backward(back, normed, inverse_std, norm_ref[2:3, :])
    norm_grad_ref[...] = grown(step, norm_grad_ref[...], norm_part)
    grad_ref[...] = cot.astype(F32) + grad_in

    @pl.when(step == pl.num_programs(0) - 1)
    def _():
        for apart in range(INNER):
            for outer in range(OUTER):
                row, lane, down_row = places(apart, outer)
                for side, halves in enumerate((own_refs, sent_refs)):
                    ref = halves[apart // 2]
                    up = up_grad_ref[side, pl.ds(row, 48), pl.ds(lane, D)]
                    down = down_grad_ref[side, pl.ds(down_row, 48), :]
                    ref[apart % 2, outer, 0] = up.astype(BF)
                    ref[apart % 2, outer, 1] = down.astype(BF)


def mlp(place, middle, second_rows, cotangent, norm_params, slabs):
    rows = middle.shape[0]
    slab = pl.BlockSpec((OUTER, 2, 48, D), lambda i: (0, 0, 0, 0))
    grads = (INNER // 2, OUTER, 2, 48, D)
    grad = pl.BlockSpec(grads, lambda i: (0, 0, 0, 0, 0))
    tile = pl.BlockSpec((TILE, D), lambda i: (i, 0))
    return pl.pallas_call(
        mlp_kernel,
        grid=(rows // TILE,),
        in_specs=[
            pl.BlockSpec(memory_space=pltpu.SMEM),
            tile,
            tile,
            tile,
            pl.BlockSpec((4, D), lambda i: (0, 0)),
            *[slab] * 2 * INNER,
        ],
        out_specs=[tile, tile, pl.BlockSpec((2, D), lambda i: (0, 0)), *[grad] * 4],
        out_shape=[
            jax.ShapeDtypeStruct((rows, D), F32),
            pltpu.HBM((rows, D), F32),
            jax.ShapeDtypeStruct((2, D), F32),
            *[jax.ShapeDtypeStruct(grads, BF)] * 4,
        ],
        scratch_shapes=[
            pltpu.VMEM((2, D, MLP // 2), BF),
            pltpu.VMEM((2, MLP // 2, D), BF),
            pltpu.VMEM((2, D, MLP // 2), F32),
            pltpu.VMEM((2, MLP // 2, D), F32),
        ],
        compiler_params=pltpu.CompilerParams(vmem_limit_bytes=VMEM_LIMIT),
        cost_estimate=pl.CostEstimate(
            flops=12 * rows * D * MLP, bytes_accessed=20 << 20, transcendentals=2 * rows * MLP
        ),
        name="mlp",
    )(place, middle, second_rows, *map(in_hbm, (cotangent, norm_params)), *slabs)


def attn_backward_kernel(
    place_ref, own_mask_ref, other_mask_ref, x_ref, grad_ref, prob_ref, qkv_ref, out_ref,
    norm_ref, later_norm_ref, wqkv_ref, wo_ref,
    dqkv_ref, own_grad_ref, sent_grad_ref, norm_grad_ref,
    cross_ref, column_ref, wo_grad_ref,
):
    step = pl.program_id(0)

    normed, _ = normalize(x_ref[...].astype(F32))
    low_grad = grad_ref[...].astype(BF)
    head_out = out_ref[...]
    wo_grad_ref[...] = grown(step, wo_grad_ref[...], tn(head_out, low_grad))
    whole_grad = nt(low_grad, wo_ref[...]).astype(BF)
    first, second = lane_halves()
    first_wide, second_wide = first.astype(F32), second.astype(F32)
    tasks = [(image, pair) for image in range(IMAGES) for pair in range(PAIRS)]

    def places(task):
        image, pair = task
        here = slice(S * image, S * image + S)
        return here, *(slice(D * t + PAIR * pair, D * t + PAIR * (pair + 1)) for t in range(3))

    def get_pair_grad(task):
        here, lanes, _, _ = places(task)
        mask = mask_lanes(place_ref, own_mask_ref, other_mask_ref, IMAGES * step + task[0], task[1])
        grad = whole_grad[here, lanes] * mask.astype(BF)
        dots = grad.astype(F32) * head_out[here, lanes].astype(F32)
        first_dot = jnp.sum(dots * first_wide, axis=-1, keepdims=True)
        second_dot = jnp.sum(dots * second_wide, axis=-1, keepdims=True)
        return stacked(grad, first, second), jnp.concatenate([first_dot, second_dot], axis=0)

    pair_grads = [get_pair_grad(task) for task in tasks]
    prob_grads = [
        nt(pair_grad[0], qkv_ref[places(task)[0], places(task)[3]])
        for task, pair_grad in zip(tasks, pair_grads)
    ]
    score_grads = [
        (prob_ref[task].astype(F32) * (prob_grad - pair_grad[1])).astype(BF)
        for task, prob_grad, pair_grad in zip(tasks, prob_grads, pair_grads)
    ]
    for task, score_grad, (pair_grad, _) in zip(tasks, score_grads, pair_grads):
        here, query_lanes, key_lanes, value_lanes = places(task)
        keys = qkv_ref[here, key_lanes]
        queries = stacked(qkv_ref[here, query_lanes], first, second)
        query_grad = nn(score_grad[:S], keys * first) + nn(score_grad[S:], keys * second)
        key_grad = nn(jnp.transpose(queries), score_grad)
        value_grad = nn(jnp.transpose(pair_grad), prob_ref[task])
        dqkv_ref[here, query_lanes] = query_grad.astype(BF)
        dqkv_ref[here, key_lanes] = jnp.transpose(key_grad).astype(BF)
        dqkv_ref[here, value_lanes] = jnp.transpose(value_grad).astype(BF)
    dqkv = dqkv_ref[...]
    cross_ref[...] = grown(step, cross_ref[...], tn(normed.astype(BF), dqkv))
    columns = jnp.sum(dqkv.astype(F32), axis=0, keepdims=True)
    column_ref[...] = grown(step, column_ref[...], columns)

    @pl.when(step == pl.num_programs(0) - 1)
    def _():
        wqkv = wqkv_ref[...]
        products = wqkv.astype(F32) * cross_ref[...]
        gain_grad = jnp.sum(products, axis=1, keepdims=True)
        gain_grad = jnp.transpose(jnp.broadcast_to(gain_grad, (D, 128)))
        columns = column_ref[...]
        shift_grad = nt(jnp.concatenate(split(jnp.broadcast_to(columns, (8, 3 * D)))), wqkv)
        norm_grad_ref[0:1, :] = gain_grad[0:1]
        norm_grad_ref[1:2, :] = shift_grad[0:1] + shift_grad[8:9]
        norm_grad_ref[2:4, :] = later_norm_ref[...]
        gain = jnp.transpose(jnp.broadcast_to(norm_ref[0:1, :], (128, D)))[:, :1]
        shift = jnp.transpose(jnp.broadcast_to(norm_ref[1:2, :], (128, D)))[:, :1]
        cross_ref[...] = cross_ref[...] * gain + shift * columns
        for side, slab_grads in enumerate((own_grad_ref, sent_grad_ref)):
            for slab in range(12):
                pieces = []
                for unit in (2 * slab, 2 * slab + 1):
                    row, part = divmod(unit, 3)
                    piece = cross_ref[48 * row : 48 * row + 48, D * part : D * part + D]
                    piece = piece[:, HALF * side : HALF * side + HALF]
                    pieces.append(piece * 0.125 if part == 0 else piece)
                slab_grads[slab_at(slab)] = jnp.concatenate(pieces, axis=1).astype(BF)
            for row in range(HALF // 48):
                start = HALF * side + 48 * row
                slab_grads[slab_at(12 + row)] = wo_grad_ref[start : start + 48, :].astype(BF)
        sent_grad_ref[SLABS, :NORM_ROWS] = jnp.concatenate(split(norm_grad_ref[...]), axis=0)
        sent_grad_ref[SLABS, NORM_ROWS:] = jnp.zeros((48 - NORM_ROWS, D), BF)


def attn_backward(
    place, own_mask, other_mask, tokens, grad, prob, qkv, out, norm_params, later_norms, wqkv, wo
):
    rows = tokens.shape[0]
    tile = pl.BlockSpec((TILE, D), lambda i: (i, 0))
    smem = pl.BlockSpec(memory_space=pltpu.SMEM)
    return pl.pallas_call(
        attn_backward_kernel,
        grid=(rows // TILE,),
        in_specs=[
            smem,
            smem,
            smem,
            tile,
            tile,
            pl.BlockSpec((IMAGES, PAIRS, 2 * S, S), lambda i: (i, 0, 0, 0)),
            pl.BlockSpec((TILE, 3 * D), lambda i: (i, 0)),
            tile,
            pl.BlockSpec((4, D), lambda i: (0, 0)),
            pl.BlockSpec((2, D), lambda i: (0, 0)),
            pl.BlockSpec((D, 3 * D), lambda i: (0, 0)),
            pl.BlockSpec((D, D), lambda i: (0, 0)),
        ],
        out_specs=[
            pl.BlockSpec((TILE, 3 * D), lambda i: (i, 0)),
            pl.BlockSpec((SLABS, 48, D), lambda i: (0, 0, 0)),
            pl.BlockSpec((SLABS + 1, 48, D), lambda i: (0, 0, 0)),
            pl.BlockSpec((4, D), lambda i: (0, 0)),
        ],
        out_shape=[
            pltpu.HBM((rows, 3 * D), BF),
            jax.ShapeDtypeStruct((SLABS, 48, D), BF),
            jax.ShapeDtypeStruct((SLABS + 1, 48, D), BF),
            jax.ShapeDtypeStruct((4, D), F32),
        ],
        scratch_shapes=[
            pltpu.VMEM((D, 3 * D), F32),
            pltpu.VMEM((1, 3 * D), F32),
            pltpu.VMEM((D, D), F32),
        ],
        compiler_params=pltpu.CompilerParams(vmem_limit_bytes=VMEM_LIMIT),
        cost_estimate=pl.CostEstimate(
            flops=rows * D * (10 * D + 32 * S), bytes_accessed=20 << 20, transcendentals=0
        ),
        name="attn_backward",
    )(
        place, own_mask, other_mask,
        in_hbm(tokens), in_hbm(grad), *map(in_hbm, (prob, qkv, out, norm_params, later_norms)), in_hbm(wqkv), in_hbm(wo),
    )


def input_grad_kernel(x_ref, grad_ref, dqkv_ref, norm_ref, wqkv_ref, out_ref):
    normed, inverse_std = normalize(x_ref[...].astype(F32))
    back = nt(dqkv_ref[...], wqkv_ref[...]) * norm_ref[0:1, :]
    mean_first = jnp.mean(back, axis=-1, keepdims=True)
    mean_second = jnp.mean(back * normed, axis=-1, keepdims=True)
    out_ref[...] = grad_ref[...] + inverse_std * (back - mean_first - normed * mean_second)


def input_gradient(tokens, grad, dqkv, norm_params, wqkv):
    rows = tokens.shape[0]
    tile = pl.BlockSpec((INPUT_TILE, D), lambda i: (i, 0))
    return pl.pallas_call(
        input_grad_kernel,
        grid=(rows // INPUT_TILE,),
        in_specs=[
            tile,
            tile,
            pl.BlockSpec((INPUT_TILE, 3 * D), lambda i: (i, 0)),
            pl.BlockSpec((4, D), lambda i: (0, 0)),
            pl.BlockSpec((D, 3 * D), lambda i: (0, 0)),
        ],
        out_specs=tile,
        out_shape=jax.ShapeDtypeStruct((rows, D), F32),
        compiler_params=pltpu.CompilerParams(vmem_limit_bytes=VMEM_LIMIT),
        cost_estimate=pl.CostEstimate(
            flops=rows * D * 6 * D, bytes_accessed=10 << 20, transcendentals=0
        ),
        name="input_gradient",
    )(in_hbm(tokens), in_hbm(grad), in_hbm(dqkv), in_hbm(norm_params), in_hbm(wqkv))


def pack_kernel(weight_ref, out_ref):
    groups, count, _, _ = weight_ref.shape
    for group in range(groups):
        blocks = [weight_ref[group, block] for block in range(count)]
        slab = jnp.concatenate(blocks, axis=1).astype(BF)
        for copy in range(OUTER):
            out_ref[copy, group] = slab


def pack(weights, first, groups):
    _, count, edge, _ = weights.shape
    shape = (OUTER, groups, edge, count * edge)
    return pl.pallas_call(
        pack_kernel,
        grid=(1,),
        in_specs=[
            pl.BlockSpec(
                (pl.Element(groups), pl.Element(count), pl.Element(edge), pl.Element(edge)),
                lambda i: (first, 0, 0, 0),
            )
        ],
        out_specs=pl.BlockSpec(shape, lambda i: (0, 0, 0, 0)),
        out_shape=jax.ShapeDtypeStruct(shape, BF),
        compiler_params=pltpu.CompilerParams(vmem_limit_bytes=SMALL_VMEM),
        name="pack",
    )(in_hbm(weights))


def add_kernel(own_ref, received_ref, *out_refs):
    for apart, out_ref in enumerate(out_refs):
        total = own_ref[apart].astype(F32) + received_ref[apart].astype(F32)
        out_ref[...] = total.astype(BF)


def add_late(own, received):
    return pl.pallas_call(
        add_kernel,
        out_shape=[jax.ShapeDtypeStruct(own.shape[1:], BF)] * own.shape[0],
        compiler_params=pltpu.CompilerParams(vmem_limit_bytes=SMALL_VMEM),
        name="add_late",
    )(own, received)


def sum_kernel(*refs):
    *in_refs, out_ref = refs
    total = in_refs[0][...].astype(F32)
    for ref in in_refs[1:]:
        total = total + ref[...].astype(F32)
    out_ref[...] = total.astype(BF)


def sum_late(pieces):
    return pl.pallas_call(
        sum_kernel,
        out_shape=jax.ShapeDtypeStruct(pieces[0].shape, BF),
        compiler_params=pltpu.CompilerParams(vmem_limit_bytes=SMALL_VMEM),
        name="sum_late",
    )(*pieces)


def combine_kernel(place_ref, own_ref, received_ref, norm_ref, *out_refs):
    norms = received_ref[SLABS, :NORM_ROWS].astype(F32)
    norms = norm_ref[...] + (norms[:4] + norms[4:])
    rows = jnp.concatenate(split(norms), axis=0)
    for apart, out_ref in enumerate(out_refs):
        start = OUTER * (place_ref[1] ^ apart)
        for outer in range(OUTER):
            total = own_ref[start + outer].astype(F32) + received_ref[start + outer].astype(F32)
            out_ref[48 * outer : 48 * outer + 48, :] = total.astype(BF)
        out_ref[48 * OUTER :, :] = rows


def combine(place, own, received, norms):
    vmem = pl.BlockSpec(memory_space=pltpu.VMEM)
    shape = jax.ShapeDtypeStruct((48 * OUTER + NORM_ROWS, D), BF)
    return pl.pallas_call(
        combine_kernel,
        in_specs=[pl.BlockSpec(memory_space=pltpu.SMEM), vmem, vmem, vmem],
        out_shape=[shape] * INNER,
        compiler_params=pltpu.CompilerParams(vmem_limit_bytes=SMALL_VMEM),
        name="combine",
    )(place, own, received, norms)


def join_kernel(*refs):
    *early_refs, out_ref = refs
    total = early_refs[0][...].astype(F32)
    for ref in early_refs[1:]:
        total = total + ref[...].astype(F32)
    norms = total[48 * OUTER : 48 * OUTER + 4] + total[48 * OUTER + 4 :]
    for outer in range(OUTER):
        out_ref[outer, :48] = total[48 * outer : 48 * outer + 48].astype(BF)
        out_ref[outer, 48:] = jnp.concatenate(split(norms), axis=0)


def join(early):
    return pl.pallas_call(
        join_kernel,
        out_shape=jax.ShapeDtypeStruct((OUTER, 48 + NORM_ROWS, D), BF),
        compiler_params=pltpu.CompilerParams(vmem_limit_bytes=SMALL_VMEM),
        name="join",
    )(*early)


def split(values):
    high = values.astype(BF)
    return high, (values - high.astype(F32)).astype(BF)


def stack(*pieces):
    return jnp.concatenate(pieces, axis=0)


def cut_rows(values, number):
    edge = values.shape[0] // number
    return [values[edge * i : edge * i + edge] for i in range(number)]


def product(left, right):
    high, low = left
    right_high, right_low = right
    one, two = cut_rows(nn(stack(high, low), right_high), 2)
    return one + (two + nn(high, right_low))


def two_products(left, middle, right):
    right_high, right_low = right
    both = cut_rows(nn(stack(left[0], middle[0], left[1], middle[1]), right_high), 4)
    high = cut_rows(nn(stack(left[0], middle[0]), right_low), 2)
    return both[0] + (both[2] + high[0]), both[1] + (both[3] + high[1])


def update_norms(scale, total, param_ref, state_ref, grad_ref, new_state_ref, new_ref):
    grads = total * scale
    state = 0.5 * state_ref[...] + 0.5 * grads * grads
    grad_ref[...] = grads
    new_state_ref[...] = state
    new_ref[...] = param_ref[...] - 0.2 * grads / jnp.sqrt(state)


def shampoo_kernel(scale, with_norms, received_ref, weight_ref, left_ref, right_ref, *refs):
    if with_norms:
        norm_ins, norm_outs, refs = refs[:2], refs[-5:-2], refs[:-5] + refs[-2:]
    out_grad_ref, left_new_ref, right_new_ref, new_weight_ref, root_ref, power_ref = refs[-6:]
    groups, count, edge = weight_ref.shape[:3]

    received = received_ref[0].astype(F32)
    for number in range(1, received_ref.shape[0]):
        received = received + received_ref[number].astype(F32)
    if with_norms:
        norms = received[0, edge:]
        update_norms(scale, norms[:4] + norms[4:], *norm_ins, *norm_outs)
    pack = min(PACK, count)
    width = pack * edge
    places = [(g, pack * n) for g in range(groups) for n in range(count // pack)]
    packs = len(places)

    def block_of(shape, dim):
        return lax.broadcasted_iota(jnp.int32, shape, dim) // edge

    row = lax.broadcasted_iota(jnp.int32, (edge, width), 0)
    lane = lax.broadcasted_iota(jnp.int32, (edge, width), 1)
    identity = (lane % edge == row).astype(F32)
    same = (block_of((width, width), 0) == block_of((width, width), 1)).astype(BF)
    lane_block = block_of((1, width), 1)

    def spread(pieces):
        return tuple(stack(*[piece] * pack) * same for piece in pieces)

    def cut(packed, index):
        return packed[:, edge * index : edge * index + edge]

    def beside(ref, place):
        return jnp.concatenate([ref[place[0], place[1] + i] for i in range(pack)], axis=1)

    grads, parts = [], []
    for group, start in places:
        grad = received[group, :edge, edge * start : edge * start + width] * scale
        blocks = [cut(grad, index) for index in range(pack)]
        for index in range(pack):
            out_grad_ref[group, start + index] = blocks[index]
        grad_t = jnp.concatenate([jnp.transpose(block) for block in blocks], axis=1)
        one, two = split(grad), split(grad_t)
        one_diagonal, two_diagonal = spread(one), spread(two)
        grads.append(one_diagonal)
        parts.append((left_ref, left_new_ref, one, two_diagonal))
        parts.append((right_ref, right_new_ref, two, one_diagonal))
    grams = [product(left, right) for _, _, left, right in parts]
    for slot, (old_ref, new_ref, _, _) in enumerate(parts):
        group, start = places[slot // 2]
        new = 0.5 * beside(old_ref, places[slot // 2]) + 0.5 * grams[slot]
        for index in range(pack):
            new_ref[group, start + index] = cut(new, index)
        columns = jnp.sum(new * new, axis=0, keepdims=True)
        squares = jnp.zeros((1, width), F32)
        for index in range(pack):
            inside = lane_block == index
            part = jnp.sum(jnp.where(inside, columns, 0.0), axis=1, keepdims=True)
            squares = jnp.where(inside, part, squares)
        factor = 2.5 / jnp.sqrt(squares)
        root_ref[slot] = jnp.broadcast_to(jnp.sqrt(jnp.sqrt(factor)), (edge, width))
        power_ref[slot] = factor * new
    slots = range(2 * packs)

    def advance(first):
        powers = [power_ref[slot] for slot in slots]
        middles = [split((5.0 * identity - power) * 0.25) for power in powers]
        rights = [spread(middle) for middle in middles]
        powers = [split(power) for power in powers]
        if first:
            squares = [product(middles[s], rights[s]) for s in slots]
            for slot in slots:
                root_ref[slot] *= (5.0 * identity - power_ref[slot]) * 0.25
        else:
            roots = [split(root_ref[slot]) for slot in slots]
            both = [two_products(roots[s], middles[s], rights[s]) for s in slots]
            squares = [pair[1] for pair in both]
            for slot in slots:
                root_ref[slot] = both[slot][0]
        rights = [spread(split(square)) for square in squares]
        powers = [split(product(powers[s], rights[s])) for s in slots]
        for slot in slots:
            power_ref[slot] = product(powers[slot], rights[slot])

    advance(True)
    for _ in range(ITERS - 2):
        advance(False)
    rights = [spread(split((5.0 * identity - power_ref[slot]) * 0.25)) for slot in slots]
    for slot in slots:
        root_ref[slot] = product(split(root_ref[slot]), rights[slot])
    steps = [product(split(root_ref[2 * n]), grads[n]) for n in range(packs)]
    rights = [spread(split(root_ref[2 * n + 1])) for n in range(packs)]
    steps = [product(split(steps[n]), rights[n]) for n in range(packs)]
    for number, (group, start) in enumerate(places):
        for index in range(pack):
            step = 0.25 * cut(steps[number], index)
            new_weight_ref[group, start + index] = weight_ref[group, start + index] - step


def shampoo(received, weights, stat_left, stat_right, scale, first, earlier=(), norms=()):
    groups = received.shape[1]
    _, count, edge, _ = weights.shape
    slots = 2 * groups * count // min(PACK, count)
    width = min(PACK, count) * edge
    block = pl.BlockSpec(
        (pl.Element(groups), pl.Element(count), pl.Element(edge), pl.Element(edge)),
        lambda i: (first, 0, 0, 0),
    )
    shape = jax.ShapeDtypeStruct(weights.shape, F32)
    norm = pl.BlockSpec((4, D), lambda i: (0, 0))
    norm_outs = 3 if norms else 0
    ins = 4 + len(norms)
    return pl.pallas_call(
        lambda *refs: shampoo_kernel(scale, bool(norms), *refs),
        grid=(1,),
        in_specs=[
            pl.BlockSpec(received.shape, lambda i: (0, 0, 0, 0)),
            *[block] * 3,
            *[norm] * len(norms),
            *[pl.BlockSpec(memory_space=pl.ANY)] * len(earlier),
        ],
        out_specs=[block] * 4 + [norm] * norm_outs,
        out_shape=[shape] * 4 + [jax.ShapeDtypeStruct((4, D), F32)] * norm_outs,
        scratch_shapes=[
            pltpu.VMEM((slots, edge, width), F32),
            pltpu.VMEM((slots, edge, width), F32),
        ],
        input_output_aliases={ins + i: i for i in range(len(earlier))},
        compiler_params=pltpu.CompilerParams(vmem_limit_bytes=SHAMPOO_VMEM),
        cost_estimate=pl.CostEstimate(
            flops=groups * (3 << 30), bytes_accessed=4 << 20, transcendentals=0
        ),
        name="shampoo",
    )(received, weights, stat_left, stat_right, *norms, *earlier)


def swap_heads(values):
    return lax.ppermute(values, "head", [(0, 1), (1, 0)])


def to_all(values, axis):
    return lax.all_to_all(values, axis, 0, 0)


def across(values, apart):
    pairs = [(i, i ^ apart) for i in range(INNER)]
    return lax.ppermute(values, "inner", pairs)


def from_all(values):
    return [values] + [across(values, apart) for apart in range(1, INNER)]


def gather_slabs(weights, small):
    _, count, edge, _ = weights.shape
    early = weights[0].astype(BF).transpose(1, 0, 2).reshape(1, edge, count * edge)
    early = to_all(jnp.broadcast_to(early, (OUTER, edge, count * edge)), "outer")
    early, late = lax.optimization_barrier((early, pack(weights, 1, 2)))
    late = to_all(late, "outer")
    early = from_all(early)
    early[1], late, small = lax.optimization_barrier((early[1], late, small))
    return early, from_all(late), small


def gather_blocks(local):
    groups, _, edge, _ = local.shape
    blocks = lax.all_gather(local, ("outer", "inner"), axis=1, tiled=True)
    blocks = blocks.reshape(groups, SLABS // INNER, INNER, D // edge, edge, edge)
    slabs = blocks.transpose(2, 1, 0, 4, 3, 5).reshape(SLABS, groups, edge, D)
    return slabs if groups > 1 else slabs[:, 0]


def scatter_blocks(slabs, count, edge):
    groups = slabs.shape[1]
    blocks = slabs.reshape(INNER, SLABS // INNER, groups, edge, D // edge, edge)
    blocks = blocks.transpose(2, 1, 0, 4, 3, 5).reshape(groups, SLABS * (D // edge), edge, edge)
    owned = lax.psum_scatter(blocks, ("outer", "inner"), scatter_dimension=1, tiled=True)
    return owned.transpose(0, 2, 1, 3).reshape(groups, edge, count * edge)


def per_device(
    tokens,
    cotangent,
    token_counts,
    head_mask,
    norm_params,
    norm_state,
    weights,
    stat_left,
    stat_right,
):
    weights, stat_left, stat_right = weights[0], stat_left[0], stat_right[0]
    _, count, edge, _ = weights.shape
    whole_slabs = count * edge == D
    other_mask = swap_heads(head_mask)
    inner = lax.axis_index("inner") if whole_slabs else 0
    place = jnp.concatenate([jnp.stack([lax.axis_index("head"), inner]), token_counts])
    if whole_slabs:
        early, late, (other_mask, place) = gather_slabs(weights, (other_mask, place))
    else:
        local = weights.astype(BF)
        early = jnp.split(gather_blocks(local[:1]), INNER)
        late = jnp.split(gather_blocks(local[1:]), INNER)
    early, late = list(early), list(late)
    masks = (head_mask, other_mask)
    early += [swap_heads(piece) for piece in early]
    prob, qkv, out, middle, second_rows, wqkv, wo = attn_forward(
        place, *masks, tokens, norm_params, early
    )
    late[1:], middle = lax.optimization_barrier((late[1:], middle))
    late += [swap_heads(piece) for piece in late]
    block_out, middle_grad, norm_two, *late_sums = mlp(
        place, middle, second_rows, cotangent, norm_params, late
    )
    own_late, late_received = late_sums[:2], [swap_heads(sent) for sent in late_sums[2:]]
    if whole_slabs:
        far = add_late(own_late[1], late_received[1])
        near = add_late(own_late[0], late_received[0])
        far = [across(far[number], 2 + number) for number in range(2)]
        near, middle_grad = lax.optimization_barrier((list(near), middle_grad))
        late_grads = [near[0], across(near[1], 1), *far]
    dqkv, own_early, sent_early, norm_sums = attn_backward(
        place, *masks, tokens, middle_grad, prob, qkv, out, norm_params, norm_two, wqkv, wo
    )
    if whole_slabs:
        late_grads, sent_early = lax.optimization_barrier((late_grads, sent_early))
    early_received = swap_heads(sent_early)
    devices = lax.axis_size("outer") * lax.axis_size("inner") * lax.axis_size("head")
    scale = 1.0 / math.sqrt(tokens.shape[0] * devices)
    state = (weights, stat_left, stat_right, scale)
    if whole_slabs:
        late_grads = to_all(sum_late(late_grads), "outer")
        early_grads = list(combine(place, own_early, early_received, norm_sums))
        early_grads, dqkv = lax.optimization_barrier((early_grads, dqkv))
        early_grads[1:] = [across(early_grads[apart], apart) for apart in range(1, INNER)]
        input_grad = input_gradient(tokens, middle_grad, dqkv, norm_params, wqkv)
        early_grads, input_grad = lax.optimization_barrier((early_grads, input_grad))
        joined, late_grads = lax.optimization_barrier((join(early_grads), late_grads))
        joined = to_all(joined, "outer")[:, None]
        results = shampoo(late_grads, *state, 1)
        results = shampoo(joined, *state, 0, results, (norm_params, norm_state))
    else:
        input_grad = input_gradient(tokens, middle_grad, dqkv, norm_params, wqkv)
        early_slabs = own_early.astype(F32) + early_received[:SLABS].astype(F32)
        late_slabs = jnp.concatenate(own_late).astype(F32) + jnp.concatenate(late_received)
        late_slabs = late_slabs.reshape(SLABS, 2, edge, D)
        slabs = jnp.concatenate([early_slabs[:, None], late_slabs], axis=1).astype(BF)
        owned = scatter_blocks(slabs, count, edge)
        results = list(shampoo(owned[None], *state, 0))
        norm_grads = lax.psum(norm_sums, ("outer", "inner", "head")) * scale
        state_new = 0.5 * norm_state + 0.5 * norm_grads * norm_grads
        results += [norm_grads, state_new, norm_params - 0.2 * norm_grads / jnp.sqrt(state_new)]
    return (block_out, input_grad, *[result[None] for result in results[:4]], *results[4:])


def solution(mesh):
    shape = (mesh.shape["dp"] // INNER, INNER, mesh.shape["head"])
    split_mesh = Mesh(mesh.devices.reshape(shape), ("outer", "inner", "head"))
    group = ("outer", "inner")
    blocks = P("head", None, group, None, None)
    rows = P(group + ("head",), None)
    return jax.shard_map(
        per_device,
        mesh=split_mesh,
        in_specs=(rows, rows, P(group), P(group, "head"), P(), P(), blocks, blocks, blocks),
        out_specs=(rows, rows, blocks, blocks, blocks, blocks, P(), P(), P()),
        check_vma=False,
    )
```

```python
import math

import jax
import jax.numpy as jnp
from jax import lax
from jax.experimental import pallas as pl
from jax.experimental.pallas import tpu as pltpu
from jax.sharding import Mesh, PartitionSpec as P

D = 384
HEAD_DIM = 64
MLP = 1536
S = 256
ITERS = 8
PAIR = 2 * HEAD_DIM
PAIRS = D // PAIR
HALF = D // 2
SLABS = 16
INNER = 4
OUTER = SLABS // INNER
TILE = 512
INPUT_TILE = 768
IMAGES = TILE // S
NORM_ROWS = 8
PACK = 2
ROOT_HALF = 0.7071067811865476
DENSITY_FACTOR = 0.3989422804014327
BF = jnp.bfloat16
F32 = jnp.float32
VMEM_LIMIT = 40 << 20
SMALL_VMEM = 8 << 20
SHAMPOO_VMEM = 24 << 20


def in_hbm(values):
    return pltpu.with_memory_space_constraint(values, pltpu.HBM)


def nn(left, right):
    return jnp.dot(left, right, preferred_element_type=F32)


def nt(left, right):
    return lax.dot_general(left, right, (((1,), (1,)), ((), ())), preferred_element_type=F32)


def tn(left, right):
    return lax.dot_general(left, right, (((0,), (0,)), ((), ())), preferred_element_type=F32)


def normalize(values):
    centered = values - jnp.mean(values, axis=-1, keepdims=True)
    variance = jnp.mean(centered * centered, axis=-1, keepdims=True)
    inverse_std = lax.rsqrt(variance + 1e-06)
    return centered * inverse_std, inverse_std


def norm_backward(grad_out, normed, inverse_std, gain):
    grad_normed = grad_out * gain
    mean_first = jnp.mean(grad_normed, axis=-1, keepdims=True)
    mean_second = jnp.mean(grad_normed * normed, axis=-1, keepdims=True)
    grad_in = inverse_std * (grad_normed - mean_first - normed * mean_second)
    gain_grad = jnp.sum(grad_out * normed, axis=0, keepdims=True)
    shift_grad = jnp.sum(grad_out, axis=0, keepdims=True)
    return grad_in, jnp.concatenate([gain_grad, shift_grad], axis=0)


def grown(step, total, part):
    return jnp.where(step == 0, part, total + part)


def slab_at(owner):
    return (owner % INNER) * OUTER + owner // INNER


def lane_halves():
    lane = lax.broadcasted_iota(jnp.int32, (1, PAIR), 1)
    first = (lane < HEAD_DIM).astype(BF)
    return first, (1 - first).astype(BF)


def stacked(values, first, second):
    return jnp.concatenate([values * first, values * second], axis=0)


def mask_lanes(place_ref, own_ref, other_ref, image, pair):
    image = place_ref[0] * (own_ref.shape[0] // 2) + image
    heads = own_ref.shape[1]
    on = [
        own_ref[image, head] if head < heads else other_ref[image, head - heads]
        for head in (2 * pair, 2 * pair + 1)
    ]
    lane = lax.broadcasted_iota(jnp.int32, (1, PAIR), 1)
    return jnp.where(lane < HEAD_DIM, on[0], on[1]).astype(F32)


def attn_forward_kernel(
    place_ref, own_mask_ref, other_mask_ref, x_ref, norm_ref, *refs
):
    slab_refs, refs = refs[: 2 * INNER], refs[2 * INNER :]
    prob_ref, qkv_ref, out_ref, middle_ref, rows_ref, wqkv_ref, wo_ref, held_ref = refs
    step = pl.program_id(0)

    @pl.when(step == 0)
    def _():
        for number, ref in enumerate(slab_refs):
            side, apart = divmod(number, INNER)
            held_ref[side, place_ref[1] ^ apart] = ref[...]

        def slab_of(side, owner):
            return held_ref[side, owner % INNER, owner // INNER]

        for row in range(D // 48):
            for part in range(3):
                pieces = []
                for number in range(2):
                    slab, side = divmod(3 * row + part, 2)
                    piece = slab_of(number, slab)[:, side * HALF : (side + 1) * HALF]
                    pieces.append(piece)
                joined = jnp.concatenate(pieces, axis=1)
                if part == 0:
                    joined = joined * 0.125
                wqkv_ref[48 * row : 48 * row + 48, D * part : D * part + D] = joined
        for side in range(2):
            for row in range(HALF // 48):
                start = side * HALF + 48 * row
                wo_ref[start : start + 48, :] = slab_of(side, 12 + row)

    x = x_ref[...].astype(F32)
    normed, _ = normalize(x)
    rows = (normed * norm_ref[0:1, :] + norm_ref[1:2, :]).astype(BF)
    qkv_ref[...] = nn(rows, wqkv_ref[...]).astype(BF)
    first, second = lane_halves()
    column = lax.broadcasted_iota(jnp.int32, (1, S), 1)
    tasks = [(image, pair) for image in range(IMAGES) for pair in range(PAIRS)]

    def places(task):
        image, pair = task
        here = slice(S * image, S * image + S)
        return here, *(slice(D * t + PAIR * pair, D * t + PAIR * (pair + 1)) for t in range(3))

    def get_scores(task):
        here, query_lanes, key_lanes, _ = places(task)
        return nt(stacked(qkv_ref[here, query_lanes], first, second), qkv_ref[here, key_lanes])

    def get_prob(task, scores):
        image = place_ref[0] * (own_mask_ref.shape[0] // 2) + IMAGES * step + task[0]
        scores = jnp.where(column < place_ref[2 + image], scores, -1e30)
        top = jnp.max(scores, axis=-1, keepdims=True)
        exp_scores = jnp.exp(scores - top)
        total = jnp.sum(exp_scores, axis=-1, keepdims=True)
        prob = (exp_scores * (1.0 / total)).astype(BF)
        prob_ref[task] = prob
        return prob

    all_scores = [get_scores(task) for task in tasks]
    probs = [get_prob(task, scores) for task, scores in zip(tasks, all_scores)]
    for task, prob in zip(tasks, probs):
        here, lanes, _, value_lanes = places(task)
        values = qkv_ref[here, value_lanes]
        head_out = nn(prob[:S], values * first) + nn(prob[S:], values * second)
        mask = mask_lanes(place_ref, own_mask_ref, other_mask_ref, IMAGES * step + task[0], task[1])
        out_ref[here, lanes] = (head_out * mask).astype(BF)
    middle = x + nn(out_ref[...], wo_ref[...])
    middle_ref[...] = middle
    normed, _ = normalize(middle)
    rows_ref[...] = (normed * norm_ref[2:3, :] + norm_ref[3:4, :]).astype(BF)


def attn_forward(place, own_mask, other_mask, tokens, norm_params, slabs):
    rows = tokens.shape[0]
    images = rows // S
    tile = pl.BlockSpec((TILE, D), lambda i: (i, 0))
    slab = pl.BlockSpec((OUTER, 48, D), lambda i: (0, 0, 0))
    smem = pl.BlockSpec(memory_space=pltpu.SMEM)
    return pl.pallas_call(
        attn_forward_kernel,
        grid=(rows // TILE,),
        in_specs=[smem] * 3 + [tile, pl.BlockSpec((4, D), lambda i: (0, 0))] + [slab] * 2 * INNER,
        out_specs=[
            pl.BlockSpec((IMAGES, PAIRS, 2 * S, S), lambda i: (i, 0, 0, 0)),
            pl.BlockSpec((TILE, 3 * D), lambda i: (i, 0)),
            tile,
            tile,
            tile,
            pl.BlockSpec((D, 3 * D), lambda i: (0, 0)),
            pl.BlockSpec((D, D), lambda i: (0, 0)),
        ],
        out_shape=[
            pltpu.HBM((images, PAIRS, 2 * S, S), BF),
            pltpu.HBM((rows, 3 * D), BF),
            pltpu.HBM((rows, D), BF),
            jax.ShapeDtypeStruct((rows, D), F32),
            jax.ShapeDtypeStruct((rows, D), BF),
            pltpu.HBM((D, 3 * D), BF),
            pltpu.HBM((D, D), BF),
        ],
        scratch_shapes=[pltpu.VMEM((2, INNER, OUTER, 48, D), BF)],
        compiler_params=pltpu.CompilerParams(vmem_limit_bytes=VMEM_LIMIT),
        cost_estimate=pl.CostEstimate(
            flops=rows * D * (8 * D + 16 * S), bytes_accessed=16 << 20, transcendentals=rows * 6 * S
        ),
        name="attn_forward",
    )(place, own_mask, other_mask, tokens, in_hbm(norm_params), *slabs)


def mlp_kernel(place_ref, middle_ref, rows_ref, cot_ref, norm_ref, *refs):
    slab_refs, refs = refs[: 2 * INNER], refs[2 * INNER :]
    out_ref, grad_ref, norm_grad_ref, *refs = refs
    own_refs, sent_refs, refs = refs[:2], refs[2:4], refs[4:]
    up_ref, down_ref, up_grad_ref, down_grad_ref = refs
    step = pl.program_id(0)
    half = MLP // 2

    def places(apart, outer):
        inner = place_ref[1] ^ apart
        row = pl.multiple_of(48 * (2 * outer + inner // 2), 16)
        lane = pl.multiple_of(D * (inner % 2), 128)
        down_row = pl.multiple_of(48 * (INNER * outer + inner), 16)
        return row, lane, down_row

    @pl.when(step == 0)
    def _():
        for number, ref in enumerate(slab_refs):
            side, apart = divmod(number, INNER)
            for outer in range(OUTER):
                row, lane, down_row = places(apart, outer)
                up_ref[side, pl.ds(row, 48), pl.ds(lane, D)] = ref[outer, 0]
                down_ref[side, pl.ds(down_row, 48), :] = ref[outer, 1]

    middle = middle_ref[...]
    normed, inverse_std = normalize(middle)
    rows, cot = rows_ref[...], cot_ref[...]
    total = middle
    back = None
    for side in range(2):
        up, down = up_ref[side], down_ref[side]
        pre = nn(rows, up)
        act_grad = nt(cot, down)
        cumulative = 0.5 * (1.0 + lax.erf(pre * ROOT_HALF))
        density = jnp.exp(-0.5 * pre * pre) * DENSITY_FACTOR
        act = (pre * cumulative).astype(BF)
        pre_grad = (act_grad * (cumulative + pre * density)).astype(BF)
        total = total + nn(act, down)
        term = nt(pre_grad, up)
        back = term if back is None else back + term
        down_grad_ref[side] = grown(step, down_grad_ref[side], tn(act, cot))
        up_grad_ref[side] = grown(step, up_grad_ref[side], tn(rows, pre_grad))
    out_ref[...] = total
    grad_in, norm_part = norm_backward(back, normed, inverse_std, norm_ref[2:3, :])
    norm_grad_ref[...] = grown(step, norm_grad_ref[...], norm_part)
    grad_ref[...] = cot.astype(F32) + grad_in

    @pl.when(step == pl.num_programs(0) - 1)
    def _():
        for apart in range(INNER):
            for outer in range(OUTER):
                row, lane, down_row = places(apart, outer)
                for side, halves in enumerate((own_refs, sent_refs)):
                    ref = halves[apart // 2]
                    up = up_grad_ref[side, pl.ds(row, 48), pl.ds(lane, D)]
                    down = down_grad_ref[side, pl.ds(down_row, 48), :]
                    ref[apart % 2, outer, 0] = up.astype(BF)
                    ref[apart % 2, outer, 1] = down.astype(BF)


def mlp(place, middle, second_rows, cotangent, norm_params, slabs):
    rows = middle.shape[0]
    slab = pl.BlockSpec((OUTER, 2, 48, D), lambda i: (0, 0, 0, 0))
    grads = (INNER // 2, OUTER, 2, 48, D)
    grad = pl.BlockSpec(grads, lambda i: (0, 0, 0, 0, 0))
    tile = pl.BlockSpec((TILE, D), lambda i: (i, 0))
    return pl.pallas_call(
        mlp_kernel,
        grid=(rows // TILE,),
        in_specs=[
            pl.BlockSpec(memory_space=pltpu.SMEM),
            tile,
            tile,
            tile,
            pl.BlockSpec((4, D), lambda i: (0, 0)),
            *[slab] * 2 * INNER,
        ],
        out_specs=[tile, tile, pl.BlockSpec((2, D), lambda i: (0, 0)), *[grad] * 4],
        out_shape=[
            jax.ShapeDtypeStruct((rows, D), F32),
            pltpu.HBM((rows, D), F32),
            jax.ShapeDtypeStruct((2, D), F32),
            *[jax.ShapeDtypeStruct(grads, BF)] * 4,
        ],
        scratch_shapes=[
            pltpu.VMEM((2, D, MLP // 2), BF),
            pltpu.VMEM((2, MLP // 2, D), BF),
            pltpu.VMEM((2, D, MLP // 2), F32),
            pltpu.VMEM((2, MLP // 2, D), F32),
        ],
        compiler_params=pltpu.CompilerParams(vmem_limit_bytes=VMEM_LIMIT),
        cost_estimate=pl.CostEstimate(
            flops=12 * rows * D * MLP, bytes_accessed=20 << 20, transcendentals=2 * rows * MLP
        ),
        name="mlp",
    )(place, middle, second_rows, cotangent, in_hbm(norm_params), *slabs)


def attn_backward_kernel(
    place_ref, own_mask_ref, other_mask_ref, x_ref, grad_ref, prob_ref, qkv_ref, out_ref,
    norm_ref, later_norm_ref, wqkv_ref, wo_ref,
    dqkv_ref, own_grad_ref, sent_grad_ref, norm_grad_ref,
    cross_ref, column_ref, wo_grad_ref,
):
    step = pl.program_id(0)

    normed, _ = normalize(x_ref[...].astype(F32))
    low_grad = grad_ref[...].astype(BF)
    head_out = out_ref[...]
    wo_grad_ref[...] = grown(step, wo_grad_ref[...], tn(head_out, low_grad))
    whole_grad = nt(low_grad, wo_ref[...]).astype(BF)
    first, second = lane_halves()
    first_wide, second_wide = first.astype(F32), second.astype(F32)
    tasks = [(image, pair) for image in range(IMAGES) for pair in range(PAIRS)]

    def places(task):
        image, pair = task
        here = slice(S * image, S * image + S)
        return here, *(slice(D * t + PAIR * pair, D * t + PAIR * (pair + 1)) for t in range(3))

    def get_pair_grad(task):
        here, lanes, _, _ = places(task)
        mask = mask_lanes(place_ref, own_mask_ref, other_mask_ref, IMAGES * step + task[0], task[1])
        grad = whole_grad[here, lanes] * mask.astype(BF)
        dots = grad.astype(F32) * head_out[here, lanes].astype(F32)
        first_dot = jnp.sum(dots * first_wide, axis=-1, keepdims=True)
        second_dot = jnp.sum(dots * second_wide, axis=-1, keepdims=True)
        return stacked(grad, first, second), jnp.concatenate([first_dot, second_dot], axis=0)

    pair_grads = [get_pair_grad(task) for task in tasks]
    prob_grads = [
        nt(pair_grad[0], qkv_ref[places(task)[0], places(task)[3]])
        for task, pair_grad in zip(tasks, pair_grads)
    ]
    score_grads = [
        (prob_ref[task].astype(F32) * (prob_grad - pair_grad[1])).astype(BF)
        for task, prob_grad, pair_grad in zip(tasks, prob_grads, pair_grads)
    ]
    for task, score_grad, (pair_grad, _) in zip(tasks, score_grads, pair_grads):
        here, query_lanes, key_lanes, value_lanes = places(task)
        keys = qkv_ref[here, key_lanes]
        queries = stacked(qkv_ref[here, query_lanes], first, second)
        query_grad = nn(score_grad[:S], keys * first) + nn(score_grad[S:], keys * second)
        key_grad = nn(jnp.transpose(queries), score_grad)
        value_grad = nn(jnp.transpose(pair_grad), prob_ref[task])
        dqkv_ref[here, query_lanes] = query_grad.astype(BF)
        dqkv_ref[here, key_lanes] = jnp.transpose(key_grad).astype(BF)
        dqkv_ref[here, value_lanes] = jnp.transpose(value_grad).astype(BF)
    dqkv = dqkv_ref[...]
    cross_ref[...] = grown(step, cross_ref[...], tn(normed.astype(BF), dqkv))
    columns = jnp.sum(dqkv.astype(F32), axis=0, keepdims=True)
    column_ref[...] = grown(step, column_ref[...], columns)

    @pl.when(step == pl.num_programs(0) - 1)
    def _():
        wqkv = wqkv_ref[...]
        products = wqkv.astype(F32) * cross_ref[...]
        gain_grad = jnp.sum(products, axis=1, keepdims=True)
        gain_grad = jnp.transpose(jnp.broadcast_to(gain_grad, (D, 128)))
        columns = column_ref[...]
        shift_grad = nt(jnp.concatenate(split(jnp.broadcast_to(columns, (8, 3 * D)))), wqkv)
        norm_grad_ref[0:1, :] = gain_grad[0:1]
        norm_grad_ref[1:2, :] = shift_grad[0:1] + shift_grad[8:9]
        norm_grad_ref[2:4, :] = later_norm_ref[...]
        gain = jnp.transpose(jnp.broadcast_to(norm_ref[0:1, :], (128, D)))[:, :1]
        shift = jnp.transpose(jnp.broadcast_to(norm_ref[1:2, :], (128, D)))[:, :1]
        cross_ref[...] = cross_ref[...] * gain + shift * columns
        for side, slab_grads in enumerate((own_grad_ref, sent_grad_ref)):
            for slab in range(12):
                pieces = []
                for unit in (2 * slab, 2 * slab + 1):
                    row, part = divmod(unit, 3)
                    piece = cross_ref[48 * row : 48 * row + 48, D * part : D * part + D]
                    piece = piece[:, HALF * side : HALF * side + HALF]
                    pieces.append(piece * 0.125 if part == 0 else piece)
                slab_grads[slab_at(slab)] = jnp.concatenate(pieces, axis=1).astype(BF)
            for row in range(HALF // 48):
                start = HALF * side + 48 * row
                slab_grads[slab_at(12 + row)] = wo_grad_ref[start : start + 48, :].astype(BF)
        sent_grad_ref[SLABS, :NORM_ROWS] = jnp.concatenate(split(norm_grad_ref[...]), axis=0)
        sent_grad_ref[SLABS, NORM_ROWS:] = jnp.zeros((48 - NORM_ROWS, D), BF)


def attn_backward(
    place, own_mask, other_mask, tokens, grad, prob, qkv, out, norm_params, later_norms, wqkv, wo
):
    rows = tokens.shape[0]
    tile = pl.BlockSpec((TILE, D), lambda i: (i, 0))
    smem = pl.BlockSpec(memory_space=pltpu.SMEM)
    return pl.pallas_call(
        attn_backward_kernel,
        grid=(rows // TILE,),
        in_specs=[
            smem,
            smem,
            smem,
            tile,
            tile,
            pl.BlockSpec((IMAGES, PAIRS, 2 * S, S), lambda i: (i, 0, 0, 0)),
            pl.BlockSpec((TILE, 3 * D), lambda i: (i, 0)),
            tile,
            pl.BlockSpec((4, D), lambda i: (0, 0)),
            pl.BlockSpec((2, D), lambda i: (0, 0)),
            pl.BlockSpec((D, 3 * D), lambda i: (0, 0)),
            pl.BlockSpec((D, D), lambda i: (0, 0)),
        ],
        out_specs=[
            pl.BlockSpec((TILE, 3 * D), lambda i: (i, 0)),
            pl.BlockSpec((SLABS, 48, D), lambda i: (0, 0, 0)),
            pl.BlockSpec((SLABS + 1, 48, D), lambda i: (0, 0, 0)),
            pl.BlockSpec((4, D), lambda i: (0, 0)),
        ],
        out_shape=[
            pltpu.HBM((rows, 3 * D), BF),
            jax.ShapeDtypeStruct((SLABS, 48, D), BF),
            jax.ShapeDtypeStruct((SLABS + 1, 48, D), BF),
            jax.ShapeDtypeStruct((4, D), F32),
        ],
        scratch_shapes=[
            pltpu.VMEM((D, 3 * D), F32),
            pltpu.VMEM((1, 3 * D), F32),
            pltpu.VMEM((D, D), F32),
        ],
        compiler_params=pltpu.CompilerParams(vmem_limit_bytes=VMEM_LIMIT),
        cost_estimate=pl.CostEstimate(
            flops=rows * D * (10 * D + 32 * S), bytes_accessed=20 << 20, transcendentals=0
        ),
        name="attn_backward",
    )(
        place, own_mask, other_mask,
        tokens, in_hbm(grad), prob, qkv, out, in_hbm(norm_params), in_hbm(later_norms), wqkv, wo,
    )


def input_grad_kernel(x_ref, grad_ref, dqkv_ref, norm_ref, wqkv_ref, out_ref):
    normed, inverse_std = normalize(x_ref[...].astype(F32))
    back = nt(dqkv_ref[...], wqkv_ref[...]) * norm_ref[0:1, :]
    mean_first = jnp.mean(back, axis=-1, keepdims=True)
    mean_second = jnp.mean(back * normed, axis=-1, keepdims=True)
    out_ref[...] = grad_ref[...] + inverse_std * (back - mean_first - normed * mean_second)


def input_gradient(tokens, grad, dqkv, norm_params, wqkv):
    rows = tokens.shape[0]
    tile = pl.BlockSpec((INPUT_TILE, D), lambda i: (i, 0))
    return pl.pallas_call(
        input_grad_kernel,
        grid=(rows // INPUT_TILE,),
        in_specs=[
            tile,
            tile,
            pl.BlockSpec((INPUT_TILE, 3 * D), lambda i: (i, 0)),
            pl.BlockSpec((4, D), lambda i: (0, 0)),
            pl.BlockSpec((D, 3 * D), lambda i: (0, 0)),
        ],
        out_specs=tile,
        out_shape=jax.ShapeDtypeStruct((rows, D), F32),
        compiler_params=pltpu.CompilerParams(vmem_limit_bytes=VMEM_LIMIT),
        cost_estimate=pl.CostEstimate(
            flops=rows * D * 6 * D, bytes_accessed=10 << 20, transcendentals=0
        ),
        name="input_gradient",
    )(in_hbm(tokens), in_hbm(grad), in_hbm(dqkv), in_hbm(norm_params), in_hbm(wqkv))


def pack_kernel(weight_ref, out_ref):
    groups, count, _, _ = weight_ref.shape
    for group in range(groups):
        blocks = [weight_ref[group, block] for block in range(count)]
        slab = jnp.concatenate(blocks, axis=1).astype(BF)
        for copy in range(OUTER):
            out_ref[copy, group] = slab


def pack(weights, first, groups):
    _, count, edge, _ = weights.shape
    shape = (OUTER, groups, edge, count * edge)
    return pl.pallas_call(
        pack_kernel,
        grid=(1,),
        in_specs=[
            pl.BlockSpec(
                (pl.Element(groups), pl.Element(count), pl.Element(edge), pl.Element(edge)),
                lambda i: (first, 0, 0, 0),
            )
        ],
        out_specs=pl.BlockSpec(shape, lambda i: (0, 0, 0, 0)),
        out_shape=jax.ShapeDtypeStruct(shape, BF),
        compiler_params=pltpu.CompilerParams(vmem_limit_bytes=SMALL_VMEM),
        name="pack",
    )(in_hbm(weights))


def add_kernel(own_ref, received_ref, *out_refs):
    for apart, out_ref in enumerate(out_refs):
        total = own_ref[apart].astype(F32) + received_ref[apart].astype(F32)
        out_ref[...] = total.astype(BF)


def add_late(own, received):
    return pl.pallas_call(
        add_kernel,
        out_shape=[jax.ShapeDtypeStruct(own.shape[1:], BF)] * own.shape[0],
        compiler_params=pltpu.CompilerParams(vmem_limit_bytes=SMALL_VMEM),
        name="add_late",
    )(own, received)


def sum_kernel(*refs):
    *in_refs, out_ref = refs
    total = in_refs[0][...].astype(F32)
    for ref in in_refs[1:]:
        total = total + ref[...].astype(F32)
    out_ref[...] = total.astype(BF)


def sum_late(pieces):
    return pl.pallas_call(
        sum_kernel,
        out_shape=jax.ShapeDtypeStruct(pieces[0].shape, BF),
        compiler_params=pltpu.CompilerParams(vmem_limit_bytes=SMALL_VMEM),
        name="sum_late",
    )(*pieces)


def combine_kernel(place_ref, own_ref, received_ref, norm_ref, *out_refs):
    norms = received_ref[SLABS, :NORM_ROWS].astype(F32)
    norms = norm_ref[...] + (norms[:4] + norms[4:])
    rows = jnp.concatenate(split(norms), axis=0)
    for apart, out_ref in enumerate(out_refs):
        start = OUTER * (place_ref[1] ^ apart)
        for outer in range(OUTER):
            total = own_ref[start + outer].astype(F32) + received_ref[start + outer].astype(F32)
            out_ref[48 * outer : 48 * outer + 48, :] = total.astype(BF)
        out_ref[48 * OUTER :, :] = rows


def combine(place, own, received, norms):
    vmem = pl.BlockSpec(memory_space=pltpu.VMEM)
    shape = jax.ShapeDtypeStruct((48 * OUTER + NORM_ROWS, D), BF)
    return pl.pallas_call(
        combine_kernel,
        in_specs=[pl.BlockSpec(memory_space=pltpu.SMEM), vmem, vmem, vmem],
        out_shape=[shape] * INNER,
        compiler_params=pltpu.CompilerParams(vmem_limit_bytes=SMALL_VMEM),
        name="combine",
    )(place, own, received, norms)


def join_kernel(*refs):
    *early_refs, out_ref = refs
    total = early_refs[0][...].astype(F32)
    for ref in early_refs[1:]:
        total = total + ref[...].astype(F32)
    norms = total[48 * OUTER : 48 * OUTER + 4] + total[48 * OUTER + 4 :]
    for outer in range(OUTER):
        out_ref[outer, :48] = total[48 * outer : 48 * outer + 48].astype(BF)
        out_ref[outer, 48:] = jnp.concatenate(split(norms), axis=0)


def join(early):
    return pl.pallas_call(
        join_kernel,
        out_shape=jax.ShapeDtypeStruct((OUTER, 48 + NORM_ROWS, D), BF),
        compiler_params=pltpu.CompilerParams(vmem_limit_bytes=SMALL_VMEM),
        name="join",
    )(*early)


def split(values):
    high = values.astype(BF)
    return high, (values - high.astype(F32)).astype(BF)


def stack(*pieces):
    return jnp.concatenate(pieces, axis=0)


def cut_rows(values, number):
    edge = values.shape[0] // number
    return [values[edge * i : edge * i + edge] for i in range(number)]


def product(left, right):
    high, low = left
    right_high, right_low = right
    one, two = cut_rows(nn(stack(high, low), right_high), 2)
    return one + (two + nn(high, right_low))


def two_products(left, middle, right):
    right_high, right_low = right
    both = cut_rows(nn(stack(left[0], middle[0], left[1], middle[1]), right_high), 4)
    high = cut_rows(nn(stack(left[0], middle[0]), right_low), 2)
    return both[0] + (both[2] + high[0]), both[1] + (both[3] + high[1])


def update_norms(scale, total, param_ref, state_ref, grad_ref, new_state_ref, new_ref):
    grads = total * scale
    state = 0.5 * state_ref[...] + 0.5 * grads * grads
    grad_ref[...] = grads
    new_state_ref[...] = state
    new_ref[...] = param_ref[...] - 0.2 * grads / jnp.sqrt(state)


def shampoo_kernel(scale, with_norms, received_ref, weight_ref, left_ref, right_ref, *refs):
    if with_norms:
        norm_ins, norm_outs, refs = refs[:2], refs[-5:-2], refs[:-5] + refs[-2:]
    out_grad_ref, left_new_ref, right_new_ref, new_weight_ref, root_ref, power_ref = refs[-6:]
    groups, count, edge = weight_ref.shape[:3]

    received = received_ref[0].astype(F32)
    for number in range(1, received_ref.shape[0]):
        received = received + received_ref[number].astype(F32)
    if with_norms:
        norms = received[0, edge:]
        update_norms(scale, norms[:4] + norms[4:], *norm_ins, *norm_outs)
    pack = min(PACK, count)
    width = pack * edge
    places = [(g, pack * n) for g in range(groups) for n in range(count // pack)]
    packs = len(places)

    def block_of(shape, dim):
        return lax.broadcasted_iota(jnp.int32, shape, dim) // edge

    row = lax.broadcasted_iota(jnp.int32, (edge, width), 0)
    lane = lax.broadcasted_iota(jnp.int32, (edge, width), 1)
    identity = (lane % edge == row).astype(F32)
    same = (block_of((width, width), 0) == block_of((width, width), 1)).astype(BF)
    lane_block = block_of((1, width), 1)

    def spread(pieces):
        return tuple(stack(*[piece] * pack) * same for piece in pieces)

    def cut(packed, index):
        return packed[:, edge * index : edge * index + edge]

    def beside(ref, place):
        return jnp.concatenate([ref[place[0], place[1] + i] for i in range(pack)], axis=1)

    grads, parts = [], []
    for group, start in places:
        grad = received[group, :edge, edge * start : edge * start + width] * scale
        blocks = [cut(grad, index) for index in range(pack)]
        for index in range(pack):
            out_grad_ref[group, start + index] = blocks[index]
        grad_t = jnp.concatenate([jnp.transpose(block) for block in blocks], axis=1)
        one, two = split(grad), split(grad_t)
        one_diagonal, two_diagonal = spread(one), spread(two)
        grads.append(one_diagonal)
        parts.append((left_ref, left_new_ref, one, two_diagonal))
        parts.append((right_ref, right_new_ref, two, one_diagonal))
    grams = [product(left, right) for _, _, left, right in parts]
    for slot, (old_ref, new_ref, _, _) in enumerate(parts):
        group, start = places[slot // 2]
        new = 0.5 * beside(old_ref, places[slot // 2]) + 0.5 * grams[slot]
        for index in range(pack):
            new_ref[group, start + index] = cut(new, index)
        columns = jnp.sum(new * new, axis=0, keepdims=True)
        squares = jnp.zeros((1, width), F32)
        for index in range(pack):
            inside = lane_block == index
            part = jnp.sum(jnp.where(inside, columns, 0.0), axis=1, keepdims=True)
            squares = jnp.where(inside, part, squares)
        factor = 2.5 / jnp.sqrt(squares)
        root_ref[slot] = jnp.broadcast_to(jnp.sqrt(jnp.sqrt(factor)), (edge, width))
        power_ref[slot] = factor * new
    slots = range(2 * packs)

    def advance(first):
        powers = [power_ref[slot] for slot in slots]
        middles = [split((5.0 * identity - power) * 0.25) for power in powers]
        rights = [spread(middle) for middle in middles]
        powers = [split(power) for power in powers]
        if first:
            squares = [product(middles[s], rights[s]) for s in slots]
            for slot in slots:
                root_ref[slot] *= (5.0 * identity - power_ref[slot]) * 0.25
        else:
            roots = [split(root_ref[slot]) for slot in slots]
            both = [two_products(roots[s], middles[s], rights[s]) for s in slots]
            squares = [pair[1] for pair in both]
            for slot in slots:
                root_ref[slot] = both[slot][0]
        rights = [spread(split(square)) for square in squares]
        powers = [split(product(powers[s], rights[s])) for s in slots]
        for slot in slots:
            power_ref[slot] = product(powers[slot], rights[slot])

    advance(True)
    for _ in range(ITERS - 2):
        advance(False)
    rights = [spread(split((5.0 * identity - power_ref[slot]) * 0.25)) for slot in slots]
    for slot in slots:
        root_ref[slot] = product(split(root_ref[slot]), rights[slot])
    steps = [product(split(root_ref[2 * n]), grads[n]) for n in range(packs)]
    rights = [spread(split(root_ref[2 * n + 1])) for n in range(packs)]
    steps = [product(split(steps[n]), rights[n]) for n in range(packs)]
    for number, (group, start) in enumerate(places):
        for index in range(pack):
            step = 0.25 * cut(steps[number], index)
            new_weight_ref[group, start + index] = weight_ref[group, start + index] - step


def shampoo(received, weights, stat_left, stat_right, scale, first, earlier=(), norms=()):
    groups = received.shape[1]
    _, count, edge, _ = weights.shape
    slots = 2 * groups * count // min(PACK, count)
    width = min(PACK, count) * edge
    block = pl.BlockSpec(
        (pl.Element(groups), pl.Element(count), pl.Element(edge), pl.Element(edge)),
        lambda i: (first, 0, 0, 0),
    )
    shape = jax.ShapeDtypeStruct(weights.shape, F32)
    norm = pl.BlockSpec((4, D), lambda i: (0, 0))
    norm_outs = 3 if norms else 0
    ins = 4 + len(norms)
    return pl.pallas_call(
        lambda *refs: shampoo_kernel(scale, bool(norms), *refs),
        grid=(1,),
        in_specs=[
            pl.BlockSpec(received.shape, lambda i: (0, 0, 0, 0)),
            *[block] * 3,
            *[norm] * len(norms),
            *[pl.BlockSpec(memory_space=pl.ANY)] * len(earlier),
        ],
        out_specs=[block] * 4 + [norm] * norm_outs,
        out_shape=[shape] * 4 + [jax.ShapeDtypeStruct((4, D), F32)] * norm_outs,
        scratch_shapes=[
            pltpu.VMEM((slots, edge, width), F32),
            pltpu.VMEM((slots, edge, width), F32),
        ],
        input_output_aliases={ins + i: i for i in range(len(earlier))},
        compiler_params=pltpu.CompilerParams(vmem_limit_bytes=SHAMPOO_VMEM),
        cost_estimate=pl.CostEstimate(
            flops=groups * (3 << 30), bytes_accessed=4 << 20, transcendentals=0
        ),
        name="shampoo",
    )(received, weights, stat_left, stat_right, *norms, *earlier)


def swap_heads(values):
    return lax.ppermute(values, "head", [(0, 1), (1, 0)])


def to_all(values, axis):
    return lax.all_to_all(values, axis, 0, 0)


def across(values, apart):
    pairs = [(i, i ^ apart) for i in range(INNER)]
    return lax.ppermute(values, "inner", pairs)


def from_all(values):
    return [values] + [across(values, apart) for apart in range(1, INNER)]


def gather_slabs(weights, small):
    early = to_all(pack(weights, 0, 1), "outer")[:, 0]
    early, late = lax.optimization_barrier((early, pack(weights, 1, 2)))
    late = to_all(late, "outer")
    early = from_all(early)
    early[1], late, small = lax.optimization_barrier((early[1], late, small))
    return early, from_all(late), small


def gather_blocks(local):
    groups, _, edge, _ = local.shape
    blocks = lax.all_gather(local, ("outer", "inner"), axis=1, tiled=True)
    blocks = blocks.reshape(groups, SLABS // INNER, INNER, D // edge, edge, edge)
    slabs = blocks.transpose(2, 1, 0, 4, 3, 5).reshape(SLABS, groups, edge, D)
    return slabs if groups > 1 else slabs[:, 0]


def scatter_blocks(slabs, count, edge):
    groups = slabs.shape[1]
    blocks = slabs.reshape(INNER, SLABS // INNER, groups, edge, D // edge, edge)
    blocks = blocks.transpose(2, 1, 0, 4, 3, 5).reshape(groups, SLABS * (D // edge), edge, edge)
    owned = lax.psum_scatter(blocks, ("outer", "inner"), scatter_dimension=1, tiled=True)
    return owned.transpose(0, 2, 1, 3).reshape(groups, edge, count * edge)


def per_device(
    tokens,
    cotangent,
    token_counts,
    head_mask,
    norm_params,
    norm_state,
    weights,
    stat_left,
    stat_right,
):
    weights, stat_left, stat_right = weights[0], stat_left[0], stat_right[0]
    _, count, edge, _ = weights.shape
    whole_slabs = count * edge == D
    other_mask = swap_heads(head_mask)
    inner = lax.axis_index("inner") if whole_slabs else 0
    place = jnp.concatenate([jnp.stack([lax.axis_index("head"), inner]), token_counts])
    if whole_slabs:
        early, late, (other_mask, place) = gather_slabs(weights, (other_mask, place))
    else:
        local = weights.astype(BF)
        early = jnp.split(gather_blocks(local[:1]), INNER)
        late = jnp.split(gather_blocks(local[1:]), INNER)
    early, late = list(early), list(late)
    masks = (head_mask, other_mask)
    early += [swap_heads(piece) for piece in early]
    prob, qkv, out, middle, second_rows, wqkv, wo = attn_forward(
        place, *masks, tokens, norm_params, early
    )
    late[1:], middle = lax.optimization_barrier((late[1:], middle))
    late += [swap_heads(piece) for piece in late]
    block_out, middle_grad, norm_two, *late_sums = mlp(
        place, middle, second_rows, cotangent, norm_params, late
    )
    own_late, late_received = late_sums[:2], [swap_heads(sent) for sent in late_sums[2:]]
    if whole_slabs:
        far = add_late(own_late[1], late_received[1])
        near = add_late(own_late[0], late_received[0])
        far = [across(far[number], 2 + number) for number in range(2)]
        near, middle_grad = lax.optimization_barrier((list(near), middle_grad))
        late_grads = [near[0], across(near[1], 1), *far]
    dqkv, own_early, sent_early, norm_sums = attn_backward(
        place, *masks, tokens, middle_grad, prob, qkv, out, norm_params, norm_two, wqkv, wo
    )
    if whole_slabs:
        late_grads, sent_early = lax.optimization_barrier((late_grads, sent_early))
    early_received = swap_heads(sent_early)
    devices = lax.axis_size("outer") * lax.axis_size("inner") * lax.axis_size("head")
    scale = 1.0 / math.sqrt(tokens.shape[0] * devices)
    state = (weights, stat_left, stat_right, scale)
    if whole_slabs:
        late_grads = to_all(sum_late(late_grads), "outer")
        early_grads = list(combine(place, own_early, early_received, norm_sums))
        early_grads, dqkv = lax.optimization_barrier((early_grads, dqkv))
        early_grads[1:] = [across(early_grads[apart], apart) for apart in range(1, INNER)]
        input_grad = input_gradient(tokens, middle_grad, dqkv, norm_params, wqkv)
        early_grads, input_grad = lax.optimization_barrier((early_grads, input_grad))
        joined, late_grads = lax.optimization_barrier((join(early_grads), late_grads))
        joined = to_all(joined, "outer")[:, None]
        results = shampoo(late_grads, *state, 1)
        results = shampoo(joined, *state, 0, results, (norm_params, norm_state))
    else:
        input_grad = input_gradient(tokens, middle_grad, dqkv, norm_params, wqkv)
        early_slabs = own_early.astype(F32) + early_received[:SLABS].astype(F32)
        late_slabs = jnp.concatenate(own_late).astype(F32) + jnp.concatenate(late_received)
        late_slabs = late_slabs.reshape(SLABS, 2, edge, D)
        slabs = jnp.concatenate([early_slabs[:, None], late_slabs], axis=1).astype(BF)
        owned = scatter_blocks(slabs, count, edge)
        results = list(shampoo(owned[None], *state, 0))
        norm_grads = lax.psum(norm_sums, ("outer", "inner", "head")) * scale
        state_new = 0.5 * norm_state + 0.5 * norm_grads * norm_grads
        results += [norm_grads, state_new, norm_params - 0.2 * norm_grads / jnp.sqrt(state_new)]
    return (block_out, input_grad, *[result[None] for result in results[:4]], *results[4:])


def solution(mesh):
    shape = (mesh.shape["dp"] // INNER, INNER, mesh.shape["head"])
    split_mesh = Mesh(mesh.devices.reshape(shape), ("outer", "inner", "head"))
    group = ("outer", "inner")
    blocks = P("head", None, group, None, None)
    rows = P(group + ("head",), None)
    return jax.shard_map(
        per_device,
        mesh=split_mesh,
        in_specs=(rows, rows, P(group), P(group, "head"), P(), P(), blocks, blocks, blocks),
        out_specs=(rows, rows, blocks, blocks, blocks, blocks, P(), P(), P()),
        check_vma=False,
    )
```

```python
import math

import jax
import jax.numpy as jnp
from jax import lax
from jax.experimental import pallas as pl
from jax.experimental.pallas import tpu as pltpu
from jax.sharding import Mesh, PartitionSpec as P

D = 384
HEAD_DIM = 64
MLP = 1536
S = 256
ITERS = 8
PAIR = 2 * HEAD_DIM
PAIRS = D // PAIR
HALF = D // 2
SLABS = 16
INNER = 4
OUTER = SLABS // INNER
TILE = 512
INPUT_TILE = 768
IMAGES = TILE // S
NORM_ROWS = 8
PACK = 2
ROOT_HALF = 0.7071067811865476
DENSITY_FACTOR = 0.3989422804014327
BF = jnp.bfloat16
F32 = jnp.float32
VMEM_LIMIT = 40 << 20
SMALL_VMEM = 8 << 20
SHAMPOO_VMEM = 24 << 20


def in_hbm(values):
    return pltpu.with_memory_space_constraint(values, pltpu.HBM)


def nn(left, right):
    return jnp.dot(left, right, preferred_element_type=F32)


def nt(left, right):
    return lax.dot_general(left, right, (((1,), (1,)), ((), ())), preferred_element_type=F32)


def tn(left, right):
    return lax.dot_general(left, right, (((0,), (0,)), ((), ())), preferred_element_type=F32)


def normalize(values):
    centered = values - jnp.mean(values, axis=-1, keepdims=True)
    variance = jnp.mean(centered * centered, axis=-1, keepdims=True)
    inverse_std = lax.rsqrt(variance + 1e-06)
    return centered * inverse_std, inverse_std


def norm_backward(grad_out, normed, inverse_std, gain):
    grad_normed = grad_out * gain
    mean_first = jnp.mean(grad_normed, axis=-1, keepdims=True)
    mean_second = jnp.mean(grad_normed * normed, axis=-1, keepdims=True)
    grad_in = inverse_std * (grad_normed - mean_first - normed * mean_second)
    gain_grad = jnp.sum(grad_out * normed, axis=0, keepdims=True)
    shift_grad = jnp.sum(grad_out, axis=0, keepdims=True)
    return grad_in, jnp.concatenate([gain_grad, shift_grad], axis=0)


def grown(step, total, part):
    return jnp.where(step == 0, part, total + part)


def slab_at(owner):
    return (owner % INNER) * OUTER + owner // INNER


def lane_halves():
    lane = lax.broadcasted_iota(jnp.int32, (1, PAIR), 1)
    first = (lane < HEAD_DIM).astype(BF)
    return first, (1 - first).astype(BF)


def stacked(values, first, second):
    return jnp.concatenate([values * first, values * second], axis=0)


def mask_lanes(place_ref, own_ref, other_ref, image, pair):
    image = place_ref[0] * (own_ref.shape[0] // 2) + image
    heads = own_ref.shape[1]
    on = [
        own_ref[image, head] if head < heads else other_ref[image, head - heads]
        for head in (2 * pair, 2 * pair + 1)
    ]
    lane = lax.broadcasted_iota(jnp.int32, (1, PAIR), 1)
    return jnp.where(lane < HEAD_DIM, on[0], on[1]).astype(F32)


def attn_forward_kernel(
    place_ref, own_mask_ref, other_mask_ref, x_ref, norm_ref, *refs
):
    slab_refs, refs = refs[: 2 * INNER], refs[2 * INNER :]
    prob_ref, qkv_ref, out_ref, middle_ref, rows_ref, wqkv_ref, wo_ref, held_ref = refs
    step = pl.program_id(0)

    @pl.when(step == 0)
    def _():
        for number, ref in enumerate(slab_refs):
            side, apart = divmod(number, INNER)
            held_ref[side, place_ref[1] ^ apart] = ref[...]

        def slab_of(side, owner):
            return held_ref[side, owner % INNER, owner // INNER]

        for row in range(D // 48):
            for part in range(3):
                pieces = []
                for number in range(2):
                    slab, side = divmod(3 * row + part, 2)
                    piece = slab_of(number, slab)[:, side * HALF : (side + 1) * HALF]
                    pieces.append(piece)
                joined = jnp.concatenate(pieces, axis=1)
                if part == 0:
                    joined = joined * 0.125
                wqkv_ref[48 * row : 48 * row + 48, D * part : D * part + D] = joined
        for side in range(2):
            for row in range(HALF // 48):
                start = side * HALF + 48 * row
                wo_ref[start : start + 48, :] = slab_of(side, 12 + row)

    x = x_ref[...].astype(F32)
    normed, _ = normalize(x)
    rows = (normed * norm_ref[0:1, :] + norm_ref[1:2, :]).astype(BF)
    qkv_ref[...] = nn(rows, wqkv_ref[...]).astype(BF)
    first, second = lane_halves()
    column = lax.broadcasted_iota(jnp.int32, (1, S), 1)
    tasks = [(image, pair) for image in range(IMAGES) for pair in range(PAIRS)]

    def places(task):
        image, pair = task
        here = slice(S * image, S * image + S)
        return here, *(slice(D * t + PAIR * pair, D * t + PAIR * (pair + 1)) for t in range(3))

    def get_scores(task):
        here, query_lanes, key_lanes, _ = places(task)
        return nt(stacked(qkv_ref[here, query_lanes], first, second), qkv_ref[here, key_lanes])

    def get_prob(task, scores):
        image = place_ref[0] * (own_mask_ref.shape[0] // 2) + IMAGES * step + task[0]
        scores = jnp.where(column < place_ref[2 + image], scores, -1e30)
        top = jnp.max(scores, axis=-1, keepdims=True)
        exp_scores = jnp.exp(scores - top)
        total = jnp.sum(exp_scores, axis=-1, keepdims=True)
        prob = (exp_scores * (1.0 / total)).astype(BF)
        prob_ref[task] = prob
        return prob

    all_scores = [get_scores(task) for task in tasks]
    probs = [get_prob(task, scores) for task, scores in zip(tasks, all_scores)]
    for task, prob in zip(tasks, probs):
        here, lanes, _, value_lanes = places(task)
        values = qkv_ref[here, value_lanes]
        head_out = nn(prob[:S], values * first) + nn(prob[S:], values * second)
        mask = mask_lanes(place_ref, own_mask_ref, other_mask_ref, IMAGES * step + task[0], task[1])
        out_ref[here, lanes] = (head_out * mask).astype(BF)
    middle = x + nn(out_ref[...], wo_ref[...])
    middle_ref[...] = middle
    normed, _ = normalize(middle)
    rows_ref[...] = (normed * norm_ref[2:3, :] + norm_ref[3:4, :]).astype(BF)


def attn_forward(place, own_mask, other_mask, tokens, norm_params, slabs):
    rows = tokens.shape[0]
    images = rows // S
    tile = pl.BlockSpec((TILE, D), lambda i: (i, 0))
    slab = pl.BlockSpec((OUTER, 48, D), lambda i: (0, 0, 0))
    smem = pl.BlockSpec(memory_space=pltpu.SMEM)
    return pl.pallas_call(
        attn_forward_kernel,
        grid=(rows // TILE,),
        in_specs=[smem] * 3 + [tile, pl.BlockSpec((4, D), lambda i: (0, 0))] + [slab] * 2 * INNER,
        out_specs=[
            pl.BlockSpec((IMAGES, PAIRS, 2 * S, S), lambda i: (i, 0, 0, 0)),
            pl.BlockSpec((TILE, 3 * D), lambda i: (i, 0)),
            tile,
            tile,
            tile,
            pl.BlockSpec((D, 3 * D), lambda i: (0, 0)),
            pl.BlockSpec((D, D), lambda i: (0, 0)),
        ],
        out_shape=[
            pltpu.HBM((images, PAIRS, 2 * S, S), BF),
            pltpu.HBM((rows, 3 * D), BF),
            pltpu.HBM((rows, D), BF),
            jax.ShapeDtypeStruct((rows, D), F32),
            jax.ShapeDtypeStruct((rows, D), BF),
            pltpu.HBM((D, 3 * D), BF),
            pltpu.HBM((D, D), BF),
        ],
        scratch_shapes=[pltpu.VMEM((2, INNER, OUTER, 48, D), BF)],
        compiler_params=pltpu.CompilerParams(vmem_limit_bytes=VMEM_LIMIT),
        cost_estimate=pl.CostEstimate(
            flops=rows * D * (8 * D + 16 * S), bytes_accessed=16 << 20, transcendentals=rows * 6 * S
        ),
        name="attn_forward",
    )(place, own_mask, other_mask, tokens, in_hbm(norm_params), *slabs)


def mlp_kernel(place_ref, middle_ref, rows_ref, cot_ref, norm_ref, *refs):
    slab_refs, refs = refs[: 2 * INNER], refs[2 * INNER :]
    out_ref, grad_ref, norm_grad_ref, *refs = refs
    own_refs, sent_refs, refs = refs[:2], refs[2:4], refs[4:]
    up_ref, down_ref, up_grad_ref, down_grad_ref = refs
    step = pl.program_id(0)
    half = MLP // 2

    def places(apart, outer):
        inner = place_ref[1] ^ apart
        row = pl.multiple_of(48 * (2 * outer + inner // 2), 16)
        lane = pl.multiple_of(D * (inner % 2), 128)
        down_row = pl.multiple_of(48 * (INNER * outer + inner), 16)
        return row, lane, down_row

    @pl.when(step == 0)
    def _():
        for number, ref in enumerate(slab_refs):
            side, apart = divmod(number, INNER)
            for outer in range(OUTER):
                row, lane, down_row = places(apart, outer)
                up_ref[side, pl.ds(row, 48), pl.ds(lane, D)] = ref[outer, 0]
                down_ref[side, pl.ds(down_row, 48), :] = ref[outer, 1]

    middle = middle_ref[...]
    normed, inverse_std = normalize(middle)
    rows, cot = rows_ref[...], cot_ref[...]
    total = middle
    back = None
    for side in range(2):
        up, down = up_ref[side], down_ref[side]
        pre = nn(rows, up)
        act_grad = nt(cot, down)
        cumulative = 0.5 * (1.0 + lax.erf(pre * ROOT_HALF))
        density = jnp.exp(-0.5 * pre * pre) * DENSITY_FACTOR
        act = (pre * cumulative).astype(BF)
        pre_grad = (act_grad * (cumulative + pre * density)).astype(BF)
        total = total + nn(act, down)
        term = nt(pre_grad, up)
        back = term if back is None else back + term
        down_grad_ref[side] = grown(step, down_grad_ref[side], tn(act, cot))
        up_grad_ref[side] = grown(step, up_grad_ref[side], tn(rows, pre_grad))
    out_ref[...] = total
    grad_in, norm_part = norm_backward(back, normed, inverse_std, norm_ref[2:3, :])
    norm_grad_ref[...] = grown(step, norm_grad_ref[...], norm_part)
    grad_ref[...] = cot.astype(F32) + grad_in

    @pl.when(step == pl.num_programs(0) - 1)
    def _():
        for apart in range(INNER):
            for outer in range(OUTER):
                row, lane, down_row = places(apart, outer)
                for side, halves in enumerate((own_refs, sent_refs)):
                    ref = halves[apart // 2]
                    up = up_grad_ref[side, pl.ds(row, 48), pl.ds(lane, D)]
                    down = down_grad_ref[side, pl.ds(down_row, 48), :]
                    ref[apart % 2, outer, 0] = up.astype(BF)
                    ref[apart % 2, outer, 1] = down.astype(BF)


def mlp(place, middle, second_rows, cotangent, norm_params, slabs):
    rows = middle.shape[0]
    slab = pl.BlockSpec((OUTER, 2, 48, D), lambda i: (0, 0, 0, 0))
    grads = (INNER // 2, OUTER, 2, 48, D)
    grad = pl.BlockSpec(grads, lambda i: (0, 0, 0, 0, 0))
    tile = pl.BlockSpec((TILE, D), lambda i: (i, 0))
    return pl.pallas_call(
        mlp_kernel,
        grid=(rows // TILE,),
        in_specs=[
            pl.BlockSpec(memory_space=pltpu.SMEM),
            tile,
            tile,
            tile,
            pl.BlockSpec((4, D), lambda i: (0, 0)),
            *[slab] * 2 * INNER,
        ],
        out_specs=[tile, tile, pl.BlockSpec((2, D), lambda i: (0, 0)), *[grad] * 4],
        out_shape=[
            jax.ShapeDtypeStruct((rows, D), F32),
            pltpu.HBM((rows, D), F32),
            jax.ShapeDtypeStruct((2, D), F32),
            *[jax.ShapeDtypeStruct(grads, BF)] * 4,
        ],
        scratch_shapes=[
            pltpu.VMEM((2, D, MLP // 2), BF),
            pltpu.VMEM((2, MLP // 2, D), BF),
            pltpu.VMEM((2, D, MLP // 2), F32),
            pltpu.VMEM((2, MLP // 2, D), F32),
        ],
        compiler_params=pltpu.CompilerParams(vmem_limit_bytes=VMEM_LIMIT),
        cost_estimate=pl.CostEstimate(
            flops=12 * rows * D * MLP, bytes_accessed=20 << 20, transcendentals=2 * rows * MLP
        ),
        name="mlp",
    )(place, middle, second_rows, cotangent, in_hbm(norm_params), *slabs)


def attn_backward_kernel(
    place_ref, own_mask_ref, other_mask_ref, x_ref, grad_ref, prob_ref, qkv_ref, out_ref,
    norm_ref, later_norm_ref, wqkv_ref, wo_ref,
    dqkv_ref, own_grad_ref, sent_grad_ref, norm_grad_ref,
    cross_ref, column_ref, wo_grad_ref,
):
    step = pl.program_id(0)

    normed, _ = normalize(x_ref[...].astype(F32))
    low_grad = grad_ref[...].astype(BF)
    head_out = out_ref[...]
    wo_grad_ref[...] = grown(step, wo_grad_ref[...], tn(head_out, low_grad))
    whole_grad = nt(low_grad, wo_ref[...]).astype(BF)
    first, second = lane_halves()
    first_wide, second_wide = first.astype(F32), second.astype(F32)
    tasks = [(image, pair) for image in range(IMAGES) for pair in range(PAIRS)]

    def places(task):
        image, pair = task
        here = slice(S * image, S * image + S)
        return here, *(slice(D * t + PAIR * pair, D * t + PAIR * (pair + 1)) for t in range(3))

    def get_pair_grad(task):
        here, lanes, _, _ = places(task)
        mask = mask_lanes(place_ref, own_mask_ref, other_mask_ref, IMAGES * step + task[0], task[1])
        grad = whole_grad[here, lanes] * mask.astype(BF)
        dots = grad.astype(F32) * head_out[here, lanes].astype(F32)
        first_dot = jnp.sum(dots * first_wide, axis=-1, keepdims=True)
        second_dot = jnp.sum(dots * second_wide, axis=-1, keepdims=True)
        return stacked(grad, first, second), jnp.concatenate([first_dot, second_dot], axis=0)

    pair_grads = [get_pair_grad(task) for task in tasks]
    prob_grads = [
        nt(pair_grad[0], qkv_ref[places(task)[0], places(task)[3]])
        for task, pair_grad in zip(tasks, pair_grads)
    ]
    score_grads = [
        (prob_ref[task].astype(F32) * (prob_grad - pair_grad[1])).astype(BF)
        for task, prob_grad, pair_grad in zip(tasks, prob_grads, pair_grads)
    ]
    for task, score_grad, (pair_grad, _) in zip(tasks, score_grads, pair_grads):
        here, query_lanes, key_lanes, value_lanes = places(task)
        keys = qkv_ref[here, key_lanes]
        queries = stacked(qkv_ref[here, query_lanes], first, second)
        query_grad = nn(score_grad[:S], keys * first) + nn(score_grad[S:], keys * second)
        key_grad = nn(jnp.transpose(queries), score_grad)
        value_grad = nn(jnp.transpose(pair_grad), prob_ref[task])
        dqkv_ref[here, query_lanes] = query_grad.astype(BF)
        dqkv_ref[here, key_lanes] = jnp.transpose(key_grad).astype(BF)
        dqkv_ref[here, value_lanes] = jnp.transpose(value_grad).astype(BF)
    dqkv = dqkv_ref[...]
    cross_ref[...] = grown(step, cross_ref[...], tn(normed.astype(BF), dqkv))
    columns = jnp.sum(dqkv.astype(F32), axis=0, keepdims=True)
    column_ref[...] = grown(step, column_ref[...], columns)

    @pl.when(step == pl.num_programs(0) - 1)
    def _():
        wqkv = wqkv_ref[...]
        products = wqkv.astype(F32) * cross_ref[...]
        gain_grad = jnp.sum(products, axis=1, keepdims=True)
        gain_grad = jnp.transpose(jnp.broadcast_to(gain_grad, (D, 128)))
        columns = column_ref[...]
        shift_grad = nt(jnp.concatenate(split(jnp.broadcast_to(columns, (8, 3 * D)))), wqkv)
        norm_grad_ref[0:1, :] = gain_grad[0:1]
        norm_grad_ref[1:2, :] = shift_grad[0:1] + shift_grad[8:9]
        norm_grad_ref[2:4, :] = later_norm_ref[...]
        gain = jnp.transpose(jnp.broadcast_to(norm_ref[0:1, :], (128, D)))[:, :1]
        shift = jnp.transpose(jnp.broadcast_to(norm_ref[1:2, :], (128, D)))[:, :1]
        cross_ref[...] = cross_ref[...] * gain + shift * columns
        for side, slab_grads in enumerate((own_grad_ref, sent_grad_ref)):
            for slab in range(12):
                pieces = []
                for unit in (2 * slab, 2 * slab + 1):
                    row, part = divmod(unit, 3)
                    piece = cross_ref[48 * row : 48 * row + 48, D * part : D * part + D]
                    piece = piece[:, HALF * side : HALF * side + HALF]
                    pieces.append(piece * 0.125 if part == 0 else piece)
                slab_grads[slab_at(slab)] = jnp.concatenate(pieces, axis=1).astype(BF)
            for row in range(HALF // 48):
                start = HALF * side + 48 * row
                slab_grads[slab_at(12 + row)] = wo_grad_ref[start : start + 48, :].astype(BF)
        sent_grad_ref[SLABS, :NORM_ROWS] = jnp.concatenate(split(norm_grad_ref[...]), axis=0)
        sent_grad_ref[SLABS, NORM_ROWS:] = jnp.zeros((48 - NORM_ROWS, D), BF)


def attn_backward(
    place, own_mask, other_mask, tokens, grad, prob, qkv, out, norm_params, later_norms, wqkv, wo
):
    rows = tokens.shape[0]
    tile = pl.BlockSpec((TILE, D), lambda i: (i, 0))
    smem = pl.BlockSpec(memory_space=pltpu.SMEM)
    return pl.pallas_call(
        attn_backward_kernel,
        grid=(rows // TILE,),
        in_specs=[
            smem,
            smem,
            smem,
            tile,
            tile,
            pl.BlockSpec((IMAGES, PAIRS, 2 * S, S), lambda i: (i, 0, 0, 0)),
            pl.BlockSpec((TILE, 3 * D), lambda i: (i, 0)),
            tile,
            pl.BlockSpec((4, D), lambda i: (0, 0)),
            pl.BlockSpec((2, D), lambda i: (0, 0)),
            pl.BlockSpec((D, 3 * D), lambda i: (0, 0)),
            pl.BlockSpec((D, D), lambda i: (0, 0)),
        ],
        out_specs=[
            pl.BlockSpec((TILE, 3 * D), lambda i: (i, 0)),
            pl.BlockSpec((SLABS, 48, D), lambda i: (0, 0, 0)),
            pl.BlockSpec((SLABS + 1, 48, D), lambda i: (0, 0, 0)),
            pl.BlockSpec((4, D), lambda i: (0, 0)),
        ],
        out_shape=[
            pltpu.HBM((rows, 3 * D), BF),
            jax.ShapeDtypeStruct((SLABS, 48, D), BF),
            jax.ShapeDtypeStruct((SLABS + 1, 48, D), BF),
            jax.ShapeDtypeStruct((4, D), F32),
        ],
        scratch_shapes=[
            pltpu.VMEM((D, 3 * D), F32),
            pltpu.VMEM((1, 3 * D), F32),
            pltpu.VMEM((D, D), F32),
        ],
        compiler_params=pltpu.CompilerParams(vmem_limit_bytes=VMEM_LIMIT),
        cost_estimate=pl.CostEstimate(
            flops=rows * D * (10 * D + 32 * S), bytes_accessed=20 << 20, transcendentals=0
        ),
        name="attn_backward",
    )(
        place, own_mask, other_mask,
        tokens, in_hbm(grad), prob, qkv, out, in_hbm(norm_params), in_hbm(later_norms), wqkv, wo,
    )


def input_grad_kernel(x_ref, grad_ref, dqkv_ref, norm_ref, wqkv_ref, out_ref):
    normed, inverse_std = normalize(x_ref[...].astype(F32))
    back = nt(dqkv_ref[...], wqkv_ref[...]) * norm_ref[0:1, :]
    mean_first = jnp.mean(back, axis=-1, keepdims=True)
    mean_second = jnp.mean(back * normed, axis=-1, keepdims=True)
    out_ref[...] = grad_ref[...] + inverse_std * (back - mean_first - normed * mean_second)


def input_gradient(tokens, grad, dqkv, norm_params, wqkv):
    rows = tokens.shape[0]
    tile = pl.BlockSpec((INPUT_TILE, D), lambda i: (i, 0))
    return pl.pallas_call(
        input_grad_kernel,
        grid=(rows // INPUT_TILE,),
        in_specs=[
            tile,
            tile,
            pl.BlockSpec((INPUT_TILE, 3 * D), lambda i: (i, 0)),
            pl.BlockSpec((4, D), lambda i: (0, 0)),
            pl.BlockSpec((D, 3 * D), lambda i: (0, 0)),
        ],
        out_specs=tile,
        out_shape=jax.ShapeDtypeStruct((rows, D), F32),
        compiler_params=pltpu.CompilerParams(vmem_limit_bytes=VMEM_LIMIT),
        cost_estimate=pl.CostEstimate(
            flops=rows * D * 6 * D, bytes_accessed=10 << 20, transcendentals=0
        ),
        name="input_gradient",
    )(in_hbm(tokens), in_hbm(grad), in_hbm(dqkv), in_hbm(norm_params), in_hbm(wqkv))


def pack_kernel(weight_ref, out_ref):
    groups, count, _, _ = weight_ref.shape
    for group in range(groups):
        blocks = [weight_ref[group, block] for block in range(count)]
        slab = jnp.concatenate(blocks, axis=1).astype(BF)
        for copy in range(OUTER):
            out_ref[copy, group] = slab


def pack(weights, first, groups):
    _, count, edge, _ = weights.shape
    shape = (OUTER, groups, edge, count * edge)
    return pl.pallas_call(
        pack_kernel,
        grid=(1,),
        in_specs=[
            pl.BlockSpec(
                (pl.Element(groups), pl.Element(count), pl.Element(edge), pl.Element(edge)),
                lambda i: (first, 0, 0, 0),
            )
        ],
        out_specs=pl.BlockSpec(shape, lambda i: (0, 0, 0, 0)),
        out_shape=jax.ShapeDtypeStruct(shape, BF),
        compiler_params=pltpu.CompilerParams(vmem_limit_bytes=SMALL_VMEM),
        name="pack",
    )(in_hbm(weights))


def add_kernel(own_ref, received_ref, *out_refs):
    for apart, out_ref in enumerate(out_refs):
        total = own_ref[apart].astype(F32) + received_ref[apart].astype(F32)
        out_ref[...] = total.astype(BF)


def add_late(own, received):
    return pl.pallas_call(
        add_kernel,
        out_shape=[jax.ShapeDtypeStruct(own.shape[1:], BF)] * own.shape[0],
        compiler_params=pltpu.CompilerParams(vmem_limit_bytes=SMALL_VMEM),
        name="add_late",
    )(own, received)


def sum_kernel(*refs):
    *in_refs, out_ref = refs
    total = in_refs[0][...].astype(F32)
    for ref in in_refs[1:]:
        total = total + ref[...].astype(F32)
    out_ref[...] = total.astype(BF)


def sum_late(pieces):
    return pl.pallas_call(
        sum_kernel,
        out_shape=jax.ShapeDtypeStruct(pieces[0].shape, BF),
        compiler_params=pltpu.CompilerParams(vmem_limit_bytes=SMALL_VMEM),
        name="sum_late",
    )(*pieces)


def combine_kernel(place_ref, own_ref, received_ref, norm_ref, *out_refs):
    norms = received_ref[SLABS, :NORM_ROWS].astype(F32)
    norms = norm_ref[...] + (norms[:4] + norms[4:])
    rows = jnp.concatenate(split(norms), axis=0)
    for apart, out_ref in enumerate(out_refs):
        start = OUTER * (place_ref[1] ^ apart)
        for outer in range(OUTER):
            total = own_ref[start + outer].astype(F32) + received_ref[start + outer].astype(F32)
            out_ref[48 * outer : 48 * outer + 48, :] = total.astype(BF)
        out_ref[48 * OUTER :, :] = rows


def combine(place, own, received, norms):
    vmem = pl.BlockSpec(memory_space=pltpu.VMEM)
    shape = jax.ShapeDtypeStruct((48 * OUTER + NORM_ROWS, D), BF)
    return pl.pallas_call(
        combine_kernel,
        in_specs=[pl.BlockSpec(memory_space=pltpu.SMEM), vmem, vmem, vmem],
        out_shape=[shape] * INNER,
        compiler_params=pltpu.CompilerParams(vmem_limit_bytes=SMALL_VMEM),
        name="combine",
    )(place, own, received, norms)


def join_kernel(*refs):
    *early_refs, out_ref = refs
    total = early_refs[0][...].astype(F32)
    for ref in early_refs[1:]:
        total = total + ref[...].astype(F32)
    norms = total[48 * OUTER : 48 * OUTER + 4] + total[48 * OUTER + 4 :]
    for outer in range(OUTER):
        out_ref[outer, :48] = total[48 * outer : 48 * outer + 48].astype(BF)
        out_ref[outer, 48:] = jnp.concatenate(split(norms), axis=0)


def join(early):
    return pl.pallas_call(
        join_kernel,
        out_shape=jax.ShapeDtypeStruct((OUTER, 48 + NORM_ROWS, D), BF),
        compiler_params=pltpu.CompilerParams(vmem_limit_bytes=SMALL_VMEM),
        name="join",
    )(*early)


def split(values):
    high = values.astype(BF)
    return high, (values - high.astype(F32)).astype(BF)


def stack(*pieces):
    return jnp.concatenate(pieces, axis=0)


def cut_rows(values, number):
    edge = values.shape[0] // number
    return [values[edge * i : edge * i + edge] for i in range(number)]


def product(left, right):
    high, low = left
    right_high, right_low = right
    one, two = cut_rows(nn(stack(high, low), right_high), 2)
    return one + (two + nn(high, right_low))


def two_products(left, middle, right):
    right_high, right_low = right
    both = cut_rows(nn(stack(left[0], middle[0], left[1], middle[1]), right_high), 4)
    high = cut_rows(nn(stack(left[0], middle[0]), right_low), 2)
    return both[0] + (both[2] + high[0]), both[1] + (both[3] + high[1])


def update_norms(scale, total, param_ref, state_ref, grad_ref, new_state_ref, new_ref):
    grads = total * scale
    state = 0.5 * state_ref[...] + 0.5 * grads * grads
    grad_ref[...] = grads
    new_state_ref[...] = state
    new_ref[...] = param_ref[...] - 0.2 * grads / jnp.sqrt(state)


def shampoo_kernel(scale, with_norms, received_ref, weight_ref, left_ref, right_ref, *refs):
    if with_norms:
        norm_ins, norm_outs, refs = refs[:2], refs[-5:-2], refs[:-5] + refs[-2:]
    out_grad_ref, left_new_ref, right_new_ref, new_weight_ref, root_ref, power_ref = refs[-6:]
    groups, count, edge = weight_ref.shape[:3]

    received = received_ref[0].astype(F32)
    for number in range(1, received_ref.shape[0]):
        received = received + received_ref[number].astype(F32)
    if with_norms:
        norms = received[0, edge:]
        update_norms(scale, norms[:4] + norms[4:], *norm_ins, *norm_outs)
    pack = min(PACK, count)
    width = pack * edge
    places = [(g, pack * n) for g in range(groups) for n in range(count // pack)]
    packs = len(places)

    def block_of(shape, dim):
        return lax.broadcasted_iota(jnp.int32, shape, dim) // edge

    row = lax.broadcasted_iota(jnp.int32, (edge, width), 0)
    lane = lax.broadcasted_iota(jnp.int32, (edge, width), 1)
    identity = (lane % edge == row).astype(F32)
    same = (block_of((width, width), 0) == block_of((width, width), 1)).astype(BF)
    lane_block = block_of((1, width), 1)

    def spread(pieces):
        return tuple(stack(*[piece] * pack) * same for piece in pieces)

    def cut(packed, index):
        return packed[:, edge * index : edge * index + edge]

    def beside(ref, place):
        return jnp.concatenate([ref[place[0], place[1] + i] for i in range(pack)], axis=1)

    grads, parts = [], []
    for group, start in places:
        grad = received[group, :edge, edge * start : edge * start + width] * scale
        blocks = [cut(grad, index) for index in range(pack)]
        for index in range(pack):
            out_grad_ref[group, start + index] = blocks[index]
        grad_t = jnp.concatenate([jnp.transpose(block) for block in blocks], axis=1)
        one, two = split(grad), split(grad_t)
        one_diagonal, two_diagonal = spread(one), spread(two)
        grads.append(one_diagonal)
        parts.append((left_ref, left_new_ref, one, two_diagonal))
        parts.append((right_ref, right_new_ref, two, one_diagonal))
    grams = [product(left, right) for _, _, left, right in parts]
    for slot, (old_ref, new_ref, _, _) in enumerate(parts):
        group, start = places[slot // 2]
        new = 0.5 * beside(old_ref, places[slot // 2]) + 0.5 * grams[slot]
        for index in range(pack):
            new_ref[group, start + index] = cut(new, index)
        columns = jnp.sum(new * new, axis=0, keepdims=True)
        squares = jnp.zeros((1, width), F32)
        for index in range(pack):
            inside = lane_block == index
            part = jnp.sum(jnp.where(inside, columns, 0.0), axis=1, keepdims=True)
            squares = jnp.where(inside, part, squares)
        factor = 2.5 / jnp.sqrt(squares)
        root_ref[slot] = jnp.broadcast_to(jnp.sqrt(jnp.sqrt(factor)), (edge, width))
        power_ref[slot] = factor * new
    slots = range(2 * packs)

    def advance(first):
        powers = [power_ref[slot] for slot in slots]
        middles = [split((5.0 * identity - power) * 0.25) for power in powers]
        rights = [spread(middle) for middle in middles]
        powers = [split(power) for power in powers]
        if first:
            squares = [product(middles[s], rights[s]) for s in slots]
            for slot in slots:
                root_ref[slot] *= (5.0 * identity - power_ref[slot]) * 0.25
        else:
            roots = [split(root_ref[slot]) for slot in slots]
            both = [two_products(roots[s], middles[s], rights[s]) for s in slots]
            squares = [pair[1] for pair in both]
            for slot in slots:
                root_ref[slot] = both[slot][0]
        rights = [spread(split(square)) for square in squares]
        powers = [split(product(powers[s], rights[s])) for s in slots]
        for slot in slots:
            power_ref[slot] = product(powers[slot], rights[slot])

    advance(True)
    for _ in range(ITERS - 2):
        advance(False)
    rights = [spread(split((5.0 * identity - power_ref[slot]) * 0.25)) for slot in slots]
    for slot in slots:
        root_ref[slot] = product(split(root_ref[slot]), rights[slot])
    steps = [product(split(root_ref[2 * n]), grads[n]) for n in range(packs)]
    rights = [spread(split(root_ref[2 * n + 1])) for n in range(packs)]
    steps = [product(split(steps[n]), rights[n]) for n in range(packs)]
    for number, (group, start) in enumerate(places):
        for index in range(pack):
            step = 0.25 * cut(steps[number], index)
            new_weight_ref[group, start + index] = weight_ref[group, start + index] - step


def shampoo(received, weights, stat_left, stat_right, scale, first, earlier=(), norms=()):
    groups = received.shape[1]
    _, count, edge, _ = weights.shape
    slots = 2 * groups * count // min(PACK, count)
    width = min(PACK, count) * edge
    block = pl.BlockSpec(
        (pl.Element(groups), pl.Element(count), pl.Element(edge), pl.Element(edge)),
        lambda i: (first, 0, 0, 0),
    )
    shape = jax.ShapeDtypeStruct(weights.shape, F32)
    norm = pl.BlockSpec((4, D), lambda i: (0, 0))
    norm_outs = 3 if norms else 0
    ins = 4 + len(norms)
    return pl.pallas_call(
        lambda *refs: shampoo_kernel(scale, bool(norms), *refs),
        grid=(1,),
        in_specs=[
            pl.BlockSpec(received.shape, lambda i: (0, 0, 0, 0)),
            *[block] * 3,
            *[norm] * len(norms),
            *[pl.BlockSpec(memory_space=pl.ANY)] * len(earlier),
        ],
        out_specs=[block] * 4 + [norm] * norm_outs,
        out_shape=[shape] * 4 + [jax.ShapeDtypeStruct((4, D), F32)] * norm_outs,
        scratch_shapes=[
            pltpu.VMEM((slots, edge, width), F32),
            pltpu.VMEM((slots, edge, width), F32),
        ],
        input_output_aliases={ins + i: i for i in range(len(earlier))},
        compiler_params=pltpu.CompilerParams(vmem_limit_bytes=SHAMPOO_VMEM),
        cost_estimate=pl.CostEstimate(
            flops=groups * (3 << 30), bytes_accessed=4 << 20, transcendentals=0
        ),
        name="shampoo",
    )(received, weights, stat_left, stat_right, *norms, *earlier)


def swap_heads(values):
    return lax.ppermute(values, "head", [(0, 1), (1, 0)])


def to_all(values, axis):
    return lax.all_to_all(values, axis, 0, 0)


def across(values, apart):
    pairs = [(i, i ^ apart) for i in range(INNER)]
    return lax.ppermute(values, "inner", pairs)


def from_all(values):
    return [values] + [across(values, apart) for apart in range(1, INNER)]


def gather_slabs(weights, small):
    early = to_all(pack(weights, 0, 1), "outer")[:, 0]
    early, late = lax.optimization_barrier((early, pack(weights, 1, 2)))
    late = to_all(late, "outer")
    early = from_all(early)
    early[1], late, small = lax.optimization_barrier((early[1], late, small))
    return early, from_all(late), small


def gather_blocks(local):
    groups, _, edge, _ = local.shape
    blocks = lax.all_gather(local, ("outer", "inner"), axis=1, tiled=True)
    blocks = blocks.reshape(groups, SLABS // INNER, INNER, D // edge, edge, edge)
    slabs = blocks.transpose(2, 1, 0, 4, 3, 5).reshape(SLABS, groups, edge, D)
    return slabs if groups > 1 else slabs[:, 0]


def scatter_blocks(slabs, count, edge):
    groups = slabs.shape[1]
    blocks = slabs.reshape(INNER, SLABS // INNER, groups, edge, D // edge, edge)
    blocks = blocks.transpose(2, 1, 0, 4, 3, 5).reshape(groups, SLABS * (D // edge), edge, edge)
    owned = lax.psum_scatter(blocks, ("outer", "inner"), scatter_dimension=1, tiled=True)
    return owned.transpose(0, 2, 1, 3).reshape(groups, edge, count * edge)


def per_device(
    tokens,
    cotangent,
    token_counts,
    head_mask,
    norm_params,
    norm_state,
    weights,
    stat_left,
    stat_right,
):
    weights, stat_left, stat_right = weights[0], stat_left[0], stat_right[0]
    _, count, edge, _ = weights.shape
    whole_slabs = count * edge == D
    other_mask = swap_heads(head_mask)
    inner = lax.axis_index("inner") if whole_slabs else 0
    place = jnp.concatenate([jnp.stack([lax.axis_index("head"), inner]), token_counts])
    if whole_slabs:
        early, late, (other_mask, place) = gather_slabs(weights, (other_mask, place))
    else:
        local = weights.astype(BF)
        early = jnp.split(gather_blocks(local[:1]), INNER)
        late = jnp.split(gather_blocks(local[1:]), INNER)
    early, late = list(early), list(late)
    masks = (head_mask, other_mask)
    early += [swap_heads(piece) for piece in early]
    prob, qkv, out, middle, second_rows, wqkv, wo = attn_forward(
        place, *masks, tokens, norm_params, early
    )
    late[1], late[3], middle = lax.optimization_barrier((late[1], late[3], middle))
    others = [swap_heads(late[0]), swap_heads(late[1]), None, swap_heads(late[3])]
    late[2], others[1], others[3] = lax.optimization_barrier((late[2], others[1], others[3]))
    others[2] = swap_heads(late[2])
    late += others
    block_out, middle_grad, norm_two, *late_sums = mlp(
        place, middle, second_rows, cotangent, norm_params, late
    )
    own_late, late_received = late_sums[:2], [swap_heads(sent) for sent in late_sums[2:]]
    if whole_slabs:
        far = add_late(own_late[1], late_received[1])
        near = add_late(own_late[0], late_received[0])
        far = [across(far[number], 2 + number) for number in range(2)]
        near, middle_grad = lax.optimization_barrier((list(near), middle_grad))
        late_grads = [near[0], across(near[1], 1), *far]
    dqkv, own_early, sent_early, norm_sums = attn_backward(
        place, *masks, tokens, middle_grad, prob, qkv, out, norm_params, norm_two, wqkv, wo
    )
    if whole_slabs:
        late_grads, sent_early = lax.optimization_barrier((late_grads, sent_early))
    early_received = swap_heads(sent_early)
    devices = lax.axis_size("outer") * lax.axis_size("inner") * lax.axis_size("head")
    scale = 1.0 / math.sqrt(tokens.shape[0] * devices)
    state = (weights, stat_left, stat_right, scale)
    if whole_slabs:
        late_grads = to_all(sum_late(late_grads), "outer")
        early_grads = list(combine(place, own_early, early_received, norm_sums))
        early_grads, dqkv = lax.optimization_barrier((early_grads, dqkv))
        early_grads[1:] = [across(early_grads[apart], apart) for apart in range(1, INNER)]
        input_grad = input_gradient(tokens, middle_grad, dqkv, norm_params, wqkv)
        early_grads, input_grad = lax.optimization_barrier((early_grads, input_grad))
        joined, late_grads = lax.optimization_barrier((join(early_grads), late_grads))
        joined = to_all(joined, "outer")[:, None]
        results = shampoo(late_grads, *state, 1)
        results = shampoo(joined, *state, 0, results, (norm_params, norm_state))
    else:
        input_grad = input_gradient(tokens, middle_grad, dqkv, norm_params, wqkv)
        early_slabs = own_early.astype(F32) + early_received[:SLABS].astype(F32)
        late_slabs = jnp.concatenate(own_late).astype(F32) + jnp.concatenate(late_received)
        late_slabs = late_slabs.reshape(SLABS, 2, edge, D)
        slabs = jnp.concatenate([early_slabs[:, None], late_slabs], axis=1).astype(BF)
        owned = scatter_blocks(slabs, count, edge)
        results = list(shampoo(owned[None], *state, 0))
        norm_grads = lax.psum(norm_sums, ("outer", "inner", "head")) * scale
        state_new = 0.5 * norm_state + 0.5 * norm_grads * norm_grads
        results += [norm_grads, state_new, norm_params - 0.2 * norm_grads / jnp.sqrt(state_new)]
    return (block_out, input_grad, *[result[None] for result in results[:4]], *results[4:])


def solution(mesh):
    shape = (mesh.shape["dp"] // INNER, INNER, mesh.shape["head"])
    split_mesh = Mesh(mesh.devices.reshape(shape), ("outer", "inner", "head"))
    group = ("outer", "inner")
    blocks = P("head", None, group, None, None)
    rows = P(group + ("head",), None)
    return jax.shard_map(
        per_device,
        mesh=split_mesh,
        in_specs=(rows, rows, P(group), P(group, "head"), P(), P(), blocks, blocks, blocks),
        out_specs=(rows, rows, blocks, blocks, blocks, blocks, P(), P(), P()),
        check_vma=False,
    )
```

```python
import math

import jax
import jax.numpy as jnp
from jax import lax
from jax.experimental import pallas as pl
from jax.experimental.pallas import tpu as pltpu
from jax.sharding import Mesh, PartitionSpec as P

D = 384
HEAD_DIM = 64
MLP = 1536
S = 256
ITERS = 8
PAIR = 2 * HEAD_DIM
PAIRS = D // PAIR
HALF = D // 2
SLABS = 16
INNER = 4
OUTER = SLABS // INNER
TILE = 512
INPUT_TILE = 768
IMAGES = TILE // S
NORM_ROWS = 8
PACK = 2
ROOT_HALF = 0.7071067811865476
DENSITY_FACTOR = 0.3989422804014327
BF = jnp.bfloat16
F32 = jnp.float32
VMEM_LIMIT = 28 << 20
SMALL_VMEM = 8 << 20
SHAMPOO_VMEM = 24 << 20


def in_hbm(values):
    return pltpu.with_memory_space_constraint(values, pltpu.HBM)


def nn(left, right):
    return jnp.dot(left, right, preferred_element_type=F32)


def nt(left, right):
    return lax.dot_general(left, right, (((1,), (1,)), ((), ())), preferred_element_type=F32)


def tn(left, right):
    return lax.dot_general(left, right, (((0,), (0,)), ((), ())), preferred_element_type=F32)


def normalize(values):
    centered = values - jnp.mean(values, axis=-1, keepdims=True)
    variance = jnp.mean(centered * centered, axis=-1, keepdims=True)
    inverse_std = lax.rsqrt(variance + 1e-06)
    return centered * inverse_std, inverse_std


def norm_backward(grad_out, normed, inverse_std, gain):
    grad_normed = grad_out * gain
    mean_first = jnp.mean(grad_normed, axis=-1, keepdims=True)
    mean_second = jnp.mean(grad_normed * normed, axis=-1, keepdims=True)
    grad_in = inverse_std * (grad_normed - mean_first - normed * mean_second)
    gain_grad = jnp.sum(grad_out * normed, axis=0, keepdims=True)
    shift_grad = jnp.sum(grad_out, axis=0, keepdims=True)
    return grad_in, jnp.concatenate([gain_grad, shift_grad], axis=0)


def grown(step, total, part):
    return jnp.where(step == 0, part, total + part)


def slab_at(owner):
    return (owner % INNER) * OUTER + owner // INNER


def lane_halves():
    lane = lax.broadcasted_iota(jnp.int32, (1, PAIR), 1)
    first = (lane < HEAD_DIM).astype(BF)
    return first, (1 - first).astype(BF)


def stacked(values, first, second):
    return jnp.concatenate([values * first, values * second], axis=0)


def mask_lanes(place_ref, own_ref, other_ref, image, pair):
    image = place_ref[0] * (own_ref.shape[0] // 2) + image
    heads = own_ref.shape[1]
    on = [
        own_ref[image, head] if head < heads else other_ref[image, head - heads]
        for head in (2 * pair, 2 * pair + 1)
    ]
    lane = lax.broadcasted_iota(jnp.int32, (1, PAIR), 1)
    return jnp.where(lane < HEAD_DIM, on[0], on[1]).astype(F32)


def attn_forward_kernel(
    place_ref, own_mask_ref, other_mask_ref, x_ref, norm_ref, *refs
):
    slab_refs, refs = refs[: 2 * INNER], refs[2 * INNER :]
    prob_ref, qkv_ref, out_ref, middle_ref, rows_ref, wqkv_ref, wo_ref, held_ref = refs
    step = pl.program_id(0)

    @pl.when(step == 0)
    def _():
        for number, ref in enumerate(slab_refs):
            side, apart = divmod(number, INNER)
            held_ref[side, place_ref[1] ^ apart] = ref[...]

        def slab_of(side, owner):
            return held_ref[side, owner % INNER, owner // INNER]

        for row in range(D // 48):
            for part in range(3):
                pieces = []
                for number in range(2):
                    slab, side = divmod(3 * row + part, 2)
                    piece = slab_of(number, slab)[:, side * HALF : (side + 1) * HALF]
                    pieces.append(piece)
                joined = jnp.concatenate(pieces, axis=1)
                if part == 0:
                    joined = joined * 0.125
                wqkv_ref[48 * row : 48 * row + 48, D * part : D * part + D] = joined
        for side in range(2):
            for row in range(HALF // 48):
                start = side * HALF + 48 * row
                wo_ref[start : start + 48, :] = slab_of(side, 12 + row)

    x = x_ref[...].astype(F32)
    normed, _ = normalize(x)
    rows = (normed * norm_ref[0:1, :] + norm_ref[1:2, :]).astype(BF)
    qkv_ref[...] = nn(rows, wqkv_ref[...]).astype(BF)
    first, second = lane_halves()
    column = lax.broadcasted_iota(jnp.int32, (1, S), 1)
    tasks = [(image, pair) for image in range(IMAGES) for pair in range(PAIRS)]

    def places(task):
        image, pair = task
        here = slice(S * image, S * image + S)
        return here, *(slice(D * t + PAIR * pair, D * t + PAIR * (pair + 1)) for t in range(3))

    def get_scores(task):
        here, query_lanes, key_lanes, _ = places(task)
        return nt(stacked(qkv_ref[here, query_lanes], first, second), qkv_ref[here, key_lanes])

    def get_prob(task, scores):
        image = place_ref[0] * (own_mask_ref.shape[0] // 2) + IMAGES * step + task[0]
        scores = jnp.where(column < place_ref[2 + image], scores, -1e30)
        top = jnp.max(scores, axis=-1, keepdims=True)
        exp_scores = jnp.exp(scores - top)
        total = jnp.sum(exp_scores, axis=-1, keepdims=True)
        prob = (exp_scores * (1.0 / total)).astype(BF)
        prob_ref[task] = prob
        return prob

    all_scores = [get_scores(task) for task in tasks]
    probs = [get_prob(task, scores) for task, scores in zip(tasks, all_scores)]
    for task, prob in zip(tasks, probs):
        here, lanes, _, value_lanes = places(task)
        values = qkv_ref[here, value_lanes]
        head_out = nn(prob[:S], values * first) + nn(prob[S:], values * second)
        mask = mask_lanes(place_ref, own_mask_ref, other_mask_ref, IMAGES * step + task[0], task[1])
        out_ref[here, lanes] = (head_out * mask).astype(BF)
    middle = x + nn(out_ref[...], wo_ref[...])
    middle_ref[...] = middle
    normed, _ = normalize(middle)
    rows_ref[...] = (normed * norm_ref[2:3, :] + norm_ref[3:4, :]).astype(BF)


def attn_forward(place, own_mask, other_mask, tokens, norm_params, slabs):
    rows = tokens.shape[0]
    images = rows // S
    tile = pl.BlockSpec((TILE, D), lambda i: (i, 0))
    slab = pl.BlockSpec((OUTER, 48, D), lambda i: (0, 0, 0))
    smem = pl.BlockSpec(memory_space=pltpu.SMEM)
    return pl.pallas_call(
        attn_forward_kernel,
        grid=(rows // TILE,),
        in_specs=[smem] * 3 + [tile, pl.BlockSpec((4, D), lambda i: (0, 0))] + [slab] * 2 * INNER,
        out_specs=[
            pl.BlockSpec((IMAGES, PAIRS, 2 * S, S), lambda i: (i, 0, 0, 0)),
            pl.BlockSpec((TILE, 3 * D), lambda i: (i, 0)),
            tile,
            tile,
            tile,
            pl.BlockSpec((D, 3 * D), lambda i: (0, 0)),
            pl.BlockSpec((D, D), lambda i: (0, 0)),
        ],
        out_shape=[
            pltpu.HBM((images, PAIRS, 2 * S, S), BF),
            pltpu.HBM((rows, 3 * D), BF),
            pltpu.HBM((rows, D), BF),
            jax.ShapeDtypeStruct((rows, D), F32),
            jax.ShapeDtypeStruct((rows, D), BF),
            pltpu.HBM((D, 3 * D), BF),
            pltpu.HBM((D, D), BF),
        ],
        scratch_shapes=[pltpu.VMEM((2, INNER, OUTER, 48, D), BF)],
        compiler_params=pltpu.CompilerParams(vmem_limit_bytes=VMEM_LIMIT),
        cost_estimate=pl.CostEstimate(
            flops=rows * D * (8 * D + 16 * S), bytes_accessed=16 << 20, transcendentals=rows * 6 * S
        ),
        name="attn_forward",
    )(place, own_mask, other_mask, tokens, in_hbm(norm_params), *slabs)


def mlp_kernel(place_ref, middle_ref, rows_ref, cot_ref, norm_ref, *refs):
    slab_refs, refs = refs[: 2 * INNER], refs[2 * INNER :]
    out_ref, grad_ref, norm_grad_ref, *refs = refs
    own_refs, sent_refs, refs = refs[:2], refs[2:4], refs[4:]
    up_ref, down_ref, up_grad_ref, down_grad_ref = refs
    step = pl.program_id(0)
    half = MLP // 2

    def places(apart, outer):
        inner = place_ref[1] ^ apart
        row = pl.multiple_of(48 * (2 * outer + inner // 2), 16)
        lane = pl.multiple_of(D * (inner % 2), 128)
        down_row = pl.multiple_of(48 * (INNER * outer + inner), 16)
        return row, lane, down_row

    @pl.when(step == 0)
    def _():
        for number, ref in enumerate(slab_refs):
            side, apart = divmod(number, INNER)
            for outer in range(OUTER):
                row, lane, down_row = places(apart, outer)
                up_ref[side, pl.ds(row, 48), pl.ds(lane, D)] = ref[outer, 0]
                down_ref[side, pl.ds(down_row, 48), :] = ref[outer, 1]

    middle = middle_ref[...]
    normed, inverse_std = normalize(middle)
    rows, cot = rows_ref[...], cot_ref[...]
    total = middle
    back = None
    for side in range(2):
        up, down = up_ref[side], down_ref[side]
        pre = nn(rows, up)
        act_grad = nt(cot, down)
        cumulative = 0.5 * (1.0 + lax.erf(pre * ROOT_HALF))
        density = jnp.exp(-0.5 * pre * pre) * DENSITY_FACTOR
        act = (pre * cumulative).astype(BF)
        pre_grad = (act_grad * (cumulative + pre * density)).astype(BF)
        total = total + nn(act, down)
        term = nt(pre_grad, up)
        back = term if back is None else back + term
        down_grad_ref[side] = grown(step, down_grad_ref[side], tn(act, cot))
        up_grad_ref[side] = grown(step, up_grad_ref[side], tn(rows, pre_grad))
    out_ref[...] = total
    grad_in, norm_part = norm_backward(back, normed, inverse_std, norm_ref[2:3, :])
    norm_grad_ref[...] = grown(step, norm_grad_ref[...], norm_part)
    grad_ref[...] = cot.astype(F32) + grad_in

    @pl.when(step == pl.num_programs(0) - 1)
    def _():
        for apart in range(INNER):
            for outer in range(OUTER):
                row, lane, down_row = places(apart, outer)
                for side, halves in enumerate((own_refs, sent_refs)):
                    ref = halves[apart // 2]
                    up = up_grad_ref[side, pl.ds(row, 48), pl.ds(lane, D)]
                    down = down_grad_ref[side, pl.ds(down_row, 48), :]
                    ref[apart % 2, outer, 0] = up.astype(BF)
                    ref[apart % 2, outer, 1] = down.astype(BF)


def mlp(place, middle, second_rows, cotangent, norm_params, slabs):
    rows = middle.shape[0]
    slab = pl.BlockSpec((OUTER, 2, 48, D), lambda i: (0, 0, 0, 0))
    grads = (INNER // 2, OUTER, 2, 48, D)
    grad = pl.BlockSpec(grads, lambda i: (0, 0, 0, 0, 0))
    tile = pl.BlockSpec((TILE, D), lambda i: (i, 0))
    return pl.pallas_call(
        mlp_kernel,
        grid=(rows // TILE,),
        in_specs=[
            pl.BlockSpec(memory_space=pltpu.SMEM),
            tile,
            tile,
            tile,
            pl.BlockSpec((4, D), lambda i: (0, 0)),
            *[slab] * 2 * INNER,
        ],
        out_specs=[tile, tile, pl.BlockSpec((2, D), lambda i: (0, 0)), *[grad] * 4],
        out_shape=[
            jax.ShapeDtypeStruct((rows, D), F32),
            jax.ShapeDtypeStruct((rows, D), F32),
            jax.ShapeDtypeStruct((2, D), F32),
            *[jax.ShapeDtypeStruct(grads, BF)] * 4,
        ],
        scratch_shapes=[
            pltpu.VMEM((2, D, MLP // 2), BF),
            pltpu.VMEM((2, MLP // 2, D), BF),
            pltpu.VMEM((2, D, MLP // 2), F32),
            pltpu.VMEM((2, MLP // 2, D), F32),
        ],
        compiler_params=pltpu.CompilerParams(vmem_limit_bytes=VMEM_LIMIT),
        cost_estimate=pl.CostEstimate(
            flops=12 * rows * D * MLP, bytes_accessed=20 << 20, transcendentals=2 * rows * MLP
        ),
        name="mlp",
    )(place, middle, second_rows, cotangent, in_hbm(norm_params), *slabs)


def attn_backward_kernel(
    place_ref, own_mask_ref, other_mask_ref, x_ref, grad_ref, prob_ref, qkv_ref, out_ref,
    norm_ref, later_norm_ref, wqkv_ref, wo_ref,
    dqkv_ref, own_grad_ref, sent_grad_ref, norm_grad_ref,
    cross_ref, column_ref, wo_grad_ref,
):
    step = pl.program_id(0)

    normed, _ = normalize(x_ref[...].astype(F32))
    low_grad = grad_ref[...].astype(BF)
    head_out = out_ref[...]
    wo_grad_ref[...] = grown(step, wo_grad_ref[...], tn(head_out, low_grad))
    whole_grad = nt(low_grad, wo_ref[...]).astype(BF)
    first, second = lane_halves()
    first_wide, second_wide = first.astype(F32), second.astype(F32)
    tasks = [(image, pair) for image in range(IMAGES) for pair in range(PAIRS)]

    def places(task):
        image, pair = task
        here = slice(S * image, S * image + S)
        return here, *(slice(D * t + PAIR * pair, D * t + PAIR * (pair + 1)) for t in range(3))

    def get_pair_grad(task):
        here, lanes, _, _ = places(task)
        mask = mask_lanes(place_ref, own_mask_ref, other_mask_ref, IMAGES * step + task[0], task[1])
        grad = whole_grad[here, lanes] * mask.astype(BF)
        dots = grad.astype(F32) * head_out[here, lanes].astype(F32)
        first_dot = jnp.sum(dots * first_wide, axis=-1, keepdims=True)
        second_dot = jnp.sum(dots * second_wide, axis=-1, keepdims=True)
        return stacked(grad, first, second), jnp.concatenate([first_dot, second_dot], axis=0)

    pair_grads = [get_pair_grad(task) for task in tasks]
    prob_grads = [
        nt(pair_grad[0], qkv_ref[places(task)[0], places(task)[3]])
        for task, pair_grad in zip(tasks, pair_grads)
    ]
    score_grads = [
        (prob_ref[task].astype(F32) * (prob_grad - pair_grad[1])).astype(BF)
        for task, prob_grad, pair_grad in zip(tasks, prob_grads, pair_grads)
    ]
    for task, score_grad, (pair_grad, _) in zip(tasks, score_grads, pair_grads):
        here, query_lanes, key_lanes, value_lanes = places(task)
        keys = qkv_ref[here, key_lanes]
        queries = stacked(qkv_ref[here, query_lanes], first, second)
        query_grad = nn(score_grad[:S], keys * first) + nn(score_grad[S:], keys * second)
        key_grad = nn(jnp.transpose(queries), score_grad)
        value_grad = nn(jnp.transpose(pair_grad), prob_ref[task])
        dqkv_ref[here, query_lanes] = query_grad.astype(BF)
        dqkv_ref[here, key_lanes] = jnp.transpose(key_grad).astype(BF)
        dqkv_ref[here, value_lanes] = jnp.transpose(value_grad).astype(BF)
    dqkv = dqkv_ref[...]
    cross_ref[...] = grown(step, cross_ref[...], tn(normed.astype(BF), dqkv))
    columns = jnp.sum(dqkv.astype(F32), axis=0, keepdims=True)
    column_ref[...] = grown(step, column_ref[...], columns)

    @pl.when(step == pl.num_programs(0) - 1)
    def _():
        wqkv = wqkv_ref[...]
        products = wqkv.astype(F32) * cross_ref[...]
        gain_grad = jnp.sum(products, axis=1, keepdims=True)
        gain_grad = jnp.transpose(jnp.broadcast_to(gain_grad, (D, 128)))
        columns = column_ref[...]
        shift_grad = nt(jnp.concatenate(split(jnp.broadcast_to(columns, (8, 3 * D)))), wqkv)
        norm_grad_ref[0:1, :] = gain_grad[0:1]
        norm_grad_ref[1:2, :] = shift_grad[0:1] + shift_grad[8:9]
        norm_grad_ref[2:4, :] = later_norm_ref[...]
        gain = jnp.transpose(jnp.broadcast_to(norm_ref[0:1, :], (128, D)))[:, :1]
        shift = jnp.transpose(jnp.broadcast_to(norm_ref[1:2, :], (128, D)))[:, :1]
        cross_ref[...] = cross_ref[...] * gain + shift * columns
        for side, slab_grads in enumerate((own_grad_ref, sent_grad_ref)):
            for slab in range(12):
                pieces = []
                for unit in (2 * slab, 2 * slab + 1):
                    row, part = divmod(unit, 3)
                    piece = cross_ref[48 * row : 48 * row + 48, D * part : D * part + D]
                    piece = piece[:, HALF * side : HALF * side + HALF]
                    pieces.append(piece * 0.125 if part == 0 else piece)
                slab_grads[slab_at(slab)] = jnp.concatenate(pieces, axis=1).astype(BF)
            for row in range(HALF // 48):
                start = HALF * side + 48 * row
                slab_grads[slab_at(12 + row)] = wo_grad_ref[start : start + 48, :].astype(BF)
        sent_grad_ref[SLABS, :NORM_ROWS] = jnp.concatenate(split(norm_grad_ref[...]), axis=0)
        sent_grad_ref[SLABS, NORM_ROWS:] = jnp.zeros((48 - NORM_ROWS, D), BF)


def attn_backward(
    place, own_mask, other_mask, tokens, grad, prob, qkv, out, norm_params, later_norms, wqkv, wo
):
    rows = tokens.shape[0]
    tile = pl.BlockSpec((TILE, D), lambda i: (i, 0))
    smem = pl.BlockSpec(memory_space=pltpu.SMEM)
    return pl.pallas_call(
        attn_backward_kernel,
        grid=(rows // TILE,),
        in_specs=[
            smem,
            smem,
            smem,
            tile,
            tile,
            pl.BlockSpec((IMAGES, PAIRS, 2 * S, S), lambda i: (i, 0, 0, 0)),
            pl.BlockSpec((TILE, 3 * D), lambda i: (i, 0)),
            tile,
            pl.BlockSpec((4, D), lambda i: (0, 0)),
            pl.BlockSpec((2, D), lambda i: (0, 0)),
            pl.BlockSpec((D, 3 * D), lambda i: (0, 0)),
            pl.BlockSpec((D, D), lambda i: (0, 0)),
        ],
        out_specs=[
            pl.BlockSpec((TILE, 3 * D), lambda i: (i, 0)),
            pl.BlockSpec((SLABS, 48, D), lambda i: (0, 0, 0)),
            pl.BlockSpec((SLABS + 1, 48, D), lambda i: (0, 0, 0)),
            pl.BlockSpec((4, D), lambda i: (0, 0)),
        ],
        out_shape=[
            pltpu.HBM((rows, 3 * D), BF),
            jax.ShapeDtypeStruct((SLABS, 48, D), BF),
            jax.ShapeDtypeStruct((SLABS + 1, 48, D), BF),
            jax.ShapeDtypeStruct((4, D), F32),
        ],
        scratch_shapes=[
            pltpu.VMEM((D, 3 * D), F32),
            pltpu.VMEM((1, 3 * D), F32),
            pltpu.VMEM((D, D), F32),
        ],
        compiler_params=pltpu.CompilerParams(vmem_limit_bytes=VMEM_LIMIT),
        cost_estimate=pl.CostEstimate(
            flops=rows * D * (10 * D + 32 * S), bytes_accessed=20 << 20, transcendentals=0
        ),
        name="attn_backward",
    )(
        place, own_mask, other_mask,
        tokens, grad, prob, qkv, out, in_hbm(norm_params), in_hbm(later_norms), wqkv, wo,
    )


def input_grad_kernel(x_ref, grad_ref, dqkv_ref, norm_ref, wqkv_ref, out_ref):
    normed, inverse_std = normalize(x_ref[...].astype(F32))
    back = nt(dqkv_ref[...], wqkv_ref[...]) * norm_ref[0:1, :]
    mean_first = jnp.mean(back, axis=-1, keepdims=True)
    mean_second = jnp.mean(back * normed, axis=-1, keepdims=True)
    out_ref[...] = grad_ref[...] + inverse_std * (back - mean_first - normed * mean_second)


def input_gradient(tokens, grad, dqkv, norm_params, wqkv):
    rows = tokens.shape[0]
    tile = pl.BlockSpec((INPUT_TILE, D), lambda i: (i, 0))
    return pl.pallas_call(
        input_grad_kernel,
        grid=(rows // INPUT_TILE,),
        in_specs=[
            tile,
            tile,
            pl.BlockSpec((INPUT_TILE, 3 * D), lambda i: (i, 0)),
            pl.BlockSpec((4, D), lambda i: (0, 0)),
            pl.BlockSpec((D, 3 * D), lambda i: (0, 0)),
        ],
        out_specs=tile,
        out_shape=jax.ShapeDtypeStruct((rows, D), F32),
        compiler_params=pltpu.CompilerParams(vmem_limit_bytes=VMEM_LIMIT),
        cost_estimate=pl.CostEstimate(
            flops=rows * D * 6 * D, bytes_accessed=10 << 20, transcendentals=0
        ),
        name="input_gradient",
    )(in_hbm(tokens), in_hbm(grad), in_hbm(dqkv), in_hbm(norm_params), in_hbm(wqkv))


def pack_kernel(weight_ref, out_ref):
    groups, count, _, _ = weight_ref.shape
    for group in range(groups):
        blocks = [weight_ref[group, block] for block in range(count)]
        slab = jnp.concatenate(blocks, axis=1).astype(BF)
        for copy in range(OUTER):
            out_ref[copy, group] = slab


def pack(weights, first, groups):
    _, count, edge, _ = weights.shape
    shape = (OUTER, groups, edge, count * edge)
    return pl.pallas_call(
        pack_kernel,
        grid=(1,),
        in_specs=[
            pl.BlockSpec(
                (pl.Element(groups), pl.Element(count), pl.Element(edge), pl.Element(edge)),
                lambda i: (first, 0, 0, 0),
            )
        ],
        out_specs=pl.BlockSpec(shape, lambda i: (0, 0, 0, 0)),
        out_shape=jax.ShapeDtypeStruct(shape, BF),
        compiler_params=pltpu.CompilerParams(vmem_limit_bytes=SMALL_VMEM),
        name="pack",
    )(in_hbm(weights))


def add_kernel(own_ref, received_ref, *out_refs):
    for apart, out_ref in enumerate(out_refs):
        total = own_ref[apart].astype(F32) + received_ref[apart].astype(F32)
        out_ref[...] = total.astype(BF)


def add_late(own, received):
    return pl.pallas_call(
        add_kernel,
        out_shape=[jax.ShapeDtypeStruct(own.shape[1:], BF)] * own.shape[0],
        compiler_params=pltpu.CompilerParams(vmem_limit_bytes=SMALL_VMEM),
        name="add_late",
    )(own, received)


def sum_kernel(*refs):
    *in_refs, out_ref = refs
    total = in_refs[0][...].astype(F32)
    for ref in in_refs[1:]:
        total = total + ref[...].astype(F32)
    out_ref[...] = total.astype(BF)


def sum_late(pieces):
    return pl.pallas_call(
        sum_kernel,
        out_shape=jax.ShapeDtypeStruct(pieces[0].shape, BF),
        compiler_params=pltpu.CompilerParams(vmem_limit_bytes=SMALL_VMEM),
        name="sum_late",
    )(*pieces)


def combine_kernel(place_ref, own_ref, received_ref, norm_ref, *out_refs):
    norms = received_ref[SLABS, :NORM_ROWS].astype(F32)
    norms = norm_ref[...] + (norms[:4] + norms[4:])
    rows = jnp.concatenate(split(norms), axis=0)
    for apart, out_ref in enumerate(out_refs):
        start = OUTER * (place_ref[1] ^ apart)
        for outer in range(OUTER):
            total = own_ref[start + outer].astype(F32) + received_ref[start + outer].astype(F32)
            out_ref[48 * outer : 48 * outer + 48, :] = total.astype(BF)
        out_ref[48 * OUTER :, :] = rows


def combine(place, own, received, norms):
    vmem = pl.BlockSpec(memory_space=pltpu.VMEM)
    shape = jax.ShapeDtypeStruct((48 * OUTER + NORM_ROWS, D), BF)
    return pl.pallas_call(
        combine_kernel,
        in_specs=[pl.BlockSpec(memory_space=pltpu.SMEM), vmem, vmem, vmem],
        out_shape=[shape] * INNER,
        compiler_params=pltpu.CompilerParams(vmem_limit_bytes=SMALL_VMEM),
        name="combine",
    )(place, own, received, norms)


def join_kernel(*refs):
    *early_refs, out_ref = refs
    total = early_refs[0][...].astype(F32)
    for ref in early_refs[1:]:
        total = total + ref[...].astype(F32)
    norms = total[48 * OUTER : 48 * OUTER + 4] + total[48 * OUTER + 4 :]
    for outer in range(OUTER):
        out_ref[outer, :48] = total[48 * outer : 48 * outer + 48].astype(BF)
        out_ref[outer, 48:] = jnp.concatenate(split(norms), axis=0)


def join(early):
    return pl.pallas_call(
        join_kernel,
        out_shape=jax.ShapeDtypeStruct((OUTER, 48 + NORM_ROWS, D), BF),
        compiler_params=pltpu.CompilerParams(vmem_limit_bytes=SMALL_VMEM),
        name="join",
    )(*early)


def split(values):
    high = values.astype(BF)
    return high, (values - high.astype(F32)).astype(BF)


def stack(*pieces):
    return jnp.concatenate(pieces, axis=0)


def cut_rows(values, number):
    edge = values.shape[0] // number
    return [values[edge * i : edge * i + edge] for i in range(number)]


def product(left, right):
    high, low = left
    right_high, right_low = right
    one, two = cut_rows(nn(stack(high, low), right_high), 2)
    return one + (two + nn(high, right_low))


def two_products(left, middle, right):
    right_high, right_low = right
    both = cut_rows(nn(stack(left[0], middle[0], left[1], middle[1]), right_high), 4)
    high = cut_rows(nn(stack(left[0], middle[0]), right_low), 2)
    return both[0] + (both[2] + high[0]), both[1] + (both[3] + high[1])


def update_norms(scale, total, param_ref, state_ref, grad_ref, new_state_ref, new_ref):
    grads = total * scale
    state = 0.5 * state_ref[...] + 0.5 * grads * grads
    grad_ref[...] = grads
    new_state_ref[...] = state
    new_ref[...] = param_ref[...] - 0.2 * grads / jnp.sqrt(state)


def shampoo_kernel(scale, with_norms, received_ref, weight_ref, left_ref, right_ref, *refs):
    if with_norms:
        norm_ins, norm_outs, refs = refs[:2], refs[-5:-2], refs[:-5] + refs[-2:]
    out_grad_ref, left_new_ref, right_new_ref, new_weight_ref, root_ref, power_ref = refs[-6:]
    groups, count, edge = weight_ref.shape[:3]

    received = received_ref[0].astype(F32)
    for number in range(1, received_ref.shape[0]):
        received = received + received_ref[number].astype(F32)
    if with_norms:
        norms = received[0, edge:]
        update_norms(scale, norms[:4] + norms[4:], *norm_ins, *norm_outs)
    pack = min(PACK, count)
    width = pack * edge
    places = [(g, pack * n) for g in range(groups) for n in range(count // pack)]
    packs = len(places)

    def block_of(shape, dim):
        return lax.broadcasted_iota(jnp.int32, shape, dim) // edge

    row = lax.broadcasted_iota(jnp.int32, (edge, width), 0)
    lane = lax.broadcasted_iota(jnp.int32, (edge, width), 1)
    identity = (lane % edge == row).astype(F32)
    same = (block_of((width, width), 0) == block_of((width, width), 1)).astype(BF)
    lane_block = block_of((1, width), 1)

    def spread(pieces):
        return tuple(stack(*[piece] * pack) * same for piece in pieces)

    def cut(packed, index):
        return packed[:, edge * index : edge * index + edge]

    def beside(ref, place):
        return jnp.concatenate([ref[place[0], place[1] + i] for i in range(pack)], axis=1)

    grads, parts = [], []
    for group, start in places:
        grad = received[group, :edge, edge * start : edge * start + width] * scale
        blocks = [cut(grad, index) for index in range(pack)]
        for index in range(pack):
            out_grad_ref[group, start + index] = blocks[index]
        grad_t = jnp.concatenate([jnp.transpose(block) for block in blocks], axis=1)
        one, two = split(grad), split(grad_t)
        one_diagonal, two_diagonal = spread(one), spread(two)
        grads.append(one_diagonal)
        parts.append((left_ref, left_new_ref, one, two_diagonal))
        parts.append((right_ref, right_new_ref, two, one_diagonal))
    grams = [product(left, right) for _, _, left, right in parts]
    for slot, (old_ref, new_ref, _, _) in enumerate(parts):
        group, start = places[slot // 2]
        new = 0.5 * beside(old_ref, places[slot // 2]) + 0.5 * grams[slot]
        for index in range(pack):
            new_ref[group, start + index] = cut(new, index)
        columns = jnp.sum(new * new, axis=0, keepdims=True)
        squares = jnp.zeros((1, width), F32)
        for index in range(pack):
            inside = lane_block == index
            part = jnp.sum(jnp.where(inside, columns, 0.0), axis=1, keepdims=True)
            squares = jnp.where(inside, part, squares)
        factor = 2.5 / jnp.sqrt(squares)
        root_ref[slot] = jnp.broadcast_to(jnp.sqrt(jnp.sqrt(factor)), (edge, width))
        power_ref[slot] = factor * new
    slots = range(2 * packs)

    def advance(first):
        powers = [power_ref[slot] for slot in slots]
        middles = [split((5.0 * identity - power) * 0.25) for power in powers]
        rights = [spread(middle) for middle in middles]
        powers = [split(power) for power in powers]
        if first:
            squares = [product(middles[s], rights[s]) for s in slots]
            for slot in slots:
                root_ref[slot] *= (5.0 * identity - power_ref[slot]) * 0.25
        else:
            roots = [split(root_ref[slot]) for slot in slots]
            both = [two_products(roots[s], middles[s], rights[s]) for s in slots]
            squares = [pair[1] for pair in both]
            for slot in slots:
                root_ref[slot] = both[slot][0]
        rights = [spread(split(square)) for square in squares]
        powers = [split(product(powers[s], rights[s])) for s in slots]
        for slot in slots:
            power_ref[slot] = product(powers[slot], rights[slot])

    advance(True)
    for _ in range(ITERS - 2):
        advance(False)
    rights = [spread(split((5.0 * identity - power_ref[slot]) * 0.25)) for slot in slots]
    for slot in slots:
        root_ref[slot] = product(split(root_ref[slot]), rights[slot])
    steps = [product(split(root_ref[2 * n]), grads[n]) for n in range(packs)]
    rights = [spread(split(root_ref[2 * n + 1])) for n in range(packs)]
    steps = [product(split(steps[n]), rights[n]) for n in range(packs)]
    for number, (group, start) in enumerate(places):
        for index in range(pack):
            step = 0.25 * cut(steps[number], index)
            new_weight_ref[group, start + index] = weight_ref[group, start + index] - step


def shampoo(received, weights, stat_left, stat_right, scale, first, earlier=(), norms=()):
    groups = received.shape[1]
    _, count, edge, _ = weights.shape
    slots = 2 * groups * count // min(PACK, count)
    width = min(PACK, count) * edge
    block = pl.BlockSpec(
        (pl.Element(groups), pl.Element(count), pl.Element(edge), pl.Element(edge)),
        lambda i: (first, 0, 0, 0),
    )
    shape = jax.ShapeDtypeStruct(weights.shape, F32)
    norm = pl.BlockSpec((4, D), lambda i: (0, 0))
    norm_outs = 3 if norms else 0
    ins = 4 + len(norms)
    return pl.pallas_call(
        lambda *refs: shampoo_kernel(scale, bool(norms), *refs),
        grid=(1,),
        in_specs=[
            pl.BlockSpec(received.shape, lambda i: (0, 0, 0, 0)),
            *[block] * 3,
            *[norm] * len(norms),
            *[pl.BlockSpec(memory_space=pl.ANY)] * len(earlier),
        ],
        out_specs=[block] * 4 + [norm] * norm_outs,
        out_shape=[shape] * 4 + [jax.ShapeDtypeStruct((4, D), F32)] * norm_outs,
        scratch_shapes=[
            pltpu.VMEM((slots, edge, width), F32),
            pltpu.VMEM((slots, edge, width), F32),
        ],
        input_output_aliases={ins + i: i for i in range(len(earlier))},
        compiler_params=pltpu.CompilerParams(vmem_limit_bytes=SHAMPOO_VMEM),
        cost_estimate=pl.CostEstimate(
            flops=groups * (3 << 30), bytes_accessed=4 << 20, transcendentals=0
        ),
        name="shampoo",
    )(received, weights, stat_left, stat_right, *norms, *earlier)


def swap_heads(values):
    return lax.ppermute(values, "head", [(0, 1), (1, 0)])


def to_all(values, axis):
    return lax.all_to_all(values, axis, 0, 0)


def across(values, apart):
    pairs = [(i, i ^ apart) for i in range(INNER)]
    return lax.ppermute(values, "inner", pairs)


def from_all(values):
    return [values] + [across(values, apart) for apart in range(1, INNER)]


def gather_slabs(weights, small):
    early = to_all(pack(weights, 0, 1), "outer")[:, 0]
    early, late = lax.optimization_barrier((early, pack(weights, 1, 2)))
    late = to_all(late, "outer")
    early = from_all(early)
    early[1], late, small = lax.optimization_barrier((early[1], late, small))
    return early, from_all(late), small


def gather_blocks(local):
    groups, _, edge, _ = local.shape
    blocks = lax.all_gather(local, ("outer", "inner"), axis=1, tiled=True)
    blocks = blocks.reshape(groups, SLABS // INNER, INNER, D // edge, edge, edge)
    slabs = blocks.transpose(2, 1, 0, 4, 3, 5).reshape(SLABS, groups, edge, D)
    return slabs if groups > 1 else slabs[:, 0]


def scatter_blocks(slabs, count, edge):
    groups = slabs.shape[1]
    blocks = slabs.reshape(INNER, SLABS // INNER, groups, edge, D // edge, edge)
    blocks = blocks.transpose(2, 1, 0, 4, 3, 5).reshape(groups, SLABS * (D // edge), edge, edge)
    owned = lax.psum_scatter(blocks, ("outer", "inner"), scatter_dimension=1, tiled=True)
    return owned.transpose(0, 2, 1, 3).reshape(groups, edge, count * edge)


def per_device(
    tokens,
    cotangent,
    token_counts,
    head_mask,
    norm_params,
    norm_state,
    weights,
    stat_left,
    stat_right,
):
    weights, stat_left, stat_right = weights[0], stat_left[0], stat_right[0]
    _, count, edge, _ = weights.shape
    whole_slabs = count * edge == D
    other_mask = swap_heads(head_mask)
    inner = lax.axis_index("inner") if whole_slabs else 0
    place = jnp.concatenate([jnp.stack([lax.axis_index("head"), inner]), token_counts])
    if whole_slabs:
        early, late, (other_mask, place) = gather_slabs(weights, (other_mask, place))
    else:
        local = weights.astype(BF)
        early = jnp.split(gather_blocks(local[:1]), INNER)
        late = jnp.split(gather_blocks(local[1:]), INNER)
    early, late = list(early), list(late)
    masks = (head_mask, other_mask)
    early += [swap_heads(piece) for piece in early]
    prob, qkv, out, middle, second_rows, wqkv, wo = attn_forward(
        place, *masks, tokens, norm_params, early
    )
    late[1:], middle = lax.optimization_barrier((late[1:], middle))
    late += [swap_heads(piece) for piece in late]
    block_out, middle_grad, norm_two, *late_sums = mlp(
        place, middle, second_rows, cotangent, norm_params, late
    )
    own_late, late_received = late_sums[:2], [swap_heads(sent) for sent in late_sums[2:]]
    if whole_slabs:
        far = add_late(own_late[1], late_received[1])
        near = add_late(own_late[0], late_received[0])
        far = [across(far[number], 2 + number) for number in range(2)]
        near, middle_grad = lax.optimization_barrier((list(near), middle_grad))
        late_grads = [near[0], across(near[1], 1), *far]
    dqkv, own_early, sent_early, norm_sums = attn_backward(
        place, *masks, tokens, middle_grad, prob, qkv, out, norm_params, norm_two, wqkv, wo
    )
    if whole_slabs:
        late_grads, sent_early = lax.optimization_barrier((late_grads, sent_early))
    early_received = swap_heads(sent_early)
    devices = lax.axis_size("outer") * lax.axis_size("inner") * lax.axis_size("head")
    scale = 1.0 / math.sqrt(tokens.shape[0] * devices)
    state = (weights, stat_left, stat_right, scale)
    if whole_slabs:
        late_grads = to_all(sum_late(late_grads), "outer")
        early_grads = list(combine(place, own_early, early_received, norm_sums))
        early_grads, dqkv = lax.optimization_barrier((early_grads, dqkv))
        early_grads[1:] = [across(early_grads[apart], apart) for apart in range(1, INNER)]
        input_grad = input_gradient(tokens, middle_grad, dqkv, norm_params, wqkv)
        early_grads, input_grad = lax.optimization_barrier((early_grads, input_grad))
        joined, late_grads = lax.optimization_barrier((join(early_grads), late_grads))
        joined = to_all(joined, "outer")[:, None]
        results = shampoo(late_grads, *state, 1)
        results = shampoo(joined, *state, 0, results, (norm_params, norm_state))
    else:
        input_grad = input_gradient(tokens, middle_grad, dqkv, norm_params, wqkv)
        early_slabs = own_early.astype(F32) + early_received[:SLABS].astype(F32)
        late_slabs = jnp.concatenate(own_late).astype(F32) + jnp.concatenate(late_received)
        late_slabs = late_slabs.reshape(SLABS, 2, edge, D)
        slabs = jnp.concatenate([early_slabs[:, None], late_slabs], axis=1).astype(BF)
        owned = scatter_blocks(slabs, count, edge)
        results = list(shampoo(owned[None], *state, 0))
        norm_grads = lax.psum(norm_sums, ("outer", "inner", "head")) * scale
        state_new = 0.5 * norm_state + 0.5 * norm_grads * norm_grads
        results += [norm_grads, state_new, norm_params - 0.2 * norm_grads / jnp.sqrt(state_new)]
    return (block_out, input_grad, *[result[None] for result in results[:4]], *results[4:])


def solution(mesh):
    shape = (mesh.shape["dp"] // INNER, INNER, mesh.shape["head"])
    split_mesh = Mesh(mesh.devices.reshape(shape), ("outer", "inner", "head"))
    group = ("outer", "inner")
    blocks = P("head", None, group, None, None)
    rows = P(group + ("head",), None)
    return jax.shard_map(
        per_device,
        mesh=split_mesh,
        in_specs=(rows, rows, P(group), P(group, "head"), P(), P(), blocks, blocks, blocks),
        out_specs=(rows, rows, blocks, blocks, blocks, blocks, P(), P(), P()),
        check_vma=False,
    )
```

```python
import math

import jax
import jax.numpy as jnp
from jax import lax
from jax.experimental import pallas as pl
from jax.experimental.pallas import tpu as pltpu
from jax.sharding import Mesh, PartitionSpec as P

D = 384
HEAD_DIM = 64
MLP = 1536
S = 256
ITERS = 8
PAIR = 2 * HEAD_DIM
PAIRS = D // PAIR
HALF = D // 2
SLABS = 16
INNER = 4
OUTER = SLABS // INNER
TILE = 512
INPUT_TILE = 768
IMAGES = TILE // S
NORM_ROWS = 8
PACK = 2
ROOT_HALF = 0.7071067811865476
DENSITY_FACTOR = 0.3989422804014327
BF = jnp.bfloat16
F32 = jnp.float32
VMEM_LIMIT = 40 << 20
SMALL_VMEM = 8 << 20
SHAMPOO_VMEM = 24 << 20


def in_hbm(values):
    return pltpu.with_memory_space_constraint(values, pltpu.HBM)


def nn(left, right):
    return jnp.dot(left, right, preferred_element_type=F32)


def nt(left, right):
    return lax.dot_general(left, right, (((1,), (1,)), ((), ())), preferred_element_type=F32)


def tn(left, right):
    return lax.dot_general(left, right, (((0,), (0,)), ((), ())), preferred_element_type=F32)


def normalize(values):
    centered = values - jnp.mean(values, axis=-1, keepdims=True)
    variance = jnp.mean(centered * centered, axis=-1, keepdims=True)
    inverse_std = lax.rsqrt(variance + 1e-06)
    return centered * inverse_std, inverse_std


def norm_backward(grad_out, normed, inverse_std, gain):
    grad_normed = grad_out * gain
    mean_first = jnp.mean(grad_normed, axis=-1, keepdims=True)
    mean_second = jnp.mean(grad_normed * normed, axis=-1, keepdims=True)
    grad_in = inverse_std * (grad_normed - mean_first - normed * mean_second)
    gain_grad = jnp.sum(grad_out * normed, axis=0, keepdims=True)
    shift_grad = jnp.sum(grad_out, axis=0, keepdims=True)
    return grad_in, jnp.concatenate([gain_grad, shift_grad], axis=0)


def grown(step, total, part):
    return jnp.where(step == 0, part, total + part)


def slab_at(owner):
    return (owner % INNER) * OUTER + owner // INNER


def lane_halves():
    lane = lax.broadcasted_iota(jnp.int32, (1, PAIR), 1)
    first = (lane < HEAD_DIM).astype(BF)
    return first, (1 - first).astype(BF)


def stacked(values, first, second):
    return jnp.concatenate([values * first, values * second], axis=0)


def mask_lanes(place_ref, own_ref, other_ref, image, pair):
    image = place_ref[0] * (own_ref.shape[0] // 2) + image
    heads = own_ref.shape[1]
    on = [
        own_ref[image, head] if head < heads else other_ref[image, head - heads]
        for head in (2 * pair, 2 * pair + 1)
    ]
    lane = lax.broadcasted_iota(jnp.int32, (1, PAIR), 1)
    return jnp.where(lane < HEAD_DIM, on[0], on[1]).astype(F32)


def attn_forward_kernel(
    place_ref, own_mask_ref, other_mask_ref, x_ref, norm_ref, *refs
):
    slab_refs, refs = refs[: 2 * INNER], refs[2 * INNER :]
    prob_ref, qkv_ref, out_ref, middle_ref, rows_ref, wqkv_ref, wo_ref, held_ref = refs
    step = pl.program_id(0)

    @pl.when(step == 0)
    def _():
        for number, ref in enumerate(slab_refs):
            side, apart = divmod(number, INNER)
            held_ref[side, place_ref[1] ^ apart] = ref[...]

        def slab_of(side, owner):
            return held_ref[side, owner % INNER, owner // INNER]

        for row in range(D // 48):
            for part in range(3):
                pieces = []
                for number in range(2):
                    slab, side = divmod(3 * row + part, 2)
                    piece = slab_of(number, slab)[:, side * HALF : (side + 1) * HALF]
                    pieces.append(piece)
                joined = jnp.concatenate(pieces, axis=1)
                if part == 0:
                    joined = joined * 0.125
                wqkv_ref[48 * row : 48 * row + 48, D * part : D * part + D] = joined
        for side in range(2):
            for row in range(HALF // 48):
                start = side * HALF + 48 * row
                wo_ref[start : start + 48, :] = slab_of(side, 12 + row)

    x = x_ref[...].astype(F32)
    normed, _ = normalize(x)
    rows = (normed * norm_ref[0:1, :] + norm_ref[1:2, :]).astype(BF)
    qkv_ref[...] = nn(rows, wqkv_ref[...]).astype(BF)
    first, second = lane_halves()
    column = lax.broadcasted_iota(jnp.int32, (1, S), 1)
    tasks = [(image, pair) for image in range(IMAGES) for pair in range(PAIRS)]

    def places(task):
        image, pair = task
        here = slice(S * image, S * image + S)
        return here, *(slice(D * t + PAIR * pair, D * t + PAIR * (pair + 1)) for t in range(3))

    def get_scores(task):
        here, query_lanes, key_lanes, _ = places(task)
        return nt(stacked(qkv_ref[here, query_lanes], first, second), qkv_ref[here, key_lanes])

    def get_prob(task, scores):
        image = place_ref[0] * (own_mask_ref.shape[0] // 2) + IMAGES * step + task[0]
        scores = jnp.where(column < place_ref[2 + image], scores, -1e30)
        top = jnp.max(scores, axis=-1, keepdims=True)
        exp_scores = jnp.exp(scores - top)
        total = jnp.sum(exp_scores, axis=-1, keepdims=True)
        prob = (exp_scores * (1.0 / total)).astype(BF)
        prob_ref[task] = prob
        return prob

    all_scores = [get_scores(task) for task in tasks]
    probs = [get_prob(task, scores) for task, scores in zip(tasks, all_scores)]
    for task, prob in zip(tasks, probs):
        here, lanes, _, value_lanes = places(task)
        values = qkv_ref[here, value_lanes]
        head_out = nn(prob[:S], values * first) + nn(prob[S:], values * second)
        mask = mask_lanes(place_ref, own_mask_ref, other_mask_ref, IMAGES * step + task[0], task[1])
        out_ref[here, lanes] = (head_out * mask).astype(BF)
    middle = x + nn(out_ref[...], wo_ref[...])
    middle_ref[...] = middle
    normed, _ = normalize(middle)
    rows_ref[...] = (normed * norm_ref[2:3, :] + norm_ref[3:4, :]).astype(BF)


def attn_forward(place, own_mask, other_mask, tokens, norm_params, slabs):
    rows = tokens.shape[0]
    images = rows // S
    tile = pl.BlockSpec((TILE, D), lambda i: (i, 0))
    slab = pl.BlockSpec((OUTER, 48, D), lambda i: (0, 0, 0))
    smem = pl.BlockSpec(memory_space=pltpu.SMEM)
    return pl.pallas_call(
        attn_forward_kernel,
        grid=(rows // TILE,),
        in_specs=[smem] * 3 + [tile, pl.BlockSpec((4, D), lambda i: (0, 0))] + [slab] * 2 * INNER,
        out_specs=[
            pl.BlockSpec((IMAGES, PAIRS, 2 * S, S), lambda i: (i, 0, 0, 0)),
            pl.BlockSpec((TILE, 3 * D), lambda i: (i, 0)),
            tile,
            tile,
            tile,
            pl.BlockSpec((D, 3 * D), lambda i: (0, 0)),
            pl.BlockSpec((D, D), lambda i: (0, 0)),
        ],
        out_shape=[
            pltpu.HBM((images, PAIRS, 2 * S, S), BF),
            pltpu.HBM((rows, 3 * D), BF),
            pltpu.HBM((rows, D), BF),
            jax.ShapeDtypeStruct((rows, D), F32),
            jax.ShapeDtypeStruct((rows, D), BF),
            pltpu.HBM((D, 3 * D), BF),
            pltpu.HBM((D, D), BF),
        ],
        scratch_shapes=[pltpu.VMEM((2, INNER, OUTER, 48, D), BF)],
        compiler_params=pltpu.CompilerParams(vmem_limit_bytes=VMEM_LIMIT),
        cost_estimate=pl.CostEstimate(
            flops=rows * D * (8 * D + 16 * S), bytes_accessed=16 << 20, transcendentals=rows * 6 * S
        ),
        name="attn_forward",
    )(place, own_mask, other_mask, tokens, in_hbm(norm_params), *slabs)


def mlp_kernel(place_ref, middle_ref, rows_ref, cot_ref, norm_ref, *refs):
    slab_refs, refs = refs[: 2 * INNER], refs[2 * INNER :]
    out_ref, grad_ref, norm_grad_ref, *refs = refs
    own_refs, sent_refs, refs = refs[:2], refs[2:4], refs[4:]
    up_ref, down_ref, up_grad_ref, down_grad_ref = refs
    step = pl.program_id(0)
    half = MLP // 2

    def places(apart, outer):
        inner = place_ref[1] ^ apart
        row = pl.multiple_of(48 * (2 * outer + inner // 2), 16)
        lane = pl.multiple_of(D * (inner % 2), 128)
        down_row = pl.multiple_of(48 * (INNER * outer + inner), 16)
        return row, lane, down_row

    @pl.when(step == 0)
    def _():
        for number, ref in enumerate(slab_refs):
            side, apart = divmod(number, INNER)
            for outer in range(OUTER):
                row, lane, down_row = places(apart, outer)
                up_ref[side, pl.ds(row, 48), pl.ds(lane, D)] = ref[outer, 0]
                down_ref[side, pl.ds(down_row, 48), :] = ref[outer, 1]

    middle = middle_ref[...]
    normed, inverse_std = normalize(middle)
    rows, cot = rows_ref[...], cot_ref[...]
    total = middle
    back = None
    for side in range(2):
        up, down = up_ref[side], down_ref[side]
        pre = nn(rows, up)
        act_grad = nt(cot, down)
        cumulative = 0.5 * (1.0 + lax.erf(pre * ROOT_HALF))
        density = jnp.exp(-0.5 * pre * pre) * DENSITY_FACTOR
        act = (pre * cumulative).astype(BF)
        pre_grad = (act_grad * (cumulative + pre * density)).astype(BF)
        total = total + nn(act, down)
        term = nt(pre_grad, up)
        back = term if back is None else back + term
        down_grad_ref[side] = grown(step, down_grad_ref[side], tn(act, cot))
        up_grad_ref[side] = grown(step, up_grad_ref[side], tn(rows, pre_grad))
    out_ref[...] = total
    grad_in, norm_part = norm_backward(back, normed, inverse_std, norm_ref[2:3, :])
    norm_grad_ref[...] = grown(step, norm_grad_ref[...], norm_part)
    grad_ref[...] = cot.astype(F32) + grad_in

    @pl.when(step == pl.num_programs(0) - 1)
    def _():
        for apart in range(INNER):
            for outer in range(OUTER):
                row, lane, down_row = places(apart, outer)
                for side, halves in enumerate((own_refs, sent_refs)):
                    ref = halves[apart // 2]
                    up = up_grad_ref[side, pl.ds(row, 48), pl.ds(lane, D)]
                    down = down_grad_ref[side, pl.ds(down_row, 48), :]
                    ref[apart % 2, outer, 0] = up.astype(BF)
                    ref[apart % 2, outer, 1] = down.astype(BF)


def mlp(place, middle, second_rows, cotangent, norm_params, slabs):
    rows = middle.shape[0]
    slab = pl.BlockSpec((OUTER, 2, 48, D), lambda i: (0, 0, 0, 0))
    grads = (INNER // 2, OUTER, 2, 48, D)
    grad = pl.BlockSpec(grads, lambda i: (0, 0, 0, 0, 0))
    tile = pl.BlockSpec((TILE, D), lambda i: (i, 0))
    return pl.pallas_call(
        mlp_kernel,
        grid=(rows // TILE,),
        in_specs=[
            pl.BlockSpec(memory_space=pltpu.SMEM),
            tile,
            tile,
            tile,
            pl.BlockSpec((4, D), lambda i: (0, 0)),
            *[slab] * 2 * INNER,
        ],
        out_specs=[tile, tile, pl.BlockSpec((2, D), lambda i: (0, 0)), *[grad] * 4],
        out_shape=[
            jax.ShapeDtypeStruct((rows, D), F32),
            pltpu.HBM((rows, D), F32),
            jax.ShapeDtypeStruct((2, D), F32),
            *[jax.ShapeDtypeStruct(grads, BF)] * 4,
        ],
        scratch_shapes=[
            pltpu.VMEM((2, D, MLP // 2), BF),
            pltpu.VMEM((2, MLP // 2, D), BF),
            pltpu.VMEM((2, D, MLP // 2), F32),
            pltpu.VMEM((2, MLP // 2, D), F32),
        ],
        compiler_params=pltpu.CompilerParams(vmem_limit_bytes=VMEM_LIMIT),
        cost_estimate=pl.CostEstimate(
            flops=12 * rows * D * MLP, bytes_accessed=20 << 20, transcendentals=2 * rows * MLP
        ),
        name="mlp",
    )(place, middle, second_rows, cotangent, in_hbm(norm_params), *slabs)


def attn_backward_kernel(
    place_ref, own_mask_ref, other_mask_ref, x_ref, grad_ref, prob_ref, qkv_ref, out_ref,
    norm_ref, later_norm_ref, wqkv_ref, wo_ref,
    dqkv_ref, own_grad_ref, sent_grad_ref, norm_grad_ref,
    cross_ref, column_ref, wo_grad_ref,
):
    step = pl.program_id(0)

    normed, _ = normalize(x_ref[...].astype(F32))
    low_grad = grad_ref[...].astype(BF)
    head_out = out_ref[...]
    wo_grad_ref[...] = grown(step, wo_grad_ref[...], tn(head_out, low_grad))
    whole_grad = nt(low_grad, wo_ref[...]).astype(BF)
    first, second = lane_halves()
    first_wide, second_wide = first.astype(F32), second.astype(F32)
    tasks = [(image, pair) for image in range(IMAGES) for pair in range(PAIRS)]

    def places(task):
        image, pair = task
        here = slice(S * image, S * image + S)
        return here, *(slice(D * t + PAIR * pair, D * t + PAIR * (pair + 1)) for t in range(3))

    def get_pair_grad(task):
        here, lanes, _, _ = places(task)
        mask = mask_lanes(place_ref, own_mask_ref, other_mask_ref, IMAGES * step + task[0], task[1])
        grad = whole_grad[here, lanes] * mask.astype(BF)
        dots = grad.astype(F32) * head_out[here, lanes].astype(F32)
        first_dot = jnp.sum(dots * first_wide, axis=-1, keepdims=True)
        second_dot = jnp.sum(dots * second_wide, axis=-1, keepdims=True)
        return stacked(grad, first, second), jnp.concatenate([first_dot, second_dot], axis=0)

    pair_grads = [get_pair_grad(task) for task in tasks]
    prob_grads = [
        nt(pair_grad[0], qkv_ref[places(task)[0], places(task)[3]])
        for task, pair_grad in zip(tasks, pair_grads)
    ]
    score_grads = [
        (prob_ref[task].astype(F32) * (prob_grad - pair_grad[1])).astype(BF)
        for task, prob_grad, pair_grad in zip(tasks, prob_grads, pair_grads)
    ]
    for task, score_grad, (pair_grad, _) in zip(tasks, score_grads, pair_grads):
        here, query_lanes, key_lanes, value_lanes = places(task)
        keys = qkv_ref[here, key_lanes]
        queries = stacked(qkv_ref[here, query_lanes], first, second)
        query_grad = nn(score_grad[:S], keys * first) + nn(score_grad[S:], keys * second)
        key_grad = nn(jnp.transpose(queries), score_grad)
        value_grad = nn(jnp.transpose(pair_grad), prob_ref[task])
        dqkv_ref[here, query_lanes] = query_grad.astype(BF)
        dqkv_ref[here, key_lanes] = jnp.transpose(key_grad).astype(BF)
        dqkv_ref[here, value_lanes] = jnp.transpose(value_grad).astype(BF)
    dqkv = dqkv_ref[...]
    cross_ref[...] = grown(step, cross_ref[...], tn(normed.astype(BF), dqkv))
    columns = jnp.sum(dqkv.astype(F32), axis=0, keepdims=True)
    column_ref[...] = grown(step, column_ref[...], columns)

    @pl.when(step == pl.num_programs(0) - 1)
    def _():
        wqkv = wqkv_ref[...]
        products = wqkv.astype(F32) * cross_ref[...]
        gain_grad = jnp.sum(products, axis=1, keepdims=True)
        gain_grad = jnp.transpose(jnp.broadcast_to(gain_grad, (D, 128)))
        columns = column_ref[...]
        shift_grad = nt(jnp.concatenate(split(jnp.broadcast_to(columns, (8, 3 * D)))), wqkv)
        norm_grad_ref[0:1, :] = gain_grad[0:1]
        norm_grad_ref[1:2, :] = shift_grad[0:1] + shift_grad[8:9]
        norm_grad_ref[2:4, :] = later_norm_ref[...]
        gain = jnp.transpose(jnp.broadcast_to(norm_ref[0:1, :], (128, D)))[:, :1]
        shift = jnp.transpose(jnp.broadcast_to(norm_ref[1:2, :], (128, D)))[:, :1]
        cross_ref[...] = cross_ref[...] * gain + shift * columns
        for side, slab_grads in enumerate((own_grad_ref, sent_grad_ref)):
            for slab in range(12):
                pieces = []
                for unit in (2 * slab, 2 * slab + 1):
                    row, part = divmod(unit, 3)
                    piece = cross_ref[48 * row : 48 * row + 48, D * part : D * part + D]
                    piece = piece[:, HALF * side : HALF * side + HALF]
                    pieces.append(piece * 0.125 if part == 0 else piece)
                slab_grads[slab_at(slab)] = jnp.concatenate(pieces, axis=1).astype(BF)
            for row in range(HALF // 48):
                start = HALF * side + 48 * row
                slab_grads[slab_at(12 + row)] = wo_grad_ref[start : start + 48, :].astype(BF)
        sent_grad_ref[SLABS, :NORM_ROWS] = jnp.concatenate(split(norm_grad_ref[...]), axis=0)
        sent_grad_ref[SLABS, NORM_ROWS:] = jnp.zeros((48 - NORM_ROWS, D), BF)


def attn_backward(
    place, own_mask, other_mask, tokens, grad, prob, qkv, out, norm_params, later_norms, wqkv, wo
):
    rows = tokens.shape[0]
    tile = pl.BlockSpec((TILE, D), lambda i: (i, 0))
    smem = pl.BlockSpec(memory_space=pltpu.SMEM)
    return pl.pallas_call(
        attn_backward_kernel,
        grid=(rows // TILE,),
        in_specs=[
            smem,
            smem,
            smem,
            tile,
            tile,
            pl.BlockSpec((IMAGES, PAIRS, 2 * S, S), lambda i: (i, 0, 0, 0)),
            pl.BlockSpec((TILE, 3 * D), lambda i: (i, 0)),
            tile,
            pl.BlockSpec((4, D), lambda i: (0, 0)),
            pl.BlockSpec((2, D), lambda i: (0, 0)),
            pl.BlockSpec((D, 3 * D), lambda i: (0, 0)),
            pl.BlockSpec((D, D), lambda i: (0, 0)),
        ],
        out_specs=[
            pl.BlockSpec((TILE, 3 * D), lambda i: (i, 0)),
            pl.BlockSpec((SLABS, 48, D), lambda i: (0, 0, 0)),
            pl.BlockSpec((SLABS + 1, 48, D), lambda i: (0, 0, 0)),
            pl.BlockSpec((4, D), lambda i: (0, 0)),
        ],
        out_shape=[
            pltpu.HBM((rows, 3 * D), BF),
            jax.ShapeDtypeStruct((SLABS, 48, D), BF),
            jax.ShapeDtypeStruct((SLABS + 1, 48, D), BF),
            jax.ShapeDtypeStruct((4, D), F32),
        ],
        scratch_shapes=[
            pltpu.VMEM((D, 3 * D), F32),
            pltpu.VMEM((1, 3 * D), F32),
            pltpu.VMEM((D, D), F32),
        ],
        compiler_params=pltpu.CompilerParams(vmem_limit_bytes=VMEM_LIMIT),
        cost_estimate=pl.CostEstimate(
            flops=rows * D * (10 * D + 32 * S), bytes_accessed=20 << 20, transcendentals=0
        ),
        name="attn_backward",
    )(
        place, own_mask, other_mask,
        tokens, in_hbm(grad), prob, qkv, out, in_hbm(norm_params), in_hbm(later_norms), wqkv, wo,
    )


def input_grad_kernel(x_ref, grad_ref, dqkv_ref, norm_ref, wqkv_ref, out_ref):
    normed, inverse_std = normalize(x_ref[...].astype(F32))
    back = nt(dqkv_ref[...], wqkv_ref[...]) * norm_ref[0:1, :]
    mean_first = jnp.mean(back, axis=-1, keepdims=True)
    mean_second = jnp.mean(back * normed, axis=-1, keepdims=True)
    out_ref[...] = grad_ref[...] + inverse_std * (back - mean_first - normed * mean_second)


def input_gradient(tokens, grad, dqkv, norm_params, wqkv):
    rows = tokens.shape[0]
    tile = pl.BlockSpec((INPUT_TILE, D), lambda i: (i, 0))
    return pl.pallas_call(
        input_grad_kernel,
        grid=(rows // INPUT_TILE,),
        in_specs=[
            tile,
            tile,
            pl.BlockSpec((INPUT_TILE, 3 * D), lambda i: (i, 0)),
            pl.BlockSpec((4, D), lambda i: (0, 0)),
            pl.BlockSpec((D, 3 * D), lambda i: (0, 0)),
        ],
        out_specs=tile,
        out_shape=jax.ShapeDtypeStruct((rows, D), F32),
        compiler_params=pltpu.CompilerParams(vmem_limit_bytes=VMEM_LIMIT),
        cost_estimate=pl.CostEstimate(
            flops=rows * D * 6 * D, bytes_accessed=10 << 20, transcendentals=0
        ),
        name="input_gradient",
    )(in_hbm(tokens), in_hbm(grad), in_hbm(dqkv), in_hbm(norm_params), in_hbm(wqkv))


def pack_kernel(weight_ref, out_ref):
    groups, count, _, _ = weight_ref.shape
    for group in range(groups):
        blocks = [weight_ref[group, block] for block in range(count)]
        slab = jnp.concatenate(blocks, axis=1).astype(BF)
        for copy in range(OUTER):
            out_ref[copy, group] = slab


def pack_early_kernel(weight_ref, out_ref):
    blocks = [weight_ref[0, block] for block in range(weight_ref.shape[1])]
    slab = jnp.concatenate(blocks, axis=1).astype(BF)
    for copy in range(OUTER):
        out_ref[copy] = slab


def pack_early(weights):
    _, count, edge, _ = weights.shape
    return pl.pallas_call(
        pack_early_kernel,
        out_shape=jax.ShapeDtypeStruct((OUTER, edge, count * edge), BF),
        compiler_params=pltpu.CompilerParams(vmem_limit_bytes=SMALL_VMEM),
        name="pack_early",
    )(in_hbm(weights))


def pack(weights, first, groups):
    _, count, edge, _ = weights.shape
    shape = (OUTER, groups, edge, count * edge)
    return pl.pallas_call(
        pack_kernel,
        grid=(1,),
        in_specs=[
            pl.BlockSpec(
                (pl.Element(groups), pl.Element(count), pl.Element(edge), pl.Element(edge)),
                lambda i: (first, 0, 0, 0),
            )
        ],
        out_specs=pl.BlockSpec(shape, lambda i: (0, 0, 0, 0)),
        out_shape=jax.ShapeDtypeStruct(shape, BF),
        compiler_params=pltpu.CompilerParams(vmem_limit_bytes=SMALL_VMEM),
        name="pack",
    )(in_hbm(weights))


def add_kernel(own_ref, received_ref, *out_refs):
    for apart, out_ref in enumerate(out_refs):
        total = own_ref[apart].astype(F32) + received_ref[apart].astype(F32)
        out_ref[...] = total.astype(BF)


def add_late(own, received):
    return pl.pallas_call(
        add_kernel,
        out_shape=[jax.ShapeDtypeStruct(own.shape[1:], BF)] * own.shape[0],
        compiler_params=pltpu.CompilerParams(vmem_limit_bytes=SMALL_VMEM),
        name="add_late",
    )(own, received)


def sum_kernel(*refs):
    *in_refs, out_ref = refs
    total = in_refs[0][...].astype(F32)
    for ref in in_refs[1:]:
        total = total + ref[...].astype(F32)
    out_ref[...] = total.astype(BF)


def sum_late(pieces):
    return pl.pallas_call(
        sum_kernel,
        out_shape=jax.ShapeDtypeStruct(pieces[0].shape, BF),
        compiler_params=pltpu.CompilerParams(vmem_limit_bytes=SMALL_VMEM),
        name="sum_late",
    )(*pieces)


def combine_kernel(place_ref, own_ref, received_ref, norm_ref, *out_refs):
    norms = received_ref[SLABS, :NORM_ROWS].astype(F32)
    norms = norm_ref[...] + (norms[:4] + norms[4:])
    rows = jnp.concatenate(split(norms), axis=0)
    for apart, out_ref in enumerate(out_refs):
        start = OUTER * (place_ref[1] ^ apart)
        for outer in range(OUTER):
            total = own_ref[start + outer].astype(F32) + received_ref[start + outer].astype(F32)
            out_ref[48 * outer : 48 * outer + 48, :] = total.astype(BF)
        out_ref[48 * OUTER :, :] = rows


def combine(place, own, received, norms):
    vmem = pl.BlockSpec(memory_space=pltpu.VMEM)
    shape = jax.ShapeDtypeStruct((48 * OUTER + NORM_ROWS, D), BF)
    return pl.pallas_call(
        combine_kernel,
        in_specs=[pl.BlockSpec(memory_space=pltpu.SMEM), vmem, vmem, vmem],
        out_shape=[shape] * INNER,
        compiler_params=pltpu.CompilerParams(vmem_limit_bytes=SMALL_VMEM),
        name="combine",
    )(place, own, received, norms)


def join_kernel(*refs):
    *early_refs, out_ref = refs
    total = early_refs[0][...].astype(F32)
    for ref in early_refs[1:]:
        total = total + ref[...].astype(F32)
    norms = total[48 * OUTER : 48 * OUTER + 4] + total[48 * OUTER + 4 :]
    for outer in range(OUTER):
        out_ref[outer, :48] = total[48 * outer : 48 * outer + 48].astype(BF)
        out_ref[outer, 48:] = jnp.concatenate(split(norms), axis=0)


def join(early):
    return pl.pallas_call(
        join_kernel,
        out_shape=jax.ShapeDtypeStruct((OUTER, 48 + NORM_ROWS, D), BF),
        compiler_params=pltpu.CompilerParams(vmem_limit_bytes=SMALL_VMEM),
        name="join",
    )(*early)


def split(values):
    high = values.astype(BF)
    return high, (values - high.astype(F32)).astype(BF)


def stack(*pieces):
    return jnp.concatenate(pieces, axis=0)


def cut_rows(values, number):
    edge = values.shape[0] // number
    return [values[edge * i : edge * i + edge] for i in range(number)]


def product(left, right):
    high, low = left
    right_high, right_low = right
    one, two = cut_rows(nn(stack(high, low), right_high), 2)
    return one + (two + nn(high, right_low))


def two_products(left, middle, right):
    right_high, right_low = right
    both = cut_rows(nn(stack(left[0], middle[0], left[1], middle[1]), right_high), 4)
    high = cut_rows(nn(stack(left[0], middle[0]), right_low), 2)
    return both[0] + (both[2] + high[0]), both[1] + (both[3] + high[1])


def update_norms(scale, total, param_ref, state_ref, grad_ref, new_state_ref, new_ref):
    grads = total * scale
    state = 0.5 * state_ref[...] + 0.5 * grads * grads
    grad_ref[...] = grads
    new_state_ref[...] = state
    new_ref[...] = param_ref[...] - 0.2 * grads / jnp.sqrt(state)


def shampoo_kernel(scale, with_norms, received_ref, weight_ref, left_ref, right_ref, *refs):
    if with_norms:
        norm_ins, norm_outs, refs = refs[:2], refs[-5:-2], refs[:-5] + refs[-2:]
    out_grad_ref, left_new_ref, right_new_ref, new_weight_ref, root_ref, power_ref = refs[-6:]
    groups, count, edge = weight_ref.shape[:3]

    received = received_ref[0].astype(F32)
    for number in range(1, received_ref.shape[0]):
        received = received + received_ref[number].astype(F32)
    if with_norms:
        norms = received[0, edge:]
        update_norms(scale, norms[:4] + norms[4:], *norm_ins, *norm_outs)
    pack = min(PACK, count)
    width = pack * edge
    places = [(g, pack * n) for g in range(groups) for n in range(count // pack)]
    packs = len(places)

    def block_of(shape, dim):
        return lax.broadcasted_iota(jnp.int32, shape, dim) // edge

    row = lax.broadcasted_iota(jnp.int32, (edge, width), 0)
    lane = lax.broadcasted_iota(jnp.int32, (edge, width), 1)
    identity = (lane % edge == row).astype(F32)
    same = (block_of((width, width), 0) == block_of((width, width), 1)).astype(BF)
    lane_block = block_of((1, width), 1)

    def spread(pieces):
        return tuple(stack(*[piece] * pack) * same for piece in pieces)

    def cut(packed, index):
        return packed[:, edge * index : edge * index + edge]

    def beside(ref, place):
        return jnp.concatenate([ref[place[0], place[1] + i] for i in range(pack)], axis=1)

    grads, parts = [], []
    for group, start in places:
        grad = received[group, :edge, edge * start : edge * start + width] * scale
        blocks = [cut(grad, index) for index in range(pack)]
        for index in range(pack):
            out_grad_ref[group, start + index] = blocks[index]
        grad_t = jnp.concatenate([jnp.transpose(block) for block in blocks], axis=1)
        one, two = split(grad), split(grad_t)
        one_diagonal, two_diagonal = spread(one), spread(two)
        grads.append(one_diagonal)
        parts.append((left_ref, left_new_ref, one, two_diagonal))
        parts.append((right_ref, right_new_ref, two, one_diagonal))
    grams = [product(left, right) for _, _, left, right in parts]
    for slot, (old_ref, new_ref, _, _) in enumerate(parts):
        group, start = places[slot // 2]
        new = 0.5 * beside(old_ref, places[slot // 2]) + 0.5 * grams[slot]
        for index in range(pack):
            new_ref[group, start + index] = cut(new, index)
        columns = jnp.sum(new * new, axis=0, keepdims=True)
        squares = jnp.zeros((1, width), F32)
        for index in range(pack):
            inside = lane_block == index
            part = jnp.sum(jnp.where(inside, columns, 0.0), axis=1, keepdims=True)
            squares = jnp.where(inside, part, squares)
        factor = 2.5 / jnp.sqrt(squares)
        root_ref[slot] = jnp.broadcast_to(jnp.sqrt(jnp.sqrt(factor)), (edge, width))
        power_ref[slot] = factor * new
    slots = range(2 * packs)

    def advance(first):
        powers = [power_ref[slot] for slot in slots]
        middles = [split((5.0 * identity - power) * 0.25) for power in powers]
        rights = [spread(middle) for middle in middles]
        powers = [split(power) for power in powers]
        if first:
            squares = [product(middles[s], rights[s]) for s in slots]
            for slot in slots:
                root_ref[slot] *= (5.0 * identity - power_ref[slot]) * 0.25
        else:
            roots = [split(root_ref[slot]) for slot in slots]
            both = [two_products(roots[s], middles[s], rights[s]) for s in slots]
            squares = [pair[1] for pair in both]
            for slot in slots:
                root_ref[slot] = both[slot][0]
        rights = [spread(split(square)) for square in squares]
        powers = [split(product(powers[s], rights[s])) for s in slots]
        for slot in slots:
            power_ref[slot] = product(powers[slot], rights[slot])

    advance(True)
    for _ in range(ITERS - 2):
        advance(False)
    rights = [spread(split((5.0 * identity - power_ref[slot]) * 0.25)) for slot in slots]
    for slot in slots:
        root_ref[slot] = product(split(root_ref[slot]), rights[slot])
    steps = [product(split(root_ref[2 * n]), grads[n]) for n in range(packs)]
    rights = [spread(split(root_ref[2 * n + 1])) for n in range(packs)]
    steps = [product(split(steps[n]), rights[n]) for n in range(packs)]
    for number, (group, start) in enumerate(places):
        for index in range(pack):
            step = 0.25 * cut(steps[number], index)
            new_weight_ref[group, start + index] = weight_ref[group, start + index] - step


def shampoo(received, weights, stat_left, stat_right, scale, first, earlier=(), norms=()):
    groups = received.shape[1]
    _, count, edge, _ = weights.shape
    slots = 2 * groups * count // min(PACK, count)
    width = min(PACK, count) * edge
    block = pl.BlockSpec(
        (pl.Element(groups), pl.Element(count), pl.Element(edge), pl.Element(edge)),
        lambda i: (first, 0, 0, 0),
    )
    shape = jax.ShapeDtypeStruct(weights.shape, F32)
    norm = pl.BlockSpec((4, D), lambda i: (0, 0))
    norm_outs = 3 if norms else 0
    ins = 4 + len(norms)
    return pl.pallas_call(
        lambda *refs: shampoo_kernel(scale, bool(norms), *refs),
        grid=(1,),
        in_specs=[
            pl.BlockSpec(received.shape, lambda i: (0, 0, 0, 0)),
            *[block] * 3,
            *[norm] * len(norms),
            *[pl.BlockSpec(memory_space=pl.ANY)] * len(earlier),
        ],
        out_specs=[block] * 4 + [norm] * norm_outs,
        out_shape=[shape] * 4 + [jax.ShapeDtypeStruct((4, D), F32)] * norm_outs,
        scratch_shapes=[
            pltpu.VMEM((slots, edge, width), F32),
            pltpu.VMEM((slots, edge, width), F32),
        ],
        input_output_aliases={ins + i: i for i in range(len(earlier))},
        compiler_params=pltpu.CompilerParams(vmem_limit_bytes=SHAMPOO_VMEM),
        cost_estimate=pl.CostEstimate(
            flops=groups * (3 << 30), bytes_accessed=4 << 20, transcendentals=0
        ),
        name="shampoo",
    )(received, weights, stat_left, stat_right, *norms, *earlier)


def swap_heads(values):
    return lax.ppermute(values, "head", [(0, 1), (1, 0)])


def to_all(values, axis):
    return lax.all_to_all(values, axis, 0, 0)


def across(values, apart):
    pairs = [(i, i ^ apart) for i in range(INNER)]
    return lax.ppermute(values, "inner", pairs)


def from_all(values):
    return [values] + [across(values, apart) for apart in range(1, INNER)]


def gather_slabs(weights, small):
    early = to_all(pack_early(weights), "outer")
    early, late = lax.optimization_barrier((early, pack(weights, 1, 2)))
    late = to_all(late, "outer")
    early = from_all(early)
    early[1], late, small = lax.optimization_barrier((early[1], late, small))
    return early, from_all(late), small


def gather_blocks(local):
    groups, _, edge, _ = local.shape
    blocks = lax.all_gather(local, ("outer", "inner"), axis=1, tiled=True)
    blocks = blocks.reshape(groups, SLABS // INNER, INNER, D // edge, edge, edge)
    slabs = blocks.transpose(2, 1, 0, 4, 3, 5).reshape(SLABS, groups, edge, D)
    return slabs if groups > 1 else slabs[:, 0]


def scatter_blocks(slabs, count, edge):
    groups = slabs.shape[1]
    blocks = slabs.reshape(INNER, SLABS // INNER, groups, edge, D // edge, edge)
    blocks = blocks.transpose(2, 1, 0, 4, 3, 5).reshape(groups, SLABS * (D // edge), edge, edge)
    owned = lax.psum_scatter(blocks, ("outer", "inner"), scatter_dimension=1, tiled=True)
    return owned.transpose(0, 2, 1, 3).reshape(groups, edge, count * edge)


def per_device(
    tokens,
    cotangent,
    token_counts,
    head_mask,
    norm_params,
    norm_state,
    weights,
    stat_left,
    stat_right,
):
    weights, stat_left, stat_right = weights[0], stat_left[0], stat_right[0]
    _, count, edge, _ = weights.shape
    whole_slabs = count * edge == D
    other_mask = swap_heads(head_mask)
    inner = lax.axis_index("inner") if whole_slabs else 0
    place = jnp.concatenate([jnp.stack([lax.axis_index("head"), inner]), token_counts])
    if whole_slabs:
        early, late, (other_mask, place) = gather_slabs(weights, (other_mask, place))
    else:
        local = weights.astype(BF)
        early = jnp.split(gather_blocks(local[:1]), INNER)
        late = jnp.split(gather_blocks(local[1:]), INNER)
    early, late = list(early), list(late)
    masks = (head_mask, other_mask)
    early += [swap_heads(piece) for piece in early]
    prob, qkv, out, middle, second_rows, wqkv, wo = attn_forward(
        place, *masks, tokens, norm_params, early
    )
    late[1:], middle = lax.optimization_barrier((late[1:], middle))
    late += [swap_heads(piece) for piece in late]
    block_out, middle_grad, norm_two, *late_sums = mlp(
        place, middle, second_rows, cotangent, norm_params, late
    )
    own_late, late_received = late_sums[:2], [swap_heads(sent) for sent in late_sums[2:]]
    if whole_slabs:
        far = add_late(own_late[1], late_received[1])
        near = add_late(own_late[0], late_received[0])
        far = [across(far[number], 2 + number) for number in range(2)]
        near, middle_grad = lax.optimization_barrier((list(near), middle_grad))
        late_grads = [near[0], across(near[1], 1), *far]
    dqkv, own_early, sent_early, norm_sums = attn_backward(
        place, *masks, tokens, middle_grad, prob, qkv, out, norm_params, norm_two, wqkv, wo
    )
    if whole_slabs:
        late_grads, sent_early = lax.optimization_barrier((late_grads, sent_early))
    early_received = swap_heads(sent_early)
    devices = lax.axis_size("outer") * lax.axis_size("inner") * lax.axis_size("head")
    scale = 1.0 / math.sqrt(tokens.shape[0] * devices)
    state = (weights, stat_left, stat_right, scale)
    if whole_slabs:
        late_grads = to_all(sum_late(late_grads), "outer")
        early_grads = list(combine(place, own_early, early_received, norm_sums))
        early_grads, dqkv = lax.optimization_barrier((early_grads, dqkv))
        early_grads[1:] = [across(early_grads[apart], apart) for apart in range(1, INNER)]
        input_grad = input_gradient(tokens, middle_grad, dqkv, norm_params, wqkv)
        early_grads, input_grad = lax.optimization_barrier((early_grads, input_grad))
        joined, late_grads = lax.optimization_barrier((join(early_grads), late_grads))
        joined = to_all(joined, "outer")[:, None]
        results = shampoo(late_grads, *state, 1)
        results = shampoo(joined, *state, 0, results, (norm_params, norm_state))
    else:
        input_grad = input_gradient(tokens, middle_grad, dqkv, norm_params, wqkv)
        early_slabs = own_early.astype(F32) + early_received[:SLABS].astype(F32)
        late_slabs = jnp.concatenate(own_late).astype(F32) + jnp.concatenate(late_received)
        late_slabs = late_slabs.reshape(SLABS, 2, edge, D)
        slabs = jnp.concatenate([early_slabs[:, None], late_slabs], axis=1).astype(BF)
        owned = scatter_blocks(slabs, count, edge)
        results = list(shampoo(owned[None], *state, 0))
        norm_grads = lax.psum(norm_sums, ("outer", "inner", "head")) * scale
        state_new = 0.5 * norm_state + 0.5 * norm_grads * norm_grads
        results += [norm_grads, state_new, norm_params - 0.2 * norm_grads / jnp.sqrt(state_new)]
    return (block_out, input_grad, *[result[None] for result in results[:4]], *results[4:])


def solution(mesh):
    shape = (mesh.shape["dp"] // INNER, INNER, mesh.shape["head"])
    split_mesh = Mesh(mesh.devices.reshape(shape), ("outer", "inner", "head"))
    group = ("outer", "inner")
    blocks = P("head", None, group, None, None)
    rows = P(group + ("head",), None)
    return jax.shard_map(
        per_device,
        mesh=split_mesh,
        in_specs=(rows, rows, P(group), P(group, "head"), P(), P(), blocks, blocks, blocks),
        out_specs=(rows, rows, blocks, blocks, blocks, blocks, P(), P(), P()),
        check_vma=False,
    )
```

```python
import math

import jax
import jax.numpy as jnp
from jax import lax
from jax.experimental import pallas as pl
from jax.experimental.pallas import tpu as pltpu
from jax.sharding import Mesh, PartitionSpec as P

D = 384
HEAD_DIM = 64
MLP = 1536
S = 256
ITERS = 8
PAIR = 2 * HEAD_DIM
PAIRS = D // PAIR
HALF = D // 2
SLABS = 16
INNER = 4
OUTER = SLABS // INNER
TILE = 512
INPUT_TILE = 768
IMAGES = TILE // S
NORM_ROWS = 8
PACK = 2
ROOT_HALF = 0.7071067811865476
DENSITY_FACTOR = 0.3989422804014327
BF = jnp.bfloat16
F32 = jnp.float32
VMEM_LIMIT = 40 << 20
SMALL_VMEM = 8 << 20
SHAMPOO_VMEM = 24 << 20


def in_hbm(values):
    return pltpu.with_memory_space_constraint(values, pltpu.HBM)


def nn(left, right):
    return jnp.dot(left, right, preferred_element_type=F32)


def nt(left, right):
    return lax.dot_general(left, right, (((1,), (1,)), ((), ())), preferred_element_type=F32)


def tn(left, right):
    return lax.dot_general(left, right, (((0,), (0,)), ((), ())), preferred_element_type=F32)


def normalize(values):
    centered = values - jnp.mean(values, axis=-1, keepdims=True)
    variance = jnp.mean(centered * centered, axis=-1, keepdims=True)
    inverse_std = lax.rsqrt(variance + 1e-06)
    return centered * inverse_std, inverse_std


def norm_backward(grad_out, normed, inverse_std, gain):
    grad_normed = grad_out * gain
    mean_first = jnp.mean(grad_normed, axis=-1, keepdims=True)
    mean_second = jnp.mean(grad_normed * normed, axis=-1, keepdims=True)
    grad_in = inverse_std * (grad_normed - mean_first - normed * mean_second)
    gain_grad = jnp.sum(grad_out * normed, axis=0, keepdims=True)
    shift_grad = jnp.sum(grad_out, axis=0, keepdims=True)
    return grad_in, jnp.concatenate([gain_grad, shift_grad], axis=0)


def grown(step, total, part):
    return jnp.where(step == 0, part, total + part)


def slab_at(owner):
    return (owner % INNER) * OUTER + owner // INNER


def lane_halves():
    lane = lax.broadcasted_iota(jnp.int32, (1, PAIR), 1)
    first = (lane < HEAD_DIM).astype(BF)
    return first, (1 - first).astype(BF)


def stacked(values, first, second):
    return jnp.concatenate([values * first, values * second], axis=0)


def mask_lanes(place_ref, own_ref, other_ref, image, pair):
    image = place_ref[0] * (own_ref.shape[0] // 2) + image
    heads = own_ref.shape[1]
    on = [
        own_ref[image, head] if head < heads else other_ref[image, head - heads]
        for head in (2 * pair, 2 * pair + 1)
    ]
    lane = lax.broadcasted_iota(jnp.int32, (1, PAIR), 1)
    return jnp.where(lane < HEAD_DIM, on[0], on[1]).astype(F32)


def attn_forward_kernel(
    place_ref, own_mask_ref, other_mask_ref, x_ref, norm_ref, *refs
):
    slab_refs, refs = refs[: 2 * INNER], refs[2 * INNER :]
    prob_ref, qkv_ref, out_ref, middle_ref, rows_ref, wqkv_ref, wo_ref, held_ref = refs
    step = pl.program_id(0)

    @pl.when(step == 0)
    def _():
        for number, ref in enumerate(slab_refs):
            side, apart = divmod(number, INNER)
            held_ref[side, place_ref[1] ^ apart] = ref[...]

        def slab_of(side, owner):
            return held_ref[side, owner % INNER, owner // INNER]

        for row in range(D // 48):
            for part in range(3):
                pieces = []
                for number in range(2):
                    slab, side = divmod(3 * row + part, 2)
                    piece = slab_of(number, slab)[:, side * HALF : (side + 1) * HALF]
                    pieces.append(piece)
                joined = jnp.concatenate(pieces, axis=1)
                if part == 0:
                    joined = joined * 0.125
                wqkv_ref[48 * row : 48 * row + 48, D * part : D * part + D] = joined
        for side in range(2):
            for row in range(HALF // 48):
                start = side * HALF + 48 * row
                wo_ref[start : start + 48, :] = slab_of(side, 12 + row)

    x = x_ref[...].astype(F32)
    normed, _ = normalize(x)
    rows = (normed * norm_ref[0:1, :] + norm_ref[1:2, :]).astype(BF)
    qkv_ref[...] = nn(rows, wqkv_ref[...]).astype(BF)
    first, second = lane_halves()
    column = lax.broadcasted_iota(jnp.int32, (1, S), 1)
    tasks = [(image, pair) for image in range(IMAGES) for pair in range(PAIRS)]

    def places(task):
        image, pair = task
        here = slice(S * image, S * image + S)
        return here, *(slice(D * t + PAIR * pair, D * t + PAIR * (pair + 1)) for t in range(3))

    def get_scores(task):
        here, query_lanes, key_lanes, _ = places(task)
        return nt(stacked(qkv_ref[here, query_lanes], first, second), qkv_ref[here, key_lanes])

    def get_prob(task, scores):
        image = place_ref[0] * (own_mask_ref.shape[0] // 2) + IMAGES * step + task[0]
        scores = jnp.where(column < place_ref[2 + image], scores, -1e30)
        top = jnp.max(scores, axis=-1, keepdims=True)
        exp_scores = jnp.exp(scores - top)
        total = jnp.sum(exp_scores, axis=-1, keepdims=True)
        prob = (exp_scores * (1.0 / total)).astype(BF)
        prob_ref[task] = prob
        return prob

    all_scores = [get_scores(task) for task in tasks]
    probs = [get_prob(task, scores) for task, scores in zip(tasks, all_scores)]
    for task, prob in zip(tasks, probs):
        here, lanes, _, value_lanes = places(task)
        values = qkv_ref[here, value_lanes]
        head_out = nn(prob[:S], values * first) + nn(prob[S:], values * second)
        mask = mask_lanes(place_ref, own_mask_ref, other_mask_ref, IMAGES * step + task[0], task[1])
        out_ref[here, lanes] = (head_out * mask).astype(BF)
    middle = x + nn(out_ref[...], wo_ref[...])
    middle_ref[...] = middle
    normed, _ = normalize(middle)
    rows_ref[...] = (normed * norm_ref[2:3, :] + norm_ref[3:4, :]).astype(BF)


def attn_forward(place, own_mask, other_mask, tokens, norm_params, slabs):
    rows = tokens.shape[0]
    images = rows // S
    tile = pl.BlockSpec((TILE, D), lambda i: (i, 0))
    slab = pl.BlockSpec((OUTER, 48, D), lambda i: (0, 0, 0))
    smem = pl.BlockSpec(memory_space=pltpu.SMEM)
    return pl.pallas_call(
        attn_forward_kernel,
        grid=(rows // TILE,),
        in_specs=[smem] * 3 + [tile, pl.BlockSpec((4, D), lambda i: (0, 0))] + [slab] * 2 * INNER,
        out_specs=[
            pl.BlockSpec((IMAGES, PAIRS, 2 * S, S), lambda i: (i, 0, 0, 0)),
            pl.BlockSpec((TILE, 3 * D), lambda i: (i, 0)),
            tile,
            tile,
            tile,
            pl.BlockSpec((D, 3 * D), lambda i: (0, 0)),
            pl.BlockSpec((D, D), lambda i: (0, 0)),
        ],
        out_shape=[
            pltpu.HBM((images, PAIRS, 2 * S, S), BF),
            pltpu.HBM((rows, 3 * D), BF),
            pltpu.HBM((rows, D), BF),
            jax.ShapeDtypeStruct((rows, D), F32),
            jax.ShapeDtypeStruct((rows, D), BF),
            pltpu.HBM((D, 3 * D), BF),
            pltpu.HBM((D, D), BF),
        ],
        scratch_shapes=[pltpu.VMEM((2, INNER, OUTER, 48, D), BF)],
        compiler_params=pltpu.CompilerParams(vmem_limit_bytes=VMEM_LIMIT),
        cost_estimate=pl.CostEstimate(
            flops=rows * D * (8 * D + 16 * S), bytes_accessed=16 << 20, transcendentals=rows * 6 * S
        ),
        name="attn_forward",
    )(place, own_mask, other_mask, tokens, in_hbm(norm_params), *slabs)


def mlp_kernel(place_ref, middle_ref, rows_ref, cot_ref, norm_ref, *refs):
    slab_refs, refs = refs[: 2 * INNER], refs[2 * INNER :]
    out_ref, grad_ref, norm_grad_ref, *refs = refs
    own_refs, sent_refs, refs = refs[:2], refs[2:4], refs[4:]
    up_ref, down_ref, up_grad_ref, down_grad_ref = refs
    step = pl.program_id(0)
    half = MLP // 2

    def places(apart, outer):
        inner = place_ref[1] ^ apart
        row = pl.multiple_of(48 * (2 * outer + inner // 2), 16)
        lane = pl.multiple_of(D * (inner % 2), 128)
        down_row = pl.multiple_of(48 * (INNER * outer + inner), 16)
        return row, lane, down_row

    @pl.when(step == 0)
    def _():
        for number, ref in enumerate(slab_refs):
            side, apart = divmod(number, INNER)
            for outer in range(OUTER):
                row, lane, down_row = places(apart, outer)
                up_ref[side, pl.ds(row, 48), pl.ds(lane, D)] = ref[outer, 0]
                down_ref[side, pl.ds(down_row, 48), :] = ref[outer, 1]

    middle = middle_ref[...]
    normed, inverse_std = normalize(middle)
    rows, cot = rows_ref[...], cot_ref[...]
    total = middle
    back = None
    for side in range(2):
        up, down = up_ref[side], down_ref[side]
        pre = nn(rows, up)
        act_grad = nt(cot, down)
        cumulative = 0.5 * (1.0 + lax.erf(pre * ROOT_HALF))
        density = jnp.exp(-0.5 * pre * pre) * DENSITY_FACTOR
        act = (pre * cumulative).astype(BF)
        pre_grad = (act_grad * (cumulative + pre * density)).astype(BF)
        total = total + nn(act, down)
        term = nt(pre_grad, up)
        back = term if back is None else back + term
        down_grad_ref[side] = grown(step, down_grad_ref[side], tn(act, cot))
        up_grad_ref[side] = grown(step, up_grad_ref[side], tn(rows, pre_grad))
    out_ref[...] = total
    grad_in, norm_part = norm_backward(back, normed, inverse_std, norm_ref[2:3, :])
    norm_grad_ref[...] = grown(step, norm_grad_ref[...], norm_part)
    grad_ref[...] = cot.astype(F32) + grad_in

    @pl.when(step == pl.num_programs(0) - 1)
    def _():
        for apart in range(INNER):
            for outer in range(OUTER):
                row, lane, down_row = places(apart, outer)
                for side, halves in enumerate((own_refs, sent_refs)):
                    ref = halves[apart // 2]
                    up = up_grad_ref[side, pl.ds(row, 48), pl.ds(lane, D)]
                    down = down_grad_ref[side, pl.ds(down_row, 48), :]
                    ref[apart % 2, outer, 0] = up.astype(BF)
                    ref[apart % 2, outer, 1] = down.astype(BF)


def mlp(place, middle, second_rows, cotangent, norm_params, slabs):
    rows = middle.shape[0]
    slab = pl.BlockSpec((OUTER, 2, 48, D), lambda i: (0, 0, 0, 0))
    grads = (INNER // 2, OUTER, 2, 48, D)
    grad = pl.BlockSpec(grads, lambda i: (0, 0, 0, 0, 0))
    tile = pl.BlockSpec((TILE, D), lambda i: (i, 0))
    return pl.pallas_call(
        mlp_kernel,
        grid=(rows // TILE,),
        in_specs=[
            pl.BlockSpec(memory_space=pltpu.SMEM),
            tile,
            tile,
            tile,
            pl.BlockSpec((4, D), lambda i: (0, 0)),
            *[slab] * 2 * INNER,
        ],
        out_specs=[tile, tile, pl.BlockSpec((2, D), lambda i: (0, 0)), *[grad] * 4],
        out_shape=[
            jax.ShapeDtypeStruct((rows, D), F32),
            pltpu.HBM((rows, D), F32),
            jax.ShapeDtypeStruct((2, D), F32),
            *[jax.ShapeDtypeStruct(grads, BF)] * 4,
        ],
        scratch_shapes=[
            pltpu.VMEM((2, D, MLP // 2), BF),
            pltpu.VMEM((2, MLP // 2, D), BF),
            pltpu.VMEM((2, D, MLP // 2), F32),
            pltpu.VMEM((2, MLP // 2, D), F32),
        ],
        compiler_params=pltpu.CompilerParams(vmem_limit_bytes=VMEM_LIMIT),
        cost_estimate=pl.CostEstimate(
            flops=12 * rows * D * MLP, bytes_accessed=20 << 20, transcendentals=2 * rows * MLP
        ),
        name="mlp",
    )(place, middle, second_rows, cotangent, in_hbm(norm_params), *slabs)


def attn_backward_kernel(
    place_ref, own_mask_ref, other_mask_ref, x_ref, grad_ref, prob_ref, qkv_ref, out_ref,
    norm_ref, later_norm_ref, wqkv_ref, wo_ref,
    dqkv_ref, own_grad_ref, sent_grad_ref, norm_grad_ref,
    cross_ref, column_ref, wo_grad_ref,
):
    step = pl.program_id(0)

    normed, _ = normalize(x_ref[...].astype(F32))
    low_grad = grad_ref[...].astype(BF)
    head_out = out_ref[...]
    wo_grad_ref[...] = grown(step, wo_grad_ref[...], tn(head_out, low_grad))
    whole_grad = nt(low_grad, wo_ref[...]).astype(BF)
    first, second = lane_halves()
    first_wide, second_wide = first.astype(F32), second.astype(F32)
    tasks = [(image, pair) for image in range(IMAGES) for pair in range(PAIRS)]

    def places(task):
        image, pair = task
        here = slice(S * image, S * image + S)
        return here, *(slice(D * t + PAIR * pair, D * t + PAIR * (pair + 1)) for t in range(3))

    def get_pair_grad(task):
        here, lanes, _, _ = places(task)
        mask = mask_lanes(place_ref, own_mask_ref, other_mask_ref, IMAGES * step + task[0], task[1])
        grad = whole_grad[here, lanes] * mask.astype(BF)
        dots = grad.astype(F32) * head_out[here, lanes].astype(F32)
        first_dot = jnp.sum(dots * first_wide, axis=-1, keepdims=True)
        second_dot = jnp.sum(dots * second_wide, axis=-1, keepdims=True)
        return stacked(grad, first, second), jnp.concatenate([first_dot, second_dot], axis=0)

    pair_grads = [get_pair_grad(task) for task in tasks]
    prob_grads = [
        nt(pair_grad[0], qkv_ref[places(task)[0], places(task)[3]])
        for task, pair_grad in zip(tasks, pair_grads)
    ]
    score_grads = [
        (prob_ref[task].astype(F32) * (prob_grad - pair_grad[1])).astype(BF)
        for task, prob_grad, pair_grad in zip(tasks, prob_grads, pair_grads)
    ]
    for task, score_grad, (pair_grad, _) in zip(tasks, score_grads, pair_grads):
        here, query_lanes, key_lanes, value_lanes = places(task)
        keys = qkv_ref[here, key_lanes]
        queries = stacked(qkv_ref[here, query_lanes], first, second)
        query_grad = nn(score_grad[:S], keys * first) + nn(score_grad[S:], keys * second)
        key_grad = nn(jnp.transpose(queries), score_grad)
        value_grad = nn(jnp.transpose(pair_grad), prob_ref[task])
        dqkv_ref[here, query_lanes] = query_grad.astype(BF)
        dqkv_ref[here, key_lanes] = jnp.transpose(key_grad).astype(BF)
        dqkv_ref[here, value_lanes] = jnp.transpose(value_grad).astype(BF)
    dqkv = dqkv_ref[...]
    cross_ref[...] = grown(step, cross_ref[...], tn(normed.astype(BF), dqkv))
    columns = jnp.sum(dqkv.astype(F32), axis=0, keepdims=True)
    column_ref[...] = grown(step, column_ref[...], columns)

    @pl.when(step == pl.num_programs(0) - 1)
    def _():
        wqkv = wqkv_ref[...]
        products = wqkv.astype(F32) * cross_ref[...]
        gain_grad = jnp.sum(products, axis=1, keepdims=True)
        gain_grad = jnp.transpose(jnp.broadcast_to(gain_grad, (D, 128)))
        columns = column_ref[...]
        shift_grad = nt(jnp.concatenate(split(jnp.broadcast_to(columns, (8, 3 * D)))), wqkv)
        norm_grad_ref[0:1, :] = gain_grad[0:1]
        norm_grad_ref[1:2, :] = shift_grad[0:1] + shift_grad[8:9]
        norm_grad_ref[2:4, :] = later_norm_ref[...]
        gain = jnp.transpose(jnp.broadcast_to(norm_ref[0:1, :], (128, D)))[:, :1]
        shift = jnp.transpose(jnp.broadcast_to(norm_ref[1:2, :], (128, D)))[:, :1]
        cross_ref[...] = cross_ref[...] * gain + shift * columns
        for side, slab_grads in enumerate((own_grad_ref, sent_grad_ref)):
            for slab in range(12):
                pieces = []
                for unit in (2 * slab, 2 * slab + 1):
                    row, part = divmod(unit, 3)
                    piece = cross_ref[48 * row : 48 * row + 48, D * part : D * part + D]
                    piece = piece[:, HALF * side : HALF * side + HALF]
                    pieces.append(piece * 0.125 if part == 0 else piece)
                slab_grads[slab_at(slab)] = jnp.concatenate(pieces, axis=1).astype(BF)
            for row in range(HALF // 48):
                start = HALF * side + 48 * row
                slab_grads[slab_at(12 + row)] = wo_grad_ref[start : start + 48, :].astype(BF)
        sent_grad_ref[SLABS, :NORM_ROWS] = jnp.concatenate(split(norm_grad_ref[...]), axis=0)
        sent_grad_ref[SLABS, NORM_ROWS:] = jnp.zeros((48 - NORM_ROWS, D), BF)


def attn_backward(
    place, own_mask, other_mask, tokens, grad, prob, qkv, out, norm_params, later_norms, wqkv, wo
):
    rows = tokens.shape[0]
    tile = pl.BlockSpec((TILE, D), lambda i: (i, 0))
    smem = pl.BlockSpec(memory_space=pltpu.SMEM)
    return pl.pallas_call(
        attn_backward_kernel,
        grid=(rows // TILE,),
        in_specs=[
            smem,
            smem,
            smem,
            tile,
            tile,
            pl.BlockSpec((IMAGES, PAIRS, 2 * S, S), lambda i: (i, 0, 0, 0)),
            pl.BlockSpec((TILE, 3 * D), lambda i: (i, 0)),
            tile,
            pl.BlockSpec((4, D), lambda i: (0, 0)),
            pl.BlockSpec((2, D), lambda i: (0, 0)),
            pl.BlockSpec((D, 3 * D), lambda i: (0, 0)),
            pl.BlockSpec((D, D), lambda i: (0, 0)),
        ],
        out_specs=[
            pl.BlockSpec((TILE, 3 * D), lambda i: (i, 0)),
            pl.BlockSpec((SLABS, 48, D), lambda i: (0, 0, 0)),
            pl.BlockSpec((SLABS + 1, 48, D), lambda i: (0, 0, 0)),
            pl.BlockSpec((4, D), lambda i: (0, 0)),
        ],
        out_shape=[
            pltpu.HBM((rows, 3 * D), BF),
            jax.ShapeDtypeStruct((SLABS, 48, D), BF),
            jax.ShapeDtypeStruct((SLABS + 1, 48, D), BF),
            jax.ShapeDtypeStruct((4, D), F32),
        ],
        scratch_shapes=[
            pltpu.VMEM((D, 3 * D), F32),
            pltpu.VMEM((1, 3 * D), F32),
            pltpu.VMEM((D, D), F32),
        ],
        compiler_params=pltpu.CompilerParams(vmem_limit_bytes=VMEM_LIMIT),
        cost_estimate=pl.CostEstimate(
            flops=rows * D * (10 * D + 32 * S), bytes_accessed=20 << 20, transcendentals=0
        ),
        name="attn_backward",
    )(
        place, own_mask, other_mask,
        tokens, in_hbm(grad), prob, qkv, out, in_hbm(norm_params), in_hbm(later_norms), wqkv, wo,
    )


def input_grad_kernel(x_ref, grad_ref, dqkv_ref, norm_ref, wqkv_ref, out_ref):
    normed, inverse_std = normalize(x_ref[...].astype(F32))
    back = nt(dqkv_ref[...], wqkv_ref[...]) * norm_ref[0:1, :]
    mean_first = jnp.mean(back, axis=-1, keepdims=True)
    mean_second = jnp.mean(back * normed, axis=-1, keepdims=True)
    out_ref[...] = grad_ref[...] + inverse_std * (back - mean_first - normed * mean_second)


def input_gradient(tokens, grad, dqkv, norm_params, wqkv):
    rows = tokens.shape[0]
    tile = pl.BlockSpec((INPUT_TILE, D), lambda i: (i, 0))
    return pl.pallas_call(
        input_grad_kernel,
        grid=(rows // INPUT_TILE,),
        in_specs=[
            tile,
            tile,
            pl.BlockSpec((INPUT_TILE, 3 * D), lambda i: (i, 0)),
            pl.BlockSpec((4, D), lambda i: (0, 0)),
            pl.BlockSpec((D, 3 * D), lambda i: (0, 0)),
        ],
        out_specs=tile,
        out_shape=jax.ShapeDtypeStruct((rows, D), F32),
        compiler_params=pltpu.CompilerParams(vmem_limit_bytes=VMEM_LIMIT),
        cost_estimate=pl.CostEstimate(
            flops=rows * D * 6 * D, bytes_accessed=10 << 20, transcendentals=0
        ),
        name="input_gradient",
    )(in_hbm(tokens), in_hbm(grad), in_hbm(dqkv), in_hbm(norm_params), in_hbm(wqkv))


def pack_kernel(weight_ref, out_ref):
    groups, count, _, _ = weight_ref.shape
    for group in range(groups):
        blocks = [weight_ref[group, block] for block in range(count)]
        slab = jnp.concatenate(blocks, axis=1).astype(BF)
        for copy in range(OUTER):
            out_ref[copy, group] = slab


def pack(weights, first, groups):
    _, count, edge, _ = weights.shape
    shape = (OUTER, groups, edge, count * edge)
    return pl.pallas_call(
        pack_kernel,
        grid=(1,),
        in_specs=[
            pl.BlockSpec(
                (pl.Element(groups), pl.Element(count), pl.Element(edge), pl.Element(edge)),
                lambda i: (first, 0, 0, 0),
            )
        ],
        out_specs=pl.BlockSpec(shape, lambda i: (0, 0, 0, 0)),
        out_shape=jax.ShapeDtypeStruct(shape, BF),
        compiler_params=pltpu.CompilerParams(vmem_limit_bytes=SMALL_VMEM),
        name="pack",
    )(in_hbm(weights))


def add_kernel(own_ref, received_ref, *out_refs):
    for apart, out_ref in enumerate(out_refs):
        total = own_ref[apart].astype(F32) + received_ref[apart].astype(F32)
        out_ref[...] = total.astype(BF)


def add_late(own, received):
    return pl.pallas_call(
        add_kernel,
        out_shape=[jax.ShapeDtypeStruct(own.shape[1:], BF)] * own.shape[0],
        compiler_params=pltpu.CompilerParams(vmem_limit_bytes=SMALL_VMEM),
        name="add_late",
    )(own, received)


def sum_kernel(*refs):
    *in_refs, out_ref = refs
    total = in_refs[0][...].astype(F32)
    for ref in in_refs[1:]:
        total = total + ref[...].astype(F32)
    out_ref[...] = total.astype(BF)


def sum_late(pieces):
    return pl.pallas_call(
        sum_kernel,
        out_shape=jax.ShapeDtypeStruct(pieces[0].shape, BF),
        compiler_params=pltpu.CompilerParams(vmem_limit_bytes=SMALL_VMEM),
        name="sum_late",
    )(*pieces)


def combine_kernel(place_ref, own_ref, received_ref, norm_ref, *out_refs):
    norms = received_ref[SLABS, :NORM_ROWS].astype(F32)
    norms = norm_ref[...] + (norms[:4] + norms[4:])
    rows = jnp.concatenate(split(norms), axis=0)
    for apart, out_ref in enumerate(out_refs):
        start = OUTER * (place_ref[1] ^ apart)
        for outer in range(OUTER):
            total = own_ref[start + outer].astype(F32) + received_ref[start + outer].astype(F32)
            out_ref[48 * outer : 48 * outer + 48, :] = total.astype(BF)
        out_ref[48 * OUTER :, :] = rows


def combine(place, own, received, norms):
    vmem = pl.BlockSpec(memory_space=pltpu.VMEM)
    shape = jax.ShapeDtypeStruct((48 * OUTER + NORM_ROWS, D), BF)
    return pl.pallas_call(
        combine_kernel,
        in_specs=[pl.BlockSpec(memory_space=pltpu.SMEM), vmem, vmem, vmem],
        out_shape=[shape] * INNER,
        compiler_params=pltpu.CompilerParams(vmem_limit_bytes=SMALL_VMEM),
        name="combine",
    )(place, own, received, norms)


def join_kernel(*refs):
    *early_refs, out_ref = refs
    total = early_refs[0][...].astype(F32)
    for ref in early_refs[1:]:
        total = total + ref[...].astype(F32)
    norms = total[48 * OUTER : 48 * OUTER + 4] + total[48 * OUTER + 4 :]
    for outer in range(OUTER):
        out_ref[outer, :48] = total[48 * outer : 48 * outer + 48].astype(BF)
        out_ref[outer, 48:] = jnp.concatenate(split(norms), axis=0)


def join(early):
    return pl.pallas_call(
        join_kernel,
        out_shape=jax.ShapeDtypeStruct((OUTER, 48 + NORM_ROWS, D), BF),
        compiler_params=pltpu.CompilerParams(vmem_limit_bytes=SMALL_VMEM),
        name="join",
    )(*early)


def split(values):
    high = values.astype(BF)
    return high, (values - high.astype(F32)).astype(BF)


def stack(*pieces):
    return jnp.concatenate(pieces, axis=0)


def cut_rows(values, number):
    edge = values.shape[0] // number
    return [values[edge * i : edge * i + edge] for i in range(number)]


def product(left, right):
    high, low = left
    right_high, right_low = right
    one, two = cut_rows(nn(stack(high, low), right_high), 2)
    return one + (two + nn(high, right_low))


def two_products(left, middle, right):
    right_high, right_low = right
    both = cut_rows(nn(stack(middle[0], middle[1], left[0], left[1]), right_high), 4)
    high = cut_rows(nn(stack(middle[0], left[0]), right_low), 2)
    return both[2] + (both[3] + high[1]), both[0] + (both[1] + high[0])


def update_norms(scale, total, param_ref, state_ref, grad_ref, new_state_ref, new_ref):
    grads = total * scale
    state = 0.5 * state_ref[...] + 0.5 * grads * grads
    grad_ref[...] = grads
    new_state_ref[...] = state
    new_ref[...] = param_ref[...] - 0.2 * grads / jnp.sqrt(state)


def shampoo_kernel(scale, with_norms, received_ref, weight_ref, left_ref, right_ref, *refs):
    if with_norms:
        norm_ins, norm_outs, refs = refs[:2], refs[-5:-2], refs[:-5] + refs[-2:]
    out_grad_ref, left_new_ref, right_new_ref, new_weight_ref, root_ref, power_ref = refs[-6:]
    groups, count, edge = weight_ref.shape[:3]

    received = received_ref[0].astype(F32)
    for number in range(1, received_ref.shape[0]):
        received = received + received_ref[number].astype(F32)
    if with_norms:
        norms = received[0, edge:]
        update_norms(scale, norms[:4] + norms[4:], *norm_ins, *norm_outs)
    pack = min(PACK, count)
    width = pack * edge
    places = [(g, pack * n) for g in range(groups) for n in range(count // pack)]
    packs = len(places)

    def block_of(shape, dim):
        return lax.broadcasted_iota(jnp.int32, shape, dim) // edge

    row = lax.broadcasted_iota(jnp.int32, (edge, width), 0)
    lane = lax.broadcasted_iota(jnp.int32, (edge, width), 1)
    identity = (lane % edge == row).astype(F32)
    same = (block_of((width, width), 0) == block_of((width, width), 1)).astype(BF)
    lane_block = block_of((1, width), 1)

    def spread(pieces):
        return tuple(stack(*[piece] * pack) * same for piece in pieces)

    def cut(packed, index):
        return packed[:, edge * index : edge * index + edge]

    def beside(ref, place):
        return jnp.concatenate([ref[place[0], place[1] + i] for i in range(pack)], axis=1)

    grads, parts = [], []
    for group, start in places:
        grad = received[group, :edge, edge * start : edge * start + width] * scale
        blocks = [cut(grad, index) for index in range(pack)]
        for index in range(pack):
            out_grad_ref[group, start + index] = blocks[index]
        grad_t = jnp.concatenate([jnp.transpose(block) for block in blocks], axis=1)
        one, two = split(grad), split(grad_t)
        one_diagonal, two_diagonal = spread(one), spread(two)
        grads.append(one_diagonal)
        parts.append((left_ref, left_new_ref, one, two_diagonal))
        parts.append((right_ref, right_new_ref, two, one_diagonal))
    grams = [product(left, right) for _, _, left, right in parts]
    for slot, (old_ref, new_ref, _, _) in enumerate(parts):
        group, start = places[slot // 2]
        new = 0.5 * beside(old_ref, places[slot // 2]) + 0.5 * grams[slot]
        for index in range(pack):
            new_ref[group, start + index] = cut(new, index)
        columns = jnp.sum(new * new, axis=0, keepdims=True)
        squares = jnp.zeros((1, width), F32)
        for index in range(pack):
            inside = lane_block == index
            part = jnp.sum(jnp.where(inside, columns, 0.0), axis=1, keepdims=True)
            squares = jnp.where(inside, part, squares)
        factor = 2.5 / jnp.sqrt(squares)
        root_ref[slot] = jnp.broadcast_to(jnp.sqrt(jnp.sqrt(factor)), (edge, width))
        power_ref[slot] = factor * new
    slots = range(2 * packs)

    def advance(first):
        powers = [power_ref[slot] for slot in slots]
        middles = [split((5.0 * identity - power) * 0.25) for power in powers]
        rights = [spread(middle) for middle in middles]
        powers = [split(power) for power in powers]
        if first:
            squares = [product(middles[s], rights[s]) for s in slots]
            for slot in slots:
                root_ref[slot] *= (5.0 * identity - power_ref[slot]) * 0.25
        else:
            roots = [split(root_ref[slot]) for slot in slots]
            both = [two_products(roots[s], middles[s], rights[s]) for s in slots]
            squares = [pair[1] for pair in both]
            for slot in slots:
                root_ref[slot] = both[slot][0]
        rights = [spread(split(square)) for square in squares]
        powers = [split(product(powers[s], rights[s])) for s in slots]
        for slot in slots:
            power_ref[slot] = product(powers[slot], rights[slot])

    advance(True)
    for _ in range(ITERS - 2):
        advance(False)
    rights = [spread(split((5.0 * identity - power_ref[slot]) * 0.25)) for slot in slots]
    for slot in slots:
        root_ref[slot] = product(split(root_ref[slot]), rights[slot])
    steps = [product(split(root_ref[2 * n]), grads[n]) for n in range(packs)]
    rights = [spread(split(root_ref[2 * n + 1])) for n in range(packs)]
    steps = [product(split(steps[n]), rights[n]) for n in range(packs)]
    for number, (group, start) in enumerate(places):
        for index in range(pack):
            step = 0.25 * cut(steps[number], index)
            new_weight_ref[group, start + index] = weight_ref[group, start + index] - step


def shampoo(received, weights, stat_left, stat_right, scale, first, earlier=(), norms=()):
    groups = received.shape[1]
    _, count, edge, _ = weights.shape
    slots = 2 * groups * count // min(PACK, count)
    width = min(PACK, count) * edge
    block = pl.BlockSpec(
        (pl.Element(groups), pl.Element(count), pl.Element(edge), pl.Element(edge)),
        lambda i: (first, 0, 0, 0),
    )
    shape = jax.ShapeDtypeStruct(weights.shape, F32)
    norm = pl.BlockSpec((4, D), lambda i: (0, 0))
    norm_outs = 3 if norms else 0
    ins = 4 + len(norms)
    return pl.pallas_call(
        lambda *refs: shampoo_kernel(scale, bool(norms), *refs),
        grid=(1,),
        in_specs=[
            pl.BlockSpec(received.shape, lambda i: (0, 0, 0, 0)),
            *[block] * 3,
            *[norm] * len(norms),
            *[pl.BlockSpec(memory_space=pl.ANY)] * len(earlier),
        ],
        out_specs=[block] * 4 + [norm] * norm_outs,
        out_shape=[shape] * 4 + [jax.ShapeDtypeStruct((4, D), F32)] * norm_outs,
        scratch_shapes=[
            pltpu.VMEM((slots, edge, width), F32),
            pltpu.VMEM((slots, edge, width), F32),
        ],
        input_output_aliases={ins + i: i for i in range(len(earlier))},
        compiler_params=pltpu.CompilerParams(vmem_limit_bytes=SHAMPOO_VMEM),
        cost_estimate=pl.CostEstimate(
            flops=groups * (3 << 30), bytes_accessed=4 << 20, transcendentals=0
        ),
        name="shampoo",
    )(received, weights, stat_left, stat_right, *norms, *earlier)


def swap_heads(values):
    return lax.ppermute(values, "head", [(0, 1), (1, 0)])


def to_all(values, axis):
    return lax.all_to_all(values, axis, 0, 0)


def across(values, apart):
    pairs = [(i, i ^ apart) for i in range(INNER)]
    return lax.ppermute(values, "inner", pairs)


def from_all(values):
    return [values] + [across(values, apart) for apart in range(1, INNER)]


def gather_slabs(weights, small):
    early = to_all(pack(weights, 0, 1), "outer")[:, 0]
    early, late = lax.optimization_barrier((early, pack(weights, 1, 2)))
    late = to_all(late, "outer")
    early = from_all(early)
    early[1], late, small = lax.optimization_barrier((early[1], late, small))
    return early, from_all(late), small


def gather_blocks(local):
    groups, _, edge, _ = local.shape
    blocks = lax.all_gather(local, ("outer", "inner"), axis=1, tiled=True)
    blocks = blocks.reshape(groups, SLABS // INNER, INNER, D // edge, edge, edge)
    slabs = blocks.transpose(2, 1, 0, 4, 3, 5).reshape(SLABS, groups, edge, D)
    return slabs if groups > 1 else slabs[:, 0]


def scatter_blocks(slabs, count, edge):
    groups = slabs.shape[1]
    blocks = slabs.reshape(INNER, SLABS // INNER, groups, edge, D // edge, edge)
    blocks = blocks.transpose(2, 1, 0, 4, 3, 5).reshape(groups, SLABS * (D // edge), edge, edge)
    owned = lax.psum_scatter(blocks, ("outer", "inner"), scatter_dimension=1, tiled=True)
    return owned.transpose(0, 2, 1, 3).reshape(groups, edge, count * edge)


def per_device(
    tokens,
    cotangent,
    token_counts,
    head_mask,
    norm_params,
    norm_state,
    weights,
    stat_left,
    stat_right,
):
    weights, stat_left, stat_right = weights[0], stat_left[0], stat_right[0]
    _, count, edge, _ = weights.shape
    whole_slabs = count * edge == D
    other_mask = swap_heads(head_mask)
    inner = lax.axis_index("inner") if whole_slabs else 0
    place = jnp.concatenate([jnp.stack([lax.axis_index("head"), inner]), token_counts])
    if whole_slabs:
        early, late, (other_mask, place) = gather_slabs(weights, (other_mask, place))
    else:
        local = weights.astype(BF)
        early = jnp.split(gather_blocks(local[:1]), INNER)
        late = jnp.split(gather_blocks(local[1:]), INNER)
    early, late = list(early), list(late)
    masks = (head_mask, other_mask)
    early += [swap_heads(piece) for piece in early]
    prob, qkv, out, middle, second_rows, wqkv, wo = attn_forward(
        place, *masks, tokens, norm_params, early
    )
    late[1:], middle = lax.optimization_barrier((late[1:], middle))
    late += [swap_heads(piece) for piece in late]
    block_out, middle_grad, norm_two, *late_sums = mlp(
        place, middle, second_rows, cotangent, norm_params, late
    )
    own_late, late_received = late_sums[:2], [swap_heads(sent) for sent in late_sums[2:]]
    if whole_slabs:
        far = add_late(own_late[1], late_received[1])
        near = add_late(own_late[0], late_received[0])
        far = [across(far[number], 2 + number) for number in range(2)]
        near, middle_grad = lax.optimization_barrier((list(near), middle_grad))
        late_grads = [near[0], across(near[1], 1), *far]
    dqkv, own_early, sent_early, norm_sums = attn_backward(
        place, *masks, tokens, middle_grad, prob, qkv, out, norm_params, norm_two, wqkv, wo
    )
    if whole_slabs:
        late_grads, sent_early = lax.optimization_barrier((late_grads, sent_early))
    early_received = swap_heads(sent_early)
    devices = lax.axis_size("outer") * lax.axis_size("inner") * lax.axis_size("head")
    scale = 1.0 / math.sqrt(tokens.shape[0] * devices)
    state = (weights, stat_left, stat_right, scale)
    if whole_slabs:
        late_grads = to_all(sum_late(late_grads), "outer")
        early_grads = list(combine(place, own_early, early_received, norm_sums))
        early_grads, dqkv = lax.optimization_barrier((early_grads, dqkv))
        early_grads[1:] = [across(early_grads[apart], apart) for apart in range(1, INNER)]
        input_grad = input_gradient(tokens, middle_grad, dqkv, norm_params, wqkv)
        early_grads, input_grad = lax.optimization_barrier((early_grads, input_grad))
        joined, late_grads = lax.optimization_barrier((join(early_grads), late_grads))
        joined = to_all(joined, "outer")[:, None]
        results = shampoo(late_grads, *state, 1)
        results = shampoo(joined, *state, 0, results, (norm_params, norm_state))
    else:
        input_grad = input_gradient(tokens, middle_grad, dqkv, norm_params, wqkv)
        early_slabs = own_early.astype(F32) + early_received[:SLABS].astype(F32)
        late_slabs = jnp.concatenate(own_late).astype(F32) + jnp.concatenate(late_received)
        late_slabs = late_slabs.reshape(SLABS, 2, edge, D)
        slabs = jnp.concatenate([early_slabs[:, None], late_slabs], axis=1).astype(BF)
        owned = scatter_blocks(slabs, count, edge)
        results = list(shampoo(owned[None], *state, 0))
        norm_grads = lax.psum(norm_sums, ("outer", "inner", "head")) * scale
        state_new = 0.5 * norm_state + 0.5 * norm_grads * norm_grads
        results += [norm_grads, state_new, norm_params - 0.2 * norm_grads / jnp.sqrt(state_new)]
    return (block_out, input_grad, *[result[None] for result in results[:4]], *results[4:])


def solution(mesh):
    shape = (mesh.shape["dp"] // INNER, INNER, mesh.shape["head"])
    split_mesh = Mesh(mesh.devices.reshape(shape), ("outer", "inner", "head"))
    group = ("outer", "inner")
    blocks = P("head", None, group, None, None)
    rows = P(group + ("head",), None)
    return jax.shard_map(
        per_device,
        mesh=split_mesh,
        in_specs=(rows, rows, P(group), P(group, "head"), P(), P(), blocks, blocks, blocks),
        out_specs=(rows, rows, blocks, blocks, blocks, blocks, P(), P(), P()),
        check_vma=False,
    )
```
